32 devices in a mesh: row: 4 (over y, x), col: 8 (over z, core).
Axes of the slice: x: 2, y: 2, z: 4, core: 2. Of those that a mesh axis runs over, the one named last changes fastest.
Arguments:
- tokens: bfloat16 [16384, 1024], P(('row', 'col')), may hold values from -6 to 6
- blocks: int32 [16384], P(('row', 'col')), may hold values from 0 to 127, never falling along the last dimension, each value on 1 to 256 neighbouring positions
- w_qkv: bfloat16 [1024, 3, 1024], P('row', None, 'col'), may hold values from -0.25 to 0.25
- b_qv: bfloat16 [2, 1024], P(None, 'col'), may hold values from -1.5 to 1.5
- w_out: bfloat16 [1024, 1024], P('col', 'row'), may hold values from -0.5 to 0.5
- b_out: bfloat16 [1024], replicated, may hold values from -3 to 3
- w_up: bfloat16 [4096, 1024], P('col', 'row'), may hold values from -0.1875 to 0.1875
- b_up: bfloat16 [4096], P('col'), may hold values from -3 to 3
- w_down: bfloat16 [4096, 1024], P('col', 'row'), may hold values from -0.09375 to 0.09375
- b_down: bfloat16 [1024], replicated, may hold values from -3 to 3
- gain1: bfloat16 [1024], replicated, may hold values from 0.5 to 1.5
- shift1: bfloat16 [1024], replicated, may hold values from -1.5 to 1.5
- gain2: bfloat16 [1024], replicated, may hold values from 0.5 to 1.5
- shift2: bfloat16 [1024], replicated, may hold values from -1.5 to 1.5
- grad_out: bfloat16 [16384, 1024], P(('row', 'col')), may hold values from -9 to 9
Outputs:
- output: bfloat16 [16384, 1024], P(('row', 'col'))
- grad_tokens: float32 [16384, 1024], P(('row', 'col'))
- grad_w_qkv: float32 [1024, 3, 1024], P('row', None, 'col')
- grad_b_qv: float32 [2, 1024], P(None, 'col')
- grad_w_out: float32 [1024, 1024], P('col', 'row')
- grad_b_out: float32 [1024], replicated
- grad_w_up: float32 [4096, 1024], P('col', 'row')
- grad_b_up: float32 [4096], P('col')
- grad_w_down: float32 [4096, 1024], P('col', 'row')
- grad_b_down: float32 [1024], replicated
- grad_gain1: float32 [1024], replicated
- grad_shift1: float32 [1024], replicated
- grad_gain2: float32 [1024], replicated
- grad_shift2: float32 [1024], replicated
The draws below stay inside these ranges and needn't reach their ends.
Inputs may be any that keep to these rules, and one draw needn't show every extreme that they name: `blocks`: block indices never fall along the tokens and every index from the least to the largest occurs; each block holds 1 to 256 tokens, and one holds exactly 256. A block may run across the end of a sequence.
All inputs are finite; a program needn't handle non-finite values.
Results may differ from the reference program's by a relative error of at most 0.012.
The reference program's roundings to bfloat16 on the way count: a program that leaves them out, or rounds other values in their place, can miss the bound.
Values may be sent and summed in bfloat16 or wider, within the bound.
A program may use at most 256 MiB of HBM per device.

```python
import math
import jax
import jax.numpy as jnp
import numpy as np
from jax import lax

D = 1024
H = 16
HD = 64
FF = 4096
SEQ_LEN = 4096
BLOCK = 256
TOKENS = 16384


def draw_grad_out(key, part):
    place = jnp.arange(TOKENS, dtype=jnp.float32) / TOKENS
    base = jnp.clip(jax.random.normal(key, (TOKENS, D), jnp.float32), -5.0, 5.0)
    factor = jnp.exp(place * 1.1) * 0.6
    return (base * factor[:, None]).astype(jnp.bfloat16)


def block_levels(own_key, shape, split, low, high):
    factor_of, own = 1.0, jax.random.fold_in(own_key, 6)
    for axis_at, parts in split:
        heights = jnp.exp(jax.random.uniform(jax.random.fold_in(own, axis_at), (parts,), jnp.float32, low / len(split), high / len(split)))
        factor_of = factor_of * jnp.repeat(heights, shape[axis_at] // parts).reshape([-1 if axis == axis_at else 1 for axis in range(len(shape))])
    return factor_of


def profile(amount, total, bound, lean):
    portions = [(1 << 20) // math.isqrt(grade ** lean) + 1 for grade in range(2, amount + 1)]
    surplus, holding = total - bound - (amount - 1), [1] * (amount - 1)
    while surplus > 0:
        movable = [i for i in range(amount - 1) if holding[i] < bound]
        mass, left = sum([portions[i] for i in movable]), surplus
        for i in movable:
            more = min(bound - holding[i], max(1, left * portions[i] // mass), surplus)
            holding[i] = holding[i] + more
            surplus = surplus - more
    return np.array([bound] + holding)


def ragged(rng, count, total, most, slope):
    if count == 2:
        one = jax.random.randint(rng, (), max(1, total - most), min(most, total - 1) + 1)
        return jnp.stack([one, total - one])
    lengths = jnp.asarray(profile(count, total, most, slope), jnp.int32)
    couples = (count - 1) // 2
    giver, receiver = lengths[1:1 + 2 * couples:2], lengths[2:2 + 2 * couples:2]
    slack = jnp.minimum(giver - 1, most - receiver)
    shifted = jax.random.randint(jax.random.fold_in(rng, 1), (couples,), 0, 1 << 20) % (slack + 1)
    lengths = lengths.at[1:1 + 2 * couples:2].set(giver - shifted).at[2:2 + 2 * couples:2].set(receiver + shifted)
    return lengths[jax.random.permutation(jax.random.fold_in(rng, 2), count)]


def gaussian(own_key, shape, deviation, bound, pieces=(), kind=jnp.bfloat16):
    values = jax.random.normal(own_key, shape, jnp.float32) * deviation
    if len(pieces) > 0:
        values = block_levels(own_key, shape, pieces, -0.22, 0.18) * values
    return jnp.clip(values, min=-bound, max=bound).astype(kind)


def setup_inputs(seed: int = 0) -> dict:
    arg_keys = jax.random.split(jax.random.key(seed), 16)
    tokens = gaussian(arg_keys[0], (TOKENS, D), 1.0, 6.0, ((0, 32),))
    blocks = jnp.searchsorted(jnp.cumsum(ragged(arg_keys[1], 2 * TOKENS // BLOCK, TOKENS, BLOCK, 0)), jnp.arange(TOKENS), side="right").astype(jnp.int32)
    w_qkv = gaussian(arg_keys[2], (D, 3, D), (D // 2) ** -0.5, 0.25, ((0, 4), (2, 8)))
    b_qv = gaussian(arg_keys[3], (2, D), 0.1, 1.5, ((1, 8),))
    w_out = gaussian(arg_keys[4], (D, D), (D // 8) ** -0.5, 0.5, ((0, 8), (1, 4)))
    b_out = gaussian(arg_keys[5], (D,), 0.5, 3.0)
    w_up = gaussian(arg_keys[6], (FF, D), D ** -0.5, 0.1875, ((0, 8), (1, 4)))
    b_up = gaussian(arg_keys[7], (FF,), 0.5, 3.0, ((0, 8),))
    w_down = gaussian(arg_keys[8], (FF, D), FF ** -0.5, 0.09375, ((0, 8), (1, 4)))
    b_down = gaussian(arg_keys[9], (D,), 0.5, 3.0)
    gain1 = jnp.clip(jax.random.uniform(arg_keys[10], (D,), jnp.float32, 0.5, 1.5), 0.5, 1.5).astype(jnp.bfloat16)
    shift1 = gaussian(arg_keys[11], (D,), 0.1, 1.5)
    gain2 = jnp.clip(jax.random.uniform(arg_keys[12], (D,), jnp.float32, 0.5, 1.5), 0.5, 1.5).astype(jnp.bfloat16)
    shift2 = gaussian(arg_keys[13], (D,), 0.1, 1.5)
    grad_out = draw_grad_out(jax.random.fold_in(arg_keys[15], 71), 0)
    return dict(tokens=tokens, blocks=blocks, w_qkv=w_qkv, b_qv=b_qv, w_out=w_out, b_out=b_out, w_up=w_up, b_up=b_up, w_down=w_down, b_down=b_down, gain1=gain1, shift1=shift1, gain2=gain2, shift2=shift2, grad_out=grad_out)


@jax.custom_vjp
def low(v):
    return lax.optimization_barrier(v.astype(jnp.bfloat16)).astype(jnp.float32)

@jax.custom_vjp
def low_back(v):
    return v

def low_keep(v):
    return (low(v), None)

def low_pass(kept, grad):
    return (grad,)

def back_keep(v):
    return (v, None)

def back_low(kept, grad):
    return (low(grad),)
low.defvjp(low_keep, low_pass)
low_back.defvjp(back_keep, back_low)
HIGH = lax.Precision.HIGHEST
EPS = 1e-05

def norm(values_in, gain, shift):
    center = lax.optimization_barrier(jnp.mean(values_in, axis=-1, keepdims=True))
    centered = values_in - center
    spread = lax.optimization_barrier(jnp.mean(centered * centered, axis=-1, keepdims=True))
    return centered * lax.rsqrt(spread + EPS) * gain + shift

def attend(queries, keys, values, block_ids):
    length = queries.shape[0]
    query_rows = min(512, length)
    score_scale = HD ** (-0.5)

    def one_block(row_start):
        query_part = lax.dynamic_slice_in_dim(queries, row_start, query_rows, 0)
        block_part = lax.dynamic_slice_in_dim(block_ids, row_start, query_rows, 0)
        raw_scores = jnp.einsum('qhd,khd->hqk', query_part, keys, precision=HIGH)
        allowed = block_part[:, None] >= block_ids[None, :]
        scores = low_back(jnp.where(allowed[None], raw_scores * score_scale, -1e+30))
        probs = low(jax.nn.softmax(scores, axis=-1))
        return jnp.einsum('hqk,khd->qhd', probs, values, precision=HIGH)
    starts = (jnp.arange(length // query_rows) * query_rows).astype(jnp.int32)
    result = lax.map(jax.checkpoint(one_block), starts)
    return result.reshape(length, H, HD)

def layer(seq_in, w_qkv, b_qv, w_out, b_out, w_up, b_up, w_down, b_down, gain1, shift1, gain2, shift2, block_ids):
    length = seq_in.shape[0]
    attn_input = low(norm(seq_in, gain1, shift1))
    mixed = low_back(jnp.dot(attn_input, w_qkv.reshape(D, 3 * D), precision=HIGH)).reshape(length, 3, D)
    queries = low(mixed[:, 0] + b_qv[0]).reshape(length, H, HD)
    keys = low(mixed[:, 1]).reshape(length, H, HD)
    values = low(mixed[:, 2] + b_qv[1]).reshape(length, H, HD)
    heads = low(low_back(attend(queries, keys, values, block_ids))).reshape(length, D)
    resid = seq_in + low_back(jnp.dot(heads, w_out, precision=HIGH)) + b_out
    ffn_input = low(norm(resid, gain2, shift2))
    up_pre = low_back(jnp.dot(ffn_input, w_up.T, precision=HIGH)) + b_up
    hidden = low(jax.nn.gelu(up_pre, approximate=True))
    return resid + low_back(jnp.dot(hidden, w_down, precision=HIGH)) + b_down

def reference(tokens, blocks, w_qkv, b_qv, w_out, b_out, w_up, b_up, w_down, b_down, gain1, shift1, gain2, shift2, grad_out):
    params = tuple((p.astype(jnp.float32) for p in (w_qkv, b_qv, w_out, b_out, w_up, b_up, w_down, b_down, gain1, shift1, gain2, shift2)))
    seq_count = TOKENS // SEQ_LEN
    seq_inputs = tokens.astype(jnp.float32).reshape(seq_count, SEQ_LEN, D)
    seq_grads = grad_out.astype(jnp.float32).reshape(seq_count, SEQ_LEN, D)
    seq_blocks = blocks.reshape(seq_count, SEQ_LEN)

    def step(running, item):
        seq_in, seq_grad, seq_block = item

        def forward(values_in, *weights):
            return layer(values_in, *weights, seq_block)
        result, back = jax.vjp(forward, seq_in, *params)
        grads = back(seq_grad)
        running = tuple((r + g for r, g in zip(running, grads[1:])))
        return (running, (result.astype(jnp.bfloat16), grads[0]))
    zeros = tuple((jnp.zeros(p.shape, jnp.float32) for p in params))
    running, (results, input_grads) = lax.scan(step, zeros, (seq_inputs, seq_grads, seq_blocks))
    return (results.reshape(TOKENS, D), input_grads.reshape(TOKENS, D), running[0], running[1], running[2], running[3], running[4], running[5], running[6], running[7], running[8], running[9], running[10], running[11])
```

```python
import functools

import jax
import jax.numpy as jnp
from jax import lax
from jax.experimental import pallas as pl
from jax.experimental.pallas import tpu as pltpu
from jax.sharding import PartitionSpec as P

HD = 64
SEQ_LEN = 4096
BLOCK = 256
EPS = 1e-05
SCALE = HD ** (-0.5)
SCALE2 = SCALE * 1.4426950408889634
MASKED = -1e30
ONES = 16
MESH = pl.DeviceIdType.MESH
VMEM_LIMIT = 60 << 20

f32 = jnp.float32
bf16 = jnp.bfloat16

NN = (((1,), (0,)), ((), ()))
NT = (((1,), (1,)), ((), ()))
TN = (((0,), (0,)), ((), ()))


def dot(a, b, dims=NN):
    return lax.dot_general(a, b, dims, preferred_element_type=f32)


def flip(x):
    return x.astype(f32).T.astype(bf16)


def params(**more):
    return pltpu.CompilerParams(vmem_limit_bytes=VMEM_LIMIT, **more)


def cost(flops, nbytes, transcendentals=0):
    return pl.CostEstimate(flops=flops, bytes_accessed=nbytes, transcendentals=transcendentals)


def whole(shape):
    return pl.BlockSpec(shape, lambda *_: (0,) * len(shape))


def moments(v):
    center = jnp.mean(v, axis=-1, keepdims=True)
    centered = v - center
    spread = jnp.mean(centered * centered, axis=-1, keepdims=True)
    inv = lax.rsqrt(spread + EPS)
    return centered * inv, inv


def norm_back(xhat, inv, e):
    return inv * (
        e - jnp.mean(e, axis=-1, keepdims=True) - xhat * jnp.mean(e * xhat, axis=-1, keepdims=True)
    )


def gather_kernel(
    rows, cols, x_ref, blk_ref, bup_ref, w_ref, xo_ref, blko_ref, bupo_ref, wo_ref,
    send_x, recv_x, send_s, recv_s, send_w, recv_w, local,
):
    row, me = lax.axis_index("row"), lax.axis_index("col")
    chips = cols // 2
    chip, lane = me // 2, lax.rem(me, 2)
    mate = chip * 2 + 1 - lane
    depth = w_ref.shape[0]

    barrier = pltpu.get_barrier_semaphore()
    for k in range(1, cols):
        pl.semaphore_signal(
            barrier, inc=1, device_id=(row, lax.rem(me + k, cols)), device_id_type=MESH
        )
    for k in range(1, rows):
        pl.semaphore_signal(
            barrier, inc=1, device_id=(lax.rem(row + k, rows), me), device_id_type=MESH
        )
    pl.semaphore_wait(barrier, rows + cols - 2)

    def chunk(src, owner, target, route, at):
        return pltpu.make_async_remote_copy(
            src_ref=src,
            dst_ref=xo_ref.at[owner],
            send_sem=send_x.at[route, at],
            recv_sem=recv_x.at[route, at],
            device_id=(row, target),
            device_id_type=MESH,
        )

    @pl.when(chip + 1 < chips)
    def _():
        chunk(x_ref, me, me + 2, 0, chip).start()

    @pl.when(chip > 0)
    def _():
        chunk(x_ref, me, me - 2, 1, chip).start()

    chunk(x_ref, me, mate, 2, chip).start()
    weights = []
    where = pl.ds(pl.multiple_of(row * depth, depth), depth)
    for k in range(1, rows):
        copy = pltpu.make_async_remote_copy(
            src_ref=w_ref,
            dst_ref=wo_ref.at[where],
            send_sem=send_w.at[k],
            recv_sem=recv_w.at[k],
            device_id=(lax.rem(row + k, rows), me),
            device_id_type=MESH,
        )
        copy.start()
        weights.append(copy)
    small = []
    for k in range(1, cols):
        for at, (src, dst) in enumerate(((blk_ref, blko_ref), (bup_ref, bupo_ref))):
            copy = pltpu.make_async_remote_copy(
                src_ref=src,
                dst_ref=dst.at[me],
                send_sem=send_s.at[at, k],
                recv_sem=recv_s.at[at, k],
                device_id=(row, lax.rem(me + k, cols)),
                device_id_type=MESH,
            )
            copy.start()
            small.append(copy)
    own = [
        pltpu.make_async_copy(x_ref, xo_ref.at[me], local.at[0]),
        pltpu.make_async_copy(blk_ref, blko_ref.at[me], local.at[1]),
        pltpu.make_async_copy(bup_ref, bupo_ref.at[me], local.at[2]),
        pltpu.make_async_copy(w_ref, wo_ref.at[where], local.at[3]),
    ]
    for copy in own:
        copy.start()

    for hop in range(1, chips):
        below, above = chip - hop, chip + hop

        @pl.when(below >= 0)
        def _():
            owner = below * 2 + lane
            chunk(xo_ref.at[owner], owner, me, 0, below).wait_recv()

            @pl.when(chip + 1 < chips)
            def _():
                chunk(xo_ref.at[owner], owner, me + 2, 0, below).start()

            chunk(xo_ref.at[owner], owner, mate, 2, below).start()

        @pl.when(above < chips)
        def _():
            owner = above * 2 + lane
            chunk(xo_ref.at[owner], owner, me, 1, above).wait_recv()

            @pl.when(chip > 0)
            def _():
                chunk(xo_ref.at[owner], owner, me - 2, 1, above).start()

            chunk(xo_ref.at[owner], owner, mate, 2, above).start()

    for at in range(chips):
        copy = chunk(x_ref, me, mate, 2, at)
        copy.wait_recv()
        copy.wait_send()

        @pl.when((at <= chip) & (chip + 1 < chips))
        def _():
            chunk(x_ref, me, me, 0, at).wait_send()

        @pl.when((at >= chip) & (chip > 0))
        def _():
            chunk(x_ref, me, me, 1, at).wait_send()

    for copy in weights + small + own:
        copy.wait()


def gather_inputs(x, blocks, b_up, w_qkv, rows, cols):
    any_space = pl.BlockSpec(memory_space=pl.ANY)
    vmem = pl.BlockSpec(memory_space=pltpu.VMEM)
    chips = cols // 2
    dma = pltpu.SemaphoreType.DMA
    return pl.pallas_call(
        functools.partial(gather_kernel, rows, cols),
        out_shape=[
            jax.ShapeDtypeStruct((cols,) + x.shape, x.dtype),
            jax.ShapeDtypeStruct((cols,) + blocks.shape, blocks.dtype),
            jax.ShapeDtypeStruct((cols,) + b_up.shape, b_up.dtype),
            jax.ShapeDtypeStruct((rows * w_qkv.shape[0], w_qkv.shape[1]), w_qkv.dtype),
        ],
        in_specs=[vmem] * 4,
        out_specs=[any_space] * 4,
        scratch_shapes=[
            dma((3, chips)), dma((3, chips)),
            dma((2, cols)), dma((2, cols)),
            dma((rows,)), dma((rows,)), dma((4,)),
        ],
        compiler_params=pltpu.CompilerParams(collective_id=0, has_side_effects=True),
        name="gather_inputs",
    )(x, blocks, b_up, w_qkv)


def qkv_kernel(x_ref, w_ref, b_ref, q_ref, k_ref, v_ref):
    mixed = dot(x_ref[...], w_ref[...])
    width = q_ref.shape[1]
    bias = b_ref[...].astype(f32)
    q_ref[...] = (mixed[:, :width] + bias[0:1]).astype(bf16)
    k_ref[...] = mixed[:, width : 2 * width].astype(bf16)
    v_ref[...] = (mixed[:, 2 * width :] + bias[1:2]).astype(bf16)


def project_qkv(x, w, bias):
    count, depth = x.shape
    width = w.shape[1] // 3
    tile = min(1024, count)
    out = pl.BlockSpec((tile, width), lambda i: (i, 0))
    return pl.pallas_call(
        qkv_kernel,
        grid=(count // tile,),
        in_specs=[pl.BlockSpec((tile, depth), lambda i: (i, 0)), whole(w.shape), whole(bias.shape)],
        out_specs=[out] * 3,
        out_shape=[jax.ShapeDtypeStruct((count, width), bf16)] * 3,
        compiler_params=params(),
        cost_estimate=cost(2 * count * depth * 3 * width, 2 * count * (depth + 3 * width)),
        name="project_qkv",
    )(x, w, bias)


def tile_mask(blk_ref, key_start, count, query_blocks):
    key_blocks = jnp.broadcast_to(blk_ref[0, :, pl.ds(key_start, count)], (128, count)).T[:, :1]
    return query_blocks >= key_blocks


def attend_kernel(head, step, blk_ref, q_ref, k_ref, v_ref, o_ref, lse_ref, values):
    i = pl.program_id(1)
    tile = q_ref.shape[0]
    chunks, _, chunk = o_ref.shape
    lanes = slice(head * HD, (head + 1) * HD)

    @pl.when(i == 0)
    def _():
        values[:HD, :] = flip(v_ref[:, lanes])
        values[HD:, :] = jnp.ones((ONES, values.shape[1]), bf16)

    start = pl.multiple_of(i * tile, tile)
    query = q_ref[:, lanes]
    query_blocks = blk_ref[0, :, pl.ds(start, tile)]

    def update(state, key_start, count, masked):
        total, top = state
        scores = dot(k_ref[pl.ds(key_start, count), lanes], query, NT)
        if masked:
            mask = tile_mask(blk_ref, key_start, count, query_blocks)
            scores = jnp.where(mask, scores, MASKED)
        higher = jnp.maximum(top, jnp.max(scores, axis=0, keepdims=True) * SCALE2)
        probs = jnp.exp2(scores * SCALE2 - higher)
        part = dot(values[:, pl.ds(key_start, count)], probs.astype(bf16))
        return total * jnp.exp2(top - higher) + part, higher

    state = (jnp.zeros((HD + ONES, tile), f32), jnp.full((1, tile), MASKED, f32))
    state = lax.fori_loop(
        0, start // step, lambda j, s: update(s, pl.multiple_of(j * step, step), step, False), state
    )
    state = update(state, start, tile, True)
    total, top = lax.fori_loop(
        0,
        jnp.where(i < pl.num_programs(1) - 1, 1, 0),
        lambda j, s: update(s, pl.multiple_of(start + tile, BLOCK), BLOCK, True),
        state,
    )
    mass = total[HD : HD + 1]
    out = (total[:HD] / mass).astype(bf16)
    for b in range(chunks):
        o_ref[b] = out[:, b * chunk : (b + 1) * chunk]
    lse_ref[0] = top + jnp.log2(mass)


def attend(q, k, v, blocks, head, chunk):
    count, width = q.shape
    seqs = count // SEQ_LEN
    tile = 1024
    tiles = SEQ_LEN // tile
    pairs = seqs * SEQ_LEN * SEQ_LEN * 5 // 8
    return pl.pallas_call(
        functools.partial(attend_kernel, head, tile),
        grid=(seqs, tiles),
        in_specs=[
            pl.BlockSpec((1, 1, SEQ_LEN), lambda s, i: (s, 0, 0)),
            pl.BlockSpec((tile, width), lambda s, i: (s * tiles + i, 0)),
            pl.BlockSpec((SEQ_LEN, width), lambda s, i: (s, 0)),
            pl.BlockSpec((SEQ_LEN, width), lambda s, i: (s, 0)),
        ],
        out_specs=[
            pl.BlockSpec((tile // chunk, HD, chunk), lambda s, i: (s * tiles + i, 0, 0)),
            pl.BlockSpec((1, 1, tile), lambda s, i: (s, 0, i)),
        ],
        out_shape=[
            jax.ShapeDtypeStruct((count // chunk, HD, chunk), bf16),
            jax.ShapeDtypeStruct((seqs, 1, SEQ_LEN), f32),
        ],
        scratch_shapes=[pltpu.VMEM((HD + ONES, SEQ_LEN), bf16)],
        compiler_params=params(),
        cost_estimate=cost(16 * pairs * HD, 4 * count * width * 2, pairs),
        name="attend",
    )(blocks, q, k, v)


def attend_back_kernel(
    head, step, sub, blk_ref, q_ref, k_ref, v_ref, do_ref, o_ref, lse_ref, dm_ref, sum_ref,
    key_grad, value_grad,
):
    turn = pl.program_id(1)
    tiles = pl.num_programs(1)
    i = tiles - 1 - turn
    tile = q_ref.shape[0]
    chunks, _, chunk = do_ref.shape
    parts = tile // sub
    lanes = slice(head * HD, (head + 1) * HD)
    start = pl.multiple_of(i * tile, tile)

    @pl.when(turn == 0)
    def _():
        key_grad[...] = jnp.zeros_like(key_grad)
        value_grad[...] = jnp.zeros_like(value_grad)
        sum_ref[...] = jnp.zeros_like(sum_ref)

    d_out = jnp.concatenate([do_ref[b] for b in range(chunks)], axis=1)
    out = jnp.concatenate([o_ref[b] for b in range(chunks)], axis=1)
    delta = jnp.sum(d_out.astype(f32) * out.astype(f32), axis=0, keepdims=True)
    lse = lse_ref[0]

    def cut(x, a):
        return x[:, a * sub : (a + 1) * sub]

    queries = [q_ref[a * sub : (a + 1) * sub, lanes] for a in range(parts)]
    query_blocks = [
        blk_ref[0, :, pl.ds(pl.multiple_of(start + a * sub, sub), sub)] for a in range(parts)
    ]

    def update(a, query_grad, key_start, count, masked):
        keys = k_ref[pl.ds(key_start, count), lanes]
        values = v_ref[pl.ds(key_start, count), lanes]
        scores = dot(keys, queries[a], NT) * SCALE2 - cut(lse, a)
        if masked:
            mask = tile_mask(blk_ref, key_start, count, query_blocks[a])
            scores = jnp.where(mask, scores, MASKED)
        probs = jnp.exp2(scores)
        d_values = dot(probs.astype(bf16), cut(d_out, a), NT)
        d_scores = (probs * (dot(values, cut(d_out, a)) - cut(delta, a))).astype(bf16)
        d_keys = dot(d_scores, queries[a])
        return query_grad + dot(keys, d_scores, TN), d_keys, d_values

    def add(key_start, count, d_keys, d_values):
        key_grad[pl.ds(key_start, count), :] += d_keys
        value_grad[pl.ds(key_start, count), :] += d_values

    def body(j, grads):
        key_start = pl.multiple_of(j * step, step)
        found = [update(a, grads[a], key_start, step, False) for a in range(parts)]
        add(key_start, step, sum(f[1] for f in found), sum(f[2] for f in found))
        return tuple(f[0] for f in found)

    grads = list(
        lax.fori_loop(0, start // step, body, (jnp.zeros((HD, sub), f32),) * parts)
    )
    for a in range(parts):
        todo = [(pl.multiple_of(start + a * sub, sub), sub, True)]
        if a > 0:
            todo.append((start, a * sub, False))
        if a < parts - 1:
            todo.append((pl.multiple_of(start + (a + 1) * sub, BLOCK), BLOCK, True))
        for key_start, count, masked in todo:
            grads[a], d_keys, d_values = update(a, grads[a], key_start, count, masked)
            add(key_start, count, d_keys, d_values)

    def beyond(j, grad):
        key_start = pl.multiple_of(start + tile, BLOCK)
        grad, d_keys, d_values = update(parts - 1, grad, key_start, BLOCK, True)
        add(key_start, BLOCK, d_keys, d_values)
        return grad

    grads[-1] = lax.fori_loop(0, jnp.where(i < tiles - 1, 1, 0), beyond, grads[-1])
    query_grad = jnp.concatenate(grads, axis=1) * SCALE
    sum_ref[0, :, :1] += jnp.sum(query_grad, axis=1, keepdims=True)
    query_grad = query_grad.astype(bf16)
    for b in range(chunks):
        dm_ref[i * chunks + b, :HD] = query_grad[:, b * chunk : (b + 1) * chunk]

    @pl.when(turn == tiles - 1)
    def _():
        value_sum = jnp.zeros((HD, 1), f32)
        for c in range(dm_ref.shape[0]):
            rows = slice(c * chunk, (c + 1) * chunk)
            dm_ref[c, HD : 2 * HD] = (key_grad[rows, :].T * SCALE).astype(bf16)
            d_values = value_grad[rows, :].T
            dm_ref[c, 2 * HD :] = d_values.astype(bf16)
            value_sum += jnp.sum(d_values, axis=1, keepdims=True)
        sum_ref[0, :, 1:2] = value_sum


def attend_back(q, k, v, d_out, out, lse, blocks, head, chunk):
    count, width = q.shape
    seqs = count // SEQ_LEN
    tile, sub = 1024, 512
    tiles = SEQ_LEN // tile
    pairs = seqs * SEQ_LEN * SEQ_LEN * 5 // 8
    heads_spec = pl.BlockSpec(
        (tile // chunk, HD, chunk), lambda s, i: (s * tiles + tiles - 1 - i, 0, 0)
    )
    return pl.pallas_call(
        functools.partial(attend_back_kernel, head, tile, sub),
        grid=(seqs, tiles),
        in_specs=[
            pl.BlockSpec((1, 1, SEQ_LEN), lambda s, i: (s, 0, 0)),
            pl.BlockSpec((tile, width), lambda s, i: (s * tiles + tiles - 1 - i, 0)),
            pl.BlockSpec((SEQ_LEN, width), lambda s, i: (s, 0)),
            pl.BlockSpec((SEQ_LEN, width), lambda s, i: (s, 0)),
            heads_spec,
            heads_spec,
            pl.BlockSpec((1, 1, tile), lambda s, i: (s, 0, tiles - 1 - i)),
        ],
        out_specs=[
            pl.BlockSpec((SEQ_LEN // chunk, 3 * HD, chunk), lambda s, i: (s, 0, 0)),
            pl.BlockSpec((1, HD, 128), lambda s, i: (s, 0, 0)),
        ],
        out_shape=[
            jax.ShapeDtypeStruct((count // chunk, 3 * HD, chunk), bf16),
            jax.ShapeDtypeStruct((seqs, HD, 128), f32),
        ],
        scratch_shapes=[pltpu.VMEM((SEQ_LEN, HD), f32)] * 2,
        compiler_params=params(),
        cost_estimate=cost(40 * pairs * HD, 8 * count * width * 2, pairs),
        name="attend_back",
    )(blocks, q, k, v, d_out, out, lse)


def stack_heads(refs):
    return jnp.concatenate([ref[s] for s in range(refs[0].shape[0]) for ref in refs], axis=0)


def project_out_kernel(heads_here, *refs):
    heads, (tok_ref, w_ref, b_ref, g_ref, s_ref, resid_ref, ffn_ref) = (
        refs[:heads_here],
        refs[heads_here:],
    )
    rows, cols, depth, width = w_ref.shape
    heads_all = flip(stack_heads(heads))
    for r in range(rows):
        here = slice(r * width, (r + 1) * width)
        branch = dot(heads_all, w_ref[r].reshape(cols * depth, width))
        resid_ref[:, here] = (
            tok_ref[:, here].astype(f32) + branch + b_ref[:, here].astype(f32)
        )
    xhat, _ = moments(resid_ref[...])
    ffn_ref[...] = (xhat * g_ref[...].astype(f32) + s_ref[...].astype(f32)).astype(bf16)


def project_out(heads, tokens, w, b_out, gain, shift):
    count, depth = tokens.shape
    tile = 256
    block = pl.BlockSpec((tile, depth), lambda i: (i, 0))
    vec = whole((1, depth))
    return pl.pallas_call(
        functools.partial(project_out_kernel, len(heads)),
        grid=(count // tile,),
        in_specs=[pl.BlockSpec((h.shape[0], HD, tile), lambda i: (0, 0, i)) for h in heads]
        + [block, whole(w.shape), vec, vec, vec],
        out_specs=[block, block],
        out_shape=[
            jax.ShapeDtypeStruct((count, depth), f32),
            jax.ShapeDtypeStruct((count, depth), bf16),
        ],
        compiler_params=params(),
        cost_estimate=cost(2 * count * depth * depth, 2 * depth * depth + 8 * count * depth),
        name="project_out",
    )(*heads, tokens, w, b_out, gain, shift)


GELU_A = 0.7978845608028654
GELU_B = 0.044715


def feed_kernel(
    heads_here, x_ref, g_ref, resid_ref, up_ref, down_ref, bup_ref, bdown_ref, gain_ref, out_w_ref,
    gup_ref, gdown_ref, gbup_ref, output_ref, dres_ref, drl_ref, sums_ref, *rest,
):
    d_heads, (out_acc, norm_acc) = rest[:heads_here], rest[heads_here:]
    step = pl.program_id(0)
    rows, width = up_ref.shape[0], up_ref.shape[3]

    @pl.when(step == 0)
    def _():
        out_acc[...] = jnp.zeros_like(out_acc)
        norm_acc[...] = jnp.zeros_like(norm_acc)

    def part(r):
        return slice(r * width, (r + 1) * width)

    up = bup_ref[0].astype(f32)
    d_hidden = 0.0
    for r in range(rows):
        up = up + dot(x_ref[:, part(r)], up_ref[r, 0], NT)
        d_hidden = d_hidden + dot(g_ref[:, part(r)], down_ref[r, 0], NT)
    square = up * up
    bent = jnp.tanh(GELU_A * up * (1.0 + GELU_B * square))
    half = 0.5 + 0.5 * bent
    hidden = (up * half).astype(bf16)
    slope = half + (0.5 * GELU_A) * up * (1.0 - bent * bent) * (1.0 + (3.0 * GELU_B) * square)
    d_up = d_hidden * slope
    gbup_ref[0] = jnp.sum(d_up, axis=0, keepdims=True)
    d_up = d_up.astype(bf16)
    for r in range(rows):
        out_acc[:, part(r)] += dot(hidden, down_ref[r, 0])
        norm_acc[:, part(r)] += dot(d_up, up_ref[r, 0])
    grad_down = dot(hidden, g_ref[...], TN)
    grad_up = dot(d_up, x_ref[...], TN)
    for r in range(rows):
        gdown_ref[0, r, 0] = grad_down[:, part(r)].astype(bf16)
        gup_ref[0, r, 0] = grad_up[:, part(r)].astype(bf16)

    @pl.when(step == pl.num_programs(0) - 1)
    def _():
        resid = resid_ref[...]
        output_ref[...] = (resid + out_acc[...] + bdown_ref[...].astype(f32)).astype(bf16)
        xhat, inv = moments(resid)
        d_norm = norm_acc[...]
        grad = g_ref[...].astype(f32)
        d_resid = grad + norm_back(xhat, inv, d_norm * gain_ref[...].astype(f32))
        dres_ref[...] = d_resid
        low = d_resid.astype(bf16)
        drl_ref[...] = low
        sums_ref[0:1] = jnp.sum(grad, axis=0, keepdims=True)
        sums_ref[1:2] = jnp.sum(d_norm * xhat, axis=0, keepdims=True)
        sums_ref[2:3] = jnp.sum(d_norm, axis=0, keepdims=True)
        sums_ref[3:4] = jnp.sum(d_resid, axis=0, keepdims=True)
        sums_ref[4:] = jnp.zeros((4, sums_ref.shape[1]), f32)
        cols, depth = out_w_ref.shape[1], out_w_ref.shape[2]
        found = 0.0
        for r in range(rows):
            found = found + dot(out_w_ref[r].reshape(cols * depth, width), low[:, part(r)], NT)
        found = found.astype(bf16)
        for c in range(cols):
            for h, ref in enumerate(d_heads):
                ref[c] = found[c * depth + h * HD : c * depth + (h + 1) * HD]


def feed_forward(x, grad, resid, w_up, w_down, b_up, b_down, gain, w_out):
    count, depth = x.shape
    rows, cols, units, width = w_up.shape
    heads_here = w_out.shape[2] // HD
    weight = pl.BlockSpec((rows, 1, units, width), lambda c: (0, c, 0, 0))
    grad_spec = pl.BlockSpec(
        (1, rows, 1, units, width), lambda c: (lax.rem(c, 2), 0, c // 2, 0, 0)
    )
    grad_shape = jax.ShapeDtypeStruct((2, rows, cols // 2, units, width), bf16)
    low, high = whole((count, depth)), whole((count, depth))
    vec = whole((1, depth))
    heads_shape = (cols, HD, count)
    return pl.pallas_call(
        functools.partial(feed_kernel, heads_here),
        grid=(cols,),
        in_specs=[
            low, low, high, weight, weight,
            pl.BlockSpec((1, 1, units), lambda c: (c, 0, 0)), vec, vec, whole(w_out.shape),
        ],
        out_specs=[
            grad_spec, grad_spec, pl.BlockSpec((1, 1, units), lambda c: (c, 0, 0)),
            low, high, low, whole((8, depth)),
        ] + [whole(heads_shape)] * heads_here,
        out_shape=[
            grad_shape, grad_shape, jax.ShapeDtypeStruct((cols, 1, units), f32),
            jax.ShapeDtypeStruct((count, depth), bf16),
            jax.ShapeDtypeStruct((count, depth), f32),
            jax.ShapeDtypeStruct((count, depth), bf16),
            jax.ShapeDtypeStruct((8, depth), f32),
        ] + [jax.ShapeDtypeStruct(heads_shape, bf16)] * heads_here,
        scratch_shapes=[pltpu.VMEM((count, depth), f32)] * 2,
        compiler_params=params(),
        cost_estimate=cost(
            12 * count * depth * cols * units, 8 * depth * cols * units + 16 * count * depth
        ),
        name="feed_forward",
    )(x, grad, resid, w_up, w_down, b_up, b_down, gain, w_out)


def grad_out_kernel(heads_here, *refs):
    heads, (d_ref, out_ref) = refs[:heads_here], refs[heads_here:]
    cores, rows, chips, depth, width = out_ref.shape
    found = dot(stack_heads(heads), d_ref[...]).astype(bf16)
    for r in range(rows):
        for c in range(cores * chips):
            out_ref[c % 2, r, c // 2] = found[
                c * depth : (c + 1) * depth, r * width : (r + 1) * width
            ]


def grad_w_out(heads, d_resid, rows):
    count, depth = d_resid.shape
    cols = heads[0].shape[0]
    shape = (2, rows, cols // 2, depth // cols, depth // rows)
    return pl.pallas_call(
        functools.partial(grad_out_kernel, len(heads)),
        in_specs=[pl.BlockSpec(memory_space=pltpu.VMEM)] * (len(heads) + 1),
        out_specs=pl.BlockSpec(memory_space=pltpu.VMEM),
        out_shape=jax.ShapeDtypeStruct(shape, bf16),
        compiler_params=params(),
        cost_estimate=cost(2 * count * depth * depth, 2 * depth * depth + 4 * count * depth),
        name="grad_w_out",
    )(*heads, d_resid)


def grad_qkv_kernel(dm_ref, x_ref, out_ref, acc):
    step = pl.program_id(0)

    @pl.when(step == 0)
    def _():
        acc[...] = jnp.zeros_like(acc)

    acc[...] += dot(dm_ref[0], x_ref[0])

    @pl.when(step == pl.num_programs(0) - 1)
    def _():
        width = out_ref.shape[2]
        for r in range(out_ref.shape[0]):
            out_ref[r] = acc[:, r * width : (r + 1) * width].astype(bf16)


def grad_w_qkv(dm, x, rows):
    chunks, parts, count = dm.shape
    depth = x.shape[2]
    shape = (rows, parts, depth // rows)
    return pl.pallas_call(
        grad_qkv_kernel,
        grid=(chunks,),
        in_specs=[
            pl.BlockSpec((1, parts, count), lambda c: (c, 0, 0)),
            pl.BlockSpec((1, count, depth), lambda c: (c, 0, 0)),
        ],
        out_specs=whole(shape),
        out_shape=jax.ShapeDtypeStruct(shape, bf16),
        scratch_shapes=[pltpu.VMEM((parts, depth), f32)],
        compiler_params=params(),
        cost_estimate=cost(2 * chunks * count * parts * depth, 2 * chunks * count * depth),
        name="grad_w_qkv",
    )(dm, x)


def finish_kernel(heads_here, *refs):
    dms, (w_ref, tok_ref, dres_ref, gain_ref, out_ref, sums_ref, acc) = (
        refs[:heads_here],
        refs[heads_here:],
    )
    step = pl.program_id(0)
    rows, width = w_ref.shape[0], w_ref.shape[2]

    @pl.when(step == 0)
    def _():
        acc[...] = jnp.zeros_like(acc)

    d_mixed = flip(
        jnp.concatenate([dm[0, j * HD : (j + 1) * HD] for j in range(3) for dm in dms], axis=0)
    )
    for r in range(rows):
        acc[:, r * width : (r + 1) * width] += dot(d_mixed, w_ref[r, 0], NT)

    @pl.when(step == pl.num_programs(0) - 1)
    def _():
        xhat, inv = moments(tok_ref[...].astype(f32))
        d_norm = acc[...]
        out_ref[...] = dres_ref[...] + norm_back(xhat, inv, d_norm * gain_ref[...].astype(f32))
        sums_ref[0:1] = jnp.sum(d_norm * xhat, axis=0, keepdims=True)
        sums_ref[1:2] = jnp.sum(d_norm, axis=0, keepdims=True)


def finish(dms, w, tokens, d_resid, gain):
    count, depth = tokens.shape
    rows, cols, width, parts = w.shape
    block = whole((count, depth))
    return pl.pallas_call(
        functools.partial(finish_kernel, len(dms)),
        grid=(cols,),
        in_specs=[pl.BlockSpec((1, 3 * HD, count), lambda c: (c, 0, 0)) for _ in dms]
        + [
            pl.BlockSpec((rows, 1, width, parts), lambda c: (0, c, 0, 0)),
            block, block, whole((1, depth)),
        ],
        out_specs=[block, whole((2, depth))],
        out_shape=[
            jax.ShapeDtypeStruct((count, depth), f32),
            jax.ShapeDtypeStruct((2, depth), f32),
        ],
        scratch_shapes=[pltpu.VMEM((count, depth), f32)],
        compiler_params=params(),
        cost_estimate=cost(2 * count * depth * cols * parts, 2 * depth * cols * parts),
        name="finish",
    )(*dms, w, tokens, d_resid, gain)


def swap(x, axis, groups=None):
    return lax.all_to_all(x, axis, 0, 0, tiled=True, axis_index_groups=groups)


def total_of(x):
    return jnp.sum(x.astype(f32), axis=0)


def body(
    tokens, blocks, w_qkv, b_qv, w_out, b_out, w_up, b_up, w_down, b_down,
    gain1, shift1, gain2, shift2, grad_out,
):
    rows, cols = lax.axis_size("row"), lax.axis_size("col")
    chips = cols // 2
    pairs = [[2 * c, 2 * c + 1] for c in range(chips)]
    lines = [[2 * c + core for c in range(chips)] for core in range(2)]
    local_rows, depth = tokens.shape
    group_rows = local_rows * cols
    head_cols = w_qkv.shape[2]
    heads = range(head_cols // HD)
    units = w_up.shape[0]

    def vec(v):
        return v.reshape(1, -1)

    xhat, _ = moments(tokens.astype(f32))
    attn_input = (xhat * gain1.astype(f32) + shift1.astype(f32)).astype(bf16)
    w_qkv_flat = w_qkv.reshape(w_qkv.shape[0], 3 * head_cols)

    def gather_all(w):
        return lax.all_gather(w, ("row", "col"), axis=0, tiled=False).reshape(
            (rows, cols) + w.shape
        )

    out_weight, up_weight, down_weight, qkv_weight = (
        gather_all(w_out), gather_all(w_up), gather_all(w_down), gather_all(w_qkv_flat)
    )

    attn_rows, block_ids, up_bias, qkv_here = gather_inputs(
        attn_input, vec(blocks), vec(b_up), w_qkv_flat, rows, cols
    )
    block_ids = block_ids.reshape(group_rows // SEQ_LEN, 1, SEQ_LEN)
    q, k, v = project_qkv(attn_rows.reshape(group_rows, depth), qkv_here, b_qv)
    found = [attend(q, k, v, block_ids, h, local_rows) for h in heads]
    arrived = [swap(out, "col") for out, _ in found]
    resid, ffn_input = project_out(
        arrived, tokens, out_weight, vec(b_out), vec(gain2), vec(shift2)
    )
    grad_up, grad_down, grad_bup, output, d_resid, d_low, sums, *d_heads = feed_forward(
        ffn_input, grad_out, resid, up_weight, down_weight, up_bias, vec(b_down), vec(gain2),
        out_weight,
    )
    d_heads = [swap(d, "col") for d in d_heads]
    grad_wout = grad_w_out(arrived, d_low, rows)

    def reduce_weight(g):
        g = total_of(swap(g, "col", pairs)).astype(bf16)
        g = total_of(swap(g, "row")).astype(bf16)
        return total_of(swap(g, "col", lines))

    grad_wdown, grad_wup, grad_wout = (
        reduce_weight(grad_down), reduce_weight(grad_up), reduce_weight(grad_wout)
    )

    d_mixed, bias_sums = [], []
    for h in heads:
        dm, bias_sum = attend_back(
            q, k, v, d_heads[h], found[h][0], found[h][1], block_ids, h, local_rows
        )
        d_mixed.append(dm)
        bias_sums.append(jnp.sum(bias_sum[:, :, :2], axis=0))
    returned = [swap(dm, "col") for dm in d_mixed]
    grad_qkv = [total_of(swap(grad_w_qkv(dm, attn_rows, rows), "row")) for dm in d_mixed]
    grad_wqkv = jnp.stack(
        [g.reshape(3, HD, depth // rows) for g in grad_qkv], axis=1
    ).reshape(3 * head_cols, depth // rows)
    grad_wqkv = grad_wqkv.T.reshape(depth // rows, 3, head_cols)
    grad_tokens, norm_sums = finish(returned, qkv_weight, tokens, d_resid, vec(gain1))

    world = rows * cols
    early = jnp.concatenate([grad_bup.reshape(-1), sums[:4].reshape(-1)]).reshape(world, -1)
    early = total_of(swap(early, ("row", "col")))
    early = swap(jnp.broadcast_to(early, (world,) + early.shape), ("row", "col")).reshape(-1)
    hidden_units = units * cols
    grad_bup = lax.dynamic_slice_in_dim(early, lax.axis_index("col") * units, units)
    grad_bdown, grad_gain2, grad_shift2, grad_bout = early[hidden_units:].reshape(4, depth)
    late = jnp.broadcast_to(norm_sums, (world,) + norm_sums.shape)
    grad_gain1, grad_shift1 = total_of(swap(late, ("row", "col")))
    bias = jnp.concatenate(bias_sums, axis=0).T
    grad_bqv = total_of(swap(jnp.broadcast_to(bias, (rows,) + bias.shape), "row"))
    return (
        output, grad_tokens, grad_wqkv, grad_bqv, grad_wout, grad_bout, grad_wup, grad_bup,
        grad_wdown, grad_bdown, grad_gain1, grad_shift1, grad_gain2, grad_shift2,
    )


def solution(mesh):
    tokens, weight, whole_vec = P(("row", "col"), None), P("col", "row"), P()
    qkv, bias_qv = P("row", None, "col"), P(None, "col")
    return jax.shard_map(
        body,
        mesh=mesh,
        in_specs=(
            tokens, P(("row", "col")), qkv, bias_qv, weight, whole_vec, weight, P("col"), weight,
            whole_vec, whole_vec, whole_vec, whole_vec, whole_vec, tokens,
        ),
        out_specs=(
            tokens, tokens, qkv, bias_qv, weight, whole_vec, weight, P("col"), weight,
            whole_vec, whole_vec, whole_vec, whole_vec, whole_vec,
        ),
        check_vma=False,
    )
```

```python
import functools

import jax
import jax.numpy as jnp
from jax import lax
from jax.experimental import pallas as pl
from jax.experimental.pallas import tpu as pltpu
from jax.sharding import PartitionSpec as P

HD = 64
SEQ_LEN = 4096
BLOCK = 256
EPS = 1e-05
SCALE = HD ** (-0.5)
SCALE2 = SCALE * 1.4426950408889634
MASKED = -1e30
ONES = 16
MESH = pl.DeviceIdType.MESH
VMEM_LIMIT = 60 << 20

f32 = jnp.float32
bf16 = jnp.bfloat16

NN = (((1,), (0,)), ((), ()))
NT = (((1,), (1,)), ((), ()))
TN = (((0,), (0,)), ((), ()))


def dot(a, b, dims=NN):
    return lax.dot_general(a, b, dims, preferred_element_type=f32)


def flip(x):
    return x.astype(f32).T.astype(bf16)


def params(**more):
    return pltpu.CompilerParams(vmem_limit_bytes=VMEM_LIMIT, **more)


def cost(flops, nbytes, transcendentals=0):
    return pl.CostEstimate(flops=flops, bytes_accessed=nbytes, transcendentals=transcendentals)


def whole(shape):
    return pl.BlockSpec(shape, lambda *_: (0,) * len(shape))


def moments(v):
    center = jnp.mean(v, axis=-1, keepdims=True)
    centered = v - center
    spread = jnp.mean(centered * centered, axis=-1, keepdims=True)
    inv = lax.rsqrt(spread + EPS)
    return centered * inv, inv


def norm_back(xhat, inv, e):
    return inv * (
        e - jnp.mean(e, axis=-1, keepdims=True) - xhat * jnp.mean(e * xhat, axis=-1, keepdims=True)
    )


def gather_kernel(
    rows, cols, x_ref, blk_ref, bup_ref, w_ref, xo_ref, blko_ref, bupo_ref, wo_ref,
    send_x, recv_x, send_s, recv_s, send_w, recv_w, local,
):
    row, me = lax.axis_index("row"), lax.axis_index("col")
    chips = cols // 2
    chip, lane = me // 2, lax.rem(me, 2)
    mate = chip * 2 + 1 - lane
    depth = w_ref.shape[0]

    barrier = pltpu.get_barrier_semaphore()
    for k in range(1, cols):
        pl.semaphore_signal(
            barrier, inc=1, device_id=(row, lax.rem(me + k, cols)), device_id_type=MESH
        )
    for k in range(1, rows):
        pl.semaphore_signal(
            barrier, inc=1, device_id=(lax.rem(row + k, rows), me), device_id_type=MESH
        )
    pl.semaphore_wait(barrier, rows + cols - 2)

    def chunk(src, owner, target, route, at):
        return pltpu.make_async_remote_copy(
            src_ref=src,
            dst_ref=xo_ref.at[owner],
            send_sem=send_x.at[route, at],
            recv_sem=recv_x.at[route, at],
            device_id=(row, target),
            device_id_type=MESH,
        )

    @pl.when(chip + 1 < chips)
    def _():
        chunk(x_ref, me, me + 2, 0, chip).start()

    @pl.when(chip > 0)
    def _():
        chunk(x_ref, me, me - 2, 1, chip).start()

    chunk(x_ref, me, mate, 2, chip).start()
    weights = []
    where = pl.ds(pl.multiple_of(row * depth, depth), depth)
    for k in range(1, rows):
        copy = pltpu.make_async_remote_copy(
            src_ref=w_ref,
            dst_ref=wo_ref.at[where],
            send_sem=send_w.at[k],
            recv_sem=recv_w.at[k],
            device_id=(lax.rem(row + k, rows), me),
            device_id_type=MESH,
        )
        copy.start()
        weights.append(copy)
    small = []
    for k in range(1, cols):
        for at, (src, dst) in enumerate(((blk_ref, blko_ref), (bup_ref, bupo_ref))):
            copy = pltpu.make_async_remote_copy(
                src_ref=src,
                dst_ref=dst.at[me],
                send_sem=send_s.at[at, k],
                recv_sem=recv_s.at[at, k],
                device_id=(row, lax.rem(me + k, cols)),
                device_id_type=MESH,
            )
            copy.start()
            small.append(copy)
    own = [
        pltpu.make_async_copy(x_ref, xo_ref.at[me], local.at[0]),
        pltpu.make_async_copy(blk_ref, blko_ref.at[me], local.at[1]),
        pltpu.make_async_copy(bup_ref, bupo_ref.at[me], local.at[2]),
        pltpu.make_async_copy(w_ref, wo_ref.at[where], local.at[3]),
    ]
    for copy in own:
        copy.start()

    for hop in range(1, chips):
        below, above = chip - hop, chip + hop

        @pl.when(below >= 0)
        def _():
            owner = below * 2 + lane
            chunk(xo_ref.at[owner], owner, me, 0, below).wait_recv()

            @pl.when(chip + 1 < chips)
            def _():
                chunk(xo_ref.at[owner], owner, me + 2, 0, below).start()

            chunk(xo_ref.at[owner], owner, mate, 2, below).start()

        @pl.when(above < chips)
        def _():
            owner = above * 2 + lane
            chunk(xo_ref.at[owner], owner, me, 1, above).wait_recv()

            @pl.when(chip > 0)
            def _():
                chunk(xo_ref.at[owner], owner, me - 2, 1, above).start()

            chunk(xo_ref.at[owner], owner, mate, 2, above).start()

    for at in range(chips):
        copy = chunk(x_ref, me, mate, 2, at)
        copy.wait_recv()
        copy.wait_send()

        @pl.when((at <= chip) & (chip + 1 < chips))
        def _():
            chunk(x_ref, me, me, 0, at).wait_send()

        @pl.when((at >= chip) & (chip > 0))
        def _():
            chunk(x_ref, me, me, 1, at).wait_send()

    for copy in weights + small + own:
        copy.wait()


def gather_inputs(x, blocks, b_up, w_qkv, rows, cols):
    any_space = pl.BlockSpec(memory_space=pl.ANY)
    vmem = pl.BlockSpec(memory_space=pltpu.VMEM)
    chips = cols // 2
    dma = pltpu.SemaphoreType.DMA
    return pl.pallas_call(
        functools.partial(gather_kernel, rows, cols),
        out_shape=[
            jax.ShapeDtypeStruct((cols,) + x.shape, x.dtype),
            jax.ShapeDtypeStruct((cols,) + blocks.shape, blocks.dtype),
            jax.ShapeDtypeStruct((cols,) + b_up.shape, b_up.dtype),
            jax.ShapeDtypeStruct((rows * w_qkv.shape[0], w_qkv.shape[1]), w_qkv.dtype),
        ],
        in_specs=[vmem] * 4,
        out_specs=[any_space] * 4,
        scratch_shapes=[
            dma((3, chips)), dma((3, chips)),
            dma((2, cols)), dma((2, cols)),
            dma((rows,)), dma((rows,)), dma((4,)),
        ],
        compiler_params=pltpu.CompilerParams(collective_id=0, has_side_effects=True),
        name="gather_inputs",
    )(x, blocks, b_up, w_qkv)


def qkv_kernel(x_ref, w_ref, b_ref, q_ref, k_ref, v_ref):
    mixed = dot(x_ref[...], w_ref[...])
    heads = q_ref.shape[0]
    width = heads * HD
    bias = b_ref[...].astype(f32)
    for h in range(heads):
        lanes = slice(h * HD, (h + 1) * HD)
        q_ref[h] = (mixed[:, :width][:, lanes] + bias[0:1, lanes]).astype(bf16)
        k_ref[h] = mixed[:, width : 2 * width][:, lanes].astype(bf16)
        v_ref[h] = (mixed[:, 2 * width :][:, lanes] + bias[1:2, lanes]).astype(bf16)


def project_qkv(x, w, bias):
    count, depth = x.shape
    width = w.shape[1] // 3
    heads = width // HD
    tile = min(1024, count)
    out = pl.BlockSpec((heads, tile, HD), lambda i: (0, i, 0))
    return pl.pallas_call(
        qkv_kernel,
        grid=(count // tile,),
        in_specs=[pl.BlockSpec((tile, depth), lambda i: (i, 0)), whole(w.shape), whole(bias.shape)],
        out_specs=[out] * 3,
        out_shape=[jax.ShapeDtypeStruct((heads, count, HD), bf16)] * 3,
        compiler_params=params(),
        cost_estimate=cost(2 * count * depth * 3 * width, 2 * count * (depth + 3 * width)),
        name="project_qkv",
    )(x, w, bias)


def tile_mask(blk_ref, key_start, count, query_blocks):
    key_blocks = jnp.broadcast_to(blk_ref[0, :, pl.ds(key_start, count)], (128, count)).T[:, :1]
    return query_blocks >= key_blocks


def attend_kernel(step, blk_ref, q_ref, k_ref, v_ref, o_ref, lse_ref, values):
    i = pl.program_id(2)
    tile = q_ref.shape[1]
    chunks, _, chunk = o_ref.shape

    @pl.when(i == 0)
    def _():
        values[:HD, :] = flip(v_ref[0])
        values[HD:, :] = jnp.ones((ONES, values.shape[1]), bf16)

    start = pl.multiple_of(i * tile, tile)
    query = q_ref[0]
    query_blocks = blk_ref[0, :, pl.ds(start, tile)]

    def update(state, key_start, count, masked):
        total, top = state
        scores = dot(k_ref[0, pl.ds(key_start, count), :], query, NT)
        if masked:
            mask = tile_mask(blk_ref, key_start, count, query_blocks)
            scores = jnp.where(mask, scores, MASKED)
        higher = jnp.maximum(top, jnp.max(scores, axis=0, keepdims=True) * SCALE2)
        probs = jnp.exp2(scores * SCALE2 - higher)
        part = dot(values[:, pl.ds(key_start, count)], probs.astype(bf16))
        return total * jnp.exp2(top - higher) + part, higher

    state = (jnp.zeros((HD + ONES, tile), f32), jnp.full((1, tile), MASKED, f32))
    state = lax.fori_loop(
        0, start // step, lambda j, s: update(s, pl.multiple_of(j * step, step), step, False), state
    )
    state = update(state, start, tile, True)
    total, top = lax.fori_loop(
        0,
        jnp.where(i < pl.num_programs(2) - 1, 1, 0),
        lambda j, s: update(s, pl.multiple_of(start + tile, BLOCK), BLOCK, True),
        state,
    )
    mass = total[HD : HD + 1]
    out = (total[:HD] / mass).astype(bf16)
    for b in range(chunks):
        o_ref[b] = out[:, b * chunk : (b + 1) * chunk]
    lse_ref[0, 0] = top + jnp.log2(mass)


def attend(q, k, v, blocks, chunk):
    heads, count, _ = q.shape
    seqs = count // SEQ_LEN
    tile = 1024
    tiles = SEQ_LEN // tile
    pairs = heads * seqs * SEQ_LEN * SEQ_LEN * 5 // 8
    keys = pl.BlockSpec((1, SEQ_LEN, HD), lambda h, s, i: (h, s, 0))
    return pl.pallas_call(
        functools.partial(attend_kernel, tile),
        grid=(heads, seqs, tiles),
        in_specs=[
            pl.BlockSpec((1, 1, SEQ_LEN), lambda h, s, i: (s, 0, 0)),
            pl.BlockSpec((1, tile, HD), lambda h, s, i: (h, s * tiles + i, 0)),
            keys,
            keys,
        ],
        out_specs=[
            pl.BlockSpec((tile // chunk, HD, chunk), lambda h, s, i: (s * tiles + i, h, 0)),
            pl.BlockSpec((1, 1, 1, tile), lambda h, s, i: (h, s, 0, i)),
        ],
        out_shape=[
            jax.ShapeDtypeStruct((count // chunk, heads * HD, chunk), bf16),
            jax.ShapeDtypeStruct((heads, seqs, 1, SEQ_LEN), f32),
        ],
        scratch_shapes=[pltpu.VMEM((HD + ONES, SEQ_LEN), bf16)],
        compiler_params=params(),
        cost_estimate=cost(16 * pairs * HD, 8 * heads * count * HD, pairs),
        name="attend",
    )(blocks, q, k, v)


def place():
    return lax.axis_index("row"), lax.axis_index("col")


def greet(rows, cols):
    row, col = place()
    barrier = pltpu.get_barrier_semaphore()

    def to_col(k, carry):
        pl.semaphore_signal(
            barrier, inc=1, device_id=(row, lax.rem(col + k, cols)), device_id_type=MESH
        )
        return carry

    def to_row(k, carry):
        pl.semaphore_signal(
            barrier, inc=1, device_id=(lax.rem(row + k, rows), col), device_id_type=MESH
        )
        return carry

    lax.fori_loop(1, cols, to_col, 0)
    lax.fori_loop(1, rows, to_row, 0)
    pl.semaphore_wait(barrier, rows + cols - 2)


def remote(src, dst, send, recv, device):
    return pltpu.make_async_remote_copy(
        src_ref=src, dst_ref=dst, send_sem=send, recv_sem=recv, device_id=device, device_id_type=MESH
    )


def each(count, act):
    def turn(k, carry):
        act(k)
        return carry

    lax.fori_loop(1, count, turn, 0)


class Exchange:
    def __init__(self, count, here, slot, to, out, into, send, recv):
        self.count, self.here, self.slot, self.to = count, here, slot, to
        self.out, self.into, self.send, self.recv = out, into, send, recv

    def copy(self, k):
        at = self.slot(k)
        return remote(
            self.out(at), self.into(self.here), self.send.at[k], self.recv.at[self.here], self.to(k)
        )

    def arrival(self, k):
        at = self.slot(k)
        return remote(self.out(at), self.into(at), self.send.at[k], self.recv.at[at], self.to(k))

    def start(self):
        each(self.count, lambda k: self.copy(k).start())

    def wait_recv(self):
        each(self.count, lambda k: self.arrival(k).wait_recv())

    def wait_send(self):
        each(self.count, lambda k: self.copy(k).wait_send())


def over_row(rows, out, into, send, recv):
    row, col = place()
    slot = lambda k: lax.rem(row + k, rows)
    return Exchange(rows, row, slot, lambda k: (slot(k), col), out, into, send, recv)


def over_col(cols, out, into, send, recv):
    row, col = place()
    slot = lambda k: lax.rem(col + k, cols)
    return Exchange(cols, col, slot, lambda k: (row, slot(k)), out, into, send, recv)


def over_line(chips, out, into, send, recv):
    row, col = place()
    chip, lane = col // 2, lax.rem(col, 2)
    slot = lambda k: lax.rem(chip + k, chips)
    return Exchange(chips, chip, slot, lambda k: (row, slot(k) * 2 + lane), out, into, send, recv)


def mate():
    row, col = place()
    return (row, col // 2 * 2 + 1 - lax.rem(col, 2))


GELU_A = 0.7978845608028654
GELU_B = 0.044715


def middle_kernel(
    rows, cols,
    heads_ref, tok_ref, g_ref, up_ref, down_ref, bup_ref, bout_ref, gain_ref, shift_ref, bdown_ref,
    wout_ref, wq_ref,
    gup_ref, gdown_ref, gout_ref, gbup_ref, output_ref, dres_ref, sums_ref, dheads_ref, wqo_ref,
    x, heads_all, resid, out_acc, norm_acc, hiddens, d_ups, low, d_send,
    mine, other, out_mine, out_other,
    send_d, recv_d, send_p, recv_p, send_o, recv_o, send_z, recv_z, send_r, recv_r, send_m, recv_m,
    local,
):
    step = pl.program_id(0)
    chips = cols // 2
    row, col = place()
    chip, lane = col // 2, lax.rem(col, 2)
    width = up_ref.shape[3]
    depth = wout_ref.shape[2]

    def part(r):
        return slice(r * width, (r + 1) * width)

    z_stage = over_line(
        chips, lambda at: wq_ref, lambda at: wqo_ref.at[lane, row, at], send_z, recv_z
    )

    def r_stage(c):
        return over_row(
            rows,
            lambda at: wqo_ref.at[lane, row, c],
            lambda at: wqo_ref.at[lane, at, c],
            send_r.at[c],
            recv_r.at[c],
        )

    m_stage = remote(wqo_ref.at[lane], wqo_ref.at[lane], send_m, recv_m, mate())
    m_arrival = remote(wqo_ref.at[1 - lane], wqo_ref.at[1 - lane], send_m, recv_m, mate())
    own_wq = pltpu.make_async_copy(wq_ref, wqo_ref.at[lane, row, chip], local.at[0])
    d_stage = over_col(
        cols, lambda at: d_send.at[at], lambda at: dheads_ref.at[at], send_d, recv_d
    )
    own_d = pltpu.make_async_copy(d_send.at[col], dheads_ref.at[col], local.at[1])

    def pair(at, which):
        return remote(
            mine.at[which, at], other.at[which, at], send_p.at[which, at], recv_p.at[which, at],
            mate(),
        )

    pair_out = remote(out_mine, out_other, send_o, recv_o, mate())

    @pl.when(step == 0)
    def _():
        greet(rows, cols)
        own_wq.start()
        z_stage.start()
        for s in range(cols):
            heads_all[s * depth : (s + 1) * depth] = heads_ref[s]
        stacked = flip(heads_all[...])
        for r in range(rows):
            branch = dot(stacked, wout_ref[r].reshape(cols * depth, width))
            resid[:, part(r)] = (
                tok_ref[:, part(r)].astype(f32) + branch + bout_ref[:, part(r)].astype(f32)
            )
        xhat, _ = moments(resid[...])
        x[...] = (xhat * gain_ref[...].astype(f32) + shift_ref[...].astype(f32)).astype(bf16)
        out_acc[...] = jnp.zeros_like(out_acc)
        norm_acc[...] = jnp.zeros_like(norm_acc)

    @pl.when(step == 1)
    def _():
        own_wq.wait()
        z_stage.wait_recv()
        for c in range(chips):
            r_stage(c).start()

    @pl.when(step < cols)
    def _():
        up = bup_ref[0].astype(f32)
        d_hidden = 0.0
        for r in range(rows):
            up = up + dot(x[:, part(r)], up_ref[r, 0], NT)
            d_hidden = d_hidden + dot(g_ref[:, part(r)], down_ref[r, 0], NT)
        square = up * up
        bent = jnp.tanh(GELU_A * up * (1.0 + GELU_B * square))
        half = 0.5 + 0.5 * bent
        hidden = (up * half).astype(bf16)
        slope = half + (0.5 * GELU_A) * up * (1.0 - bent * bent) * (1.0 + (3.0 * GELU_B) * square)
        d_up = d_hidden * slope
        gbup_ref[0] = jnp.sum(d_up, axis=0, keepdims=True)
        d_up = d_up.astype(bf16)
        hiddens[step] = hidden
        d_ups[step] = d_up
        for r in range(rows):
            out_acc[:, part(r)] += dot(hidden, down_ref[r, 0])
            norm_acc[:, part(r)] += dot(d_up, up_ref[r, 0])

    @pl.when(step == cols - 1)
    def _():
        output_ref[...] = (resid[...] + out_acc[...] + bdown_ref[...].astype(f32)).astype(bf16)
        xhat, inv = moments(resid[...])
        d_norm = norm_acc[...]
        grad = g_ref[...].astype(f32)
        d_resid = grad + norm_back(xhat, inv, d_norm * gain_ref[...].astype(f32))
        dres_ref[...] = d_resid
        low[...] = d_resid.astype(bf16)
        sums_ref[0:1] = jnp.sum(grad, axis=0, keepdims=True)
        sums_ref[1:2] = jnp.sum(d_norm * xhat, axis=0, keepdims=True)
        sums_ref[2:3] = jnp.sum(d_norm, axis=0, keepdims=True)
        sums_ref[3:4] = jnp.sum(d_resid, axis=0, keepdims=True)
        sums_ref[4:] = jnp.zeros((4, sums_ref.shape[1]), f32)
        for c in range(cols):
            found = 0.0
            for r in range(rows):
                found = found + dot(wout_ref[r, c], low[:, part(r)], NT)
            d_send[c] = found.astype(bf16)
        own_d.start()
        d_stage.start()
        found = dot(heads_all[...], low[...])
        for c in range(chips):
            first = found[2 * c * depth : (2 * c + 1) * depth]
            second = found[(2 * c + 1) * depth : (2 * c + 2) * depth]
            out_mine[c] = jnp.where(lane == 0, second, first).astype(bf16)
            kept = jnp.where(lane == 0, first, second)
            for r in range(rows):
                out_acc[c * depth : (c + 1) * depth, part(r)] = kept[:, part(r)]
        pair_out.start()

    at = step - cols

    @pl.when((at >= 0) & (at < chips))
    def _():
        c = at * 2 + 1 - lane
        mine[0, at] = dot(hiddens[c], g_ref[...], TN).astype(bf16)
        pair(at, 0).start()
        mine[1, at] = dot(d_ups[c], x[...], TN).astype(bf16)
        pair(at, 1).start()

    @pl.when(at == 0)
    def _():
        for c in range(chips):
            r_stage(c).wait_recv()
        m_stage.start()

    @pl.when(at >= chips)
    def _():
        k = at - chips
        c = k * 2 + lane
        grad_down = dot(hiddens[c], g_ref[...], TN)
        pair(k, 0).wait_recv()
        grad_down = (grad_down + other[0, k].astype(f32)).astype(bf16)
        grad_up = dot(d_ups[c], x[...], TN)
        pair(k, 1).wait_recv()
        grad_up = (grad_up + other[1, k].astype(f32)).astype(bf16)
        for r in range(rows):
            gdown_ref[r, 0] = grad_down[:, part(r)]
            gup_ref[r, 0] = grad_up[:, part(r)]

    @pl.when(step == 2 * cols - 1)
    def _():
        pair_out.wait_recv()
        for c in range(chips):
            for r in range(rows):
                kept = out_acc[c * depth : (c + 1) * depth, part(r)]
                gout_ref[r, c] = (kept + out_other[c, :, part(r)].astype(f32)).astype(bf16)
        d_stage.wait_recv()
        m_arrival.wait_recv()
        pair_out.wait_send()
        for k in range(chips):
            pair(k, 0).wait_send()
            pair(k, 1).wait_send()
            r_stage(k).wait_send()
        z_stage.wait_send()
        d_stage.wait_send()
        m_stage.wait_send()
        own_d.wait()


def middle(heads, tokens, grad, w_up, w_down, b_up, b_out, gain, shift, b_down, w_out, w_qkv):
    count, depth = tokens.shape
    rows, cols, units, width = w_up.shape
    chips = cols // 2
    head_cols = w_out.shape[2]
    any_space = pl.BlockSpec(memory_space=pl.ANY)
    weight = pl.BlockSpec(
        (rows, 1, units, width), lambda s: (0, jnp.minimum(s, cols - 1), 0, 0)
    )
    grad_spec = pl.BlockSpec(
        (rows, 1, units, width), lambda s: (0, jnp.maximum(s - cols - chips, 0), 0, 0)
    )
    grad_shape = jax.ShapeDtypeStruct((rows, chips, units, width), bf16)
    bias = pl.BlockSpec((1, 1, units), lambda s: (jnp.minimum(s, cols - 1), 0, 0))
    block, vec = whole((count, depth)), whole((1, depth))
    dma = pltpu.SemaphoreType.DMA
    vmem = pltpu.VMEM
    return pl.pallas_call(
        functools.partial(middle_kernel, rows, cols),
        grid=(2 * cols,),
        in_specs=[
            whole(heads.shape), block, block, weight, weight, bias, vec, vec, vec, vec,
            whole(w_out.shape), any_space,
        ],
        out_specs=[
            grad_spec, grad_spec, whole((rows, chips, head_cols, width)), bias, block, block,
            whole((8, depth)), any_space, any_space,
        ],
        out_shape=[
            grad_shape, grad_shape,
            jax.ShapeDtypeStruct((rows, chips, head_cols, width), bf16),
            jax.ShapeDtypeStruct((cols, 1, units), f32),
            jax.ShapeDtypeStruct((count, depth), bf16),
            jax.ShapeDtypeStruct((count, depth), f32),
            jax.ShapeDtypeStruct((8, depth), f32),
            jax.ShapeDtypeStruct((cols, head_cols, count), bf16),
            jax.ShapeDtypeStruct((2, rows, chips) + w_qkv.shape, bf16),
        ],
        scratch_shapes=[
            vmem((count, depth), bf16), vmem((depth, count), bf16),
            vmem((count, depth), f32), vmem((count, depth), f32), vmem((count, depth), f32),
            vmem((cols, count, units), bf16), vmem((cols, count, units), bf16),
            vmem((count, depth), bf16), vmem((cols, head_cols, count), bf16),
            vmem((2, chips, units, depth), bf16), vmem((2, chips, units, depth), bf16),
            vmem((chips, head_cols, depth), bf16), vmem((chips, head_cols, depth), bf16),
            dma((cols,)), dma((cols,)), dma((2, chips)), dma((2, chips)), dma, dma,
            dma((chips,)), dma((chips,)), dma((chips, rows)), dma((chips, rows)), dma, dma,
            dma((2,)),
        ],
        compiler_params=pltpu.CompilerParams(
            vmem_limit_bytes=63 << 20, collective_id=1, has_side_effects=True
        ),
        cost_estimate=cost(
            12 * count * depth * cols * units, 8 * depth * cols * units + 16 * count * depth
        ),
        name="middle",
    )(heads, tokens, grad, w_up, w_down, b_up, b_out, gain, shift, b_down, w_out, w_qkv)


def back_kernel(
    rows, cols, heads, seqs, tiles, sub,
    blk_ref, q_ref, k_ref, v_ref, do_ref, o_ref, lse_ref, x_ref, w_ref, tok_ref, dres_ref, gain_ref,
    gup_ref, gdown_ref, gout_ref, early_ref,
    dtok_ref, wup_ref, wdown_ref, wout_ref, wqkv_ref, all_ref, bias_ref,
    d_mixed, d_arrived, key_grad, value_grad, bias_sum, qkv_acc, qkv_send, qkv_recv, norm_acc,
    up_recv, down_recv, out_recv, up_send, down_send, out_send, up_line, down_line, out_line,
    small, small_core, small_row, small_line, bias_send, bias_recv,
    send_r, recv_r, send_z, recv_z, send_d, recv_d, send_q, recv_q, send_b, recv_b,
    send_s0, recv_s0, send_s1, recv_s1, send_s2, recv_s2, local,
):
    step = pl.program_id(0)
    chips = cols // 2
    row, col = place()
    chip, lane = col // 2, lax.rem(col, 2)
    work = heads * seqs * tiles
    last = work + 2 * cols - 1
    head = step // (seqs * tiles)
    seq = lax.rem(step // tiles, seqs)
    turn = lax.rem(step, tiles)
    i = tiles - 1 - turn
    tile = q_ref.shape[1]
    chunks, _, chunk = do_ref.shape
    chunks_seq = SEQ_LEN // chunk
    parts = tile // sub
    steps = tile
    start = pl.multiple_of(i * tile, tile)

    given = (gdown_ref, gup_ref, gout_ref)
    by_row = (down_recv, up_recv, out_recv)
    to_line = (down_send, up_send, out_send)
    by_line = (down_line, up_line, out_line)
    results = (wdown_ref, wup_ref, wout_ref)

    def row_stage(n):
        return over_row(
            rows, lambda at: given[n].at[at], lambda at: by_row[n].at[at], send_r.at[n],
            recv_r.at[n],
        )

    def own_row(n):
        return pltpu.make_async_copy(given[n].at[row], by_row[n].at[row], local.at[n])

    def line_stage(n):
        return over_line(
            chips, lambda at: to_line[n].at[at], lambda at: by_line[n].at[at], send_z.at[n],
            recv_z.at[n],
        )

    def add_rows(n):
        own_row(n).wait()
        row_stage(n).wait_recv()

        def one(c, carry):
            total = by_row[n][0, c].astype(f32)
            for r in range(1, rows):
                total = total + by_row[n][r, c].astype(f32)
            to_line[n][c] = total.astype(bf16)
            return carry

        lax.fori_loop(0, chips, one, 0)
        by_line[n][chip] = to_line[n][chip]
        line_stage(n).start()

    def d_stage(h):
        return over_col(
            cols, lambda at: d_mixed.at[h, at], lambda at: d_arrived.at[h, at], send_d.at[h],
            recv_d.at[h],
        )

    def own_d(h):
        return pltpu.make_async_copy(d_mixed.at[h, col], d_arrived.at[h, col], local.at[3 + h])

    q_stage = over_row(
        rows, lambda at: qkv_send.at[at], lambda at: qkv_recv.at[at], send_q, recv_q
    )
    b_stage = over_row(rows, lambda at: bias_send, lambda at: bias_recv.at[at], send_b, recv_b)
    s_core = remote(small.at[0], small_core, send_s0, recv_s0, mate())
    s_row = over_row(
        rows, lambda at: small.at[1], lambda at: small_row.at[at], send_s1, recv_s1
    )
    s_line = over_line(
        chips, lambda at: small.at[2], lambda at: small_line.at[at], send_s2, recv_s2
    )

    @pl.when(step == 0)
    def _():
        greet(rows, cols)
        for n in range(3):
            own_row(n).start()
            row_stage(n).start()

    @pl.when(step == work // 2 + 1)
    def _():
        add_rows(0)

    @pl.when((step < work) & (turn == 0))
    def _():
        key_grad[...] = jnp.zeros_like(key_grad)
        value_grad[...] = jnp.zeros_like(value_grad)

    @pl.when((step < work) & (turn == 0) & (seq == 0))
    def _():
        bias_sum[head] = jnp.zeros((HD, 128), f32)

    @pl.when(step < work)
    def _():
        d_out = jnp.concatenate([do_ref[b] for b in range(chunks)], axis=1)
        out = jnp.concatenate([o_ref[b] for b in range(chunks)], axis=1)
        delta = jnp.sum(d_out.astype(f32) * out.astype(f32), axis=0, keepdims=True)
        lse = lse_ref[0, 0]

        def cut(x, a):
            return x[:, a * sub : (a + 1) * sub]

        queries = [q_ref[0, a * sub : (a + 1) * sub, :] for a in range(parts)]
        query_blocks = [
            blk_ref[0, :, pl.ds(pl.multiple_of(start + a * sub, sub), sub)] for a in range(parts)
        ]

        def update(a, query_grad, key_start, count, masked):
            keys = k_ref[0, pl.ds(key_start, count), :]
            values = v_ref[0, pl.ds(key_start, count), :]
            scores = dot(keys, queries[a], NT) * SCALE2 - cut(lse, a)
            if masked:
                mask = tile_mask(blk_ref, key_start, count, query_blocks[a])
                scores = jnp.where(mask, scores, MASKED)
            probs = jnp.exp2(scores)
            d_values = dot(probs.astype(bf16), cut(d_out, a), NT)
            d_scores = (probs * (dot(values, cut(d_out, a)) - cut(delta, a))).astype(bf16)
            d_keys = dot(d_scores, queries[a])
            return query_grad + dot(keys, d_scores, TN), d_keys, d_values

        def add(key_start, count, d_keys, d_values):
            key_grad[pl.ds(key_start, count), :] += d_keys
            value_grad[pl.ds(key_start, count), :] += d_values

        def sweep(j, grads):
            key_start = pl.multiple_of(j * steps, steps)
            found = [update(a, grads[a], key_start, steps, False) for a in range(parts)]
            add(key_start, steps, sum(f[1] for f in found), sum(f[2] for f in found))
            return tuple(f[0] for f in found)

        grads = list(
            lax.fori_loop(0, start // steps, sweep, (jnp.zeros((HD, sub), f32),) * parts)
        )
        for a in range(parts):
            todo = [(pl.multiple_of(start + a * sub, sub), sub, True)]
            if a > 0:
                todo.append((start, a * sub, False))
            if a < parts - 1:
                todo.append((pl.multiple_of(start + (a + 1) * sub, BLOCK), BLOCK, True))
            for key_start, count, masked in todo:
                grads[a], d_keys, d_values = update(a, grads[a], key_start, count, masked)
                add(key_start, count, d_keys, d_values)

        def beyond(j, grad):
            key_start = pl.multiple_of(start + tile, BLOCK)
            grad, d_keys, d_values = update(parts - 1, grad, key_start, BLOCK, True)
            add(key_start, BLOCK, d_keys, d_values)
            return grad

        grads[-1] = lax.fori_loop(0, jnp.where(i < tiles - 1, 1, 0), beyond, grads[-1])
        query_grad = jnp.concatenate(grads, axis=1) * SCALE
        bias_sum[head, :, :1] += jnp.sum(query_grad, axis=1, keepdims=True)
        query_grad = query_grad.astype(bf16)
        for b in range(chunks):
            d_mixed[head, seq * chunks_seq + i * chunks + b, :HD] = query_grad[
                :, b * chunk : (b + 1) * chunk
            ]

    @pl.when((step < work) & (turn == tiles - 1))
    def _():
        def one(c, value_sum):
            where = pl.ds(pl.multiple_of(c * chunk, chunk), chunk)
            at = seq * chunks_seq + c
            d_mixed[head, at, HD : 2 * HD] = (key_grad[where, :].T * SCALE).astype(bf16)
            d_values = value_grad[where, :].T
            d_mixed[head, at, 2 * HD :] = d_values.astype(bf16)
            return value_sum + jnp.sum(d_values, axis=1, keepdims=True)

        value_sum = lax.fori_loop(0, chunks_seq, one, jnp.zeros((HD, 1), f32))
        bias_sum[head, :, 1:2] += value_sum

    for h in range(heads):

        @pl.when(step == (h + 1) * seqs * tiles - 1)
        def _():
            own_d(h).start()
            d_stage(h).start()

    at = step - work

    @pl.when(at == 0)
    def _():
        qkv_acc[...] = jnp.zeros_like(qkv_acc)
        bias_send[...] = bias_sum[...]
        bias_recv[row] = bias_sum[...]
        b_stage.start()

    @pl.when((at >= 0) & (at < cols))
    def _():
        grads = jnp.concatenate([d_mixed[h, at] for h in range(heads)], axis=0)
        qkv_acc[...] += dot(grads, x_ref[0])

    @pl.when(at == cols - 1)
    def _():
        width = qkv_send.shape[2]
        for r in range(rows):
            qkv_send[r] = qkv_acc[:, r * width : (r + 1) * width].astype(bf16)
        qkv_recv[row] = qkv_send[row]
        q_stage.start()
        add_rows(1)
        add_rows(2)
        norm_acc[...] = jnp.zeros_like(norm_acc)
        for h in range(heads):
            own_d(h).wait()
            d_stage(h).wait_recv()

    @pl.when(at >= cols)
    def _():
        c = at - cols
        width = w_ref.shape[3]
        found = flip(
            jnp.concatenate(
                [
                    d_arrived[h, c, j * HD : (j + 1) * HD, :]
                    for j in range(3)
                    for h in range(heads)
                ],
                axis=0,
            )
        )
        for r in range(rows):
            norm_acc[:, r * width : (r + 1) * width] += dot(found, w_ref[0, r, 0], NT)

    @pl.when(step == last)
    def _():
        xhat, inv = moments(tok_ref[...].astype(f32))
        d_norm = norm_acc[...]
        late = early_ref.shape[0] - 2
        small[0] = early_ref[...]
        small[0, late : late + 1] = jnp.sum(d_norm * xhat, axis=0, keepdims=True)
        small[0, late + 1 : late + 2] = jnp.sum(d_norm, axis=0, keepdims=True)
        s_core.start()
        dtok_ref[...] = dres_ref[...] + norm_back(xhat, inv, d_norm * gain_ref[...].astype(f32))
        s_core.wait_recv()
        small[1] = small[0] + small_core[...]
        small_row[row] = small[1]
        s_row.start()
        b_stage.wait_recv()
        bias_ref[...] = sum(bias_recv[r] for r in range(1, rows)) + bias_recv[0]
        q_stage.wait_recv()
        total = qkv_recv[0].astype(f32)
        for r in range(1, rows):
            total = total + qkv_recv[r].astype(f32)
        wqkv_ref[...] = total
        s_row.wait_recv()
        small[2] = sum(small_row[r] for r in range(1, rows)) + small_row[0]
        small_line[chip] = small[2]
        s_line.start()
        for n in range(3):
            line_stage(n).wait_recv()
            total = by_line[n][0].astype(f32)
            for c in range(1, chips):
                total = total + by_line[n][c].astype(f32)
            results[n][...] = total
        s_line.wait_recv()
        all_ref[...] = sum(small_line[c] for c in range(1, chips)) + small_line[0]
        for n in range(3):
            row_stage(n).wait_send()
            line_stage(n).wait_send()
        for h in range(heads):
            d_stage(h).wait_send()
        q_stage.wait_send()
        b_stage.wait_send()
        s_core.wait_send()
        s_row.wait_send()
        s_line.wait_send()


def backward(
    blocks, q, k, v, d_heads, out, lse, x, w_qkv, tokens, d_resid, gain, grad_up, grad_down,
    grad_out, early,
):
    heads, total, _ = q.shape
    count, depth = tokens.shape
    rows, chips, units, width = grad_up.shape
    cols = 2 * chips
    head_cols = grad_out.shape[2]
    seqs = total // SEQ_LEN
    tile, sub = 1024, 512
    tiles = SEQ_LEN // tile
    work = heads * seqs * tiles
    pairs = heads * seqs * SEQ_LEN * SEQ_LEN * 5 // 8

    def unpack(s):
        s = jnp.minimum(s, work - 1)
        return s // (seqs * tiles), lax.rem(s // tiles, seqs), tiles - 1 - lax.rem(s, tiles)

    def queries_map(s):
        h, b, i = unpack(s)
        return (h, b * tiles + i, 0)

    def keys_map(s):
        h, b, _ = unpack(s)
        return (h, b, 0)

    def heads_map(s):
        h, b, i = unpack(s)
        return (b * tiles + i, h, 0)

    def lse_map(s):
        h, b, i = unpack(s)
        return (h, b, 0, i)

    def w_map(s):
        c = jnp.maximum(s - work - cols, 0)
        return (lax.rem(c, 2), 0, c // 2, 0, 0)

    keys = pl.BlockSpec((1, SEQ_LEN, HD), keys_map)
    heads_spec = pl.BlockSpec((tile // chunk_of(tokens), HD, count), heads_map)
    any_space = pl.BlockSpec(memory_space=pl.ANY)
    block = whole((count, depth))
    dma, vmem = pltpu.SemaphoreType.DMA, pltpu.VMEM
    parts = heads * 3 * HD
    shape = jax.ShapeDtypeStruct
    small = early.shape
    return pl.pallas_call(
        functools.partial(back_kernel, rows, cols, heads, seqs, tiles, sub),
        grid=(work + 2 * cols,),
        in_specs=[
            pl.BlockSpec((1, 1, SEQ_LEN), lambda s: (unpack(s)[1], 0, 0)),
            pl.BlockSpec((1, tile, HD), queries_map), keys, keys, heads_spec, heads_spec,
            pl.BlockSpec((1, 1, 1, tile), lse_map),
            pl.BlockSpec((1, count, depth), lambda s: (jnp.clip(s - work, 0, cols - 1), 0, 0)),
            pl.BlockSpec((1, rows, 1) + w_qkv.shape[3:], w_map),
            block, block, whole((1, depth)), any_space, any_space, any_space, whole(small),
        ],
        out_specs=[
            block, whole((units, width)), whole((units, width)), whole((head_cols, width)),
            whole((parts, width)), whole(small), whole((heads, HD, 128)),
        ],
        out_shape=[
            shape((count, depth), f32), shape((units, width), f32), shape((units, width), f32),
            shape((head_cols, width), f32), shape((parts, width), f32), shape(small, f32),
            shape((heads, HD, 128), f32),
        ],
        scratch_shapes=[
            vmem((heads, cols, 3 * HD, count), bf16), vmem((heads, cols, 3 * HD, count), bf16),
            vmem((SEQ_LEN, HD), f32), vmem((SEQ_LEN, HD), f32), vmem((heads, HD, 128), f32),
            vmem((parts, depth), f32), vmem((rows, parts, width), bf16),
            vmem((rows, parts, width), bf16), vmem((count, depth), f32),
            vmem((rows, chips, units, width), bf16), vmem((rows, chips, units, width), bf16),
            vmem((rows, chips, head_cols, width), bf16),
            vmem((chips, units, width), bf16), vmem((chips, units, width), bf16),
            vmem((chips, head_cols, width), bf16),
            vmem((chips, units, width), bf16), vmem((chips, units, width), bf16),
            vmem((chips, head_cols, width), bf16),
            vmem((3,) + small, f32), vmem(small, f32), vmem((rows,) + small, f32),
            vmem((chips,) + small, f32),
            vmem((heads, HD, 128), f32), vmem((rows, heads, HD, 128), f32),
            dma((3, rows)), dma((3, rows)), dma((3, chips)), dma((3, chips)),
            dma((heads, cols)), dma((heads, cols)), dma((rows,)), dma((rows,)),
            dma((rows,)), dma((rows,)), dma, dma, dma((rows,)), dma((rows,)),
            dma((chips,)), dma((chips,)), dma((3 + heads,)),
        ],
        compiler_params=pltpu.CompilerParams(
            vmem_limit_bytes=63 << 20, collective_id=2, has_side_effects=True
        ),
        cost_estimate=cost(40 * pairs * HD, 16 * heads * total * HD, pairs),
        name="backward",
    )(
        blocks, q, k, v, d_heads, out, lse, x, w_qkv, tokens, d_resid, gain, grad_up, grad_down,
        grad_out, early,
    )


def chunk_of(tokens):
    return tokens.shape[0]


def swap(x, axis, groups=None):
    return lax.all_to_all(x, axis, 0, 0, tiled=True, axis_index_groups=groups)


def body(
    tokens, blocks, w_qkv, b_qv, w_out, b_out, w_up, b_up, w_down, b_down,
    gain1, shift1, gain2, shift2, grad_out,
):
    rows, cols = lax.axis_size("row"), lax.axis_size("col")
    local_rows, depth = tokens.shape
    group_rows = local_rows * cols
    head_cols = w_qkv.shape[2]
    heads = head_cols // HD
    units = w_up.shape[0]

    def vec(v):
        return v.reshape(1, -1)

    xhat, _ = moments(tokens.astype(f32))
    attn_input = (xhat * gain1.astype(f32) + shift1.astype(f32)).astype(bf16)
    w_qkv_flat = w_qkv.reshape(w_qkv.shape[0], 3 * head_cols)

    def gather_all(w):
        return lax.all_gather(w, ("row", "col"), axis=0, tiled=False).reshape(
            (rows, cols) + w.shape
        )

    out_weight, up_weight, down_weight = gather_all(w_out), gather_all(w_up), gather_all(w_down)

    attn_rows, block_ids, up_bias, qkv_here = gather_inputs(
        attn_input, vec(blocks), vec(b_up), w_qkv_flat, rows, cols
    )
    block_ids = block_ids.reshape(group_rows // SEQ_LEN, 1, SEQ_LEN)
    q, k, v = project_qkv(attn_rows.reshape(group_rows, depth), qkv_here, b_qv)
    found, lse = attend(q, k, v, block_ids, local_rows)
    arrived = swap(found, "col")
    grad_up, grad_down, grad_wout, grad_bup, output, d_resid, sums, d_heads, qkv_all = middle(
        arrived, tokens, grad_out, up_weight, down_weight, up_bias, vec(b_out), vec(gain2),
        vec(shift2), vec(b_down), out_weight, w_qkv_flat,
    )
    hidden_units = units * cols
    used = 4 + hidden_units // depth
    spare = (used + 9) // 8 * 8 - used
    early = jnp.concatenate(
        [sums[:4], grad_bup.reshape(-1, depth), jnp.zeros((spare, depth), f32)]
    )
    grad_tokens, grad_wup, grad_wdown, grad_wout, grad_wqkv, small, bias = backward(
        block_ids, q, k, v, d_heads, found, lse, attn_rows, qkv_all, tokens, d_resid, vec(gain1),
        grad_up, grad_down, grad_wout, early,
    )
    grad_wqkv = (
        grad_wqkv.reshape(heads, 3, HD, depth // rows)
        .transpose(3, 1, 0, 2)
        .reshape(depth // rows, 3, head_cols)
    )
    grad_bqv = bias[:, :, :2].reshape(head_cols, 2).T
    grad_bdown, grad_gain2, grad_shift2, grad_bout = small[:4]
    grad_bup = lax.dynamic_slice_in_dim(
        small[4:used].reshape(-1), lax.axis_index("col") * units, units
    )
    grad_gain1, grad_shift1 = small[-2:]
    return (
        output, grad_tokens, grad_wqkv, grad_bqv, grad_wout, grad_bout, grad_wup, grad_bup,
        grad_wdown, grad_bdown, grad_gain1, grad_shift1, grad_gain2, grad_shift2,
    )


def solution(mesh):
    tokens, weight, whole_vec = P(("row", "col"), None), P("col", "row"), P()
    qkv, bias_qv = P("row", None, "col"), P(None, "col")
    return jax.shard_map(
        body,
        mesh=mesh,
        in_specs=(
            tokens, P(("row", "col")), qkv, bias_qv, weight, whole_vec, weight, P("col"), weight,
            whole_vec, whole_vec, whole_vec, whole_vec, whole_vec, tokens,
        ),
        out_specs=(
            tokens, tokens, qkv, bias_qv, weight, whole_vec, weight, P("col"), weight,
            whole_vec, whole_vec, whole_vec, whole_vec, whole_vec,
        ),
        check_vma=False,
    )
```

```python
import functools

import jax
import jax.numpy as jnp
from jax import lax
from jax.experimental import pallas as pl
from jax.experimental.pallas import tpu as pltpu
from jax.sharding import PartitionSpec as P

HD = 64
SEQ_LEN = 4096
BLOCK = 256
EPS = 1e-05
SCALE = HD ** (-0.5)
SCALE2 = SCALE * 1.4426950408889634
MASKED = -1e30
ONES = 16
MESH = pl.DeviceIdType.MESH
VMEM_LIMIT = 60 << 20

f32 = jnp.float32
bf16 = jnp.bfloat16

NN = (((1,), (0,)), ((), ()))
NT = (((1,), (1,)), ((), ()))
TN = (((0,), (0,)), ((), ()))


def dot(a, b, dims=NN):
    return lax.dot_general(a, b, dims, preferred_element_type=f32)


def flip(x):
    return x.astype(f32).T.astype(bf16)


def params(**more):
    return pltpu.CompilerParams(vmem_limit_bytes=VMEM_LIMIT, **more)


def cost(flops, nbytes, transcendentals=0):
    return pl.CostEstimate(flops=flops, bytes_accessed=nbytes, transcendentals=transcendentals)


def whole(shape):
    return pl.BlockSpec(shape, lambda *_: (0,) * len(shape))


def moments(v):
    center = jnp.mean(v, axis=-1, keepdims=True)
    centered = v - center
    spread = jnp.mean(centered * centered, axis=-1, keepdims=True)
    inv = lax.rsqrt(spread + EPS)
    return centered * inv, inv


def norm_back(xhat, inv, e):
    return inv * (
        e - jnp.mean(e, axis=-1, keepdims=True) - xhat * jnp.mean(e * xhat, axis=-1, keepdims=True)
    )


def place():
    return lax.axis_index("row"), lax.axis_index("col")


def greet(rows, cols):
    row, col = place()
    barrier = pltpu.get_barrier_semaphore()

    def to_col(k, carry):
        pl.semaphore_signal(
            barrier, inc=1, device_id=(row, lax.rem(col + k, cols)), device_id_type=MESH
        )
        return carry

    def to_row(k, carry):
        pl.semaphore_signal(
            barrier, inc=1, device_id=(lax.rem(row + k, rows), col), device_id_type=MESH
        )
        return carry

    lax.fori_loop(1, cols, to_col, 0)
    lax.fori_loop(1, rows, to_row, 0)
    pl.semaphore_wait(barrier, rows + cols - 2)


def remote(src, dst, send, recv, device):
    return pltpu.make_async_remote_copy(
        src_ref=src, dst_ref=dst, send_sem=send, recv_sem=recv, device_id=device, device_id_type=MESH
    )


def each(count, act):
    def turn(k, carry):
        act(k)
        return carry

    lax.fori_loop(1, count, turn, 0)


class Exchange:
    def __init__(self, count, here, slot, to, out, into, send, recv):
        self.count, self.here, self.slot, self.to = count, here, slot, to
        self.out, self.into, self.send, self.recv = out, into, send, recv

    def copy(self, k):
        at = self.slot(k)
        return remote(
            self.out(at), self.into(self.here), self.send.at[k], self.recv.at[self.here], self.to(k)
        )

    def arrival(self, k):
        at = self.slot(k)
        return remote(self.out(at), self.into(at), self.send.at[k], self.recv.at[at], self.to(k))

    def start(self):
        each(self.count, lambda k: self.copy(k).start())

    def wait_recv(self):
        each(self.count, lambda k: self.arrival(k).wait_recv())

    def wait_send(self):
        each(self.count, lambda k: self.copy(k).wait_send())


def over_row(rows, out, into, send, recv):
    row, col = place()
    slot = lambda k: lax.rem(row + k, rows)
    return Exchange(rows, row, slot, lambda k: (slot(k), col), out, into, send, recv)


def over_col(cols, out, into, send, recv):
    row, col = place()
    slot = lambda k: lax.rem(col + k, cols)
    return Exchange(cols, col, slot, lambda k: (row, slot(k)), out, into, send, recv)


def over_line(chips, out, into, send, recv):
    row, col = place()
    chip, lane = col // 2, lax.rem(col, 2)
    slot = lambda k: lax.rem(chip + k, chips)
    return Exchange(chips, chip, slot, lambda k: (row, slot(k) * 2 + lane), out, into, send, recv)


def mate():
    row, col = place()
    return (row, col // 2 * 2 + 1 - lax.rem(col, 2))


def front_kernel(
    rows, cols, heads,
    tok_ref, gain_ref, shift_ref, blk_ref, bup_ref, wq_ref, bias_ref, wout_ref, wup_ref, wdown_ref,
    xo_ref, q_ref, k_ref, v_ref, found_ref, arrived_ref, lse_ref, blko_ref, bupo_ref,
    wouto_ref, wupo_ref, wdowno_ref,
    xs, wqs, qs, ks, vs, vt, totals, tops, founds, blks, bups,
    send_x, recv_x, send_q, recv_q, send_s, recv_s, send_f, recv_f,
    send_wz, recv_wz, send_wr, recv_wr, send_wm, recv_wm, local_x, local_q, local_f, local_w,
):
    chips = cols // 2
    row, me = place()
    chip, lane = me // 2, lax.rem(me, 2)
    count = tok_ref.shape[0]
    tile = 2 * count
    seq_chips = SEQ_LEN // tile
    depth = wq_ref.shape[0]
    width = heads * HD

    xhat, _ = moments(tok_ref[...].astype(f32))
    xs[me] = (xhat * gain_ref[...].astype(f32) + shift_ref[...].astype(f32)).astype(bf16)
    blks[me] = blk_ref[...]
    bups[me] = bup_ref[...]
    own_rows = pl.ds(pl.multiple_of(row * depth, depth), depth)
    wqs[own_rows] = wq_ref[...]
    vt[:, HD:, :] = jnp.ones((heads, ONES, vt.shape[2]), bf16)
    greet(rows, cols)

    def chunk(owner, target, route, at):
        return remote(
            xs.at[owner], xs.at[owner], send_x.at[route, at], recv_x.at[route, at], (row, target)
        )

    def to_mate(owner, at):
        return remote(xs.at[owner], xs.at[owner], send_x.at[2, at], recv_x.at[2, at], mate())

    given = (wout_ref, wup_ref, wdown_ref)
    gathered = (wouto_ref, wupo_ref, wdowno_ref)

    q_stage = over_row(
        rows,
        lambda at: wq_ref,
        lambda at: wqs.at[pl.ds(pl.multiple_of(at * depth, depth), depth)],
        send_q,
        recv_q,
    )
    small = [
        over_col(cols, lambda at: blk_ref, lambda at: blks.at[at], send_s.at[0], recv_s.at[0]),
        over_col(cols, lambda at: bup_ref, lambda at: bups.at[at], send_s.at[1], recv_s.at[1]),
    ]
    f_stage_out = lambda at: founds.at[at]
    f_stage = over_col(cols, f_stage_out, lambda at: arrived_ref.at[at], send_f, recv_f)

    def w_line(n):
        return over_line(
            chips, lambda at: given[n], lambda at: gathered[n].at[lane, at, row], send_wz.at[n],
            recv_wz.at[n],
        )

    def w_row(n, c, out):
        return over_row(
            rows, lambda at: out, lambda at: gathered[n].at[lane, c, at], send_wr.at[n, c],
            recv_wr.at[n, c],
        )

    def w_own(n):
        return pltpu.make_async_copy(given[n], gathered[n].at[lane, chip, row], local_w.at[n])

    def w_mate(n, c, side):
        block = gathered[n].at[side, c]
        return remote(block, block, send_wm.at[n, c], recv_wm.at[n, c], mate())

    q_stage.start()
    for exchange in small:
        exchange.start()

    @pl.when(chip + 1 < chips)
    def _():
        chunk(me, me + 2, 0, chip).start()

    @pl.when(chip > 0)
    def _():
        chunk(me, me - 2, 1, chip).start()

    to_mate(me, chip).start()
    for n in range(3):
        w_own(n).start()
        w_row(n, chip, given[n]).start()
        w_line(n).start()
    q_stage.wait_recv()
    for exchange in small:
        exchange.wait_recv()

    def update(h, q_tile, q_low, q_count, key_start, key_count, mask):
        lanes = pl.ds(q_low, q_count)
        query = qs[h, pl.ds(pl.multiple_of(q_tile * tile + q_low, BLOCK), q_count), :]
        keys = pl.ds(pl.multiple_of(key_start, BLOCK), key_count)
        scores = dot(ks[h, keys, :], query, NT)
        if mask is not None:
            scores = jnp.where(mask, scores, MASKED)
        top = tops[h, q_tile, :, lanes]
        higher = jnp.maximum(top, jnp.max(scores, axis=0, keepdims=True) * SCALE2)
        probs = jnp.exp2(scores * SCALE2 - higher)
        part = dot(vt[h, :, keys], probs.astype(bf16))
        totals[h, q_tile, :, lanes] = totals[h, q_tile, :, lanes] * jnp.exp2(top - higher) + part
        tops[h, q_tile, :, lanes] = higher

    def column(blocks, amount):
        return jnp.broadcast_to(blocks, (128, amount)).T[:, :1]

    def diagonal(p):
        low, high = blks[2 * p], blks[2 * p + 1]
        first = column(jnp.concatenate([low, high[:, :BLOCK]], axis=1), count + BLOCK)
        second = column(jnp.concatenate([low, high], axis=1), tile)
        for h in range(heads):
            update(h, p, 0, count, p * tile, count + BLOCK, low >= first)
            update(h, p, count, count, p * tile, tile, high >= second)

    def boundary(p):
        mask = blks[2 * p + 1][:, count - BLOCK :] >= column(blks[2 * p + 2][:, :BLOCK], BLOCK)
        for h in range(heads):
            update(h, p, tile - BLOCK, BLOCK, (p + 1) * tile, BLOCK, mask)

    def project(p):
        both = jnp.concatenate([xs[2 * p], xs[2 * p + 1]], axis=0)
        mixed = dot(both, wqs[...])
        bias = bias_ref[...].astype(f32)
        where = pl.ds(pl.multiple_of(p * tile, tile), tile)
        for h in range(heads):
            at = [slice(j * width + h * HD, j * width + (h + 1) * HD) for j in range(3)]
            here = slice(h * HD, (h + 1) * HD)
            qs[h, where, :] = (mixed[:, at[0]] + bias[0:1, here]).astype(bf16)
            ks[h, where, :] = mixed[:, at[1]].astype(bf16)
            values = (mixed[:, at[2]] + bias[1:2, here]).astype(bf16)
            vs[h, where, :] = values
            vt[h, :HD, where] = flip(values)
            totals[h, p] = jnp.zeros(totals.shape[2:], f32)
            tops[h, p] = jnp.full(tops.shape[2:], MASKED, f32)

    def keep(p):
        where = pl.ds(pl.multiple_of(p * tile, tile), tile)
        pairs = [
            pltpu.make_async_copy(held.at[:, where, :], out.at[:, where, :], local_q.at[n, p])
            for n, (held, out) in enumerate(((qs, q_ref), (ks, k_ref), (vs, v_ref)))
        ]
        return pairs + [
            pltpu.make_async_copy(xs.at[2 * p + c], xo_ref.at[2 * p + c], local_x.at[2 * p + c])
            for c in range(2)
        ]

    def kept(c):
        return pltpu.make_async_copy(founds.at[c], found_ref.at[c], local_f.at[0, c])

    def own(c):
        return pltpu.make_async_copy(founds.at[c], arrived_ref.at[c], local_f.at[1, 0])

    def conclude(p):
        for h in range(heads):
            mass = totals[h, p, HD : HD + 1, :]
            out = (totals[h, p, :HD, :] / mass).astype(bf16)
            for c in range(2):
                founds[2 * p + c, h * HD : (h + 1) * HD, :] = out[:, c * count : (c + 1) * count]
            lse_ref[
                h, p // seq_chips, :, pl.ds(pl.multiple_of(lax.rem(p, seq_chips) * tile, tile), tile)
            ] = tops[h, p] + jnp.log2(mass)
        for c in range(2):
            owner = 2 * p + c
            kept(owner).start()

            @pl.when(owner == me)
            def _():
                own(owner).start()

            @pl.when(owner != me)
            def _():
                f_stage.copy(lax.rem(owner - me + cols, cols)).start()

    def event(e, carry):
        hop = (e + 1) // 2
        lower = lax.rem(e, 2) == 1
        p = jnp.where(lower, chip - hop, chip + hop)

        @pl.when(lower)
        def _():
            below, above = chip - hop, chip + hop

            @pl.when(below >= 0)
            def _():
                owner = below * 2 + lane
                chunk(owner, me, 0, below).wait_recv()

                @pl.when(chip + 1 < chips)
                def _():
                    chunk(owner, me + 2, 0, below).start()

                to_mate(owner, below).start()

            @pl.when(above < chips)
            def _():
                owner = above * 2 + lane
                chunk(owner, me, 1, above).wait_recv()

                @pl.when(chip > 0)
                def _():
                    chunk(owner, me - 2, 1, above).start()

                to_mate(owner, above).start()

        @pl.when(e == min(3, 2 * chips - 3))
        def _():
            for n in range(3):
                w_line(n).wait_recv()

                def onward(k, carry):
                    c = lax.rem(chip + k, chips)
                    w_row(n, c, gathered[n].at[lane, c, row]).start()
                    return carry

                lax.fori_loop(1, chips, onward, 0)

        @pl.when(e == 2 * chips - 3)
        def _():
            for n in range(3):
                w_own(n).wait()
                w_row(n, chip, given[n]).wait_recv()
                w_mate(n, chip, lane).start()

        @pl.when((p >= 0) & (p < chips))
        def _():
            to_mate(2 * p + 1 - lane, p).wait_recv()
            project(p)
            for copy in keep(p):
                copy.start()
            first = p // seq_chips * seq_chips
            final = first + seq_chips - 1
            high = jnp.minimum(chip + hop - 1, final)
            low = jnp.maximum(jnp.maximum(chip - hop, 0), first)
            diagonal(p)

            @pl.when(lower & (p < final))
            def _():
                boundary(p)

            @pl.when(lower & (p == first))
            def _():
                conclude(p)

            amount = jnp.where(lower, high - p, p - low)

            def pair(j, carry):
                q_tile = jnp.where(lower, p + 1 + j, p)
                key_tile = jnp.where(lower, p, low + j)
                for h in range(heads):
                    update(h, q_tile, 0, tile, key_tile * tile, tile, None)

                @pl.when(lower & (p == first) & ((q_tile == final) | (q_tile < high)))
                def _():
                    conclude(q_tile)

                return carry

            lax.fori_loop(0, amount, pair, 0)

            @pl.when(jnp.logical_not(lower) & (p > first) & (hop > 0))
            def _():
                boundary(p - 1)

                @pl.when(low == first)
                def _():
                    conclude(p - 1)

            @pl.when(jnp.logical_not(lower) & (p == final) & (low == first))
            def _():
                conclude(p)

        return carry

    lax.fori_loop(0, 2 * chips - 1, event, 0)

    for n in range(3):

        def across(k, carry):
            c = lax.rem(chip + k, chips)
            w_row(n, c, given[n]).wait_recv()
            w_mate(n, c, lane).start()
            return carry

        lax.fori_loop(1, chips, across, 0)
    for c in range(cols):
        bupo_ref[c] = bups[c]
        at = c * count
        blko_ref[at // SEQ_LEN, :, at % SEQ_LEN : at % SEQ_LEN + count] = blks[c]
    f_stage.wait_recv()
    for c in range(chips):
        for n in range(3):
            w_mate(n, c, 1 - lane).wait_recv()
            w_mate(n, c, lane).wait_send()
            w_row(n, c, given[n]).wait_send()
        for copy in keep(c):
            copy.wait()
        kept(2 * c).wait()
        kept(2 * c + 1).wait()
        to_mate(me, c).wait_send()

        @pl.when((c <= chip) & (chip + 1 < chips))
        def _():
            chunk(me, me, 0, c).wait_send()

        @pl.when((c >= chip) & (chip > 0))
        def _():
            chunk(me, me, 1, c).wait_send()

    own(me).wait()
    for n in range(3):
        w_line(n).wait_send()
    f_stage.wait_send()
    q_stage.wait_send()
    for exchange in small:
        exchange.wait_send()


def front(tokens, gain, shift, blocks, b_up, w_qkv, b_qv, w_out, w_up, w_down, rows, cols):
    count, depth = tokens.shape
    head_cols = w_qkv.shape[1] // 3
    heads = head_cols // HD
    chips = cols // 2
    total = count * cols
    tile = 2 * count
    any_space = pl.BlockSpec(memory_space=pl.ANY)
    in_vmem = pl.BlockSpec(memory_space=pltpu.VMEM)
    dma, vmem, shape = pltpu.SemaphoreType.DMA, pltpu.VMEM, jax.ShapeDtypeStruct
    pairs = heads * total * SEQ_LEN * 5 // 8
    held = (heads, total, HD)
    return pl.pallas_call(
        functools.partial(front_kernel, rows, cols, heads),
        in_specs=[in_vmem] * 10,
        out_specs=[any_space] * 6 + [in_vmem] * 3 + [any_space] * 3,
        out_shape=[
            shape((cols, count, depth), bf16), shape(held, bf16), shape(held, bf16),
            shape(held, bf16), shape((cols, head_cols, count), bf16),
            shape((cols, head_cols, count), bf16),
            shape((heads, total // SEQ_LEN, 1, SEQ_LEN), f32),
            shape((total // SEQ_LEN, 1, SEQ_LEN), jnp.int32), shape((cols,) + b_up.shape, bf16),
        ] + [shape((2, chips, rows) + w.shape, bf16) for w in (w_out, w_up, w_down)],
        scratch_shapes=[
            vmem((cols, count, depth), bf16), vmem((depth, 3 * head_cols), bf16),
            vmem(held, bf16), vmem(held, bf16), vmem(held, bf16),
            vmem((heads, HD + ONES, total), bf16),
            vmem((heads, chips, HD + ONES, tile), f32), vmem((heads, chips, 1, tile), f32),
            vmem((cols, head_cols, count), bf16), vmem((cols,) + blocks.shape, jnp.int32),
            vmem((cols,) + b_up.shape, bf16),
            dma((3, chips)), dma((3, chips)), dma((rows,)), dma((rows,)),
            dma((2, cols)), dma((2, cols)), dma((cols,)), dma((cols,)),
            dma((3, chips)), dma((3, chips)), dma((3, chips, rows)), dma((3, chips, rows)),
            dma((3, chips)), dma((3, chips)),
            dma((cols,)), dma((3, chips)), dma((2, cols)), dma((3,)),
        ],
        compiler_params=pltpu.CompilerParams(
            vmem_limit_bytes=63 << 20, collective_id=0, has_side_effects=True
        ),
        cost_estimate=cost(16 * pairs * HD, 16 * heads * total * HD, pairs),
        name="front",
    )(tokens, gain, shift, blocks, b_up, w_qkv, b_qv, w_out, w_up, w_down)


def tile_mask(blk_ref, key_start, count, query_blocks):
    key_blocks = jnp.broadcast_to(blk_ref[0, :, pl.ds(key_start, count)], (128, count)).T[:, :1]
    return query_blocks >= key_blocks


GELU_A = 0.7978845608028654
GELU_B = 0.044715


def middle_kernel(
    rows, cols,
    heads_ref, tok_ref, g_ref, up_ref, down_ref, bup_ref, bout_ref, gain_ref, shift_ref, bdown_ref,
    wout_ref, wq_ref,
    gup_ref, gdown_ref, gout_ref, gbup_ref, output_ref, dres_ref, sums_ref, dheads_ref, wqo_ref,
    x, heads_all, resid, out_acc, norm_acc, hiddens, d_ups, low, d_send,
    mine, other, out_mine, out_other,
    send_d, recv_d, send_p, recv_p, send_o, recv_o, send_z, recv_z, send_r, recv_r, send_m, recv_m,
    local,
):
    step = pl.program_id(0)
    chips = cols // 2
    row, col = place()
    chip, lane = col // 2, lax.rem(col, 2)
    width = up_ref.shape[4]
    depth = wout_ref.shape[3]

    def part(r):
        return slice(r * width, (r + 1) * width)

    z_stage = over_line(
        chips, lambda at: wq_ref, lambda at: wqo_ref.at[lane, row, at], send_z, recv_z
    )

    def r_stage(c):
        return over_row(
            rows,
            lambda at: wqo_ref.at[lane, row, c],
            lambda at: wqo_ref.at[lane, at, c],
            send_r.at[c],
            recv_r.at[c],
        )

    m_stage = remote(wqo_ref.at[lane], wqo_ref.at[lane], send_m, recv_m, mate())
    m_arrival = remote(wqo_ref.at[1 - lane], wqo_ref.at[1 - lane], send_m, recv_m, mate())
    own_wq = pltpu.make_async_copy(wq_ref, wqo_ref.at[lane, row, chip], local.at[0])
    d_stage = over_col(
        cols, lambda at: d_send.at[at], lambda at: dheads_ref.at[at], send_d, recv_d
    )
    own_d = pltpu.make_async_copy(d_send.at[col], dheads_ref.at[col], local.at[1])

    def pair(at, which):
        return remote(
            mine.at[which, at], other.at[which, at], send_p.at[which, at], recv_p.at[which, at],
            mate(),
        )

    pair_out = remote(out_mine, out_other, send_o, recv_o, mate())

    @pl.when(step == 0)
    def _():
        greet(rows, cols)
        own_wq.start()
        z_stage.start()
        for s in range(cols):
            heads_all[s * depth : (s + 1) * depth] = heads_ref[s]
        stacked = flip(heads_all[...])
        for r in range(rows):
            branch = sum(
                dot(
                    stacked[:, c * depth : (c + 1) * depth],
                    wout_ref[c % 2, c // 2, r],
                )
                for c in range(cols)
            )
            resid[:, part(r)] = (
                tok_ref[:, part(r)].astype(f32) + branch + bout_ref[:, part(r)].astype(f32)
            )
        xhat, _ = moments(resid[...])
        x[...] = (xhat * gain_ref[...].astype(f32) + shift_ref[...].astype(f32)).astype(bf16)
        out_acc[...] = jnp.zeros_like(out_acc)
        norm_acc[...] = jnp.zeros_like(norm_acc)

    @pl.when(step == 1)
    def _():
        own_wq.wait()
        z_stage.wait_recv()
        for c in range(chips):
            r_stage(c).start()

    @pl.when(step < cols)
    def _():
        up = bup_ref[0].astype(f32)
        d_hidden = 0.0
        for r in range(rows):
            up = up + dot(x[:, part(r)], up_ref[0, 0, r], NT)
            d_hidden = d_hidden + dot(g_ref[:, part(r)], down_ref[0, 0, r], NT)
        square = up * up
        bent = jnp.tanh(GELU_A * up * (1.0 + GELU_B * square))
        half = 0.5 + 0.5 * bent
        hidden = (up * half).astype(bf16)
        slope = half + (0.5 * GELU_A) * up * (1.0 - bent * bent) * (1.0 + (3.0 * GELU_B) * square)
        d_up = d_hidden * slope
        gbup_ref[0] = jnp.sum(d_up, axis=0, keepdims=True)
        d_up = d_up.astype(bf16)
        hiddens[step] = hidden
        d_ups[step] = d_up
        for r in range(rows):
            out_acc[:, part(r)] += dot(hidden, down_ref[0, 0, r])
            norm_acc[:, part(r)] += dot(d_up, up_ref[0, 0, r])

    @pl.when(step == cols - 1)
    def _():
        output_ref[...] = (resid[...] + out_acc[...] + bdown_ref[...].astype(f32)).astype(bf16)
        xhat, inv = moments(resid[...])
        d_norm = norm_acc[...]
        grad = g_ref[...].astype(f32)
        d_resid = grad + norm_back(xhat, inv, d_norm * gain_ref[...].astype(f32))
        dres_ref[...] = d_resid
        low[...] = d_resid.astype(bf16)
        sums_ref[0:1] = jnp.sum(grad, axis=0, keepdims=True)
        sums_ref[1:2] = jnp.sum(d_norm * xhat, axis=0, keepdims=True)
        sums_ref[2:3] = jnp.sum(d_norm, axis=0, keepdims=True)
        sums_ref[3:4] = jnp.sum(d_resid, axis=0, keepdims=True)
        sums_ref[4:] = jnp.zeros((4, sums_ref.shape[1]), f32)
        for c in range(cols):
            found = 0.0
            for r in range(rows):
                found = found + dot(wout_ref[c % 2, c // 2, r], low[:, part(r)], NT)
            d_send[c] = found.astype(bf16)
        own_d.start()
        d_stage.start()
        found = dot(heads_all[...], low[...])
        for c in range(chips):
            first = found[2 * c * depth : (2 * c + 1) * depth]
            second = found[(2 * c + 1) * depth : (2 * c + 2) * depth]
            out_mine[c] = jnp.where(lane == 0, second, first).astype(bf16)
            kept = jnp.where(lane == 0, first, second)
            for r in range(rows):
                out_acc[c * depth : (c + 1) * depth, part(r)] = kept[:, part(r)]
        pair_out.start()

    at = step - cols

    @pl.when((at >= 0) & (at < chips))
    def _():
        c = at * 2 + 1 - lane
        mine[0, at] = dot(hiddens[c], g_ref[...], TN).astype(bf16)
        pair(at, 0).start()
        mine[1, at] = dot(d_ups[c], x[...], TN).astype(bf16)
        pair(at, 1).start()

    @pl.when(at == 0)
    def _():
        for c in range(chips):
            r_stage(c).wait_recv()
        m_stage.start()

    @pl.when(at >= chips)
    def _():
        k = at - chips
        c = k * 2 + lane
        grad_down = dot(hiddens[c], g_ref[...], TN)
        pair(k, 0).wait_recv()
        grad_down = (grad_down + other[0, k].astype(f32)).astype(bf16)
        grad_up = dot(d_ups[c], x[...], TN)
        pair(k, 1).wait_recv()
        grad_up = (grad_up + other[1, k].astype(f32)).astype(bf16)
        for r in range(rows):
            gdown_ref[r, 0] = grad_down[:, part(r)]
            gup_ref[r, 0] = grad_up[:, part(r)]

    @pl.when(step == 2 * cols - 1)
    def _():
        pair_out.wait_recv()
        for c in range(chips):
            for r in range(rows):
                kept = out_acc[c * depth : (c + 1) * depth, part(r)]
                gout_ref[r, c] = (kept + out_other[c, :, part(r)].astype(f32)).astype(bf16)
        d_stage.wait_recv()
        m_arrival.wait_recv()
        pair_out.wait_send()
        for k in range(chips):
            pair(k, 0).wait_send()
            pair(k, 1).wait_send()
            r_stage(k).wait_send()
        z_stage.wait_send()
        d_stage.wait_send()
        m_stage.wait_send()
        own_d.wait()


def middle(heads, tokens, grad, w_up, w_down, b_up, b_out, gain, shift, b_down, w_out, w_qkv):
    count, depth = tokens.shape
    _, chips, rows, units, width = w_up.shape
    cols = 2 * chips
    head_cols = w_out.shape[3]
    any_space = pl.BlockSpec(memory_space=pl.ANY)

    def weight_map(s):
        c = jnp.minimum(s, cols - 1)
        return (lax.rem(c, 2), c // 2, 0, 0, 0)

    weight = pl.BlockSpec((1, 1, rows, units, width), weight_map)
    grad_spec = pl.BlockSpec(
        (rows, 1, units, width), lambda s: (0, jnp.maximum(s - cols - chips, 0), 0, 0)
    )
    grad_shape = jax.ShapeDtypeStruct((rows, chips, units, width), bf16)
    bias = pl.BlockSpec((1, 1, units), lambda s: (jnp.minimum(s, cols - 1), 0, 0))
    block, vec = whole((count, depth)), whole((1, depth))
    dma = pltpu.SemaphoreType.DMA
    vmem = pltpu.VMEM
    return pl.pallas_call(
        functools.partial(middle_kernel, rows, cols),
        grid=(2 * cols,),
        in_specs=[
            whole(heads.shape), block, block, weight, weight, bias, vec, vec, vec, vec,
            whole(w_out.shape), any_space,
        ],
        out_specs=[
            grad_spec, grad_spec, whole((rows, chips, head_cols, width)), bias, block, block,
            whole((8, depth)), any_space, any_space,
        ],
        out_shape=[
            grad_shape, grad_shape,
            jax.ShapeDtypeStruct((rows, chips, head_cols, width), bf16),
            jax.ShapeDtypeStruct((cols, 1, units), f32),
            jax.ShapeDtypeStruct((count, depth), bf16),
            jax.ShapeDtypeStruct((count, depth), f32),
            jax.ShapeDtypeStruct((8, depth), f32),
            jax.ShapeDtypeStruct((cols, head_cols, count), bf16),
            jax.ShapeDtypeStruct((2, rows, chips) + w_qkv.shape, bf16),
        ],
        scratch_shapes=[
            vmem((count, depth), bf16), vmem((depth, count), bf16),
            vmem((count, depth), f32), vmem((count, depth), f32), vmem((count, depth), f32),
            vmem((cols, count, units), bf16), vmem((cols, count, units), bf16),
            vmem((count, depth), bf16), vmem((cols, head_cols, count), bf16),
            vmem((2, chips, units, depth), bf16), vmem((2, chips, units, depth), bf16),
            vmem((chips, head_cols, depth), bf16), vmem((chips, head_cols, depth), bf16),
            dma((cols,)), dma((cols,)), dma((2, chips)), dma((2, chips)), dma, dma,
            dma((chips,)), dma((chips,)), dma((chips, rows)), dma((chips, rows)), dma, dma,
            dma((2,)),
        ],
        compiler_params=pltpu.CompilerParams(
            vmem_limit_bytes=63 << 20, collective_id=1, has_side_effects=True
        ),
        cost_estimate=cost(
            12 * count * depth * cols * units, 8 * depth * cols * units + 16 * count * depth
        ),
        name="middle",
    )(heads, tokens, grad, w_up, w_down, b_up, b_out, gain, shift, b_down, w_out, w_qkv)


def back_kernel(
    rows, cols, heads, seqs, tiles, sub,
    blk_ref, q_ref, k_ref, v_ref, do_ref, o_ref, lse_ref, x_ref, w_ref, tok_ref, dres_ref, gain_ref,
    gup_ref, gdown_ref, gout_ref, early_ref,
    dtok_ref, wup_ref, wdown_ref, wout_ref, wqkv_ref, all_ref, bias_ref,
    d_mixed, d_arrived, key_grad, value_grad, bias_sum, qkv_acc, qkv_send, qkv_recv, norm_acc,
    up_recv, down_recv, out_recv, up_send, down_send, out_send, up_line, down_line, out_line,
    small, small_core, small_row, small_line, bias_send, bias_recv,
    send_r, recv_r, send_z, recv_z, send_d, recv_d, send_q, recv_q, send_b, recv_b,
    send_s0, recv_s0, send_s1, recv_s1, send_s2, recv_s2, local,
):
    step = pl.program_id(0)
    chips = cols // 2
    row, col = place()
    chip, lane = col // 2, lax.rem(col, 2)
    work = heads * seqs * tiles
    last = work + 2 * cols - 1
    head = step // (seqs * tiles)
    seq = lax.rem(step // tiles, seqs)
    turn = lax.rem(step, tiles)
    i = tiles - 1 - turn
    tile = q_ref.shape[1]
    chunks, _, chunk = do_ref.shape
    chunks_seq = SEQ_LEN // chunk
    parts = tile // sub
    steps = tile
    start = pl.multiple_of(i * tile, tile)

    given = (gdown_ref, gup_ref, gout_ref)
    by_row = (down_recv, up_recv, out_recv)
    to_line = (down_send, up_send, out_send)
    by_line = (down_line, up_line, out_line)
    results = (wdown_ref, wup_ref, wout_ref)

    def row_stage(n):
        return over_row(
            rows, lambda at: given[n].at[at], lambda at: by_row[n].at[at], send_r.at[n],
            recv_r.at[n],
        )

    def own_row(n):
        return pltpu.make_async_copy(given[n].at[row], by_row[n].at[row], local.at[n])

    def line_stage(n):
        return over_line(
            chips, lambda at: to_line[n].at[at], lambda at: by_line[n].at[at], send_z.at[n],
            recv_z.at[n],
        )

    def add_rows(n):
        own_row(n).wait()
        row_stage(n).wait_recv()

        def one(c, carry):
            total = by_row[n][0, c].astype(f32)
            for r in range(1, rows):
                total = total + by_row[n][r, c].astype(f32)
            to_line[n][c] = total.astype(bf16)
            return carry

        lax.fori_loop(0, chips, one, 0)
        by_line[n][chip] = to_line[n][chip]
        line_stage(n).start()

    def d_stage(h):
        return over_col(
            cols, lambda at: d_mixed.at[h, at], lambda at: d_arrived.at[h, at], send_d.at[h],
            recv_d.at[h],
        )

    def own_d(h):
        return pltpu.make_async_copy(d_mixed.at[h, col], d_arrived.at[h, col], local.at[3 + h])

    q_stage = over_row(
        rows, lambda at: qkv_send.at[at], lambda at: qkv_recv.at[at], send_q, recv_q
    )
    b_stage = over_row(rows, lambda at: bias_send, lambda at: bias_recv.at[at], send_b, recv_b)
    s_core = remote(small.at[0], small_core, send_s0, recv_s0, mate())
    s_row = over_row(
        rows, lambda at: small.at[1], lambda at: small_row.at[at], send_s1, recv_s1
    )
    s_line = over_line(
        chips, lambda at: small.at[2], lambda at: small_line.at[at], send_s2, recv_s2
    )

    @pl.when(step == 0)
    def _():
        greet(rows, cols)
        for n in range(3):
            own_row(n).start()
            row_stage(n).start()

    @pl.when(step == work // 2 + 1)
    def _():
        add_rows(0)

    @pl.when((step < work) & (turn == 0))
    def _():
        key_grad[...] = jnp.zeros_like(key_grad)
        value_grad[...] = jnp.zeros_like(value_grad)

    @pl.when((step < work) & (turn == 0) & (seq == 0))
    def _():
        bias_sum[head] = jnp.zeros((HD, 128), f32)

    @pl.when(step < work)
    def _():
        d_out = jnp.concatenate([do_ref[b] for b in range(chunks)], axis=1)
        out = jnp.concatenate([o_ref[b] for b in range(chunks)], axis=1)
        delta = jnp.sum(d_out.astype(f32) * out.astype(f32), axis=0, keepdims=True)
        lse = lse_ref[0, 0]

        def cut(x, a):
            return x[:, a * sub : (a + 1) * sub]

        queries = [q_ref[0, a * sub : (a + 1) * sub, :] for a in range(parts)]
        query_blocks = [
            blk_ref[0, :, pl.ds(pl.multiple_of(start + a * sub, sub), sub)] for a in range(parts)
        ]

        def update(a, query_grad, key_start, count, masked):
            keys = k_ref[0, pl.ds(key_start, count), :]
            values = v_ref[0, pl.ds(key_start, count), :]
            scores = dot(keys, queries[a], NT) * SCALE2 - cut(lse, a)
            if masked:
                mask = tile_mask(blk_ref, key_start, count, query_blocks[a])
                scores = jnp.where(mask, scores, MASKED)
            probs = jnp.exp2(scores)
            d_values = dot(probs.astype(bf16), cut(d_out, a), NT)
            d_scores = (probs * (dot(values, cut(d_out, a)) - cut(delta, a))).astype(bf16)
            d_keys = dot(d_scores, queries[a])
            return query_grad + dot(keys, d_scores, TN), d_keys, d_values

        def add(key_start, count, d_keys, d_values):
            key_grad[pl.ds(key_start, count), :] += d_keys
            value_grad[pl.ds(key_start, count), :] += d_values

        def sweep(j, grads):
            key_start = pl.multiple_of(j * steps, steps)
            found = [update(a, grads[a], key_start, steps, False) for a in range(parts)]
            add(key_start, steps, sum(f[1] for f in found), sum(f[2] for f in found))
            return tuple(f[0] for f in found)

        grads = list(
            lax.fori_loop(0, start // steps, sweep, (jnp.zeros((HD, sub), f32),) * parts)
        )
        for a in range(parts):
            todo = [(pl.multiple_of(start + a * sub, sub), sub, True)]
            if a > 0:
                todo.append((start, a * sub, False))
            if a < parts - 1:
                todo.append((pl.multiple_of(start + (a + 1) * sub, BLOCK), BLOCK, True))
            for key_start, count, masked in todo:
                grads[a], d_keys, d_values = update(a, grads[a], key_start, count, masked)
                add(key_start, count, d_keys, d_values)

        def beyond(j, grad):
            key_start = pl.multiple_of(start + tile, BLOCK)
            grad, d_keys, d_values = update(parts - 1, grad, key_start, BLOCK, True)
            add(key_start, BLOCK, d_keys, d_values)
            return grad

        grads[-1] = lax.fori_loop(0, jnp.where(i < tiles - 1, 1, 0), beyond, grads[-1])
        query_grad = jnp.concatenate(grads, axis=1) * SCALE
        bias_sum[head, :, :1] += jnp.sum(query_grad, axis=1, keepdims=True)
        query_grad = query_grad.astype(bf16)
        for b in range(chunks):
            d_mixed[head, seq * chunks_seq + i * chunks + b, :HD] = query_grad[
                :, b * chunk : (b + 1) * chunk
            ]

    @pl.when((step < work) & (turn == tiles - 1))
    def _():
        def one(c, value_sum):
            where = pl.ds(pl.multiple_of(c * chunk, chunk), chunk)
            at = seq * chunks_seq + c
            d_mixed[head, at, HD : 2 * HD] = (key_grad[where, :].T * SCALE).astype(bf16)
            d_values = value_grad[where, :].T
            d_mixed[head, at, 2 * HD :] = d_values.astype(bf16)
            return value_sum + jnp.sum(d_values, axis=1, keepdims=True)

        value_sum = lax.fori_loop(0, chunks_seq, one, jnp.zeros((HD, 1), f32))
        bias_sum[head, :, 1:2] += value_sum

    for h in range(heads):

        @pl.when(step == (h + 1) * seqs * tiles - 1)
        def _():
            own_d(h).start()
            d_stage(h).start()

    at = step - work

    @pl.when(at == 0)
    def _():
        qkv_acc[...] = jnp.zeros_like(qkv_acc)
        bias_send[...] = bias_sum[...]
        bias_recv[row] = bias_sum[...]
        b_stage.start()

    @pl.when((at >= 0) & (at < cols))
    def _():
        grads = jnp.concatenate([d_mixed[h, at] for h in range(heads)], axis=0)
        qkv_acc[...] += dot(grads, x_ref[0])

    @pl.when(at == cols - 1)
    def _():
        width = qkv_send.shape[2]
        for r in range(rows):
            qkv_send[r] = qkv_acc[:, r * width : (r + 1) * width].astype(bf16)
        qkv_recv[row] = qkv_send[row]
        q_stage.start()
        add_rows(1)
        add_rows(2)
        norm_acc[...] = jnp.zeros_like(norm_acc)
        for h in range(heads):
            own_d(h).wait()
            d_stage(h).wait_recv()

    @pl.when(at >= cols)
    def _():
        c = at - cols
        width = w_ref.shape[3]
        found = flip(
            jnp.concatenate(
                [
                    d_arrived[h, c, j * HD : (j + 1) * HD, :]
                    for j in range(3)
                    for h in range(heads)
                ],
                axis=0,
            )
        )
        for r in range(rows):
            norm_acc[:, r * width : (r + 1) * width] += dot(found, w_ref[0, r, 0], NT)

    @pl.when(step == last)
    def _():
        xhat, inv = moments(tok_ref[...].astype(f32))
        d_norm = norm_acc[...]
        late = early_ref.shape[0] - 2
        small[0] = early_ref[...]
        small[0, late : late + 1] = jnp.sum(d_norm * xhat, axis=0, keepdims=True)
        small[0, late + 1 : late + 2] = jnp.sum(d_norm, axis=0, keepdims=True)
        s_core.start()
        dtok_ref[...] = dres_ref[...] + norm_back(xhat, inv, d_norm * gain_ref[...].astype(f32))
        s_core.wait_recv()
        small[1] = small[0] + small_core[...]
        small_row[row] = small[1]
        s_row.start()
        b_stage.wait_recv()
        bias_ref[...] = sum(bias_recv[r] for r in range(1, rows)) + bias_recv[0]
        q_stage.wait_recv()
        total = qkv_recv[0].astype(f32)
        for r in range(1, rows):
            total = total + qkv_recv[r].astype(f32)
        wqkv_ref[...] = total
        s_row.wait_recv()
        small[2] = sum(small_row[r] for r in range(1, rows)) + small_row[0]
        small_line[chip] = small[2]
        s_line.start()
        for n in range(3):
            line_stage(n).wait_recv()
            total = by_line[n][0].astype(f32)
            for c in range(1, chips):
                total = total + by_line[n][c].astype(f32)
            results[n][...] = total
        s_line.wait_recv()
        all_ref[...] = sum(small_line[c] for c in range(1, chips)) + small_line[0]
        for n in range(3):
            row_stage(n).wait_send()
            line_stage(n).wait_send()
        for h in range(heads):
            d_stage(h).wait_send()
        q_stage.wait_send()
        b_stage.wait_send()
        s_core.wait_send()
        s_row.wait_send()
        s_line.wait_send()


def backward(
    blocks, q, k, v, d_heads, out, lse, x, w_qkv, tokens, d_resid, gain, grad_up, grad_down,
    grad_out, early,
):
    heads, total, _ = q.shape
    count, depth = tokens.shape
    rows, chips, units, width = grad_up.shape
    cols = 2 * chips
    head_cols = grad_out.shape[2]
    seqs = total // SEQ_LEN
    tile, sub = 1024, 512
    tiles = SEQ_LEN // tile
    work = heads * seqs * tiles
    pairs = heads * seqs * SEQ_LEN * SEQ_LEN * 5 // 8

    def unpack(s):
        s = jnp.minimum(s, work - 1)
        return s // (seqs * tiles), lax.rem(s // tiles, seqs), tiles - 1 - lax.rem(s, tiles)

    def queries_map(s):
        h, b, i = unpack(s)
        return (h, b * tiles + i, 0)

    def keys_map(s):
        h, b, _ = unpack(s)
        return (h, b, 0)

    def heads_map(s):
        h, b, i = unpack(s)
        return (b * tiles + i, h, 0)

    def lse_map(s):
        h, b, i = unpack(s)
        return (h, b, 0, i)

    def w_map(s):
        c = jnp.maximum(s - work - cols, 0)
        return (lax.rem(c, 2), 0, c // 2, 0, 0)

    keys = pl.BlockSpec((1, SEQ_LEN, HD), keys_map)
    heads_spec = pl.BlockSpec((tile // chunk_of(tokens), HD, count), heads_map)
    any_space = pl.BlockSpec(memory_space=pl.ANY)
    block = whole((count, depth))
    dma, vmem = pltpu.SemaphoreType.DMA, pltpu.VMEM
    parts = heads * 3 * HD
    shape = jax.ShapeDtypeStruct
    small = early.shape
    return pl.pallas_call(
        functools.partial(back_kernel, rows, cols, heads, seqs, tiles, sub),
        grid=(work + 2 * cols,),
        in_specs=[
            pl.BlockSpec((1, 1, SEQ_LEN), lambda s: (unpack(s)[1], 0, 0)),
            pl.BlockSpec((1, tile, HD), queries_map), keys, keys, heads_spec, heads_spec,
            pl.BlockSpec((1, 1, 1, tile), lse_map),
            pl.BlockSpec((1, count, depth), lambda s: (jnp.clip(s - work, 0, cols - 1), 0, 0)),
            pl.BlockSpec((1, rows, 1) + w_qkv.shape[3:], w_map),
            block, block, whole((1, depth)), any_space, any_space, any_space, whole(small),
        ],
        out_specs=[
            block, whole((units, width)), whole((units, width)), whole((head_cols, width)),
            whole((parts, width)), whole(small), whole((heads, HD, 128)),
        ],
        out_shape=[
            shape((count, depth), f32), shape((units, width), f32), shape((units, width), f32),
            shape((head_cols, width), f32), shape((parts, width), f32), shape(small, f32),
            shape((heads, HD, 128), f32),
        ],
        scratch_shapes=[
            vmem((heads, cols, 3 * HD, count), bf16), vmem((heads, cols, 3 * HD, count), bf16),
            vmem((SEQ_LEN, HD), f32), vmem((SEQ_LEN, HD), f32), vmem((heads, HD, 128), f32),
            vmem((parts, depth), f32), vmem((rows, parts, width), bf16),
            vmem((rows, parts, width), bf16), vmem((count, depth), f32),
            vmem((rows, chips, units, width), bf16), vmem((rows, chips, units, width), bf16),
            vmem((rows, chips, head_cols, width), bf16),
            vmem((chips, units, width), bf16), vmem((chips, units, width), bf16),
            vmem((chips, head_cols, width), bf16),
            vmem((chips, units, width), bf16), vmem((chips, units, width), bf16),
            vmem((chips, head_cols, width), bf16),
            vmem((3,) + small, f32), vmem(small, f32), vmem((rows,) + small, f32),
            vmem((chips,) + small, f32),
            vmem((heads, HD, 128), f32), vmem((rows, heads, HD, 128), f32),
            dma((3, rows)), dma((3, rows)), dma((3, chips)), dma((3, chips)),
            dma((heads, cols)), dma((heads, cols)), dma((rows,)), dma((rows,)),
            dma((rows,)), dma((rows,)), dma, dma, dma((rows,)), dma((rows,)),
            dma((chips,)), dma((chips,)), dma((3 + heads,)),
        ],
        compiler_params=pltpu.CompilerParams(
            vmem_limit_bytes=63 << 20, collective_id=2, has_side_effects=True
        ),
        cost_estimate=cost(40 * pairs * HD, 16 * heads * total * HD, pairs),
        name="backward",
    )(
        blocks, q, k, v, d_heads, out, lse, x, w_qkv, tokens, d_resid, gain, grad_up, grad_down,
        grad_out, early,
    )


def chunk_of(tokens):
    return tokens.shape[0]


def body(
    tokens, blocks, w_qkv, b_qv, w_out, b_out, w_up, b_up, w_down, b_down,
    gain1, shift1, gain2, shift2, grad_out,
):
    rows, cols = lax.axis_size("row"), lax.axis_size("col")
    depth = tokens.shape[1]
    head_cols = w_qkv.shape[2]
    heads = head_cols // HD
    units = w_up.shape[0]

    def vec(v):
        return v.reshape(1, -1)

    w_qkv_flat = w_qkv.reshape(w_qkv.shape[0], 3 * head_cols)

    (
        attn_rows, q, k, v, found, arrived, lse, block_ids, up_bias, out_weight, up_weight,
        down_weight,
    ) = front(
        tokens, vec(gain1), vec(shift1), vec(blocks), vec(b_up), w_qkv_flat, b_qv, w_out, w_up,
        w_down, rows, cols,
    )
    grad_up, grad_down, grad_wout, grad_bup, output, d_resid, sums, d_heads, qkv_all = middle(
        arrived, tokens, grad_out, up_weight, down_weight, up_bias, vec(b_out), vec(gain2),
        vec(shift2), vec(b_down), out_weight, w_qkv_flat,
    )
    hidden_units = units * cols
    used = 4 + hidden_units // depth
    spare = (used + 9) // 8 * 8 - used
    early = jnp.concatenate(
        [sums[:4], grad_bup.reshape(-1, depth), jnp.zeros((spare, depth), f32)]
    )
    grad_tokens, grad_wup, grad_wdown, grad_wout, grad_wqkv, small, bias = backward(
        block_ids, q, k, v, d_heads, found, lse, attn_rows, qkv_all, tokens, d_resid, vec(gain1),
        grad_up, grad_down, grad_wout, early,
    )
    grad_wqkv = (
        grad_wqkv.reshape(heads, 3, HD, depth // rows)
        .transpose(3, 1, 0, 2)
        .reshape(depth // rows, 3, head_cols)
    )
    grad_bqv = bias[:, :, :2].reshape(head_cols, 2).T
    grad_bdown, grad_gain2, grad_shift2, grad_bout = small[:4]
    grad_bup = lax.dynamic_slice_in_dim(
        small[4:used].reshape(-1), lax.axis_index("col") * units, units
    )
    grad_gain1, grad_shift1 = small[-2:]
    return (
        output, grad_tokens, grad_wqkv, grad_bqv, grad_wout, grad_bout, grad_wup, grad_bup,
        grad_wdown, grad_bdown, grad_gain1, grad_shift1, grad_gain2, grad_shift2,
    )


def solution(mesh):
    tokens, weight, whole_vec = P(("row", "col"), None), P("col", "row"), P()
    qkv, bias_qv = P("row", None, "col"), P(None, "col")
    return jax.shard_map(
        body,
        mesh=mesh,
        in_specs=(
            tokens, P(("row", "col")), qkv, bias_qv, weight, whole_vec, weight, P("col"), weight,
            whole_vec, whole_vec, whole_vec, whole_vec, whole_vec, tokens,
        ),
        out_specs=(
            tokens, tokens, qkv, bias_qv, weight, whole_vec, weight, P("col"), weight,
            whole_vec, whole_vec, whole_vec, whole_vec, whole_vec,
        ),
        check_vma=False,
    )
```

```python
import functools

import jax
import jax.numpy as jnp
from jax import lax
from jax.experimental import pallas as pl
from jax.experimental.pallas import tpu as pltpu
from jax.sharding import PartitionSpec as P

HD = 64
SEQ_LEN = 4096
BLOCK = 256
EPS = 1e-05
SCALE = HD ** (-0.5)
SCALE2 = SCALE * 1.4426950408889634
MASKED = -1e30
ONES = 16
MESH = pl.DeviceIdType.MESH
VMEM_LIMIT = 60 << 20

f32 = jnp.float32
bf16 = jnp.bfloat16

NN = (((1,), (0,)), ((), ()))
NT = (((1,), (1,)), ((), ()))
TN = (((0,), (0,)), ((), ()))


def dot(a, b, dims=NN):
    return lax.dot_general(a, b, dims, preferred_element_type=f32)


def flip(x):
    return x.astype(f32).T.astype(bf16)


def params(**more):
    return pltpu.CompilerParams(vmem_limit_bytes=VMEM_LIMIT, **more)


def cost(flops, nbytes, transcendentals=0):
    return pl.CostEstimate(flops=flops, bytes_accessed=nbytes, transcendentals=transcendentals)


def whole(shape):
    return pl.BlockSpec(shape, lambda *_: (0,) * len(shape))


def moments(v):
    center = jnp.mean(v, axis=-1, keepdims=True)
    centered = v - center
    spread = jnp.mean(centered * centered, axis=-1, keepdims=True)
    inv = lax.rsqrt(spread + EPS)
    return centered * inv, inv


def norm_back(xhat, inv, e):
    return inv * (
        e - jnp.mean(e, axis=-1, keepdims=True) - xhat * jnp.mean(e * xhat, axis=-1, keepdims=True)
    )


def place():
    return lax.axis_index("row"), lax.axis_index("col")


def greet(rows, cols):
    row, col = place()
    barrier = pltpu.get_barrier_semaphore()

    def to_col(k, carry):
        pl.semaphore_signal(
            barrier, inc=1, device_id=(row, lax.rem(col + k, cols)), device_id_type=MESH
        )
        return carry

    def to_row(k, carry):
        pl.semaphore_signal(
            barrier, inc=1, device_id=(lax.rem(row + k, rows), col), device_id_type=MESH
        )
        return carry

    lax.fori_loop(1, cols, to_col, 0)
    lax.fori_loop(1, rows, to_row, 0)
    pl.semaphore_wait(barrier, rows + cols - 2)


def remote(src, dst, send, recv, device):
    return pltpu.make_async_remote_copy(
        src_ref=src, dst_ref=dst, send_sem=send, recv_sem=recv, device_id=device, device_id_type=MESH
    )


def each(count, act):
    def turn(k, carry):
        act(k)
        return carry

    lax.fori_loop(1, count, turn, 0)


class Exchange:
    def __init__(self, count, here, slot, to, out, into, send, recv):
        self.count, self.here, self.slot, self.to = count, here, slot, to
        self.out, self.into, self.send, self.recv = out, into, send, recv

    def copy(self, k):
        at = self.slot(k)
        return remote(
            self.out(at), self.into(self.here), self.send.at[k], self.recv.at[self.here], self.to(k)
        )

    def arrival(self, k):
        at = self.slot(k)
        return remote(self.out(at), self.into(at), self.send.at[k], self.recv.at[at], self.to(k))

    def start(self):
        each(self.count, lambda k: self.copy(k).start())

    def wait_recv(self):
        each(self.count, lambda k: self.arrival(k).wait_recv())

    def wait_send(self):
        each(self.count, lambda k: self.copy(k).wait_send())


def over_row(rows, out, into, send, recv):
    row, col = place()
    slot = lambda k: lax.rem(row + k, rows)
    return Exchange(rows, row, slot, lambda k: (slot(k), col), out, into, send, recv)


def over_col(cols, out, into, send, recv):
    row, col = place()
    slot = lambda k: lax.rem(col + k, cols)
    return Exchange(cols, col, slot, lambda k: (row, slot(k)), out, into, send, recv)


def over_line(chips, out, into, send, recv):
    row, col = place()
    chip, lane = col // 2, lax.rem(col, 2)
    slot = lambda k: lax.rem(chip + k, chips)
    return Exchange(chips, chip, slot, lambda k: (row, slot(k) * 2 + lane), out, into, send, recv)


def mate():
    row, col = place()
    return (row, col // 2 * 2 + 1 - lax.rem(col, 2))


def front_kernel(
    rows, cols, heads,
    tok_ref, vec_ref, blk_ref, bup_ref, wq_ref, bias_ref, wout_ref, wup_ref, wdown_ref,
    xo_ref, q_ref, k_ref, v_ref, found_ref, arrived_ref, lse_ref, blko_ref, bupo_ref,
    wouto_ref, wupo_ref, wdowno_ref,
    xs, wqs, qs, ks, vs, vt, totals, tops, founds, blks, bups,
    send_x, recv_x, send_q, recv_q, send_s, recv_s, send_f, recv_f,
    send_wz, recv_wz, send_wr, recv_wr, send_wm, recv_wm, local_x, local_q, local_f, local_w,
):
    chips = cols // 2
    row, me = place()
    chip, lane = me // 2, lax.rem(me, 2)
    count = tok_ref.shape[0]
    tile = 2 * count
    seq_chips = SEQ_LEN // tile
    depth = wq_ref.shape[0]
    width = heads * HD

    xhat, _ = moments(tok_ref[...].astype(f32))
    xs[me] = (xhat * vec_ref[0:1] + vec_ref[1:2]).astype(bf16)
    blks[me] = blk_ref[...]
    bups[me] = bup_ref[...]
    own_rows = pl.ds(pl.multiple_of(row * depth, depth), depth)
    wqs[own_rows] = wq_ref[...]
    vt[:, HD:, :] = jnp.ones((heads, ONES, vt.shape[2]), bf16)
    greet(rows, cols)

    def chunk(owner, target, route, at):
        return remote(
            xs.at[owner], xs.at[owner], send_x.at[route, at], recv_x.at[route, at], (row, target)
        )

    def to_mate(owner, at):
        return remote(xs.at[owner], xs.at[owner], send_x.at[2, at], recv_x.at[2, at], mate())

    given = (wout_ref, wup_ref, wdown_ref)
    gathered = (wouto_ref, wupo_ref, wdowno_ref)

    q_stage = over_row(
        rows,
        lambda at: wq_ref,
        lambda at: wqs.at[pl.ds(pl.multiple_of(at * depth, depth), depth)],
        send_q,
        recv_q,
    )
    small = [
        over_col(cols, lambda at: blk_ref, lambda at: blks.at[at], send_s.at[0], recv_s.at[0]),
        over_col(cols, lambda at: bup_ref, lambda at: bups.at[at], send_s.at[1], recv_s.at[1]),
    ]
    f_stage_out = lambda at: founds.at[at]
    f_stage = over_col(cols, f_stage_out, lambda at: arrived_ref.at[at], send_f, recv_f)

    def w_line(n, at, to, route):
        block = gathered[n].at[lane, at, row]
        out = given[n] if at is chip else block
        return remote(
            out, block, send_wz.at[n, route, at], recv_wz.at[n, at], (row, to * 2 + lane)
        )

    def w_row(n, c, out):
        return over_row(
            rows, lambda at: out, lambda at: gathered[n].at[lane, c, at], send_wr.at[n, c],
            recv_wr.at[n, c],
        )

    square = rows == 4
    next_x = row + 1 - 2 * lax.rem(row, 2)
    next_y = lax.rem(row + 2, 4)
    across_x = lax.rem(next_x + 2, 4)
    relayed = jnp.where(lane == 0, next_y, next_x)
    relay_to = jnp.where(lane == 0, next_x, next_y)

    def w_step(n, c, slot, k, to):
        block = gathered[n].at[lane, c, slot]
        out = given[n] if (slot is row and c is chip) else block
        return remote(out, block, send_wr.at[n, c, k], recv_wr.at[n, c, slot], (to, me))

    def rows_start(n, c):
        if square:
            w_step(n, c, row, 0, next_x).start()
            w_step(n, c, row, 1, next_y).start()
        else:
            w_row(n, c, given[n] if c is chip else gathered[n].at[lane, c, row]).start()

    def rows_relay(n, c):
        if square:
            w_step(n, c, relayed, 2, relay_to).wait_recv()
            w_step(n, c, relayed, 2, relay_to).start()

    def rows_wait_recv(n, c):
        if square:
            w_step(n, c, relay_to, 0, next_x).wait_recv()
            w_step(n, c, across_x, 0, next_x).wait_recv()
        else:
            w_row(n, c, given[n]).wait_recv()

    def rows_wait_send(n, c):
        if square:
            for k in range(3):
                w_step(n, c, row, k, next_x).wait_send()
        else:
            w_row(n, c, given[n]).wait_send()

    def w_own(n):
        return pltpu.make_async_copy(given[n], gathered[n].at[lane, chip, row], local_w.at[n])

    def w_mate(n, c, side):
        block = gathered[n].at[side, c]
        return remote(block, block, send_wm.at[n, c], recv_wm.at[n, c], mate())

    to_mate(me, chip).start()
    q_stage.start()
    for exchange in small:
        exchange.start()

    @pl.when(chip + 1 < chips)
    def _():
        for n in range(3):
            w_line(n, chip, chip + 1, 0).start()
        chunk(me, me + 2, 0, chip).start()

    @pl.when(chip > 0)
    def _():
        for n in range(3):
            w_line(n, chip, chip - 1, 1).start()
        chunk(me, me - 2, 1, chip).start()

    for n in range(3):
        w_own(n).start()
        rows_start(n, chip)
    q_stage.wait_recv()
    for exchange in small:
        exchange.wait_recv()

    def update(h, q_tile, q_low, q_count, key_start, key_count, mask):
        lanes = pl.ds(q_low, q_count)
        query = qs[h, pl.ds(pl.multiple_of(q_tile * tile + q_low, BLOCK), q_count), :]
        keys = pl.ds(pl.multiple_of(key_start, BLOCK), key_count)
        scores = dot(ks[h, keys, :], query, NT)
        if mask is not None:
            scores = jnp.where(mask, scores, MASKED)
        top = tops[h, q_tile, :, lanes]
        higher = jnp.maximum(top, jnp.max(scores, axis=0, keepdims=True) * SCALE2)
        probs = jnp.exp2(scores * SCALE2 - higher)
        part = dot(vt[h, :, keys], probs.astype(bf16))
        totals[h, q_tile, :, lanes] = totals[h, q_tile, :, lanes] * jnp.exp2(top - higher) + part
        tops[h, q_tile, :, lanes] = higher

    def column(blocks, amount):
        return jnp.broadcast_to(blocks, (128, amount)).T[:, :1]

    def diagonal(p):
        low, high = blks[2 * p], blks[2 * p + 1]
        first = column(jnp.concatenate([low, high[:, :BLOCK]], axis=1), count + BLOCK)
        second = column(jnp.concatenate([low, high], axis=1), tile)
        for h in range(heads):
            update(h, p, 0, count, p * tile, count + BLOCK, low >= first)
            update(h, p, count, count, p * tile, tile, high >= second)

    def boundary(p):
        mask = blks[2 * p + 1][:, count - BLOCK :] >= column(blks[2 * p + 2][:, :BLOCK], BLOCK)
        for h in range(heads):
            update(h, p, tile - BLOCK, BLOCK, (p + 1) * tile, BLOCK, mask)

    def project(p):
        both = jnp.concatenate([xs[2 * p], xs[2 * p + 1]], axis=0)
        mixed = dot(both, wqs[...])
        bias = bias_ref[...].astype(f32)
        where = pl.ds(pl.multiple_of(p * tile, tile), tile)
        for h in range(heads):
            at = [slice(j * width + h * HD, j * width + (h + 1) * HD) for j in range(3)]
            here = slice(h * HD, (h + 1) * HD)
            qs[h, where, :] = (mixed[:, at[0]] + bias[0:1, here]).astype(bf16)
            ks[h, where, :] = mixed[:, at[1]].astype(bf16)
            values = (mixed[:, at[2]] + bias[1:2, here]).astype(bf16)
            vs[h, where, :] = values
            vt[h, :HD, where] = flip(values)
            totals[h, p] = jnp.zeros(totals.shape[2:], f32)
            tops[h, p] = jnp.full(tops.shape[2:], MASKED, f32)

    def keep(p):
        where = pl.ds(pl.multiple_of(p * tile, tile), tile)
        pairs = [
            pltpu.make_async_copy(held.at[:, where, :], out.at[:, where, :], local_q.at[n, p])
            for n, (held, out) in enumerate(((qs, q_ref), (ks, k_ref), (vs, v_ref)))
        ]
        return pairs + [
            pltpu.make_async_copy(xs.at[2 * p + c], xo_ref.at[2 * p + c], local_x.at[2 * p + c])
            for c in range(2)
        ]

    def kept(c):
        return pltpu.make_async_copy(founds.at[c], found_ref.at[c], local_f.at[0, c])

    def own(c):
        return pltpu.make_async_copy(founds.at[c], arrived_ref.at[c], local_f.at[1, 0])

    def conclude(p):
        for h in range(heads):
            mass = totals[h, p, HD : HD + 1, :]
            out = (totals[h, p, :HD, :] / mass).astype(bf16)
            for c in range(2):
                founds[2 * p + c, h * HD : (h + 1) * HD, :] = out[:, c * count : (c + 1) * count]
            lse_ref[
                h, p // seq_chips, :, pl.ds(pl.multiple_of(lax.rem(p, seq_chips) * tile, tile), tile)
            ] = tops[h, p] + jnp.log2(mass)
        for c in range(2):
            owner = 2 * p + c
            kept(owner).start()

            @pl.when(owner == me)
            def _():
                own(owner).start()

            @pl.when(owner != me)
            def _():
                f_stage.copy(lax.rem(owner - me + cols, cols)).start()

    def pass_weights():
        for n in range(3):
            w_own(n).wait()

            def across(c, carry):
                rows_wait_recv(n, c)
                w_mate(n, c, lane).start()
                return carry

            lax.fori_loop(0, chips, across, 0)

    def event(e, carry):
        hop = (e + 1) // 2
        lower = lax.rem(e, 2) == 1
        p = jnp.where(lower, chip - hop, chip + hop)

        @pl.when(e == 1)
        def _():
            for hop in range(1, chips):
                for at, step, route in ((chip - hop, 1, 0), (chip + hop, -1, 1)):

                    @pl.when((at >= 0) & (at < chips))
                    def _():
                        onward = chip + step
                        for n in range(3):
                            w_line(n, at, onward, route).wait_recv()

                            @pl.when((onward >= 0) & (onward < chips))
                            def _():
                                w_line(n, at, onward, route).start()

                            rows_start(n, at)

        @pl.when(e == 2 * chips - 3)
        def _():
            pass_weights()

        @pl.when(lower)
        def _():
            below, above = chip - hop, chip + hop

            @pl.when(below >= 0)
            def _():
                owner = below * 2 + lane
                chunk(owner, me, 0, below).wait_recv()

                @pl.when(chip + 1 < chips)
                def _():
                    chunk(owner, me + 2, 0, below).start()

                to_mate(owner, below).start()

            @pl.when(above < chips)
            def _():
                owner = above * 2 + lane
                chunk(owner, me, 1, above).wait_recv()

                @pl.when(chip > 0)
                def _():
                    chunk(owner, me - 2, 1, above).start()

                to_mate(owner, above).start()

        @pl.when(e == 1)
        def _():
            def relay(c, carry):
                for n in range(3):
                    rows_relay(n, c)
                return carry

            lax.fori_loop(0, chips, relay, 0)

        @pl.when((p >= 0) & (p < chips))
        def _():
            to_mate(2 * p + 1 - lane, p).wait_recv()
            project(p)
            for copy in keep(p):
                copy.start()
            first = p // seq_chips * seq_chips
            final = first + seq_chips - 1
            high = jnp.minimum(chip + hop - 1, final)
            low = jnp.maximum(jnp.maximum(chip - hop, 0), first)
            diagonal(p)

            @pl.when(lower & (p < final))
            def _():
                boundary(p)

            @pl.when(lower & (p == first))
            def _():
                conclude(p)

            @pl.when(jnp.logical_not(lower) & (p > first) & (hop > 0))
            def _():
                boundary(p - 1)

                @pl.when(low == first)
                def _():
                    conclude(p - 1)

            amount = jnp.where(lower, high - p, p - low)

            def pair(j, carry):
                q_tile = jnp.where(lower, p + 1 + j, p)
                key_tile = jnp.where(lower, p, low + j)
                for h in range(heads):
                    update(h, q_tile, 0, tile, key_tile * tile, tile, None)

                @pl.when(lower & (p == first) & ((q_tile == final) | (q_tile < high)))
                def _():
                    conclude(q_tile)

                return carry

            lax.fori_loop(0, amount, pair, 0)

            @pl.when(jnp.logical_not(lower) & (p == final) & (low == first))
            def _():
                conclude(p)

        return carry

    lax.fori_loop(0, 2 * chips - 1, event, 0)

    for c in range(cols):
        bupo_ref[c] = bups[c]
        at = c * count
        blko_ref[at // SEQ_LEN, :, at % SEQ_LEN : at % SEQ_LEN + count] = blks[c]
    f_stage.wait_recv()
    for c in range(chips):
        for n in range(3):
            w_mate(n, c, 1 - lane).wait_recv()
            w_mate(n, c, lane).wait_send()
            rows_wait_send(n, c)

            @pl.when((c <= chip) & (chip + 1 < chips))
            def _():
                w_line(n, c, chip, 0).wait_send()

            @pl.when((c >= chip) & (chip > 0))
            def _():
                w_line(n, c, chip, 1).wait_send()

        for copy in keep(c):
            copy.wait()
        kept(2 * c).wait()
        kept(2 * c + 1).wait()
        to_mate(me, c).wait_send()

        @pl.when((c <= chip) & (chip + 1 < chips))
        def _():
            chunk(me, me, 0, c).wait_send()

        @pl.when((c >= chip) & (chip > 0))
        def _():
            chunk(me, me, 1, c).wait_send()

    own(me).wait()
    f_stage.wait_send()
    q_stage.wait_send()
    for exchange in small:
        exchange.wait_send()


def front(tokens, vecs, blocks, b_up, w_qkv, b_qv, w_out, w_up, w_down, rows, cols):
    count, depth = tokens.shape
    head_cols = w_qkv.shape[1] // 3
    heads = head_cols // HD
    chips = cols // 2
    total = count * cols
    tile = 2 * count
    any_space = pl.BlockSpec(memory_space=pl.ANY)
    in_vmem = pl.BlockSpec(memory_space=pltpu.VMEM)
    dma, vmem, shape = pltpu.SemaphoreType.DMA, pltpu.VMEM, jax.ShapeDtypeStruct
    pairs = heads * total * SEQ_LEN * 5 // 8
    held = (heads, total, HD)
    return pl.pallas_call(
        functools.partial(front_kernel, rows, cols, heads),
        in_specs=[in_vmem] * 9,
        out_specs=[any_space] * 6 + [in_vmem] * 3 + [any_space] * 3,
        out_shape=[
            shape((cols, count, depth), bf16), shape(held, bf16), shape(held, bf16),
            shape(held, bf16), shape((cols, head_cols, count), bf16),
            shape((cols, head_cols, count), bf16),
            shape((heads, total // SEQ_LEN, 1, SEQ_LEN), f32),
            shape((total // SEQ_LEN, 1, SEQ_LEN), jnp.int32), shape((cols,) + b_up.shape, bf16),
        ] + [shape((2, chips, rows) + w.shape, bf16) for w in (w_out, w_up, w_down)],
        scratch_shapes=[
            vmem((cols, count, depth), bf16), vmem((depth, 3 * head_cols), bf16),
            vmem(held, bf16), vmem(held, bf16), vmem(held, bf16),
            vmem((heads, HD + ONES, total), bf16),
            vmem((heads, chips, HD + ONES, tile), f32), vmem((heads, chips, 1, tile), f32),
            vmem((cols, head_cols, count), bf16), vmem((cols,) + blocks.shape, jnp.int32),
            vmem((cols,) + b_up.shape, bf16),
            dma((3, chips)), dma((3, chips)), dma((rows,)), dma((rows,)),
            dma((2, cols)), dma((2, cols)), dma((cols,)), dma((cols,)),
            dma((3, 2, chips)), dma((3, chips)), dma((3, chips, rows)), dma((3, chips, rows)),
            dma((3, chips)), dma((3, chips)),
            dma((cols,)), dma((3, chips)), dma((2, cols)), dma((3,)),
        ],
        compiler_params=pltpu.CompilerParams(
            vmem_limit_bytes=63 << 20, collective_id=0, has_side_effects=True
        ),
        cost_estimate=cost(16 * pairs * HD, 16 * heads * total * HD, pairs),
        name="front",
    )(tokens, vecs, blocks, b_up, w_qkv, b_qv, w_out, w_up, w_down)


def tile_mask(blk_ref, key_start, count, query_blocks):
    key_blocks = jnp.broadcast_to(blk_ref[0, :, pl.ds(key_start, count)], (128, count)).T[:, :1]
    return query_blocks >= key_blocks


GELU_A = 0.7978845608028654
GELU_B = 0.044715


def middle_kernel(
    rows, cols,
    heads_ref, tok_ref, g_ref, up_ref, down_ref, bup_ref, vec_ref, wout_ref, wq_ref,
    gup_ref, gdown_ref, gout_ref, gbup_ref, output_ref, dres_ref, sums_ref, dheads_ref, wqo_ref,
    x, heads_all, resid, out_acc, norm_acc, hiddens, d_ups, low, d_send,
    mine, other, out_mine, out_other,
    send_d, recv_d, send_p, recv_p, send_o, recv_o, send_z, recv_z, send_r, recv_r, send_m, recv_m,
    local,
):
    step = pl.program_id(0)
    chips = cols // 2
    row, col = place()
    chip, lane = col // 2, lax.rem(col, 2)
    width = up_ref.shape[4]
    depth = wout_ref.shape[3]

    def part(r):
        return slice(r * width, (r + 1) * width)

    def out_weight(r):
        return jnp.concatenate([wout_ref[c % 2, c // 2, r] for c in range(cols)], axis=0)

    z_stage = over_line(
        chips, lambda at: wq_ref, lambda at: wqo_ref.at[lane, row, at], send_z, recv_z
    )

    def r_stage(c):
        return over_row(
            rows,
            lambda at: wqo_ref.at[lane, row, c],
            lambda at: wqo_ref.at[lane, at, c],
            send_r.at[c],
            recv_r.at[c],
        )

    m_stage = remote(wqo_ref.at[lane], wqo_ref.at[lane], send_m, recv_m, mate())
    m_arrival = remote(wqo_ref.at[1 - lane], wqo_ref.at[1 - lane], send_m, recv_m, mate())
    own_wq = pltpu.make_async_copy(wq_ref, wqo_ref.at[lane, row, chip], local.at[0])
    d_stage = over_col(
        cols, lambda at: d_send.at[at], lambda at: dheads_ref.at[at], send_d, recv_d
    )
    own_d = pltpu.make_async_copy(d_send.at[col], dheads_ref.at[col], local.at[1])

    def pair(at, which):
        return remote(
            mine.at[which, at], other.at[which, at], send_p.at[which, at], recv_p.at[which, at],
            mate(),
        )

    pair_out = remote(out_mine, out_other, send_o, recv_o, mate())

    @pl.when(step == 0)
    def _():
        greet(rows, cols)
        own_wq.start()
        z_stage.start()
        for s in range(cols):
            heads_all[s * depth : (s + 1) * depth] = heads_ref[s]
        stacked = flip(heads_all[...])
        for r in range(rows):
            branch = dot(stacked, out_weight(r))
            resid[:, part(r)] = tok_ref[:, part(r)].astype(f32) + branch + vec_ref[2:3, part(r)]
        xhat, _ = moments(resid[...])
        x[...] = (xhat * vec_ref[3:4] + vec_ref[4:5]).astype(bf16)
        out_acc[...] = jnp.zeros_like(out_acc)
        norm_acc[...] = jnp.zeros_like(norm_acc)

    @pl.when(step == 1)
    def _():
        own_wq.wait()
        z_stage.wait_recv()
        for c in range(chips):
            r_stage(c).start()

    @pl.when(step < cols)
    def _():
        up = bup_ref[0].astype(f32)
        d_hidden = 0.0
        for r in range(rows):
            up = up + dot(x[:, part(r)], up_ref[0, 0, r], NT)
            d_hidden = d_hidden + dot(g_ref[:, part(r)], down_ref[0, 0, r], NT)
        square = up * up
        bent = jnp.tanh(GELU_A * up * (1.0 + GELU_B * square))
        half = 0.5 + 0.5 * bent
        hidden = (up * half).astype(bf16)
        slope = half + (0.5 * GELU_A) * up * (1.0 - bent * bent) * (1.0 + (3.0 * GELU_B) * square)
        d_up = d_hidden * slope
        gbup_ref[0] = jnp.sum(d_up, axis=0, keepdims=True)
        d_up = d_up.astype(bf16)
        hiddens[step] = hidden
        d_ups[step] = d_up
        for r in range(rows):
            out_acc[:, part(r)] += dot(hidden, down_ref[0, 0, r])
            norm_acc[:, part(r)] += dot(d_up, up_ref[0, 0, r])

    @pl.when(step == cols - 1)
    def _():
        output_ref[...] = (resid[...] + out_acc[...] + vec_ref[5:6]).astype(bf16)
        xhat, inv = moments(resid[...])
        d_norm = norm_acc[...]
        grad = g_ref[...].astype(f32)
        d_resid = grad + norm_back(xhat, inv, d_norm * vec_ref[3:4])
        dres_ref[...] = d_resid
        low[...] = d_resid.astype(bf16)
        sums_ref[0:1] = jnp.sum(grad, axis=0, keepdims=True)
        sums_ref[1:2] = jnp.sum(d_norm * xhat, axis=0, keepdims=True)
        sums_ref[2:3] = jnp.sum(d_norm, axis=0, keepdims=True)
        sums_ref[3:4] = jnp.sum(d_resid, axis=0, keepdims=True)
        sums_ref[4:] = jnp.zeros((4, sums_ref.shape[1]), f32)
        found = 0.0
        for r in range(rows):
            found = found + dot(out_weight(r), low[:, part(r)], NT)
        found = found.astype(bf16)
        for c in range(cols):
            d_send[c] = found[c * depth : (c + 1) * depth]
        own_d.start()
        d_stage.start()
        found = dot(heads_all[...], low[...])
        for c in range(chips):
            first = found[2 * c * depth : (2 * c + 1) * depth]
            second = found[(2 * c + 1) * depth : (2 * c + 2) * depth]
            out_mine[c] = jnp.where(lane == 0, second, first).astype(bf16)
            kept = jnp.where(lane == 0, first, second)
            for r in range(rows):
                out_acc[c * depth : (c + 1) * depth, part(r)] = kept[:, part(r)]
        pair_out.start()

    at = step - cols

    @pl.when((at >= 0) & (at < chips))
    def _():
        c = at * 2 + 1 - lane
        mine[0, at] = dot(hiddens[c], g_ref[...], TN).astype(bf16)
        pair(at, 0).start()
        mine[1, at] = dot(d_ups[c], x[...], TN).astype(bf16)
        pair(at, 1).start()

    @pl.when(at == 0)
    def _():
        for c in range(chips):
            r_stage(c).wait_recv()
        m_stage.start()

    @pl.when(at >= chips)
    def _():
        k = at - chips
        c = k * 2 + lane
        grad_down = dot(hiddens[c], g_ref[...], TN)
        pair(k, 0).wait_recv()
        grad_down = (grad_down + other[0, k].astype(f32)).astype(bf16)
        grad_up = dot(d_ups[c], x[...], TN)
        pair(k, 1).wait_recv()
        grad_up = (grad_up + other[1, k].astype(f32)).astype(bf16)
        for r in range(rows):
            gdown_ref[r, 0] = grad_down[:, part(r)]
            gup_ref[r, 0] = grad_up[:, part(r)]

    @pl.when(step == 2 * cols - 1)
    def _():
        pair_out.wait_recv()
        for c in range(chips):
            for r in range(rows):
                kept = out_acc[c * depth : (c + 1) * depth, part(r)]
                gout_ref[r, c] = (kept + out_other[c, :, part(r)].astype(f32)).astype(bf16)
        d_stage.wait_recv()
        m_arrival.wait_recv()
        pair_out.wait_send()
        for k in range(chips):
            pair(k, 0).wait_send()
            pair(k, 1).wait_send()
            r_stage(k).wait_send()
        z_stage.wait_send()
        d_stage.wait_send()
        m_stage.wait_send()
        own_d.wait()


def middle(heads, tokens, grad, w_up, w_down, b_up, vecs, w_out, w_qkv):
    count, depth = tokens.shape
    _, chips, rows, units, width = w_up.shape
    cols = 2 * chips
    head_cols = w_out.shape[3]
    any_space = pl.BlockSpec(memory_space=pl.ANY)

    def weight_map(s):
        c = jnp.minimum(s, cols - 1)
        return (lax.rem(c, 2), c // 2, 0, 0, 0)

    weight = pl.BlockSpec((1, 1, rows, units, width), weight_map)
    grad_spec = pl.BlockSpec(
        (rows, 1, units, width), lambda s: (0, jnp.maximum(s - cols - chips, 0), 0, 0)
    )
    grad_shape = jax.ShapeDtypeStruct((rows, chips, units, width), bf16)
    bias = pl.BlockSpec((1, 1, units), lambda s: (jnp.minimum(s, cols - 1), 0, 0))
    block = whole((count, depth))
    dma = pltpu.SemaphoreType.DMA
    vmem = pltpu.VMEM
    return pl.pallas_call(
        functools.partial(middle_kernel, rows, cols),
        grid=(2 * cols,),
        in_specs=[
            whole(heads.shape), block, block, weight, weight, bias, whole(vecs.shape),
            whole(w_out.shape), any_space,
        ],
        out_specs=[
            grad_spec, grad_spec, whole((rows, chips, head_cols, width)), bias, block, block,
            whole((8, depth)), any_space, any_space,
        ],
        out_shape=[
            grad_shape, grad_shape,
            jax.ShapeDtypeStruct((rows, chips, head_cols, width), bf16),
            jax.ShapeDtypeStruct((cols, 1, units), f32),
            jax.ShapeDtypeStruct((count, depth), bf16),
            jax.ShapeDtypeStruct((count, depth), f32),
            jax.ShapeDtypeStruct((8, depth), f32),
            jax.ShapeDtypeStruct((cols, head_cols, count), bf16),
            jax.ShapeDtypeStruct((2, rows, chips) + w_qkv.shape, bf16),
        ],
        scratch_shapes=[
            vmem((count, depth), bf16), vmem((depth, count), bf16),
            vmem((count, depth), f32), vmem((count, depth), f32), vmem((count, depth), f32),
            vmem((cols, count, units), bf16), vmem((cols, count, units), bf16),
            vmem((count, depth), bf16), vmem((cols, head_cols, count), bf16),
            vmem((2, chips, units, depth), bf16), vmem((2, chips, units, depth), bf16),
            vmem((chips, head_cols, depth), bf16), vmem((chips, head_cols, depth), bf16),
            dma((cols,)), dma((cols,)), dma((2, chips)), dma((2, chips)), dma, dma,
            dma((chips,)), dma((chips,)), dma((chips, rows)), dma((chips, rows)), dma, dma,
            dma((2,)),
        ],
        compiler_params=pltpu.CompilerParams(
            vmem_limit_bytes=63 << 20, collective_id=1, has_side_effects=True
        ),
        cost_estimate=cost(
            12 * count * depth * cols * units, 8 * depth * cols * units + 16 * count * depth
        ),
        name="middle",
    )(heads, tokens, grad, w_up, w_down, b_up, vecs, w_out, w_qkv)


def back_kernel(
    rows, cols, heads, seqs, tiles, sub,
    blk_ref, q_ref, k_ref, v_ref, do_ref, o_ref, lse_ref, x_ref, w_ref, tok_ref, dres_ref, vec_ref,
    gup_ref, gdown_ref, gout_ref, early_ref,
    dtok_ref, wup_ref, wdown_ref, wout_ref, wqkv_ref, all_ref, bias_ref,
    d_mixed, d_arrived, key_grad, value_grad, bias_sum, qkv_acc, qkv_send, qkv_recv, norm_acc,
    up_recv, down_recv, out_recv, up_send, down_send, out_send, up_line, down_line, out_line,
    small, small_core, small_row, small_line, bias_send, bias_recv,
    send_r, recv_r, send_z, recv_z, send_d, recv_d, send_q, recv_q, send_b, recv_b,
    send_s0, recv_s0, send_s1, recv_s1, send_s2, recv_s2, local,
):
    step = pl.program_id(0)
    chips = cols // 2
    row, col = place()
    chip, lane = col // 2, lax.rem(col, 2)
    work = heads * seqs * tiles
    last = work + 2 * cols - 1
    head = step // (seqs * tiles)
    seq = lax.rem(step // tiles, seqs)
    turn = lax.rem(step, tiles)
    i = tiles - 1 - turn
    tile = q_ref.shape[1]
    chunks, _, chunk = do_ref.shape
    chunks_seq = SEQ_LEN // chunk
    parts = tile // sub
    steps = tile
    start = pl.multiple_of(i * tile, tile)

    given = (gdown_ref, gup_ref, gout_ref)
    by_row = (down_recv, up_recv, out_recv)
    to_line = (down_send, up_send, out_send)
    by_line = (down_line, up_line, out_line)
    results = (wdown_ref, wup_ref, wout_ref)

    def row_stage(n):
        return over_row(
            rows, lambda at: given[n].at[at], lambda at: by_row[n].at[at], send_r.at[n],
            recv_r.at[n],
        )

    def own_row(n):
        return pltpu.make_async_copy(given[n].at[row], by_row[n].at[row], local.at[n])

    def line_stage(n):
        return over_line(
            chips, lambda at: to_line[n].at[at], lambda at: by_line[n].at[at], send_z.at[n],
            recv_z.at[n],
        )

    def add_rows(n):
        own_row(n).wait()
        row_stage(n).wait_recv()

        def one(c, carry):
            total = by_row[n][0, c].astype(f32)
            for r in range(1, rows):
                total = total + by_row[n][r, c].astype(f32)
            to_line[n][c] = total.astype(bf16)
            return carry

        lax.fori_loop(0, chips, one, 0)
        by_line[n][chip] = to_line[n][chip]
        line_stage(n).start()

    def d_stage(h):
        return over_col(
            cols, lambda at: d_mixed.at[h, at], lambda at: d_arrived.at[h, at], send_d.at[h],
            recv_d.at[h],
        )

    def own_d(h):
        return pltpu.make_async_copy(d_mixed.at[h, col], d_arrived.at[h, col], local.at[3 + h])

    q_stage = over_row(
        rows, lambda at: qkv_send.at[at], lambda at: qkv_recv.at[at], send_q, recv_q
    )
    b_stage = over_row(rows, lambda at: bias_send, lambda at: bias_recv.at[at], send_b, recv_b)
    s_core = remote(small.at[0], small_core, send_s0, recv_s0, mate())
    s_row = over_row(
        rows, lambda at: small.at[1], lambda at: small_row.at[at], send_s1, recv_s1
    )
    s_line = over_line(
        chips, lambda at: small.at[2], lambda at: small_line.at[at], send_s2, recv_s2
    )

    @pl.when(step == 0)
    def _():
        greet(rows, cols)
        for n in range(3):
            own_row(n).start()
            row_stage(n).start()

    @pl.when(step == work // 2 + 1)
    def _():
        add_rows(0)

    @pl.when((step < work) & (turn == 0))
    def _():
        key_grad[...] = jnp.zeros_like(key_grad)
        value_grad[...] = jnp.zeros_like(value_grad)

    @pl.when((step < work) & (turn == 0) & (seq == 0))
    def _():
        bias_sum[head] = jnp.zeros((HD, 128), f32)

    @pl.when(step < work)
    def _():
        d_out = jnp.concatenate([do_ref[b] for b in range(chunks)], axis=1)
        out = jnp.concatenate([o_ref[b] for b in range(chunks)], axis=1)
        delta = jnp.sum(d_out.astype(f32) * out.astype(f32), axis=0, keepdims=True)
        lse = lse_ref[0, 0]

        def cut(x, a):
            return x[:, a * sub : (a + 1) * sub]

        queries = [q_ref[0, a * sub : (a + 1) * sub, :] for a in range(parts)]
        query_blocks = [
            blk_ref[0, :, pl.ds(pl.multiple_of(start + a * sub, sub), sub)] for a in range(parts)
        ]

        def update(a, query_grad, key_start, count, masked):
            keys = k_ref[0, pl.ds(key_start, count), :]
            values = v_ref[0, pl.ds(key_start, count), :]
            scores = dot(keys, queries[a], NT) * SCALE2 - cut(lse, a)
            if masked:
                mask = tile_mask(blk_ref, key_start, count, query_blocks[a])
                scores = jnp.where(mask, scores, MASKED)
            probs = jnp.exp2(scores)
            d_values = dot(probs.astype(bf16), cut(d_out, a), NT)
            d_scores = (probs * (dot(values, cut(d_out, a)) - cut(delta, a))).astype(bf16)
            d_keys = dot(d_scores, queries[a])
            return query_grad + dot(keys, d_scores, TN), d_keys, d_values

        def add(key_start, count, d_keys, d_values):
            key_grad[pl.ds(key_start, count), :] += d_keys
            value_grad[pl.ds(key_start, count), :] += d_values

        def sweep(j, grads):
            key_start = pl.multiple_of(j * steps, steps)
            found = [update(a, grads[a], key_start, steps, False) for a in range(parts)]
            add(key_start, steps, sum(f[1] for f in found), sum(f[2] for f in found))
            return tuple(f[0] for f in found)

        grads = list(
            lax.fori_loop(0, start // steps, sweep, (jnp.zeros((HD, sub), f32),) * parts)
        )
        for a in range(parts):
            todo = [(pl.multiple_of(start + a * sub, sub), sub, True)]
            if a > 0:
                todo.append((start, a * sub, False))
            if a < parts - 1:
                todo.append((pl.multiple_of(start + (a + 1) * sub, BLOCK), BLOCK, True))
            for key_start, count, masked in todo:
                grads[a], d_keys, d_values = update(a, grads[a], key_start, count, masked)
                add(key_start, count, d_keys, d_values)

        def beyond(j, grad):
            key_start = pl.multiple_of(start + tile, BLOCK)
            grad, d_keys, d_values = update(parts - 1, grad, key_start, BLOCK, True)
            add(key_start, BLOCK, d_keys, d_values)
            return grad

        grads[-1] = lax.fori_loop(0, jnp.where(i < tiles - 1, 1, 0), beyond, grads[-1])
        query_grad = jnp.concatenate(grads, axis=1) * SCALE
        bias_sum[head, :, :1] += jnp.sum(query_grad, axis=1, keepdims=True)
        query_grad = query_grad.astype(bf16)
        for b in range(chunks):
            d_mixed[head, seq * chunks_seq + i * chunks + b, :HD] = query_grad[
                :, b * chunk : (b + 1) * chunk
            ]

    @pl.when((step < work) & (turn == tiles - 1))
    def _():
        def one(c, value_sum):
            where = pl.ds(pl.multiple_of(c * chunk, chunk), chunk)
            at = seq * chunks_seq + c
            d_mixed[head, at, HD : 2 * HD] = (key_grad[where, :].T * SCALE).astype(bf16)
            d_values = value_grad[where, :].T
            d_mixed[head, at, 2 * HD :] = d_values.astype(bf16)
            return value_sum + jnp.sum(d_values, axis=1, keepdims=True)

        value_sum = lax.fori_loop(0, chunks_seq, one, jnp.zeros((HD, 1), f32))
        bias_sum[head, :, 1:2] += value_sum

    for h in range(heads):

        @pl.when(step == (h + 1) * seqs * tiles - 1)
        def _():
            own_d(h).start()
            d_stage(h).start()

    at = step - work

    @pl.when(at == 0)
    def _():
        qkv_acc[...] = jnp.zeros_like(qkv_acc)
        bias_send[...] = bias_sum[...]
        bias_recv[row] = bias_sum[...]
        b_stage.start()

    @pl.when((at >= 0) & (at < cols))
    def _():
        grads = jnp.concatenate([d_mixed[h, at] for h in range(heads)], axis=0)
        qkv_acc[...] += dot(grads, x_ref[0])

    @pl.when(at == cols - 1)
    def _():
        width = qkv_send.shape[2]
        for r in range(rows):
            qkv_send[r] = qkv_acc[:, r * width : (r + 1) * width].astype(bf16)
        qkv_recv[row] = qkv_send[row]
        q_stage.start()
        add_rows(1)
        add_rows(2)
        norm_acc[...] = jnp.zeros_like(norm_acc)
        for h in range(heads):
            own_d(h).wait()
            d_stage(h).wait_recv()

    @pl.when(at >= cols)
    def _():
        c = at - cols
        width = w_ref.shape[3]
        found = flip(
            jnp.concatenate(
                [
                    d_arrived[h, c, j * HD : (j + 1) * HD, :]
                    for j in range(3)
                    for h in range(heads)
                ],
                axis=0,
            )
        )
        for r in range(rows):
            norm_acc[:, r * width : (r + 1) * width] += dot(found, w_ref[0, r, 0], NT)

    @pl.when(step == last)
    def _():
        xhat, inv = moments(tok_ref[...].astype(f32))
        d_norm = norm_acc[...]
        late = early_ref.shape[0] - 2
        small[0] = early_ref[...]
        small[0, late : late + 1] = jnp.sum(d_norm * xhat, axis=0, keepdims=True)
        small[0, late + 1 : late + 2] = jnp.sum(d_norm, axis=0, keepdims=True)
        s_core.start()
        dtok_ref[...] = dres_ref[...] + norm_back(xhat, inv, d_norm * vec_ref[0:1])
        s_core.wait_recv()
        small[1] = small[0] + small_core[...]
        small_row[row] = small[1]
        s_row.start()
        b_stage.wait_recv()
        bias_ref[...] = sum(bias_recv[r] for r in range(1, rows)) + bias_recv[0]
        q_stage.wait_recv()
        total = qkv_recv[0].astype(f32)
        for r in range(1, rows):
            total = total + qkv_recv[r].astype(f32)
        wqkv_ref[...] = total
        s_row.wait_recv()
        small[2] = sum(small_row[r] for r in range(1, rows)) + small_row[0]
        small_line[chip] = small[2]
        s_line.start()
        for n in range(3):
            line_stage(n).wait_recv()
            total = by_line[n][0].astype(f32)
            for c in range(1, chips):
                total = total + by_line[n][c].astype(f32)
            results[n][...] = total
        s_line.wait_recv()
        all_ref[...] = sum(small_line[c] for c in range(1, chips)) + small_line[0]
        for n in range(3):
            row_stage(n).wait_send()
            line_stage(n).wait_send()
        for h in range(heads):
            d_stage(h).wait_send()
        q_stage.wait_send()
        b_stage.wait_send()
        s_core.wait_send()
        s_row.wait_send()
        s_line.wait_send()


def backward(
    blocks, q, k, v, d_heads, out, lse, x, w_qkv, tokens, d_resid, vecs, grad_up, grad_down,
    grad_out, early,
):
    heads, total, _ = q.shape
    count, depth = tokens.shape
    rows, chips, units, width = grad_up.shape
    cols = 2 * chips
    head_cols = grad_out.shape[2]
    seqs = total // SEQ_LEN
    tile, sub = 1024, 512
    tiles = SEQ_LEN // tile
    work = heads * seqs * tiles
    pairs = heads * seqs * SEQ_LEN * SEQ_LEN * 5 // 8

    def unpack(s):
        s = jnp.minimum(s, work - 1)
        return s // (seqs * tiles), lax.rem(s // tiles, seqs), tiles - 1 - lax.rem(s, tiles)

    def queries_map(s):
        h, b, i = unpack(s)
        return (h, b * tiles + i, 0)

    def keys_map(s):
        h, b, _ = unpack(s)
        return (h, b, 0)

    def heads_map(s):
        h, b, i = unpack(s)
        return (b * tiles + i, h, 0)

    def lse_map(s):
        h, b, i = unpack(s)
        return (h, b, 0, i)

    def w_map(s):
        c = jnp.maximum(s - work - cols, 0)
        return (lax.rem(c, 2), 0, c // 2, 0, 0)

    keys = pl.BlockSpec((1, SEQ_LEN, HD), keys_map)
    heads_spec = pl.BlockSpec((tile // chunk_of(tokens), HD, count), heads_map)
    any_space = pl.BlockSpec(memory_space=pl.ANY)
    block = whole((count, depth))
    dma, vmem = pltpu.SemaphoreType.DMA, pltpu.VMEM
    parts = heads * 3 * HD
    shape = jax.ShapeDtypeStruct
    small = early.shape
    return pl.pallas_call(
        functools.partial(back_kernel, rows, cols, heads, seqs, tiles, sub),
        grid=(work + 2 * cols,),
        in_specs=[
            pl.BlockSpec((1, 1, SEQ_LEN), lambda s: (unpack(s)[1], 0, 0)),
            pl.BlockSpec((1, tile, HD), queries_map), keys, keys, heads_spec, heads_spec,
            pl.BlockSpec((1, 1, 1, tile), lse_map),
            pl.BlockSpec((1, count, depth), lambda s: (jnp.clip(s - work, 0, cols - 1), 0, 0)),
            pl.BlockSpec((1, rows, 1) + w_qkv.shape[3:], w_map),
            block, block, whole(vecs.shape), any_space, any_space, any_space, whole(small),
        ],
        out_specs=[
            block, whole((units, width)), whole((units, width)), whole((head_cols, width)),
            whole((parts, width)), whole(small), whole((heads, HD, 128)),
        ],
        out_shape=[
            shape((count, depth), f32), shape((units, width), f32), shape((units, width), f32),
            shape((head_cols, width), f32), shape((parts, width), f32), shape(small, f32),
            shape((heads, HD, 128), f32),
        ],
        scratch_shapes=[
            vmem((heads, cols, 3 * HD, count), bf16), vmem((heads, cols, 3 * HD, count), bf16),
            vmem((SEQ_LEN, HD), f32), vmem((SEQ_LEN, HD), f32), vmem((heads, HD, 128), f32),
            vmem((parts, depth), f32), vmem((rows, parts, width), bf16),
            vmem((rows, parts, width), bf16), vmem((count, depth), f32),
            vmem((rows, chips, units, width), bf16), vmem((rows, chips, units, width), bf16),
            vmem((rows, chips, head_cols, width), bf16),
            vmem((chips, units, width), bf16), vmem((chips, units, width), bf16),
            vmem((chips, head_cols, width), bf16),
            vmem((chips, units, width), bf16), vmem((chips, units, width), bf16),
            vmem((chips, head_cols, width), bf16),
            vmem((3,) + small, f32), vmem(small, f32), vmem((rows,) + small, f32),
            vmem((chips,) + small, f32),
            vmem((heads, HD, 128), f32), vmem((rows, heads, HD, 128), f32),
            dma((3, rows)), dma((3, rows)), dma((3, chips)), dma((3, chips)),
            dma((heads, cols)), dma((heads, cols)), dma((rows,)), dma((rows,)),
            dma((rows,)), dma((rows,)), dma, dma, dma((rows,)), dma((rows,)),
            dma((chips,)), dma((chips,)), dma((3 + heads,)),
        ],
        compiler_params=pltpu.CompilerParams(
            vmem_limit_bytes=63 << 20, collective_id=2, has_side_effects=True
        ),
        cost_estimate=cost(40 * pairs * HD, 16 * heads * total * HD, pairs),
        name="backward",
    )(
        blocks, q, k, v, d_heads, out, lse, x, w_qkv, tokens, d_resid, vecs, grad_up, grad_down,
        grad_out, early,
    )


def chunk_of(tokens):
    return tokens.shape[0]


def body(
    tokens, blocks, w_qkv, b_qv, w_out, b_out, w_up, b_up, w_down, b_down,
    gain1, shift1, gain2, shift2, grad_out,
):
    rows, cols = lax.axis_size("row"), lax.axis_size("col")
    depth = tokens.shape[1]
    head_cols = w_qkv.shape[2]
    heads = head_cols // HD
    units = w_up.shape[0]

    def vec(v):
        return v.reshape(1, -1)

    vecs = jnp.stack([gain1, shift1, b_out, gain2, shift2, b_down] + [gain1] * 2).astype(f32)
    w_qkv_flat = w_qkv.reshape(w_qkv.shape[0], 3 * head_cols)

    (
        attn_rows, q, k, v, found, arrived, lse, block_ids, up_bias, out_weight, up_weight,
        down_weight,
    ) = front(
        tokens, vecs, vec(blocks), vec(b_up), w_qkv_flat, b_qv, w_out, w_up,
        w_down, rows, cols,
    )
    grad_up, grad_down, grad_wout, grad_bup, output, d_resid, sums, d_heads, qkv_all = middle(
        arrived, tokens, grad_out, up_weight, down_weight, up_bias, vecs, out_weight, w_qkv_flat,
    )
    hidden_units = units * cols
    used = 4 + hidden_units // depth
    spare = (used + 9) // 8 * 8 - used
    early = jnp.concatenate(
        [sums[:4], grad_bup.reshape(-1, depth), jnp.zeros((spare, depth), f32)]
    )
    grad_tokens, grad_wup, grad_wdown, grad_wout, grad_wqkv, small, bias = backward(
        block_ids, q, k, v, d_heads, found, lse, attn_rows, qkv_all, tokens, d_resid, vecs,
        grad_up, grad_down, grad_wout, early,
    )
    grad_wqkv = (
        grad_wqkv.reshape(heads, 3, HD, depth // rows)
        .transpose(3, 1, 0, 2)
        .reshape(depth // rows, 3, head_cols)
    )
    grad_bqv = bias[:, :, :2].reshape(head_cols, 2).T
    grad_bdown, grad_gain2, grad_shift2, grad_bout = small[:4]
    grad_bup = lax.dynamic_slice_in_dim(
        small[4:used].reshape(-1), lax.axis_index("col") * units, units
    )
    grad_gain1, grad_shift1 = small[-2:]
    return (
        output, grad_tokens, grad_wqkv, grad_bqv, grad_wout, grad_bout, grad_wup, grad_bup,
        grad_wdown, grad_bdown, grad_gain1, grad_shift1, grad_gain2, grad_shift2,
    )


def solution(mesh):
    tokens, weight, whole_vec = P(("row", "col"), None), P("col", "row"), P()
    qkv, bias_qv = P("row", None, "col"), P(None, "col")
    return jax.shard_map(
        body,
        mesh=mesh,
        in_specs=(
            tokens, P(("row", "col")), qkv, bias_qv, weight, whole_vec, weight, P("col"), weight,
            whole_vec, whole_vec, whole_vec, whole_vec, whole_vec, tokens,
        ),
        out_specs=(
            tokens, tokens, qkv, bias_qv, weight, whole_vec, weight, P("col"), weight,
            whole_vec, whole_vec, whole_vec, whole_vec, whole_vec,
        ),
        check_vma=False,
    )
```

```python
import functools

import jax
import jax.numpy as jnp
from jax import lax
from jax.experimental import pallas as pl
from jax.experimental.pallas import tpu as pltpu
from jax.sharding import PartitionSpec as P

HD = 64
SEQ_LEN = 4096
BLOCK = 256
EPS = 1e-05
SCALE = HD ** (-0.5)
SCALE2 = SCALE * 1.4426950408889634
MASKED = -1e30
ONES = 16
MESH = pl.DeviceIdType.MESH
VMEM_LIMIT = 60 << 20

f32 = jnp.float32
bf16 = jnp.bfloat16

NN = (((1,), (0,)), ((), ()))
NT = (((1,), (1,)), ((), ()))
TN = (((0,), (0,)), ((), ()))


def dot(a, b, dims=NN):
    return lax.dot_general(a, b, dims, preferred_element_type=f32)


def flip(x):
    return x.astype(f32).T.astype(bf16)


def params(**more):
    return pltpu.CompilerParams(vmem_limit_bytes=VMEM_LIMIT, **more)


def cost(flops, nbytes, transcendentals=0):
    return pl.CostEstimate(flops=flops, bytes_accessed=nbytes, transcendentals=transcendentals)


def whole(shape):
    return pl.BlockSpec(shape, lambda *_: (0,) * len(shape))


def moments(v):
    center = jnp.mean(v, axis=-1, keepdims=True)
    centered = v - center
    spread = jnp.mean(centered * centered, axis=-1, keepdims=True)
    inv = lax.rsqrt(spread + EPS)
    return centered * inv, inv


def norm_back(xhat, inv, e):
    return inv * (
        e - jnp.mean(e, axis=-1, keepdims=True) - xhat * jnp.mean(e * xhat, axis=-1, keepdims=True)
    )


def place():
    return lax.axis_index("row"), lax.axis_index("col")


def greet(rows, cols):
    row, col = place()
    barrier = pltpu.get_barrier_semaphore()

    def to_col(k, carry):
        pl.semaphore_signal(
            barrier, inc=1, device_id=(row, lax.rem(col + k, cols)), device_id_type=MESH
        )
        return carry

    def to_row(k, carry):
        pl.semaphore_signal(
            barrier, inc=1, device_id=(lax.rem(row + k, rows), col), device_id_type=MESH
        )
        return carry

    lax.fori_loop(1, cols, to_col, 0)
    lax.fori_loop(1, rows, to_row, 0)
    pl.semaphore_wait(barrier, rows + cols - 2)


def remote(src, dst, send, recv, device):
    return pltpu.make_async_remote_copy(
        src_ref=src, dst_ref=dst, send_sem=send, recv_sem=recv, device_id=device, device_id_type=MESH
    )


def each(count, act):
    def turn(k, carry):
        act(k)
        return carry

    lax.fori_loop(1, count, turn, 0)


class Exchange:
    def __init__(self, count, here, slot, to, out, into, send, recv):
        self.count, self.here, self.slot, self.to = count, here, slot, to
        self.out, self.into, self.send, self.recv = out, into, send, recv

    def copy(self, k):
        at = self.slot(k)
        return remote(
            self.out(at), self.into(self.here), self.send.at[k], self.recv.at[self.here], self.to(k)
        )

    def arrival(self, k):
        at = self.slot(k)
        return remote(self.out(at), self.into(at), self.send.at[k], self.recv.at[at], self.to(k))

    def start(self):
        each(self.count, lambda k: self.copy(k).start())

    def wait_recv(self):
        each(self.count, lambda k: self.arrival(k).wait_recv())

    def wait_send(self):
        each(self.count, lambda k: self.copy(k).wait_send())


def over_row(rows, out, into, send, recv):
    row, col = place()
    slot = lambda k: lax.rem(row + k, rows)
    return Exchange(rows, row, slot, lambda k: (slot(k), col), out, into, send, recv)


def over_col(cols, out, into, send, recv):
    row, col = place()
    slot = lambda k: lax.rem(col + k, cols)
    return Exchange(cols, col, slot, lambda k: (row, slot(k)), out, into, send, recv)


def over_line(chips, out, into, send, recv):
    row, col = place()
    chip, lane = col // 2, lax.rem(col, 2)
    slot = lambda k: lax.rem(chip + k, chips)
    return Exchange(chips, chip, slot, lambda k: (row, slot(k) * 2 + lane), out, into, send, recv)


class Plane:
    def __init__(self):
        row, col = place()
        lane = lax.rem(col, 2)
        self.next_x = row + 1 - 2 * lax.rem(row, 2)
        self.next_y = lax.rem(row + 2, 4)
        self.across = lax.rem(self.next_x + 2, 4)
        self.first = jnp.where(lane == 0, self.next_y, self.next_x)
        self.second = jnp.where(lane == 0, self.next_x, self.next_y)


def mate():
    row, col = place()
    return (row, col // 2 * 2 + 1 - lax.rem(col, 2))


def front_kernel(
    rows, cols, heads,
    tok_ref, vec_ref, blk_ref, bup_ref, wq_ref, bias_ref, wout_ref, wup_ref, wdown_ref,
    xo_ref, q_ref, k_ref, v_ref, found_ref, arrived_ref, lse_ref, blko_ref, bupo_ref,
    wouto_ref, wupo_ref, wdowno_ref,
    xs, wqs, qs, ks, vs, vt, totals, tops, founds, blks, bups,
    send_x, recv_x, send_q, recv_q, send_s, recv_s, send_f, recv_f,
    send_wz, recv_wz, send_wr, recv_wr, send_wm, recv_wm, local_x, local_q, local_f, local_w,
):
    chips = cols // 2
    row, me = place()
    chip, lane = me // 2, lax.rem(me, 2)
    count = tok_ref.shape[0]
    tile = 2 * count
    seq_chips = SEQ_LEN // tile
    depth = wq_ref.shape[0]
    width = heads * HD

    xhat, _ = moments(tok_ref[...].astype(f32))
    xs[me] = (xhat * vec_ref[0:1] + vec_ref[1:2]).astype(bf16)
    blks[me] = blk_ref[...]
    bups[me] = bup_ref[...]
    own_rows = pl.ds(pl.multiple_of(row * depth, depth), depth)
    wqs[own_rows] = wq_ref[...]
    vt[:, HD:, :] = jnp.ones((heads, ONES, vt.shape[2]), bf16)
    greet(rows, cols)

    def chunk(owner, target, route, at):
        return remote(
            xs.at[owner], xs.at[owner], send_x.at[route, at], recv_x.at[route, at], (row, target)
        )

    def to_mate(owner, at):
        return remote(xs.at[owner], xs.at[owner], send_x.at[2, at], recv_x.at[2, at], mate())

    given = (wout_ref, wup_ref, wdown_ref)
    gathered = (wouto_ref, wupo_ref, wdowno_ref)

    q_stage = over_row(
        rows,
        lambda at: wq_ref,
        lambda at: wqs.at[pl.ds(pl.multiple_of(at * depth, depth), depth)],
        send_q,
        recv_q,
    )
    small = [
        over_col(cols, lambda at: blk_ref, lambda at: blks.at[at], send_s.at[0], recv_s.at[0]),
        over_col(cols, lambda at: bup_ref, lambda at: bups.at[at], send_s.at[1], recv_s.at[1]),
    ]
    f_stage_out = lambda at: founds.at[at]
    f_stage = over_col(cols, f_stage_out, lambda at: arrived_ref.at[at], send_f, recv_f)

    def w_line(n, at, to, route):
        block = gathered[n].at[lane, at, row]
        out = given[n] if at is chip else block
        return remote(
            out, block, send_wz.at[n, route, at], recv_wz.at[n, at], (row, to * 2 + lane)
        )

    def w_row(n, c, out):
        return over_row(
            rows, lambda at: out, lambda at: gathered[n].at[lane, c, at], send_wr.at[n, c],
            recv_wr.at[n, c],
        )

    square = rows == 4
    plane = Plane()
    next_x, next_y, across_x = plane.next_x, plane.next_y, plane.across
    relayed, relay_to = plane.first, plane.second

    def w_step(n, c, slot, k, to):
        block = gathered[n].at[lane, c, slot]
        out = given[n] if (slot is row and c is chip) else block
        return remote(out, block, send_wr.at[n, c, k], recv_wr.at[n, c, slot], (to, me))

    def rows_start(n, c):
        if square:
            w_step(n, c, row, 0, next_x).start()
            w_step(n, c, row, 1, next_y).start()
        else:
            w_row(n, c, given[n] if c is chip else gathered[n].at[lane, c, row]).start()

    def rows_relay(n, c):
        if square:
            w_step(n, c, relayed, 2, relay_to).wait_recv()
            w_step(n, c, relayed, 2, relay_to).start()

    def rows_wait_recv(n, c):
        if square:
            w_step(n, c, relay_to, 0, next_x).wait_recv()
            w_step(n, c, across_x, 0, next_x).wait_recv()
        else:
            w_row(n, c, given[n]).wait_recv()

    def rows_wait_send(n, c):
        if square:
            for k in range(3):
                w_step(n, c, row, k, next_x).wait_send()
        else:
            w_row(n, c, given[n]).wait_send()

    def w_own(n):
        return pltpu.make_async_copy(given[n], gathered[n].at[lane, chip, row], local_w.at[n])

    def w_mate(n, c, side):
        block = gathered[n].at[side, c]
        return remote(block, block, send_wm.at[n, c], recv_wm.at[n, c], mate())

    to_mate(me, chip).start()
    q_stage.start()
    for exchange in small:
        exchange.start()

    @pl.when(chip + 1 < chips)
    def _():
        for n in range(3):
            w_line(n, chip, chip + 1, 0).start()
        chunk(me, me + 2, 0, chip).start()

    @pl.when(chip > 0)
    def _():
        for n in range(3):
            w_line(n, chip, chip - 1, 1).start()
        chunk(me, me - 2, 1, chip).start()

    for n in range(3):
        w_own(n).start()
        rows_start(n, chip)
    q_stage.wait_recv()
    for exchange in small:
        exchange.wait_recv()

    def update(h, q_tile, q_low, q_count, key_start, key_count, mask):
        lanes = pl.ds(q_low, q_count)
        query = qs[h, pl.ds(pl.multiple_of(q_tile * tile + q_low, BLOCK), q_count), :]
        keys = pl.ds(pl.multiple_of(key_start, BLOCK), key_count)
        scores = dot(ks[h, keys, :], query, NT)
        if mask is not None:
            scores = jnp.where(mask, scores, MASKED)
        top = tops[h, q_tile, :, lanes]
        higher = jnp.maximum(top, jnp.max(scores, axis=0, keepdims=True) * SCALE2)
        probs = jnp.exp2(scores * SCALE2 - higher)
        part = dot(vt[h, :, keys], probs.astype(bf16))
        totals[h, q_tile, :, lanes] = totals[h, q_tile, :, lanes] * jnp.exp2(top - higher) + part
        tops[h, q_tile, :, lanes] = higher

    def column(blocks, amount):
        return jnp.broadcast_to(blocks, (128, amount)).T[:, :1]

    def diagonal(p):
        low, high = blks[2 * p], blks[2 * p + 1]
        first = column(jnp.concatenate([low, high[:, :BLOCK]], axis=1), count + BLOCK)
        second = column(jnp.concatenate([low, high], axis=1), tile)
        for h in range(heads):
            update(h, p, 0, count, p * tile, count + BLOCK, low >= first)
            update(h, p, count, count, p * tile, tile, high >= second)

    def boundary(p):
        mask = blks[2 * p + 1][:, count - BLOCK :] >= column(blks[2 * p + 2][:, :BLOCK], BLOCK)
        for h in range(heads):
            update(h, p, tile - BLOCK, BLOCK, (p + 1) * tile, BLOCK, mask)

    def project(p):
        both = jnp.concatenate([xs[2 * p], xs[2 * p + 1]], axis=0)
        mixed = dot(both, wqs[...])
        bias = bias_ref[...].astype(f32)
        where = pl.ds(pl.multiple_of(p * tile, tile), tile)
        for h in range(heads):
            at = [slice(j * width + h * HD, j * width + (h + 1) * HD) for j in range(3)]
            here = slice(h * HD, (h + 1) * HD)
            qs[h, where, :] = (mixed[:, at[0]] + bias[0:1, here]).astype(bf16)
            ks[h, where, :] = mixed[:, at[1]].astype(bf16)
            values = (mixed[:, at[2]] + bias[1:2, here]).astype(bf16)
            vs[h, where, :] = values
            vt[h, :HD, where] = flip(values)
            totals[h, p] = jnp.zeros(totals.shape[2:], f32)
            tops[h, p] = jnp.full(tops.shape[2:], MASKED, f32)

    def keep(p):
        where = pl.ds(pl.multiple_of(p * tile, tile), tile)
        pairs = [
            pltpu.make_async_copy(held.at[:, where, :], out.at[:, where, :], local_q.at[n, p])
            for n, (held, out) in enumerate(((qs, q_ref), (ks, k_ref), (vs, v_ref)))
        ]
        return pairs + [
            pltpu.make_async_copy(xs.at[2 * p + c], xo_ref.at[2 * p + c], local_x.at[2 * p + c])
            for c in range(2)
        ]

    def kept(c):
        return pltpu.make_async_copy(founds.at[c], found_ref.at[c], local_f.at[0, c])

    def own(c):
        return pltpu.make_async_copy(founds.at[c], arrived_ref.at[c], local_f.at[1, 0])

    def conclude(p):
        for h in range(heads):
            mass = totals[h, p, HD : HD + 1, :]
            out = (totals[h, p, :HD, :] / mass).astype(bf16)
            for c in range(2):
                founds[2 * p + c, h * HD : (h + 1) * HD, :] = out[:, c * count : (c + 1) * count]
            lse_ref[
                h, p // seq_chips, :, pl.ds(pl.multiple_of(lax.rem(p, seq_chips) * tile, tile), tile)
            ] = tops[h, p] + jnp.log2(mass)
        for c in range(2):
            owner = 2 * p + c
            kept(owner).start()

            @pl.when(owner == me)
            def _():
                own(owner).start()

            @pl.when(owner != me)
            def _():
                f_stage.copy(lax.rem(owner - me + cols, cols)).start()

    def pass_weights():
        for n in range(3):
            w_own(n).wait()

            def across(c, carry):
                rows_wait_recv(n, c)
                w_mate(n, c, lane).start()
                return carry

            lax.fori_loop(0, chips, across, 0)

    def event(e, carry):
        hop = (e + 1) // 2
        lower = lax.rem(e, 2) == 1
        p = jnp.where(lower, chip - hop, chip + hop)

        @pl.when(e == 1)
        def _():
            for hop in range(1, chips):
                for at, step, route in ((chip - hop, 1, 0), (chip + hop, -1, 1)):

                    @pl.when((at >= 0) & (at < chips))
                    def _():
                        onward = chip + step
                        for n in range(3):
                            w_line(n, at, onward, route).wait_recv()

                            @pl.when((onward >= 0) & (onward < chips))
                            def _():
                                w_line(n, at, onward, route).start()

                            rows_start(n, at)

        @pl.when(e == 2 * chips - 3)
        def _():
            pass_weights()

        @pl.when(lower)
        def _():
            below, above = chip - hop, chip + hop

            @pl.when(below >= 0)
            def _():
                owner = below * 2 + lane
                chunk(owner, me, 0, below).wait_recv()

                @pl.when(chip + 1 < chips)
                def _():
                    chunk(owner, me + 2, 0, below).start()

                to_mate(owner, below).start()

            @pl.when(above < chips)
            def _():
                owner = above * 2 + lane
                chunk(owner, me, 1, above).wait_recv()

                @pl.when(chip > 0)
                def _():
                    chunk(owner, me - 2, 1, above).start()

                to_mate(owner, above).start()

        @pl.when(e == 1)
        def _():
            def relay(c, carry):
                for n in range(3):
                    rows_relay(n, c)
                return carry

            lax.fori_loop(0, chips, relay, 0)

        @pl.when((p >= 0) & (p < chips))
        def _():
            to_mate(2 * p + 1 - lane, p).wait_recv()
            project(p)
            for copy in keep(p):
                copy.start()
            first = p // seq_chips * seq_chips
            final = first + seq_chips - 1
            high = jnp.minimum(chip + hop - 1, final)
            low = jnp.maximum(jnp.maximum(chip - hop, 0), first)
            diagonal(p)

            @pl.when(lower & (p < final))
            def _():
                boundary(p)

            @pl.when(lower & (p == first))
            def _():
                conclude(p)

            @pl.when(jnp.logical_not(lower) & (p > first) & (hop > 0))
            def _():
                boundary(p - 1)

                @pl.when(low == first)
                def _():
                    conclude(p - 1)

            amount = jnp.where(lower, high - p, p - low)

            def pair(j, carry):
                q_tile = jnp.where(lower, p + 1 + j, p)
                key_tile = jnp.where(lower, p, low + j)
                for h in range(heads):
                    update(h, q_tile, 0, tile, key_tile * tile, tile, None)

                @pl.when(lower & (p == first) & ((q_tile == final) | (q_tile < high)))
                def _():
                    conclude(q_tile)

                return carry

            lax.fori_loop(0, amount, pair, 0)

            @pl.when(jnp.logical_not(lower) & (p == final) & (low == first))
            def _():
                conclude(p)

        return carry

    lax.fori_loop(0, 2 * chips - 1, event, 0)

    for c in range(cols):
        bupo_ref[c] = bups[c]
        at = c * count
        blko_ref[at // SEQ_LEN, :, at % SEQ_LEN : at % SEQ_LEN + count] = blks[c]
    f_stage.wait_recv()
    for c in range(chips):
        for n in range(3):
            w_mate(n, c, 1 - lane).wait_recv()
            w_mate(n, c, lane).wait_send()
            rows_wait_send(n, c)

            @pl.when((c <= chip) & (chip + 1 < chips))
            def _():
                w_line(n, c, chip, 0).wait_send()

            @pl.when((c >= chip) & (chip > 0))
            def _():
                w_line(n, c, chip, 1).wait_send()

        for copy in keep(c):
            copy.wait()
        kept(2 * c).wait()
        kept(2 * c + 1).wait()
        to_mate(me, c).wait_send()

        @pl.when((c <= chip) & (chip + 1 < chips))
        def _():
            chunk(me, me, 0, c).wait_send()

        @pl.when((c >= chip) & (chip > 0))
        def _():
            chunk(me, me, 1, c).wait_send()

    own(me).wait()
    f_stage.wait_send()
    q_stage.wait_send()
    for exchange in small:
        exchange.wait_send()


def front(tokens, vecs, blocks, b_up, w_qkv, b_qv, w_out, w_up, w_down, rows, cols):
    count, depth = tokens.shape
    head_cols = w_qkv.shape[1] // 3
    heads = head_cols // HD
    chips = cols // 2
    total = count * cols
    tile = 2 * count
    any_space = pl.BlockSpec(memory_space=pl.ANY)
    in_vmem = pl.BlockSpec(memory_space=pltpu.VMEM)
    dma, vmem, shape = pltpu.SemaphoreType.DMA, pltpu.VMEM, jax.ShapeDtypeStruct
    pairs = heads * total * SEQ_LEN * 5 // 8
    held = (heads, total, HD)
    return pl.pallas_call(
        functools.partial(front_kernel, rows, cols, heads),
        in_specs=[in_vmem] * 9,
        out_specs=[any_space] * 6 + [in_vmem] * 3 + [any_space] * 3,
        out_shape=[
            shape((cols, count, depth), bf16), shape(held, bf16), shape(held, bf16),
            shape(held, bf16), shape((cols, head_cols, count), bf16),
            shape((cols, head_cols, count), bf16),
            shape((heads, total // SEQ_LEN, 1, SEQ_LEN), f32),
            shape((total // SEQ_LEN, 1, SEQ_LEN), jnp.int32), shape((cols,) + b_up.shape, bf16),
        ] + [shape((2, chips, rows) + w.shape, bf16) for w in (w_out, w_up, w_down)],
        scratch_shapes=[
            vmem((cols, count, depth), bf16), vmem((depth, 3 * head_cols), bf16),
            vmem(held, bf16), vmem(held, bf16), vmem(held, bf16),
            vmem((heads, HD + ONES, total), bf16),
            vmem((heads, chips, HD + ONES, tile), f32), vmem((heads, chips, 1, tile), f32),
            vmem((cols, head_cols, count), bf16), vmem((cols,) + blocks.shape, jnp.int32),
            vmem((cols,) + b_up.shape, bf16),
            dma((3, chips)), dma((3, chips)), dma((rows,)), dma((rows,)),
            dma((2, cols)), dma((2, cols)), dma((cols,)), dma((cols,)),
            dma((3, 2, chips)), dma((3, chips)), dma((3, chips, rows)), dma((3, chips, rows)),
            dma((3, chips)), dma((3, chips)),
            dma((cols,)), dma((3, chips)), dma((2, cols)), dma((3,)),
        ],
        compiler_params=pltpu.CompilerParams(
            vmem_limit_bytes=63 << 20, collective_id=0, has_side_effects=True
        ),
        cost_estimate=cost(16 * pairs * HD, 16 * heads * total * HD, pairs),
        name="front",
    )(tokens, vecs, blocks, b_up, w_qkv, b_qv, w_out, w_up, w_down)


def tile_mask(blk_ref, key_start, count, query_blocks):
    key_blocks = jnp.broadcast_to(blk_ref[0, :, pl.ds(key_start, count)], (128, count)).T[:, :1]
    return query_blocks >= key_blocks


GELU_A = 0.7978845608028654
GELU_B = 0.044715


def middle_kernel(
    rows, cols,
    heads_ref, tok_ref, g_ref, up_ref, down_ref, bup_ref, vec_ref, wout_ref, wq_ref,
    gup_ref, gdown_ref, gout_ref, output_ref, dres_ref, sums_ref, dheads_ref, wqo_ref,
    x, heads_all, resid, out_acc, norm_acc, hiddens, d_ups, low, d_send,
    mine, other, out_mine, out_other,
    send_d, recv_d, send_p, recv_p, send_o, recv_o, send_z, recv_z, send_r, recv_r, send_m, recv_m,
    local,
):
    step = pl.program_id(0)
    chips = cols // 2
    row, col = place()
    chip, lane = col // 2, lax.rem(col, 2)
    width = up_ref.shape[4]
    depth = wout_ref.shape[3]

    def part(r):
        return slice(r * width, (r + 1) * width)

    def out_weight(r):
        return jnp.concatenate([wout_ref[c % 2, c // 2, r] for c in range(cols)], axis=0)

    z_stage = over_line(
        chips, lambda at: wq_ref, lambda at: wqo_ref.at[lane, row, at], send_z, recv_z
    )

    def r_stage(c):
        return over_row(
            rows,
            lambda at: wqo_ref.at[lane, row, c],
            lambda at: wqo_ref.at[lane, at, c],
            send_r.at[c],
            recv_r.at[c],
        )

    m_stage = remote(wqo_ref.at[lane], wqo_ref.at[lane], send_m, recv_m, mate())
    m_arrival = remote(wqo_ref.at[1 - lane], wqo_ref.at[1 - lane], send_m, recv_m, mate())
    own_wq = pltpu.make_async_copy(wq_ref, wqo_ref.at[lane, row, chip], local.at[0])
    d_stage = over_col(
        cols, lambda at: d_send.at[at], lambda at: dheads_ref.at[at], send_d, recv_d
    )
    own_d = pltpu.make_async_copy(d_send.at[col], dheads_ref.at[col], local.at[1])

    def pair(at, which):
        return remote(
            mine.at[which, at], other.at[which, at], send_p.at[which, at], recv_p.at[which, at],
            mate(),
        )

    pair_out = remote(out_mine, out_other, send_o, recv_o, mate())

    @pl.when(step == 0)
    def _():
        greet(rows, cols)
        own_wq.start()
        z_stage.start()
        for s in range(cols):
            heads_all[s * depth : (s + 1) * depth] = heads_ref[s]
        stacked = flip(heads_all[...])
        for r in range(rows):
            branch = dot(stacked, out_weight(r))
            resid[:, part(r)] = tok_ref[:, part(r)].astype(f32) + branch + vec_ref[2:3, part(r)]
        xhat, _ = moments(resid[...])
        x[...] = (xhat * vec_ref[3:4] + vec_ref[4:5]).astype(bf16)
        out_acc[...] = jnp.zeros_like(out_acc)
        norm_acc[...] = jnp.zeros_like(norm_acc)

    @pl.when(step == 1)
    def _():
        own_wq.wait()
        z_stage.wait_recv()
        for c in range(chips):
            r_stage(c).start()

    @pl.when(step < cols)
    def _():
        up = bup_ref[0].astype(f32)
        d_hidden = 0.0
        for r in range(rows):
            up = up + dot(x[:, part(r)], up_ref[0, 0, r], NT)
            d_hidden = d_hidden + dot(g_ref[:, part(r)], down_ref[0, 0, r], NT)
        square = up * up
        bent = jnp.tanh(GELU_A * up * (1.0 + GELU_B * square))
        half = 0.5 + 0.5 * bent
        hidden = (up * half).astype(bf16)
        slope = half + (0.5 * GELU_A) * up * (1.0 - bent * bent) * (1.0 + (3.0 * GELU_B) * square)
        d_up = d_hidden * slope
        units = d_up.shape[1]
        per = sums_ref.shape[1] // units
        lanes = pl.ds(pl.multiple_of(lax.rem(step, per) * units, units), units)
        sums_ref[pl.ds(4 + step // per, 1), lanes] = jnp.sum(d_up, axis=0, keepdims=True)
        d_up = d_up.astype(bf16)
        hiddens[step] = hidden
        d_ups[step] = d_up
        for r in range(rows):
            out_acc[:, part(r)] += dot(hidden, down_ref[0, 0, r])
            norm_acc[:, part(r)] += dot(d_up, up_ref[0, 0, r])

    @pl.when(step == cols - 1)
    def _():
        output_ref[...] = (resid[...] + out_acc[...] + vec_ref[5:6]).astype(bf16)
        xhat, inv = moments(resid[...])
        d_norm = norm_acc[...]
        grad = g_ref[...].astype(f32)
        d_resid = grad + norm_back(xhat, inv, d_norm * vec_ref[3:4])
        dres_ref[...] = d_resid
        low[...] = d_resid.astype(bf16)
        sums_ref[0:1] = jnp.sum(grad, axis=0, keepdims=True)
        sums_ref[1:2] = jnp.sum(d_norm * xhat, axis=0, keepdims=True)
        sums_ref[2:3] = jnp.sum(d_norm, axis=0, keepdims=True)
        sums_ref[3:4] = jnp.sum(d_resid, axis=0, keepdims=True)
        found = 0.0
        for r in range(rows):
            found = found + dot(out_weight(r), low[:, part(r)], NT)
        found = found.astype(bf16)
        for c in range(cols):
            d_send[c] = found[c * depth : (c + 1) * depth]
        own_d.start()
        d_stage.start()
        found = dot(heads_all[...], low[...])
        for c in range(chips):
            first = found[2 * c * depth : (2 * c + 1) * depth]
            second = found[(2 * c + 1) * depth : (2 * c + 2) * depth]
            out_mine[c] = jnp.where(lane == 0, second, first).astype(bf16)
            kept = jnp.where(lane == 0, first, second)
            for r in range(rows):
                out_acc[c * depth : (c + 1) * depth, part(r)] = kept[:, part(r)]
        pair_out.start()

    at = step - cols

    @pl.when((at >= 0) & (at < chips))
    def _():
        c = at * 2 + 1 - lane
        mine[0, at] = dot(hiddens[c], g_ref[...], TN).astype(bf16)
        pair(at, 0).start()
        mine[1, at] = dot(d_ups[c], x[...], TN).astype(bf16)
        pair(at, 1).start()

    @pl.when(at == 0)
    def _():
        for c in range(chips):
            r_stage(c).wait_recv()
        m_stage.start()

    @pl.when(at >= chips)
    def _():
        k = at - chips
        c = k * 2 + lane
        grad_down = dot(hiddens[c], g_ref[...], TN)
        pair(k, 0).wait_recv()
        grad_down = (grad_down + other[0, k].astype(f32)).astype(bf16)
        grad_up = dot(d_ups[c], x[...], TN)
        pair(k, 1).wait_recv()
        grad_up = (grad_up + other[1, k].astype(f32)).astype(bf16)
        for r in range(rows):
            gdown_ref[r, 0] = grad_down[:, part(r)]
            gup_ref[r, 0] = grad_up[:, part(r)]

    @pl.when(step == 2 * cols - 1)
    def _():
        pair_out.wait_recv()
        for c in range(chips):
            for r in range(rows):
                kept = out_acc[c * depth : (c + 1) * depth, part(r)]
                gout_ref[r, c] = (kept + out_other[c, :, part(r)].astype(f32)).astype(bf16)
        d_stage.wait_recv()
        m_arrival.wait_recv()
        pair_out.wait_send()
        for k in range(chips):
            pair(k, 0).wait_send()
            pair(k, 1).wait_send()
            r_stage(k).wait_send()
        z_stage.wait_send()
        d_stage.wait_send()
        m_stage.wait_send()
        own_d.wait()


def middle(heads, tokens, grad, w_up, w_down, b_up, vecs, w_out, w_qkv):
    count, depth = tokens.shape
    _, chips, rows, units, width = w_up.shape
    cols = 2 * chips
    head_cols = w_out.shape[3]
    sum_rows = 4 + cols * units // depth
    any_space = pl.BlockSpec(memory_space=pl.ANY)

    def weight_map(s):
        c = jnp.minimum(s, cols - 1)
        return (lax.rem(c, 2), c // 2, 0, 0, 0)

    weight = pl.BlockSpec((1, 1, rows, units, width), weight_map)
    grad_spec = pl.BlockSpec(
        (rows, 1, units, width), lambda s: (0, jnp.maximum(s - cols - chips, 0), 0, 0)
    )
    grad_shape = jax.ShapeDtypeStruct((rows, chips, units, width), bf16)
    bias = pl.BlockSpec((1, 1, units), lambda s: (jnp.minimum(s, cols - 1), 0, 0))
    block = whole((count, depth))
    dma = pltpu.SemaphoreType.DMA
    vmem = pltpu.VMEM
    return pl.pallas_call(
        functools.partial(middle_kernel, rows, cols),
        grid=(2 * cols,),
        in_specs=[
            whole(heads.shape), block, block, weight, weight, bias, whole(vecs.shape),
            whole(w_out.shape), any_space,
        ],
        out_specs=[
            grad_spec, grad_spec, whole((rows, chips, head_cols, width)), block, block,
            whole((sum_rows, depth)), any_space, any_space,
        ],
        out_shape=[
            grad_shape, grad_shape,
            jax.ShapeDtypeStruct((rows, chips, head_cols, width), bf16),
            jax.ShapeDtypeStruct((count, depth), bf16),
            jax.ShapeDtypeStruct((count, depth), f32),
            jax.ShapeDtypeStruct((sum_rows, depth), f32),
            jax.ShapeDtypeStruct((cols, head_cols, count), bf16),
            jax.ShapeDtypeStruct((2, rows, chips) + w_qkv.shape, bf16),
        ],
        scratch_shapes=[
            vmem((count, depth), bf16), vmem((depth, count), bf16),
            vmem((count, depth), f32), vmem((count, depth), f32), vmem((count, depth), f32),
            vmem((cols, count, units), bf16), vmem((cols, count, units), bf16),
            vmem((count, depth), bf16), vmem((cols, head_cols, count), bf16),
            vmem((2, chips, units, depth), bf16), vmem((2, chips, units, depth), bf16),
            vmem((chips, head_cols, depth), bf16), vmem((chips, head_cols, depth), bf16),
            dma((cols,)), dma((cols,)), dma((2, chips)), dma((2, chips)), dma, dma,
            dma((chips,)), dma((chips,)), dma((chips, rows)), dma((chips, rows)), dma, dma,
            dma((2,)),
        ],
        compiler_params=pltpu.CompilerParams(
            vmem_limit_bytes=63 << 20, collective_id=1, has_side_effects=True
        ),
        cost_estimate=cost(
            12 * count * depth * cols * units, 8 * depth * cols * units + 16 * count * depth
        ),
        name="middle",
    )(heads, tokens, grad, w_up, w_down, b_up, vecs, w_out, w_qkv)


class SmallSum:
    def __init__(self, rows, chips, scratch):
        row, col = place()
        self.rows, self.chips, self.row, self.chip = rows, chips, row, col // 2
        self.held, self.core, self.by_row, self.by_line, *sems = scratch
        held = self.held
        self.stages = [
            remote(held.at[0], self.core, sems[0], sems[1], mate()),
            over_row(
                rows, lambda at: held.at[1], lambda at: self.by_row.at[at], sems[2], sems[3]
            ),
            over_line(
                chips, lambda at: held.at[2], lambda at: self.by_line.at[at], sems[4], sems[5]
            ),
        ]

    def first(self, value):
        self.held[0] = value
        self.stages[0].start()

    def second(self):
        self.stages[0].wait_recv()
        value = self.held[0] + self.core[...]
        self.held[1] = value
        self.by_row[self.row] = value
        self.stages[1].start()

    def third(self):
        self.stages[1].wait_recv()
        value = sum(self.by_row[r] for r in range(1, self.rows)) + self.by_row[0]
        self.held[2] = value
        self.by_line[self.chip] = value
        self.stages[2].start()

    def result(self):
        self.stages[2].wait_recv()
        return sum(self.by_line[c] for c in range(1, self.chips)) + self.by_line[0]

    def wait_send(self):
        for stage in self.stages:
            stage.wait_send()


def sum_scratch(rows, chips, shapes):
    dma, vmem = pltpu.SemaphoreType.DMA, pltpu.VMEM
    found = []
    for shape in shapes:
        found += [
            vmem((3,) + shape, f32), vmem(shape, f32), vmem((rows,) + shape, f32),
            vmem((chips,) + shape, f32), dma, dma, dma((rows,)), dma((rows,)), dma((chips,)),
            dma((chips,)),
        ]
    return found


SUM_REFS = 10


def add_into(into, other):
    into[...] = (into[...].astype(f32) + other[...].astype(f32)).astype(bf16)


class HalvedSum:
    REFS = 16

    @staticmethod
    def scratch(rows, chips, block):
        dma, vmem = pltpu.SemaphoreType.DMA, pltpu.VMEM
        return [
            vmem((2, chips) + block, bf16), vmem((2, chips) + block, bf16),
            vmem((chips,) + block, bf16), vmem((2,) + block, bf16), vmem(block, bf16),
            dma((2,)), dma((2,)), dma((2,)), dma, dma, dma((2,)), dma((2,)), dma, dma,
        ]

    def __init__(self, rows, chips, given, scratch):
        self.own, self.came, self.came_row, self.came_line, self.came_far, *sems = scratch
        local, send_a, recv_a, send_b, recv_b, send_c, recv_c, send_d, recv_d = sems
        row, col = place()
        plane = Plane()
        chip, lane = col // 2, lax.rem(col, 2)
        near = chip + 1 - 2 * lax.rem(chip, 2)
        self.chip, self.far = chip, lax.rem(chip + 2, 4)
        own = self.own
        self.loads = [
            pltpu.make_async_copy(given.at[at], own.at[k], local.at[k])
            for k, at in enumerate((row, plane.second))
        ]
        self.a = [
            remote(given.at[at], self.came.at[k], send_a.at[k], recv_a.at[k], (plane.first, col))
            for k, at in enumerate((plane.first, plane.across))
        ]
        self.b = [remote(own.at[1], self.came_row, send_b, recv_b, (plane.second, col))]
        self.c = [
            remote(
                own.at[0, at], self.came_line.at[k], send_c.at[k], recv_c.at[k],
                (row, near * 2 + lane),
            )
            for k, at in enumerate((near, lax.rem(near + 2, 4)))
        ]
        self.d = [
            remote(own.at[0, self.far], self.came_far, send_d, recv_d, (row, self.far * 2 + lane))
        ]

    def begin(self):
        for copy in self.a + self.loads:
            copy.start()

    def step(self, n):
        if n == 0:
            for copy in self.loads:
                copy.wait()
            for copy in self.a:
                copy.wait_recv()
            for k in (1, 0):
                for c in range(self.own.shape[1]):
                    add_into(self.own.at[k, c], self.came.at[k, c])
                if k == 1:
                    self.b[0].start()
        elif n == 1:
            self.b[0].wait_recv()
            for c in range(self.own.shape[1]):
                add_into(self.own.at[0, c], self.came_row.at[c])
            for copy in self.c:
                copy.start()
        else:
            for copy in self.c:
                copy.wait_recv()
            add_into(self.own.at[0, self.far], self.came_line.at[1])
            self.d[0].start()
            add_into(self.own.at[0, self.chip], self.came_line.at[0])

    def result(self):
        self.d[0].wait_recv()
        return self.own[0, self.chip].astype(f32) + self.came_far[...].astype(f32)

    def wait_send(self):
        for copy in self.a + self.b + self.c + self.d:
            copy.wait_send()


class DirectSum:
    @staticmethod
    def scratch(rows, chips, block):
        dma, vmem = pltpu.SemaphoreType.DMA, pltpu.VMEM
        return [
            vmem((rows, chips) + block, bf16), vmem((chips,) + block, bf16),
            vmem((chips,) + block, bf16),
            dma, dma((rows,)), dma((rows,)), dma((chips,)), dma((chips,)),
        ]

    def __init__(self, rows, chips, given, scratch):
        by_row, total, by_line, local, send_r, recv_r, send_l, recv_l = scratch
        row, col = place()
        self.rows, self.chips, self.chip = rows, chips, col // 2
        self.by_row, self.total, self.by_line = by_row, total, by_line
        self.load = pltpu.make_async_copy(given.at[row], by_row.at[row], local)
        self.r = over_row(
            rows, lambda at: given.at[at], lambda at: by_row.at[at], send_r, recv_r
        )
        self.l = over_line(
            chips, lambda at: total.at[at], lambda at: by_line.at[at], send_l, recv_l
        )

    def begin(self):
        self.load.start()
        self.r.start()

    def step(self, n):
        if n != 1:
            return
        self.load.wait()
        self.r.wait_recv()

        def one(c, carry):
            total = self.by_row[0, c].astype(f32)
            for r in range(1, self.rows):
                total = total + self.by_row[r, c].astype(f32)
            self.total[c] = total.astype(bf16)
            return carry

        lax.fori_loop(0, self.chips, one, 0)
        self.by_line[self.chip] = self.total[self.chip]
        self.l.start()

    def result(self):
        self.l.wait_recv()
        total = self.by_line[0].astype(f32)
        for c in range(1, self.chips):
            total = total + self.by_line[c].astype(f32)
        return total

    def wait_send(self):
        self.r.wait_send()
        self.l.wait_send()


def weight_sum(rows, chips):
    return HalvedSum if (rows, chips) == (4, 4) else DirectSum


def weight_scratch(rows, chips, blocks):
    return [ref for block in blocks for ref in weight_sum(rows, chips).scratch(rows, chips, block)]


def back_kernel(
    rows, cols, heads, seqs, tiles, sub,
    blk_ref, q_ref, k_ref, v_ref, do_ref, o_ref, lse_ref, x_ref, w_ref, tok_ref, dres_ref, vec_ref,
    gup_ref, gdown_ref, gout_ref, early_ref,
    dtok_ref, wup_ref, wdown_ref, wout_ref, wqkv_ref, all_ref, late_ref, bias_ref,
    d_mixed, d_arrived, key_grad, value_grad, bias_sum, qkv_acc, qkv_send, qkv_recv, norm_acc,
    bias_send, bias_recv, send_d, recv_d, send_q, recv_q, send_b, recv_b, local_d, *rest,
):
    step = pl.program_id(0)
    chips = cols // 2
    row, col = place()
    work = heads * seqs * tiles
    last = work + 2 * cols - 1
    head = jnp.minimum(step // (seqs * tiles), heads - 1)
    seq = lax.rem(step // tiles, seqs)
    turn = lax.rem(step, tiles)
    i = tiles - 1 - turn
    tile = q_ref.shape[1]
    chunks, _, chunk = do_ref.shape
    chunks_seq = SEQ_LEN // chunk
    parts = tile // sub
    start = pl.multiple_of(i * tile, tile)

    early = SmallSum(rows, chips, rest[:SUM_REFS])
    late = SmallSum(rows, chips, rest[SUM_REFS : 2 * SUM_REFS])
    rest = rest[2 * SUM_REFS :]
    each_refs = len(rest) // 3
    weights = [
        weight_sum(rows, chips)(rows, chips, given, rest[n * each_refs : (n + 1) * each_refs])
        for n, given in enumerate((gdown_ref, gup_ref, gout_ref))
    ]
    results = (wdown_ref, wup_ref, wout_ref)

    def d_stage(h):
        return over_col(
            cols, lambda at: d_mixed.at[h, at], lambda at: d_arrived.at[h, at], send_d.at[h],
            recv_d.at[h],
        )

    def own_d(h):
        return pltpu.make_async_copy(d_mixed.at[h, col], d_arrived.at[h, col], local_d.at[h])

    q_stage = over_row(
        rows, lambda at: qkv_send.at[at], lambda at: qkv_recv.at[at], send_q, recv_q
    )
    b_stage = over_row(rows, lambda at: bias_send, lambda at: bias_recv.at[at], send_b, recv_b)

    def at_step(when, act):
        @pl.when(step == when)
        def _():
            act()

    @pl.when(step == 0)
    def _():
        greet(rows, cols)
        weights[0].begin()
        early.first(early_ref[...])

    at_step(work // 8, early.second)
    at_step(
        work // 4, lambda: (weights[0].step(0), weights[1].begin(), weights[2].begin())
    )
    at_step(work * 3 // 8, early.third)
    at_step(work * 5 // 8, lambda: weights[0].step(1))
    at_step(work * 6 // 8, lambda: (weights[1].step(0), weights[2].step(0)))
    at_step(work * 7 // 8, lambda: weights[0].step(2))
    at_step(work + cols // 2, lambda: (weights[1].step(1), weights[2].step(1)))
    at_step(work + cols + cols // 2, lambda: (weights[1].step(2), weights[2].step(2)))

    @pl.when((step < work) & (turn == 0))
    def _():
        key_grad[...] = jnp.zeros_like(key_grad)
        value_grad[...] = jnp.zeros_like(value_grad)

    @pl.when((step < work) & (turn == 0) & (seq == 0))
    def _():
        bias_sum[head] = jnp.zeros((HD, 128), f32)

    def hand_over(t):
        for b in range(chunks):
            where = pl.ds(pl.multiple_of(t * tile + b * chunk, chunk), chunk)
            at = seq * chunks_seq + t * chunks + b
            d_mixed[head, at, HD : 2 * HD] = (key_grad[where, :].T * SCALE).astype(bf16)
            d_values = value_grad[where, :].T
            d_mixed[head, at, 2 * HD :] = d_values.astype(bf16)
            bias_sum[head, :, 1:2] += jnp.sum(d_values, axis=1, keepdims=True)

            @pl.when(at == col)
            def _():
                own_d(head).start()

            @pl.when(at != col)
            def _():
                d_stage(head).copy(lax.rem(at - col + cols, cols)).start()

    @pl.when(step < work)
    def _():
        d_out = jnp.concatenate([do_ref[b] for b in range(chunks)], axis=1)
        out = jnp.concatenate([o_ref[b] for b in range(chunks)], axis=1)
        delta = jnp.sum(d_out.astype(f32) * out.astype(f32), axis=0, keepdims=True)
        lse = lse_ref[0, 0]

        def cut(x, a):
            return x[:, a * sub : (a + 1) * sub]

        queries = [q_ref[0, a * sub : (a + 1) * sub, :] for a in range(parts)]
        query_blocks = [
            blk_ref[0, :, pl.ds(pl.multiple_of(start + a * sub, sub), sub)] for a in range(parts)
        ]

        def update(a, query_grad, key_start, count, masked):
            keys = k_ref[0, pl.ds(key_start, count), :]
            values = v_ref[0, pl.ds(key_start, count), :]
            scores = dot(keys, queries[a], NT) * SCALE2 - cut(lse, a)
            if masked:
                mask = tile_mask(blk_ref, key_start, count, query_blocks[a])
                scores = jnp.where(mask, scores, MASKED)
            probs = jnp.exp2(scores)
            d_values = dot(probs.astype(bf16), cut(d_out, a), NT)
            d_scores = (probs * (dot(values, cut(d_out, a)) - cut(delta, a))).astype(bf16)
            d_keys = dot(d_scores, queries[a])
            return query_grad + dot(keys, d_scores, TN), d_keys, d_values

        def add(key_start, count, d_keys, d_values):
            key_grad[pl.ds(key_start, count), :] += d_keys
            value_grad[pl.ds(key_start, count), :] += d_values

        def sweep(j, grads):
            key_start = pl.multiple_of(j * tile, tile)
            found = [update(a, grads[a], key_start, tile, False) for a in range(parts)]
            add(key_start, tile, sum(f[1] for f in found), sum(f[2] for f in found))
            return tuple(f[0] for f in found)

        grads = list(lax.fori_loop(0, i, sweep, (jnp.zeros((HD, sub), f32),) * parts))
        for a in range(parts):
            todo = [(pl.multiple_of(start + a * sub, sub), sub, True)]
            if a > 0:
                todo.append((start, a * sub, False))
            if a < parts - 1:
                todo.append((pl.multiple_of(start + (a + 1) * sub, BLOCK), BLOCK, True))
            for key_start, count, masked in todo:
                grads[a], d_keys, d_values = update(a, grads[a], key_start, count, masked)
                add(key_start, count, d_keys, d_values)

        def beyond(j, grad):
            key_start = pl.multiple_of(start + tile, BLOCK)
            grad, d_keys, d_values = update(parts - 1, grad, key_start, BLOCK, True)
            add(key_start, BLOCK, d_keys, d_values)
            return grad

        grads[-1] = lax.fori_loop(0, jnp.where(i < tiles - 1, 1, 0), beyond, grads[-1])
        query_grad = jnp.concatenate(grads, axis=1) * SCALE
        bias_sum[head, :, :1] += jnp.sum(query_grad, axis=1, keepdims=True)
        query_grad = query_grad.astype(bf16)
        for b in range(chunks):
            d_mixed[head, seq * chunks_seq + i * chunks + b, :HD] = query_grad[
                :, b * chunk : (b + 1) * chunk
            ]

    @pl.when((step < work) & (turn > 0))
    def _():
        hand_over(i + 1)

    @pl.when((step < work) & (i == 0))
    def _():
        hand_over(i)

    at = step - work

    @pl.when(at == 0)
    def _():
        qkv_acc[...] = jnp.zeros_like(qkv_acc)
        bias_send[...] = bias_sum[...]
        bias_recv[row] = bias_sum[...]
        b_stage.start()

    @pl.when((at >= 0) & (at < cols))
    def _():
        grads = jnp.concatenate([d_mixed[h, at] for h in range(heads)], axis=0)
        qkv_acc[...] += dot(grads, x_ref[0])

    @pl.when(at == cols - 1)
    def _():
        width = qkv_send.shape[2]
        for r in range(rows):
            qkv_send[r] = qkv_acc[:, r * width : (r + 1) * width].astype(bf16)
        qkv_recv[row] = qkv_send[row]
        q_stage.start()
        norm_acc[...] = jnp.zeros_like(norm_acc)
        for h in range(heads):
            own_d(h).wait()
            d_stage(h).wait_recv()

    @pl.when(at >= cols)
    def _():
        c = at - cols
        width = w_ref.shape[3]
        found = flip(
            jnp.concatenate(
                [
                    d_arrived[h, c, j * HD : (j + 1) * HD, :]
                    for j in range(3)
                    for h in range(heads)
                ],
                axis=0,
            )
        )
        for r in range(rows):
            norm_acc[:, r * width : (r + 1) * width] += dot(found, w_ref[0, r, 0], NT)

    @pl.when(step == last)
    def _():
        xhat, inv = moments(tok_ref[...].astype(f32))
        d_norm = norm_acc[...]
        late.first(
            jnp.concatenate(
                [
                    jnp.sum(d_norm * xhat, axis=0, keepdims=True),
                    jnp.sum(d_norm, axis=0, keepdims=True),
                ],
                axis=0,
            )
        )
        dtok_ref[...] = dres_ref[...] + norm_back(xhat, inv, d_norm * vec_ref[0:1])
        late.second()
        b_stage.wait_recv()
        bias_ref[...] = sum(bias_recv[r] for r in range(1, rows)) + bias_recv[0]
        all_ref[...] = early.result()
        late.third()
        q_stage.wait_recv()
        total = qkv_recv[0].astype(f32)
        for r in range(1, rows):
            total = total + qkv_recv[r].astype(f32)
        wqkv_ref[...] = total
        for weight, result in zip(weights, results):
            result[...] = weight.result()
        late_ref[...] = late.result()
        for weight in weights:
            weight.wait_send()
        for h in range(heads):
            d_stage(h).wait_send()
        q_stage.wait_send()
        b_stage.wait_send()
        early.wait_send()
        late.wait_send()


def backward(
    blocks, q, k, v, d_heads, out, lse, x, w_qkv, tokens, d_resid, vecs, grad_up, grad_down,
    grad_out, early,
):
    heads, total, _ = q.shape
    count, depth = tokens.shape
    rows, chips, units, width = grad_up.shape
    cols = 2 * chips
    head_cols = grad_out.shape[2]
    seqs = total // SEQ_LEN
    tile, sub = 1024, 512
    tiles = SEQ_LEN // tile
    work = heads * seqs * tiles
    pairs = heads * seqs * SEQ_LEN * SEQ_LEN * 5 // 8

    def unpack(s):
        s = jnp.minimum(s, work - 1)
        return s // (seqs * tiles), lax.rem(s // tiles, seqs), tiles - 1 - lax.rem(s, tiles)

    def queries_map(s):
        h, b, i = unpack(s)
        return (h, b * tiles + i, 0)

    def keys_map(s):
        h, b, _ = unpack(s)
        return (h, b, 0)

    def heads_map(s):
        h, b, i = unpack(s)
        return (b * tiles + i, h, 0)

    def lse_map(s):
        h, b, i = unpack(s)
        return (h, b, 0, i)

    def w_map(s):
        c = jnp.maximum(s - work - cols, 0)
        return (lax.rem(c, 2), 0, c // 2, 0, 0)

    keys = pl.BlockSpec((1, SEQ_LEN, HD), keys_map)
    heads_spec = pl.BlockSpec((tile // chunk_of(tokens), HD, count), heads_map)
    any_space = pl.BlockSpec(memory_space=pl.ANY)
    block = whole((count, depth))
    dma, vmem = pltpu.SemaphoreType.DMA, pltpu.VMEM
    parts = heads * 3 * HD
    shape = jax.ShapeDtypeStruct
    small = early.shape
    return pl.pallas_call(
        functools.partial(back_kernel, rows, cols, heads, seqs, tiles, sub),
        grid=(work + 2 * cols,),
        in_specs=[
            pl.BlockSpec((1, 1, SEQ_LEN), lambda s: (unpack(s)[1], 0, 0)),
            pl.BlockSpec((1, tile, HD), queries_map), keys, keys, heads_spec, heads_spec,
            pl.BlockSpec((1, 1, 1, tile), lse_map),
            pl.BlockSpec((1, count, depth), lambda s: (jnp.clip(s - work, 0, cols - 1), 0, 0)),
            pl.BlockSpec((1, rows, 1) + w_qkv.shape[3:], w_map),
            block, block, whole(vecs.shape), any_space, any_space, any_space, whole(small),
        ],
        out_specs=[
            block, whole((units, width)), whole((units, width)), whole((head_cols, width)),
            whole((parts, width)), whole(small), whole((2, depth)), whole((heads, HD, 128)),
        ],
        out_shape=[
            shape((count, depth), f32), shape((units, width), f32), shape((units, width), f32),
            shape((head_cols, width), f32), shape((parts, width), f32), shape(small, f32), shape((2, depth), f32),
            shape((heads, HD, 128), f32),
        ],
        scratch_shapes=[
            vmem((heads, cols, 3 * HD, count), bf16), vmem((heads, cols, 3 * HD, count), bf16),
            vmem((SEQ_LEN, HD), f32), vmem((SEQ_LEN, HD), f32), vmem((heads, HD, 128), f32),
            vmem((parts, depth), f32), vmem((rows, parts, width), bf16),
            vmem((rows, parts, width), bf16), vmem((count, depth), f32),
            vmem((heads, HD, 128), f32), vmem((rows, heads, HD, 128), f32),
            dma((heads, cols)), dma((heads, cols)), dma((rows,)), dma((rows,)),
            dma((rows,)), dma((rows,)), dma((heads,)),
        ] + sum_scratch(rows, chips, [small, (2, depth)]) + weight_scratch(
            rows, chips, [(units, width), (units, width), (head_cols, width)]
        ),
        compiler_params=pltpu.CompilerParams(
            vmem_limit_bytes=63 << 20, collective_id=2, has_side_effects=True
        ),
        cost_estimate=cost(40 * pairs * HD, 16 * heads * total * HD, pairs),
        name="backward",
    )(
        blocks, q, k, v, d_heads, out, lse, x, w_qkv, tokens, d_resid, vecs, grad_up, grad_down,
        grad_out, early,
    )


def chunk_of(tokens):
    return tokens.shape[0]


def body(
    tokens, blocks, w_qkv, b_qv, w_out, b_out, w_up, b_up, w_down, b_down,
    gain1, shift1, gain2, shift2, grad_out,
):
    rows, cols = lax.axis_size("row"), lax.axis_size("col")
    depth = tokens.shape[1]
    head_cols = w_qkv.shape[2]
    heads = head_cols // HD
    units = w_up.shape[0]

    def vec(v):
        return v.reshape(1, -1)

    vecs = jnp.stack([gain1, shift1, b_out, gain2, shift2, b_down] + [gain1] * 2).astype(f32)
    w_qkv_flat = w_qkv.reshape(w_qkv.shape[0], 3 * head_cols)

    (
        attn_rows, q, k, v, found, arrived, lse, block_ids, up_bias, out_weight, up_weight,
        down_weight,
    ) = front(
        tokens, vecs, vec(blocks), vec(b_up), w_qkv_flat, b_qv, w_out, w_up,
        w_down, rows, cols,
    )
    grad_up, grad_down, grad_wout, output, d_resid, sums, d_heads, qkv_all = middle(
        arrived, tokens, grad_out, up_weight, down_weight, up_bias, vecs, out_weight, w_qkv_flat,
    )
    grad_tokens, grad_wup, grad_wdown, grad_wout, grad_wqkv, small, late, bias = backward(
        block_ids, q, k, v, d_heads, found, lse, attn_rows, qkv_all, tokens, d_resid, vecs,
        grad_up, grad_down, grad_wout, sums,
    )
    grad_wqkv = (
        grad_wqkv.reshape(heads, 3, HD, depth // rows)
        .transpose(3, 1, 0, 2)
        .reshape(depth // rows, 3, head_cols)
    )
    grad_bqv = bias[:, :, :2].reshape(head_cols, 2).T
    grad_bdown, grad_gain2, grad_shift2, grad_bout = small[:4]
    grad_bup = lax.dynamic_slice_in_dim(
        small[4:].reshape(-1), lax.axis_index("col") * units, units
    )
    grad_gain1, grad_shift1 = late
    return (
        output, grad_tokens, grad_wqkv, grad_bqv, grad_wout, grad_bout, grad_wup, grad_bup,
        grad_wdown, grad_bdown, grad_gain1, grad_shift1, grad_gain2, grad_shift2,
    )


def solution(mesh):
    tokens, weight, whole_vec = P(("row", "col"), None), P("col", "row"), P()
    qkv, bias_qv = P("row", None, "col"), P(None, "col")
    return jax.shard_map(
        body,
        mesh=mesh,
        in_specs=(
            tokens, P(("row", "col")), qkv, bias_qv, weight, whole_vec, weight, P("col"), weight,
            whole_vec, whole_vec, whole_vec, whole_vec, whole_vec, tokens,
        ),
        out_specs=(
            tokens, tokens, qkv, bias_qv, weight, whole_vec, weight, P("col"), weight,
            whole_vec, whole_vec, whole_vec, whole_vec, whole_vec,
        ),
        check_vma=False,
    )
```

```python
import functools

import jax
import jax.numpy as jnp
from jax import lax
from jax.experimental import pallas as pl
from jax.experimental.pallas import tpu as pltpu
from jax.sharding import PartitionSpec as P

HD = 64
SEQ_LEN = 4096
BLOCK = 256
EPS = 1e-05
SCALE = HD ** (-0.5)
SCALE2 = SCALE * 1.4426950408889634
MASKED = -1e30
ONES = 16
MESH = pl.DeviceIdType.MESH
VMEM_LIMIT = 60 << 20

f32 = jnp.float32
bf16 = jnp.bfloat16

NN = (((1,), (0,)), ((), ()))
NT = (((1,), (1,)), ((), ()))
TN = (((0,), (0,)), ((), ()))


def dot(a, b, dims=NN):
    return lax.dot_general(a, b, dims, preferred_element_type=f32)


def flip(x):
    return x.astype(f32).T.astype(bf16)


def params(**more):
    return pltpu.CompilerParams(vmem_limit_bytes=VMEM_LIMIT, **more)


def cost(flops, nbytes, transcendentals=0):
    return pl.CostEstimate(flops=flops, bytes_accessed=nbytes, transcendentals=transcendentals)


def whole(shape):
    return pl.BlockSpec(shape, lambda *_: (0,) * len(shape))


def moments(v):
    center = jnp.mean(v, axis=-1, keepdims=True)
    centered = v - center
    spread = jnp.mean(centered * centered, axis=-1, keepdims=True)
    inv = lax.rsqrt(spread + EPS)
    return centered * inv, inv


def norm_back(xhat, inv, e):
    return inv * (
        e - jnp.mean(e, axis=-1, keepdims=True) - xhat * jnp.mean(e * xhat, axis=-1, keepdims=True)
    )


def place():
    return lax.axis_index("row"), lax.axis_index("col")


def greet(rows, cols):
    row, col = place()
    barrier = pltpu.get_barrier_semaphore()

    def to_col(k, carry):
        pl.semaphore_signal(
            barrier, inc=1, device_id=(row, lax.rem(col + k, cols)), device_id_type=MESH
        )
        return carry

    def to_row(k, carry):
        pl.semaphore_signal(
            barrier, inc=1, device_id=(lax.rem(row + k, rows), col), device_id_type=MESH
        )
        return carry

    lax.fori_loop(1, cols, to_col, 0)
    lax.fori_loop(1, rows, to_row, 0)
    pl.semaphore_wait(barrier, rows + cols - 2)


def remote(src, dst, send, recv, device):
    return pltpu.make_async_remote_copy(
        src_ref=src, dst_ref=dst, send_sem=send, recv_sem=recv, device_id=device, device_id_type=MESH
    )


def each(count, act):
    def turn(k, carry):
        act(k)
        return carry

    lax.fori_loop(1, count, turn, 0)


class Exchange:
    def __init__(self, count, here, slot, to, out, into, send, recv):
        self.count, self.here, self.slot, self.to = count, here, slot, to
        self.out, self.into, self.send, self.recv = out, into, send, recv

    def copy(self, k):
        at = self.slot(k)
        return remote(
            self.out(at), self.into(self.here), self.send.at[k], self.recv.at[self.here], self.to(k)
        )

    def arrival(self, k):
        at = self.slot(k)
        return remote(self.out(at), self.into(at), self.send.at[k], self.recv.at[at], self.to(k))

    def start(self):
        each(self.count, lambda k: self.copy(k).start())

    def wait_recv(self):
        each(self.count, lambda k: self.arrival(k).wait_recv())

    def wait_send(self):
        each(self.count, lambda k: self.copy(k).wait_send())


def over_row(rows, out, into, send, recv):
    row, col = place()
    slot = lambda k: lax.rem(row + k, rows)
    return Exchange(rows, row, slot, lambda k: (slot(k), col), out, into, send, recv)


def over_col(cols, out, into, send, recv):
    row, col = place()
    slot = lambda k: lax.rem(col + k, cols)
    return Exchange(cols, col, slot, lambda k: (row, slot(k)), out, into, send, recv)


def over_line(chips, out, into, send, recv):
    row, col = place()
    chip, lane = col // 2, lax.rem(col, 2)
    slot = lambda k: lax.rem(chip + k, chips)
    return Exchange(chips, chip, slot, lambda k: (row, slot(k) * 2 + lane), out, into, send, recv)


class Plane:
    def __init__(self):
        row, col = place()
        lane = lax.rem(col, 2)
        self.next_x = row + 1 - 2 * lax.rem(row, 2)
        self.next_y = lax.rem(row + 2, 4)
        self.across = lax.rem(self.next_x + 2, 4)
        self.first = jnp.where(lane == 0, self.next_y, self.next_x)
        self.second = jnp.where(lane == 0, self.next_x, self.next_y)


def mate():
    row, col = place()
    return (row, col // 2 * 2 + 1 - lax.rem(col, 2))


def front_kernel(
    rows, cols, heads,
    tok_ref, vec_ref, blk_ref, bup_ref, wq_ref, bias_ref, wout_ref, wup_ref, wdown_ref,
    xo_ref, q_ref, k_ref, v_ref, found_ref, arrived_ref, lse_ref, blko_ref, bupo_ref,
    wouto_ref, wupo_ref, wdowno_ref,
    xs, wqs, qs, ks, vs, vt, totals, tops, founds, blks, bups,
    send_x, recv_x, send_q, recv_q, send_s, recv_s, send_f, recv_f,
    send_wz, recv_wz, send_wr, recv_wr, send_wm, recv_wm, local_x, local_q, local_f, local_w,
):
    chips = cols // 2
    row, me = place()
    chip, lane = me // 2, lax.rem(me, 2)
    count = tok_ref.shape[0]
    tile = 2 * count
    seq_chips = SEQ_LEN // tile
    depth = wq_ref.shape[0]
    width = heads * HD

    xhat, _ = moments(tok_ref[...].astype(f32))
    xs[me] = (xhat * vec_ref[0:1] + vec_ref[1:2]).astype(bf16)
    blks[me] = blk_ref[...]
    bups[me] = bup_ref[...]
    own_rows = pl.ds(pl.multiple_of(row * depth, depth), depth)
    wqs[own_rows] = wq_ref[...]
    vt[:, HD:, :] = jnp.ones((heads, ONES, vt.shape[2]), bf16)
    greet(rows, cols)

    def chunk(owner, target, route, at):
        return remote(
            xs.at[owner], xs.at[owner], send_x.at[route, at], recv_x.at[route, at], (row, target)
        )

    def to_mate(owner, at):
        return remote(xs.at[owner], xs.at[owner], send_x.at[2, at], recv_x.at[2, at], mate())

    given = (wout_ref, wup_ref, wdown_ref)
    gathered = (wouto_ref, wupo_ref, wdowno_ref)

    q_stage = over_row(
        rows,
        lambda at: wq_ref,
        lambda at: wqs.at[pl.ds(pl.multiple_of(at * depth, depth), depth)],
        send_q,
        recv_q,
    )
    small = [
        over_col(cols, lambda at: blk_ref, lambda at: blks.at[at], send_s.at[0], recv_s.at[0]),
        over_col(cols, lambda at: bup_ref, lambda at: bups.at[at], send_s.at[1], recv_s.at[1]),
    ]
    f_stage_out = lambda at: founds.at[at]
    f_stage = over_col(cols, f_stage_out, lambda at: arrived_ref.at[at], send_f, recv_f)

    def w_line(n, at, to, route):
        block = gathered[n].at[lane, at, row]
        out = given[n] if at is chip else block
        return remote(
            out, block, send_wz.at[n, route, at], recv_wz.at[n, at], (row, to * 2 + lane)
        )

    def w_row(n, c, out):
        return over_row(
            rows, lambda at: out, lambda at: gathered[n].at[lane, c, at], send_wr.at[n, c],
            recv_wr.at[n, c],
        )

    square = rows == 4
    plane = Plane()
    next_x, next_y, across_x = plane.next_x, plane.next_y, plane.across
    relayed, relay_to = plane.first, plane.second

    def w_step(n, c, slot, k, to):
        block = gathered[n].at[lane, c, slot]
        out = given[n] if (slot is row and c is chip) else block
        return remote(out, block, send_wr.at[n, c, k], recv_wr.at[n, c, slot], (to, me))

    def rows_start(n, c):
        if square:
            w_step(n, c, row, 0, next_x).start()
            w_step(n, c, row, 1, next_y).start()
        else:
            w_row(n, c, given[n] if c is chip else gathered[n].at[lane, c, row]).start()

    def rows_relay(n, c):
        if square:
            w_step(n, c, relayed, 2, relay_to).wait_recv()
            w_step(n, c, relayed, 2, relay_to).start()

    def rows_wait_recv(n, c):
        if square:
            w_step(n, c, relay_to, 0, next_x).wait_recv()
            w_step(n, c, across_x, 0, next_x).wait_recv()
        else:
            w_row(n, c, given[n]).wait_recv()

    def rows_wait_send(n, c):
        if square:
            for k in range(3):
                w_step(n, c, row, k, next_x).wait_send()
        else:
            w_row(n, c, given[n]).wait_send()

    def w_own(n):
        return pltpu.make_async_copy(given[n], gathered[n].at[lane, chip, row], local_w.at[n])

    def w_mate(n, c, side):
        block = gathered[n].at[side, c]
        return remote(block, block, send_wm.at[n, c], recv_wm.at[n, c], mate())

    to_mate(me, chip).start()
    q_stage.start()
    for exchange in small:
        exchange.start()

    @pl.when(chip + 1 < chips)
    def _():
        for n in range(3):
            w_line(n, chip, chip + 1, 0).start()
        chunk(me, me + 2, 0, chip).start()

    @pl.when(chip > 0)
    def _():
        for n in range(3):
            w_line(n, chip, chip - 1, 1).start()
        chunk(me, me - 2, 1, chip).start()

    for n in range(3):
        w_own(n).start()
        rows_start(n, chip)
    q_stage.wait_recv()
    for exchange in small:
        exchange.wait_recv()

    def update(h, q_tile, q_low, q_count, key_start, key_count, mask):
        lanes = pl.ds(q_low, q_count)
        query = qs[h, pl.ds(pl.multiple_of(q_tile * tile + q_low, BLOCK), q_count), :]
        keys = pl.ds(pl.multiple_of(key_start, BLOCK), key_count)
        scores = dot(ks[h, keys, :], query, NT)
        if mask is not None:
            scores = jnp.where(mask, scores, MASKED)
        top = tops[h, q_tile, :, lanes]
        higher = jnp.maximum(top, jnp.max(scores, axis=0, keepdims=True) * SCALE2)
        probs = jnp.exp2(scores * SCALE2 - higher)
        part = dot(vt[h, :, keys], probs.astype(bf16))
        totals[h, q_tile, :, lanes] = totals[h, q_tile, :, lanes] * jnp.exp2(top - higher) + part
        tops[h, q_tile, :, lanes] = higher

    def column(blocks, amount):
        return jnp.broadcast_to(blocks, (128, amount)).T[:, :1]

    def diagonal(p):
        low, high = blks[2 * p], blks[2 * p + 1]
        first = column(jnp.concatenate([low, high[:, :BLOCK]], axis=1), count + BLOCK)
        second = column(jnp.concatenate([low, high], axis=1), tile)
        for h in range(heads):
            update(h, p, 0, count, p * tile, count + BLOCK, low >= first)
            update(h, p, count, count, p * tile, tile, high >= second)

    def boundary(p):
        mask = blks[2 * p + 1][:, count - BLOCK :] >= column(blks[2 * p + 2][:, :BLOCK], BLOCK)
        for h in range(heads):
            update(h, p, tile - BLOCK, BLOCK, (p + 1) * tile, BLOCK, mask)

    def project(p):
        both = jnp.concatenate([xs[2 * p], xs[2 * p + 1]], axis=0)
        mixed = dot(both, wqs[...])
        bias = bias_ref[...].astype(f32)
        where = pl.ds(pl.multiple_of(p * tile, tile), tile)
        for h in range(heads):
            at = [slice(j * width + h * HD, j * width + (h + 1) * HD) for j in range(3)]
            here = slice(h * HD, (h + 1) * HD)
            qs[h, where, :] = (mixed[:, at[0]] + bias[0:1, here]).astype(bf16)
            ks[h, where, :] = mixed[:, at[1]].astype(bf16)
            values = (mixed[:, at[2]] + bias[1:2, here]).astype(bf16)
            vs[h, where, :] = values
            vt[h, :HD, where] = flip(values)
            totals[h, p] = jnp.zeros(totals.shape[2:], f32)
            tops[h, p] = jnp.full(tops.shape[2:], MASKED, f32)

    def keep(p):
        where = pl.ds(pl.multiple_of(p * tile, tile), tile)
        pairs = [
            pltpu.make_async_copy(held.at[:, where, :], out.at[:, where, :], local_q.at[n, p])
            for n, (held, out) in enumerate(((qs, q_ref), (ks, k_ref), (vs, v_ref)))
        ]
        return pairs + [
            pltpu.make_async_copy(xs.at[2 * p + c], xo_ref.at[2 * p + c], local_x.at[2 * p + c])
            for c in range(2)
        ]

    def kept(c):
        return pltpu.make_async_copy(founds.at[c], found_ref.at[c], local_f.at[0, c])

    def own(c):
        return pltpu.make_async_copy(founds.at[c], arrived_ref.at[c], local_f.at[1, 0])

    def conclude(p):
        for h in range(heads):
            mass = totals[h, p, HD : HD + 1, :]
            out = (totals[h, p, :HD, :] / mass).astype(bf16)
            for c in range(2):
                founds[2 * p + c, h * HD : (h + 1) * HD, :] = out[:, c * count : (c + 1) * count]
            lse_ref[
                h, p // seq_chips, :, pl.ds(pl.multiple_of(lax.rem(p, seq_chips) * tile, tile), tile)
            ] = tops[h, p] + jnp.log2(mass)
        for c in range(2):
            owner = 2 * p + c
            kept(owner).start()

            @pl.when(owner == me)
            def _():
                own(owner).start()

            @pl.when(owner != me)
            def _():
                f_stage.copy(lax.rem(owner - me + cols, cols)).start()

    def pass_weights():
        for n in range(3):
            w_own(n).wait()

            def across(c, carry):
                rows_wait_recv(n, c)
                w_mate(n, c, lane).start()
                return carry

            lax.fori_loop(0, chips, across, 0)

    def event(e, carry):
        hop = (e + 1) // 2
        lower = lax.rem(e, 2) == 1
        p = jnp.where(lower, chip - hop, chip + hop)

        @pl.when(e == 1)
        def _():
            for hop in range(1, chips):
                for at, step, route in ((chip - hop, 1, 0), (chip + hop, -1, 1)):

                    @pl.when((at >= 0) & (at < chips))
                    def _():
                        onward = chip + step
                        for n in range(3):
                            w_line(n, at, onward, route).wait_recv()

                            @pl.when((onward >= 0) & (onward < chips))
                            def _():
                                w_line(n, at, onward, route).start()

                            rows_start(n, at)

        @pl.when(e == 2 * chips - 3)
        def _():
            pass_weights()

        @pl.when(lower)
        def _():
            below, above = chip - hop, chip + hop

            @pl.when(below >= 0)
            def _():
                owner = below * 2 + lane
                chunk(owner, me, 0, below).wait_recv()

                @pl.when(chip + 1 < chips)
                def _():
                    chunk(owner, me + 2, 0, below).start()

                to_mate(owner, below).start()

            @pl.when(above < chips)
            def _():
                owner = above * 2 + lane
                chunk(owner, me, 1, above).wait_recv()

                @pl.when(chip > 0)
                def _():
                    chunk(owner, me - 2, 1, above).start()

                to_mate(owner, above).start()

        @pl.when(e == 1)
        def _():
            def relay(c, carry):
                for n in range(3):
                    rows_relay(n, c)
                return carry

            lax.fori_loop(0, chips, relay, 0)

        @pl.when((p >= 0) & (p < chips))
        def _():
            to_mate(2 * p + 1 - lane, p).wait_recv()
            project(p)
            for copy in keep(p):
                copy.start()
            first = p // seq_chips * seq_chips
            final = first + seq_chips - 1
            high = jnp.minimum(chip + hop - 1, final)
            low = jnp.maximum(jnp.maximum(chip - hop, 0), first)
            diagonal(p)

            @pl.when(lower & (p < final))
            def _():
                boundary(p)

            @pl.when(lower & (p == first))
            def _():
                conclude(p)

            @pl.when(jnp.logical_not(lower) & (p > first) & (hop > 0))
            def _():
                boundary(p - 1)

                @pl.when(low == first)
                def _():
                    conclude(p - 1)

            amount = jnp.where(lower, high - p, p - low)

            def pair(j, carry):
                q_tile = jnp.where(lower, p + 1 + j, p)
                key_tile = jnp.where(lower, p, low + j)
                for h in range(heads):
                    update(h, q_tile, 0, tile, key_tile * tile, tile, None)

                @pl.when(lower & (p == first) & ((q_tile == final) | (q_tile < high)))
                def _():
                    conclude(q_tile)

                return carry

            lax.fori_loop(0, amount, pair, 0)

            @pl.when(jnp.logical_not(lower) & (p == final) & (low == first))
            def _():
                conclude(p)

        return carry

    lax.fori_loop(0, 2 * chips - 1, event, 0)

    for c in range(cols):
        bupo_ref[c] = bups[c]
        at = c * count
        blko_ref[at // SEQ_LEN, :, at % SEQ_LEN : at % SEQ_LEN + count] = blks[c]
    f_stage.wait_recv()
    for c in range(chips):
        for n in range(3):
            w_mate(n, c, 1 - lane).wait_recv()
            w_mate(n, c, lane).wait_send()
            rows_wait_send(n, c)

            @pl.when((c <= chip) & (chip + 1 < chips))
            def _():
                w_line(n, c, chip, 0).wait_send()

            @pl.when((c >= chip) & (chip > 0))
            def _():
                w_line(n, c, chip, 1).wait_send()

        for copy in keep(c):
            copy.wait()
        kept(2 * c).wait()
        kept(2 * c + 1).wait()
        to_mate(me, c).wait_send()

        @pl.when((c <= chip) & (chip + 1 < chips))
        def _():
            chunk(me, me, 0, c).wait_send()

        @pl.when((c >= chip) & (chip > 0))
        def _():
            chunk(me, me, 1, c).wait_send()

    own(me).wait()
    f_stage.wait_send()
    q_stage.wait_send()
    for exchange in small:
        exchange.wait_send()


def front(tokens, vecs, blocks, b_up, w_qkv, b_qv, w_out, w_up, w_down, rows, cols):
    count, depth = tokens.shape
    head_cols = w_qkv.shape[1] // 3
    heads = head_cols // HD
    chips = cols // 2
    total = count * cols
    tile = 2 * count
    any_space = pl.BlockSpec(memory_space=pl.ANY)
    in_vmem = pl.BlockSpec(memory_space=pltpu.VMEM)
    dma, vmem, shape = pltpu.SemaphoreType.DMA, pltpu.VMEM, jax.ShapeDtypeStruct
    pairs = heads * total * SEQ_LEN * 5 // 8
    held = (heads, total, HD)
    return pl.pallas_call(
        functools.partial(front_kernel, rows, cols, heads),
        in_specs=[in_vmem] * 9,
        out_specs=[any_space] * 6 + [in_vmem] * 3 + [any_space] * 3,
        out_shape=[
            shape((cols, count, depth), bf16), shape(held, bf16), shape(held, bf16),
            shape(held, bf16), shape((cols, head_cols, count), bf16),
            shape((cols, head_cols, count), bf16),
            shape((heads, total // SEQ_LEN, 1, SEQ_LEN), f32),
            shape((total // SEQ_LEN, 1, SEQ_LEN), jnp.int32), shape((cols,) + b_up.shape, bf16),
        ] + [shape((2, chips, rows) + w.shape, bf16) for w in (w_out, w_up, w_down)],
        scratch_shapes=[
            vmem((cols, count, depth), bf16), vmem((depth, 3 * head_cols), bf16),
            vmem(held, bf16), vmem(held, bf16), vmem(held, bf16),
            vmem((heads, HD + ONES, total), bf16),
            vmem((heads, chips, HD + ONES, tile), f32), vmem((heads, chips, 1, tile), f32),
            vmem((cols, head_cols, count), bf16), vmem((cols,) + blocks.shape, jnp.int32),
            vmem((cols,) + b_up.shape, bf16),
            dma((3, chips)), dma((3, chips)), dma((rows,)), dma((rows,)),
            dma((2, cols)), dma((2, cols)), dma((cols,)), dma((cols,)),
            dma((3, 2, chips)), dma((3, chips)), dma((3, chips, rows)), dma((3, chips, rows)),
            dma((3, chips)), dma((3, chips)),
            dma((cols,)), dma((3, chips)), dma((2, cols)), dma((3,)),
        ],
        compiler_params=pltpu.CompilerParams(
            vmem_limit_bytes=63 << 20, collective_id=0, has_side_effects=True
        ),
        cost_estimate=cost(16 * pairs * HD, 16 * heads * total * HD, pairs),
        name="front",
    )(tokens, vecs, blocks, b_up, w_qkv, b_qv, w_out, w_up, w_down)


def tile_mask(blk_ref, key_start, count, query_blocks):
    key_blocks = jnp.broadcast_to(blk_ref[0, :, pl.ds(key_start, count)], (128, count)).T[:, :1]
    return query_blocks >= key_blocks


GELU_A = 0.7978845608028654
GELU_B = 0.044715


def middle_kernel(
    rows, cols,
    heads_ref, tok_ref, g_ref, up_ref, down_ref, bup_ref, vec_ref, wout_ref, wq_ref,
    gup_ref, gdown_ref, gout_ref, output_ref, dres_ref, sums_ref, dheads_ref, wqo_ref,
    x, heads_all, resid, out_acc, norm_acc, hiddens, d_ups, low, d_send,
    mine, other, out_mine, out_other,
    send_d, recv_d, send_p, recv_p, send_o, recv_o, send_z, recv_z, send_r, recv_r, send_m, recv_m,
    local,
):
    step = pl.program_id(0)
    chips = cols // 2
    row, col = place()
    chip, lane = col // 2, lax.rem(col, 2)
    width = up_ref.shape[4]
    depth = wout_ref.shape[3]

    def part(r):
        return slice(r * width, (r + 1) * width)

    def out_weight(r):
        return jnp.concatenate([wout_ref[c % 2, c // 2, r] for c in range(cols)], axis=0)

    z_stage = over_line(
        chips, lambda at: wq_ref, lambda at: wqo_ref.at[lane, row, at], send_z, recv_z
    )

    def r_stage(c):
        return over_row(
            rows,
            lambda at: wqo_ref.at[lane, row, c],
            lambda at: wqo_ref.at[lane, at, c],
            send_r.at[c],
            recv_r.at[c],
        )

    m_stage = remote(wqo_ref.at[lane], wqo_ref.at[lane], send_m, recv_m, mate())
    m_arrival = remote(wqo_ref.at[1 - lane], wqo_ref.at[1 - lane], send_m, recv_m, mate())
    own_wq = pltpu.make_async_copy(wq_ref, wqo_ref.at[lane, row, chip], local.at[0])
    d_stage = over_col(
        cols, lambda at: d_send.at[at], lambda at: dheads_ref.at[at], send_d, recv_d
    )
    own_d = pltpu.make_async_copy(d_send.at[col], dheads_ref.at[col], local.at[1])

    def pair(at, which):
        return remote(
            mine.at[which, at], other.at[which, at], send_p.at[which, at], recv_p.at[which, at],
            mate(),
        )

    pair_out = remote(out_mine, out_other, send_o, recv_o, mate())

    @pl.when(step == 0)
    def _():
        greet(rows, cols)
        own_wq.start()
        z_stage.start()
        for s in range(cols):
            heads_all[s * depth : (s + 1) * depth] = heads_ref[s]
        stacked = flip(heads_all[...])
        for r in range(rows):
            branch = dot(stacked, out_weight(r))
            resid[:, part(r)] = tok_ref[:, part(r)].astype(f32) + branch + vec_ref[2:3, part(r)]
        xhat, _ = moments(resid[...])
        x[...] = (xhat * vec_ref[3:4] + vec_ref[4:5]).astype(bf16)
        out_acc[...] = jnp.zeros_like(out_acc)
        norm_acc[...] = jnp.zeros_like(norm_acc)

    @pl.when(step == cols // 2)
    def _():
        own_wq.wait()
        z_stage.wait_recv()
        for c in range(chips):
            r_stage(c).start()

    @pl.when(step < cols)
    def _():
        up = bup_ref[0].astype(f32)
        d_hidden = 0.0
        for r in range(rows):
            up = up + dot(x[:, part(r)], up_ref[0, 0, r], NT)
            d_hidden = d_hidden + dot(g_ref[:, part(r)], down_ref[0, 0, r], NT)
        square = up * up
        bent = jnp.tanh(GELU_A * up * (1.0 + GELU_B * square))
        half = 0.5 + 0.5 * bent
        hidden = (up * half).astype(bf16)
        slope = half + (0.5 * GELU_A) * up * (1.0 - bent * bent) * (1.0 + (3.0 * GELU_B) * square)
        d_up = d_hidden * slope
        units = d_up.shape[1]
        per = sums_ref.shape[1] // units
        lanes = pl.ds(pl.multiple_of(lax.rem(step, per) * units, units), units)
        sums_ref[pl.ds(4 + step // per, 1), lanes] = jnp.sum(d_up, axis=0, keepdims=True)
        d_up = d_up.astype(bf16)
        hiddens[step] = hidden
        d_ups[step] = d_up
        for r in range(rows):
            out_acc[:, part(r)] += dot(hidden, down_ref[0, 0, r])
            norm_acc[:, part(r)] += dot(d_up, up_ref[0, 0, r])

    @pl.when(step == cols - 1)
    def _():
        output_ref[...] = (resid[...] + out_acc[...] + vec_ref[5:6]).astype(bf16)
        xhat, inv = moments(resid[...])
        d_norm = norm_acc[...]
        grad = g_ref[...].astype(f32)
        d_resid = grad + norm_back(xhat, inv, d_norm * vec_ref[3:4])
        dres_ref[...] = d_resid
        low[...] = d_resid.astype(bf16)
        sums_ref[0:1] = jnp.sum(grad, axis=0, keepdims=True)
        sums_ref[1:2] = jnp.sum(d_norm * xhat, axis=0, keepdims=True)
        sums_ref[2:3] = jnp.sum(d_norm, axis=0, keepdims=True)
        sums_ref[3:4] = jnp.sum(d_resid, axis=0, keepdims=True)
        found = 0.0
        for r in range(rows):
            found = found + dot(out_weight(r), low[:, part(r)], NT)
        found = found.astype(bf16)
        for c in range(cols):
            d_send[c] = found[c * depth : (c + 1) * depth]
        own_d.start()
        d_stage.start()
        found = dot(heads_all[...], low[...])
        for c in range(chips):
            first = found[2 * c * depth : (2 * c + 1) * depth]
            second = found[(2 * c + 1) * depth : (2 * c + 2) * depth]
            out_mine[c] = jnp.where(lane == 0, second, first).astype(bf16)
            kept = jnp.where(lane == 0, first, second)
            for r in range(rows):
                out_acc[c * depth : (c + 1) * depth, part(r)] = kept[:, part(r)]
        pair_out.start()

    at = step - cols

    @pl.when((at >= 0) & (at < chips))
    def _():
        c = at * 2 + 1 - lane
        mine[0, at] = dot(hiddens[c], g_ref[...], TN).astype(bf16)
        pair(at, 0).start()
        mine[1, at] = dot(d_ups[c], x[...], TN).astype(bf16)
        pair(at, 1).start()

    @pl.when(step == 2 * cols - 1)
    def _():
        for c in range(chips):
            r_stage(c).wait_recv()
        m_stage.start()

    @pl.when(at >= chips)
    def _():
        k = at - chips
        c = k * 2 + lane
        grad_down = dot(hiddens[c], g_ref[...], TN)
        pair(k, 0).wait_recv()
        grad_down = (grad_down + other[0, k].astype(f32)).astype(bf16)
        grad_up = dot(d_ups[c], x[...], TN)
        pair(k, 1).wait_recv()
        grad_up = (grad_up + other[1, k].astype(f32)).astype(bf16)
        for r in range(rows):
            gdown_ref[r, 0] = grad_down[:, part(r)]
            gup_ref[r, 0] = grad_up[:, part(r)]

    @pl.when(step == 2 * cols - 1)
    def _():
        pair_out.wait_recv()
        for c in range(chips):
            for r in range(rows):
                kept = out_acc[c * depth : (c + 1) * depth, part(r)]
                gout_ref[r, c] = (kept + out_other[c, :, part(r)].astype(f32)).astype(bf16)
        d_stage.wait_recv()
        m_arrival.wait_recv()
        pair_out.wait_send()
        for k in range(chips):
            pair(k, 0).wait_send()
            pair(k, 1).wait_send()
            r_stage(k).wait_send()
        z_stage.wait_send()
        d_stage.wait_send()
        m_stage.wait_send()
        own_d.wait()


def middle(heads, tokens, grad, w_up, w_down, b_up, vecs, w_out, w_qkv):
    count, depth = tokens.shape
    _, chips, rows, units, width = w_up.shape
    cols = 2 * chips
    head_cols = w_out.shape[3]
    sum_rows = 4 + cols * units // depth
    any_space = pl.BlockSpec(memory_space=pl.ANY)

    def weight_map(s):
        c = jnp.minimum(s, cols - 1)
        return (lax.rem(c, 2), c // 2, 0, 0, 0)

    weight = pl.BlockSpec((1, 1, rows, units, width), weight_map)
    grad_spec = pl.BlockSpec(
        (rows, 1, units, width), lambda s: (0, jnp.maximum(s - cols - chips, 0), 0, 0)
    )
    grad_shape = jax.ShapeDtypeStruct((rows, chips, units, width), bf16)
    bias = pl.BlockSpec((1, 1, units), lambda s: (jnp.minimum(s, cols - 1), 0, 0))
    block = whole((count, depth))
    dma = pltpu.SemaphoreType.DMA
    vmem = pltpu.VMEM
    return pl.pallas_call(
        functools.partial(middle_kernel, rows, cols),
        grid=(2 * cols,),
        in_specs=[
            whole(heads.shape), block, block, weight, weight, bias, whole(vecs.shape),
            whole(w_out.shape), any_space,
        ],
        out_specs=[
            grad_spec, grad_spec, whole((rows, chips, head_cols, width)), block, block,
            whole((sum_rows, depth)), any_space, any_space,
        ],
        out_shape=[
            grad_shape, grad_shape,
            jax.ShapeDtypeStruct((rows, chips, head_cols, width), bf16),
            jax.ShapeDtypeStruct((count, depth), bf16),
            jax.ShapeDtypeStruct((count, depth), f32),
            jax.ShapeDtypeStruct((sum_rows, depth), f32),
            jax.ShapeDtypeStruct((cols, head_cols, count), bf16),
            jax.ShapeDtypeStruct((2, rows, chips) + w_qkv.shape, bf16),
        ],
        scratch_shapes=[
            vmem((count, depth), bf16), vmem((depth, count), bf16),
            vmem((count, depth), f32), vmem((count, depth), f32), vmem((count, depth), f32),
            vmem((cols, count, units), bf16), vmem((cols, count, units), bf16),
            vmem((count, depth), bf16), vmem((cols, head_cols, count), bf16),
            vmem((2, chips, units, depth), bf16), vmem((2, chips, units, depth), bf16),
            vmem((chips, head_cols, depth), bf16), vmem((chips, head_cols, depth), bf16),
            dma((cols,)), dma((cols,)), dma((2, chips)), dma((2, chips)), dma, dma,
            dma((chips,)), dma((chips,)), dma((chips, rows)), dma((chips, rows)), dma, dma,
            dma((2,)),
        ],
        compiler_params=pltpu.CompilerParams(
            vmem_limit_bytes=63 << 20, collective_id=1, has_side_effects=True
        ),
        cost_estimate=cost(
            12 * count * depth * cols * units, 8 * depth * cols * units + 16 * count * depth
        ),
        name="middle",
    )(heads, tokens, grad, w_up, w_down, b_up, vecs, w_out, w_qkv)


class SmallSum:
    def __init__(self, rows, chips, scratch):
        row, col = place()
        self.rows, self.chips, self.row, self.chip = rows, chips, row, col // 2
        self.held, self.core, self.by_row, self.by_line, *sems = scratch
        held = self.held
        self.stages = [
            remote(held.at[0], self.core, sems[0], sems[1], mate()),
            over_row(
                rows, lambda at: held.at[1], lambda at: self.by_row.at[at], sems[2], sems[3]
            ),
            over_line(
                chips, lambda at: held.at[2], lambda at: self.by_line.at[at], sems[4], sems[5]
            ),
        ]

    def first(self, value):
        self.held[0] = value
        self.stages[0].start()

    def second(self):
        self.stages[0].wait_recv()
        value = self.held[0] + self.core[...]
        self.held[1] = value
        self.by_row[self.row] = value
        self.stages[1].start()

    def third(self):
        self.stages[1].wait_recv()
        value = sum(self.by_row[r] for r in range(1, self.rows)) + self.by_row[0]
        self.held[2] = value
        self.by_line[self.chip] = value
        self.stages[2].start()

    def result(self):
        self.stages[2].wait_recv()
        return sum(self.by_line[c] for c in range(1, self.chips)) + self.by_line[0]

    def wait_send(self):
        for stage in self.stages:
            stage.wait_send()


def sum_scratch(rows, chips, shapes):
    dma, vmem = pltpu.SemaphoreType.DMA, pltpu.VMEM
    found = []
    for shape in shapes:
        found += [
            vmem((3,) + shape, f32), vmem(shape, f32), vmem((rows,) + shape, f32),
            vmem((chips,) + shape, f32), dma, dma, dma((rows,)), dma((rows,)), dma((chips,)),
            dma((chips,)),
        ]
    return found


SUM_REFS = 10


def add_into(into, other):
    into[...] = (into[...].astype(f32) + other[...].astype(f32)).astype(bf16)


class HalvedSum:
    REFS = 16

    @staticmethod
    def scratch(rows, chips, block):
        dma, vmem = pltpu.SemaphoreType.DMA, pltpu.VMEM
        return [
            vmem((2, chips) + block, bf16), vmem((2, chips) + block, bf16),
            vmem((chips,) + block, bf16), vmem((2,) + block, bf16), vmem(block, bf16),
            dma((2,)), dma((2,)), dma((2,)), dma, dma, dma((2,)), dma((2,)), dma, dma,
        ]

    def __init__(self, rows, chips, given, scratch):
        self.own, self.came, self.came_row, self.came_line, self.came_far, *sems = scratch
        local, send_a, recv_a, send_b, recv_b, send_c, recv_c, send_d, recv_d = sems
        row, col = place()
        plane = Plane()
        chip, lane = col // 2, lax.rem(col, 2)
        near = chip + 1 - 2 * lax.rem(chip, 2)
        self.chip, self.far = chip, lax.rem(chip + 2, 4)
        own = self.own
        self.loads = [
            pltpu.make_async_copy(given.at[at], own.at[k], local.at[k])
            for k, at in enumerate((row, plane.second))
        ]
        self.a = [
            remote(given.at[at], self.came.at[k], send_a.at[k], recv_a.at[k], (plane.first, col))
            for k, at in enumerate((plane.first, plane.across))
        ]
        self.b = [remote(own.at[1], self.came_row, send_b, recv_b, (plane.second, col))]
        self.c = [
            remote(
                own.at[0, at], self.came_line.at[k], send_c.at[k], recv_c.at[k],
                (row, near * 2 + lane),
            )
            for k, at in enumerate((near, lax.rem(near + 2, 4)))
        ]
        self.d = [
            remote(own.at[0, self.far], self.came_far, send_d, recv_d, (row, self.far * 2 + lane))
        ]

    def begin(self):
        for copy in self.a + self.loads:
            copy.start()

    def step(self, n):
        if n == 0:
            for copy in self.loads:
                copy.wait()
            for copy in self.a:
                copy.wait_recv()
            for k in (1, 0):
                for c in range(self.own.shape[1]):
                    add_into(self.own.at[k, c], self.came.at[k, c])
                if k == 1:
                    self.b[0].start()
        elif n == 1:
            self.b[0].wait_recv()
            for c in range(self.own.shape[1]):
                add_into(self.own.at[0, c], self.came_row.at[c])
            for copy in self.c:
                copy.start()
        else:
            for copy in self.c:
                copy.wait_recv()
            add_into(self.own.at[0, self.far], self.came_line.at[1])
            self.d[0].start()
            add_into(self.own.at[0, self.chip], self.came_line.at[0])

    def result(self):
        self.d[0].wait_recv()
        return self.own[0, self.chip].astype(f32) + self.came_far[...].astype(f32)

    def wait_send(self):
        for copy in self.a + self.b + self.c + self.d:
            copy.wait_send()


class DirectSum:
    @staticmethod
    def scratch(rows, chips, block):
        dma, vmem = pltpu.SemaphoreType.DMA, pltpu.VMEM
        return [
            vmem((rows, chips) + block, bf16), vmem((chips,) + block, bf16),
            vmem((chips,) + block, bf16),
            dma, dma((rows,)), dma((rows,)), dma((chips,)), dma((chips,)),
        ]

    def __init__(self, rows, chips, given, scratch):
        by_row, total, by_line, local, send_r, recv_r, send_l, recv_l = scratch
        row, col = place()
        self.rows, self.chips, self.chip = rows, chips, col // 2
        self.by_row, self.total, self.by_line = by_row, total, by_line
        self.load = pltpu.make_async_copy(given.at[row], by_row.at[row], local)
        self.r = over_row(
            rows, lambda at: given.at[at], lambda at: by_row.at[at], send_r, recv_r
        )
        self.l = over_line(
            chips, lambda at: total.at[at], lambda at: by_line.at[at], send_l, recv_l
        )

    def begin(self):
        self.load.start()
        self.r.start()

    def step(self, n):
        if n != 1:
            return
        self.load.wait()
        self.r.wait_recv()

        def one(c, carry):
            total = self.by_row[0, c].astype(f32)
            for r in range(1, self.rows):
                total = total + self.by_row[r, c].astype(f32)
            self.total[c] = total.astype(bf16)
            return carry

        lax.fori_loop(0, self.chips, one, 0)
        self.by_line[self.chip] = self.total[self.chip]
        self.l.start()

    def result(self):
        self.l.wait_recv()
        total = self.by_line[0].astype(f32)
        for c in range(1, self.chips):
            total = total + self.by_line[c].astype(f32)
        return total

    def wait_send(self):
        self.r.wait_send()
        self.l.wait_send()


def weight_sum(rows, chips):
    return HalvedSum if (rows, chips) == (4, 4) else DirectSum


def weight_scratch(rows, chips, blocks):
    return [ref for block in blocks for ref in weight_sum(rows, chips).scratch(rows, chips, block)]


def back_kernel(
    rows, cols, heads, seqs, tiles, sub,
    blk_ref, q_ref, k_ref, v_ref, do_ref, o_ref, lse_ref, x_ref, w_ref, tok_ref, dres_ref, vec_ref,
    gup_ref, gdown_ref, gout_ref, early_ref,
    dtok_ref, wup_ref, wdown_ref, wout_ref, wqkv_ref, all_ref, late_ref, bias_ref,
    d_mixed, d_arrived, key_grad, value_grad, bias_sum, qkv_acc, qkv_send, qkv_recv, norm_acc,
    bias_send, bias_recv, send_d, recv_d, send_q, recv_q, send_b, recv_b, local_d, *rest,
):
    step = pl.program_id(0)
    chips = cols // 2
    row, col = place()
    work = heads * seqs * tiles
    last = work + 2 * cols - 1
    head = jnp.minimum(step // (seqs * tiles), heads - 1)
    seq = lax.rem(step // tiles, seqs)
    turn = lax.rem(step, tiles)
    i = tiles - 1 - turn
    tile = q_ref.shape[1]
    chunks, _, chunk = do_ref.shape
    chunks_seq = SEQ_LEN // chunk
    parts = tile // sub
    start = pl.multiple_of(i * tile, tile)

    early = SmallSum(rows, chips, rest[:SUM_REFS])
    late = SmallSum(rows, chips, rest[SUM_REFS : 2 * SUM_REFS])
    rest = rest[2 * SUM_REFS :]
    each_refs = len(rest) // 3
    weights = [
        weight_sum(rows, chips)(rows, chips, given, rest[n * each_refs : (n + 1) * each_refs])
        for n, given in enumerate((gdown_ref, gup_ref, gout_ref))
    ]
    results = (wdown_ref, wup_ref, wout_ref)

    def d_stage(h):
        return over_col(
            cols, lambda at: d_mixed.at[h, at], lambda at: d_arrived.at[h, at], send_d.at[h],
            recv_d.at[h],
        )

    def own_d(h):
        return pltpu.make_async_copy(d_mixed.at[h, col], d_arrived.at[h, col], local_d.at[h])

    q_stage = over_row(
        rows, lambda at: qkv_send.at[at], lambda at: qkv_recv.at[at], send_q, recv_q
    )
    b_stage = over_row(rows, lambda at: bias_send, lambda at: bias_recv.at[at], send_b, recv_b)

    def at_step(when, act):
        @pl.when(step == when)
        def _():
            act()

    @pl.when(step == 0)
    def _():
        greet(rows, cols)
        weights[0].begin()
        weights[2].begin()
        early.first(early_ref[...])

    at_step(work // 8, early.second)
    at_step(
        work * 3 // 8,
        lambda: (early.third(), weights[0].step(0), weights[2].step(0), weights[1].begin()),
    )
    at_step(work * 6 // 8, lambda: (weights[0].step(1), weights[2].step(1)))
    at_step(work, lambda: weights[1].step(0))
    at_step(work + cols // 2, lambda: (weights[0].step(2), weights[2].step(2)))

    @pl.when((step < work) & (turn == 0))
    def _():
        key_grad[...] = jnp.zeros_like(key_grad)
        value_grad[...] = jnp.zeros_like(value_grad)

    @pl.when((step < work) & (turn == 0) & (seq == 0))
    def _():
        bias_sum[head] = jnp.zeros((HD, 128), f32)

    def hand_over(c):
        where = pl.ds(pl.multiple_of(c * chunk, chunk), chunk)
        at = seq * chunks_seq + c
        d_mixed[head, at, HD : 2 * HD] = (key_grad[where, :].T * SCALE).astype(bf16)
        d_values = value_grad[where, :].T
        d_mixed[head, at, 2 * HD :] = d_values.astype(bf16)
        bias_sum[head, :, 1:2] += jnp.sum(d_values, axis=1, keepdims=True)

        @pl.when(at == col)
        def _():
            own_d(head).start()

        @pl.when(at != col)
        def _():
            d_stage(head).copy(lax.rem(at - col + cols, cols)).start()

    @pl.when(step < work)
    def _():
        d_out = jnp.concatenate([do_ref[b] for b in range(chunks)], axis=1)
        out = jnp.concatenate([o_ref[b] for b in range(chunks)], axis=1)
        delta = jnp.sum(d_out.astype(f32) * out.astype(f32), axis=0, keepdims=True)
        lse = lse_ref[0, 0]

        def cut(x, a):
            return x[:, a * sub : (a + 1) * sub]

        queries = [q_ref[0, a * sub : (a + 1) * sub, :] for a in range(parts)]
        query_blocks = [
            blk_ref[0, :, pl.ds(pl.multiple_of(start + a * sub, sub), sub)] for a in range(parts)
        ]

        def update(a, query_grad, key_start, count, masked):
            keys = k_ref[0, pl.ds(key_start, count), :]
            values = v_ref[0, pl.ds(key_start, count), :]
            scores = dot(keys, queries[a], NT) * SCALE2 - cut(lse, a)
            if masked:
                mask = tile_mask(blk_ref, key_start, count, query_blocks[a])
                scores = jnp.where(mask, scores, MASKED)
            probs = jnp.exp2(scores)
            d_values = dot(probs.astype(bf16), cut(d_out, a), NT)
            d_scores = (probs * (dot(values, cut(d_out, a)) - cut(delta, a))).astype(bf16)
            d_keys = dot(d_scores, queries[a])
            return query_grad + dot(keys, d_scores, TN), d_keys, d_values

        def add(key_start, count, d_keys, d_values):
            key_grad[pl.ds(key_start, count), :] += d_keys
            value_grad[pl.ds(key_start, count), :] += d_values

        def sweep(j, grads):
            key_start = pl.multiple_of(j * tile, tile)
            found = [update(a, grads[a], key_start, tile, False) for a in range(parts)]
            add(key_start, tile, sum(f[1] for f in found), sum(f[2] for f in found))
            return tuple(f[0] for f in found)

        grads = list(lax.fori_loop(0, i, sweep, (jnp.zeros((HD, sub), f32),) * parts))
        for a in range(parts):
            todo = [(pl.multiple_of(start + a * sub, sub), sub, True)]
            if a > 0:
                todo.append((start, a * sub, False))
            if a < parts - 1:
                todo.append((pl.multiple_of(start + (a + 1) * sub, BLOCK), BLOCK, True))
            for key_start, count, masked in todo:
                grads[a], d_keys, d_values = update(a, grads[a], key_start, count, masked)
                add(key_start, count, d_keys, d_values)

        def beyond(j, grad):
            key_start = pl.multiple_of(start + tile, BLOCK)
            grad, d_keys, d_values = update(parts - 1, grad, key_start, BLOCK, True)
            add(key_start, BLOCK, d_keys, d_values)
            return grad

        grads[-1] = lax.fori_loop(0, jnp.where(i < tiles - 1, 1, 0), beyond, grads[-1])
        query_grad = jnp.concatenate(grads, axis=1) * SCALE
        bias_sum[head, :, :1] += jnp.sum(query_grad, axis=1, keepdims=True)
        query_grad = query_grad.astype(bf16)
        for b in range(chunks):
            d_mixed[head, seq * chunks_seq + i * chunks + b, :HD] = query_grad[
                :, b * chunk : (b + 1) * chunk
            ]

    @pl.when((step < work) & (i == 0))
    def _():
        hand_over(0)

    @pl.when(step < work)
    def _():
        for b in range(1, chunks):
            hand_over(i * chunks + b)

    @pl.when((step < work) & (turn > 0))
    def _():
        hand_over((i + 1) * chunks)

    at = step - work

    @pl.when(at == 0)
    def _():
        qkv_acc[...] = jnp.zeros_like(qkv_acc)
        bias_send[...] = bias_sum[...]
        bias_recv[row] = bias_sum[...]
        b_stage.start()

    @pl.when((at >= 0) & (at < cols))
    def _():
        grads = jnp.concatenate([d_mixed[h, at] for h in range(heads)], axis=0)
        qkv_acc[...] += dot(grads, x_ref[0])

    @pl.when(at == cols - 1)
    def _():
        width = qkv_send.shape[2]
        for r in range(rows):
            qkv_send[r] = qkv_acc[:, r * width : (r + 1) * width].astype(bf16)
        qkv_recv[row] = qkv_send[row]
        q_stage.start()
        norm_acc[...] = jnp.zeros_like(norm_acc)
        for h in range(heads):
            own_d(h).wait()
            d_stage(h).wait_recv()
        for n, stage in ((1, 1),):
            weights[n].step(stage)

    @pl.when(at >= cols)
    def _():
        c = at - cols
        width = w_ref.shape[3]
        found = flip(
            jnp.concatenate(
                [
                    d_arrived[h, c, j * HD : (j + 1) * HD, :]
                    for j in range(3)
                    for h in range(heads)
                ],
                axis=0,
            )
        )
        for r in range(rows):
            norm_acc[:, r * width : (r + 1) * width] += dot(found, w_ref[0, r, 0], NT)

    @pl.when(step == last)
    def _():
        for n, stage in ((1, 2),):
            weights[n].step(stage)
        xhat, inv = moments(tok_ref[...].astype(f32))
        d_norm = norm_acc[...]
        late.first(
            jnp.concatenate(
                [
                    jnp.sum(d_norm * xhat, axis=0, keepdims=True),
                    jnp.sum(d_norm, axis=0, keepdims=True),
                ],
                axis=0,
            )
        )
        dtok_ref[...] = dres_ref[...] + norm_back(xhat, inv, d_norm * vec_ref[0:1])
        late.second()
        b_stage.wait_recv()
        bias_ref[...] = sum(bias_recv[r] for r in range(1, rows)) + bias_recv[0]
        all_ref[...] = early.result()
        late.third()
        q_stage.wait_recv()
        total = qkv_recv[0].astype(f32)
        for r in range(1, rows):
            total = total + qkv_recv[r].astype(f32)
        wqkv_ref[...] = total
        for weight, result in zip(weights, results):
            result[...] = weight.result()
        late_ref[...] = late.result()
        for weight in weights:
            weight.wait_send()
        for h in range(heads):
            d_stage(h).wait_send()
        q_stage.wait_send()
        b_stage.wait_send()
        early.wait_send()
        late.wait_send()


def backward(
    blocks, q, k, v, d_heads, out, lse, x, w_qkv, tokens, d_resid, vecs, grad_up, grad_down,
    grad_out, early,
):
    heads, total, _ = q.shape
    count, depth = tokens.shape
    rows, chips, units, width = grad_up.shape
    cols = 2 * chips
    head_cols = grad_out.shape[2]
    seqs = total // SEQ_LEN
    tile, sub = 1024, 512
    tiles = SEQ_LEN // tile
    work = heads * seqs * tiles
    pairs = heads * seqs * SEQ_LEN * SEQ_LEN * 5 // 8

    def unpack(s):
        s = jnp.minimum(s, work - 1)
        return s // (seqs * tiles), lax.rem(s // tiles, seqs), tiles - 1 - lax.rem(s, tiles)

    def queries_map(s):
        h, b, i = unpack(s)
        return (h, b * tiles + i, 0)

    def keys_map(s):
        h, b, _ = unpack(s)
        return (h, b, 0)

    def heads_map(s):
        h, b, i = unpack(s)
        return (b * tiles + i, h, 0)

    def lse_map(s):
        h, b, i = unpack(s)
        return (h, b, 0, i)

    def w_map(s):
        c = jnp.maximum(s - work - cols, 0)
        return (lax.rem(c, 2), 0, c // 2, 0, 0)

    keys = pl.BlockSpec((1, SEQ_LEN, HD), keys_map)
    heads_spec = pl.BlockSpec((tile // chunk_of(tokens), HD, count), heads_map)
    any_space = pl.BlockSpec(memory_space=pl.ANY)
    block = whole((count, depth))
    dma, vmem = pltpu.SemaphoreType.DMA, pltpu.VMEM
    parts = heads * 3 * HD
    shape = jax.ShapeDtypeStruct
    small = early.shape
    return pl.pallas_call(
        functools.partial(back_kernel, rows, cols, heads, seqs, tiles, sub),
        grid=(work + 2 * cols,),
        in_specs=[
            pl.BlockSpec((1, 1, SEQ_LEN), lambda s: (unpack(s)[1], 0, 0)),
            pl.BlockSpec((1, tile, HD), queries_map), keys, keys, heads_spec, heads_spec,
            pl.BlockSpec((1, 1, 1, tile), lse_map),
            pl.BlockSpec((1, count, depth), lambda s: (jnp.clip(s - work, 0, cols - 1), 0, 0)),
            pl.BlockSpec((1, rows, 1) + w_qkv.shape[3:], w_map),
            block, block, whole(vecs.shape), any_space, any_space, any_space, whole(small),
        ],
        out_specs=[
            block, whole((units, width)), whole((units, width)), whole((head_cols, width)),
            whole((parts, width)), whole(small), whole((2, depth)), whole((heads, HD, 128)),
        ],
        out_shape=[
            shape((count, depth), f32), shape((units, width), f32), shape((units, width), f32),
            shape((head_cols, width), f32), shape((parts, width), f32), shape(small, f32), shape((2, depth), f32),
            shape((heads, HD, 128), f32),
        ],
        scratch_shapes=[
            vmem((heads, cols, 3 * HD, count), bf16), vmem((heads, cols, 3 * HD, count), bf16),
            vmem((SEQ_LEN, HD), f32), vmem((SEQ_LEN, HD), f32), vmem((heads, HD, 128), f32),
            vmem((parts, depth), f32), vmem((rows, parts, width), bf16),
            vmem((rows, parts, width), bf16), vmem((count, depth), f32),
            vmem((heads, HD, 128), f32), vmem((rows, heads, HD, 128), f32),
            dma((heads, cols)), dma((heads, cols)), dma((rows,)), dma((rows,)),
            dma((rows,)), dma((rows,)), dma((heads,)),
        ] + sum_scratch(rows, chips, [small, (2, depth)]) + weight_scratch(
            rows, chips, [(units, width), (units, width), (head_cols, width)]
        ),
        compiler_params=pltpu.CompilerParams(
            vmem_limit_bytes=63 << 20, collective_id=2, has_side_effects=True
        ),
        cost_estimate=cost(40 * pairs * HD, 16 * heads * total * HD, pairs),
        name="backward",
    )(
        blocks, q, k, v, d_heads, out, lse, x, w_qkv, tokens, d_resid, vecs, grad_up, grad_down,
        grad_out, early,
    )


def chunk_of(tokens):
    return tokens.shape[0]


def body(
    tokens, blocks, w_qkv, b_qv, w_out, b_out, w_up, b_up, w_down, b_down,
    gain1, shift1, gain2, shift2, grad_out,
):
    rows, cols = lax.axis_size("row"), lax.axis_size("col")
    depth = tokens.shape[1]
    head_cols = w_qkv.shape[2]
    heads = head_cols // HD
    units = w_up.shape[0]

    def vec(v):
        return v.reshape(1, -1)

    vecs = jnp.stack([gain1, shift1, b_out, gain2, shift2, b_down] + [gain1] * 2).astype(f32)
    w_qkv_flat = w_qkv.reshape(w_qkv.shape[0], 3 * head_cols)

    (
        attn_rows, q, k, v, found, arrived, lse, block_ids, up_bias, out_weight, up_weight,
        down_weight,
    ) = front(
        tokens, vecs, vec(blocks), vec(b_up), w_qkv_flat, b_qv, w_out, w_up,
        w_down, rows, cols,
    )
    grad_up, grad_down, grad_wout, output, d_resid, sums, d_heads, qkv_all = middle(
        arrived, tokens, grad_out, up_weight, down_weight, up_bias, vecs, out_weight, w_qkv_flat,
    )
    grad_tokens, grad_wup, grad_wdown, grad_wout, grad_wqkv, small, late, bias = backward(
        block_ids, q, k, v, d_heads, found, lse, attn_rows, qkv_all, tokens, d_resid, vecs,
        grad_up, grad_down, grad_wout, sums,
    )
    grad_wqkv = (
        grad_wqkv.reshape(heads, 3, HD, depth // rows)
        .transpose(3, 1, 0, 2)
        .reshape(depth // rows, 3, head_cols)
    )
    grad_bqv = bias[:, :, :2].reshape(head_cols, 2).T
    grad_bdown, grad_gain2, grad_shift2, grad_bout = small[:4]
    grad_bup = lax.dynamic_slice_in_dim(
        small[4:].reshape(-1), lax.axis_index("col") * units, units
    )
    grad_gain1, grad_shift1 = late
    return (
        output, grad_tokens, grad_wqkv, grad_bqv, grad_wout, grad_bout, grad_wup, grad_bup,
        grad_wdown, grad_bdown, grad_gain1, grad_shift1, grad_gain2, grad_shift2,
    )


def solution(mesh):
    tokens, weight, whole_vec = P(("row", "col"), None), P("col", "row"), P()
    qkv, bias_qv = P("row", None, "col"), P(None, "col")
    return jax.shard_map(
        body,
        mesh=mesh,
        in_specs=(
            tokens, P(("row", "col")), qkv, bias_qv, weight, whole_vec, weight, P("col"), weight,
            whole_vec, whole_vec, whole_vec, whole_vec, whole_vec, tokens,
        ),
        out_specs=(
            tokens, tokens, qkv, bias_qv, weight, whole_vec, weight, P("col"), weight,
            whole_vec, whole_vec, whole_vec, whole_vec, whole_vec,
        ),
        check_vma=False,
    )
```

```python
import functools

import jax
import jax.numpy as jnp
from jax import lax
from jax.experimental import pallas as pl
from jax.experimental.pallas import tpu as pltpu
from jax.sharding import PartitionSpec as P

HD = 64
SEQ_LEN = 4096
BLOCK = 256
EPS = 1e-05
SCALE = HD ** (-0.5)
SCALE2 = SCALE * 1.4426950408889634
MASKED = -1e30
ONES = 16
MESH = pl.DeviceIdType.MESH
VMEM_LIMIT = 60 << 20

f32 = jnp.float32
bf16 = jnp.bfloat16

NN = (((1,), (0,)), ((), ()))
NT = (((1,), (1,)), ((), ()))
TN = (((0,), (0,)), ((), ()))


def dot(a, b, dims=NN):
    return lax.dot_general(a, b, dims, preferred_element_type=f32)


def flip(x):
    return x.astype(f32).T.astype(bf16)


def params(**more):
    return pltpu.CompilerParams(vmem_limit_bytes=VMEM_LIMIT, **more)


def cost(flops, nbytes, transcendentals=0):
    return pl.CostEstimate(flops=flops, bytes_accessed=nbytes, transcendentals=transcendentals)


def whole(shape):
    return pl.BlockSpec(shape, lambda *_: (0,) * len(shape))


def moments(v):
    center = jnp.mean(v, axis=-1, keepdims=True)
    centered = v - center
    spread = jnp.mean(centered * centered, axis=-1, keepdims=True)
    inv = lax.rsqrt(spread + EPS)
    return centered * inv, inv


def norm_back(xhat, inv, e):
    return inv * (
        e - jnp.mean(e, axis=-1, keepdims=True) - xhat * jnp.mean(e * xhat, axis=-1, keepdims=True)
    )


def place():
    return lax.axis_index("row"), lax.axis_index("col")


def greet(rows, cols):
    row, col = place()
    barrier = pltpu.get_barrier_semaphore()

    def to_col(k, carry):
        pl.semaphore_signal(
            barrier, inc=1, device_id=(row, lax.rem(col + k, cols)), device_id_type=MESH
        )
        return carry

    def to_row(k, carry):
        pl.semaphore_signal(
            barrier, inc=1, device_id=(lax.rem(row + k, rows), col), device_id_type=MESH
        )
        return carry

    lax.fori_loop(1, cols, to_col, 0)
    lax.fori_loop(1, rows, to_row, 0)
    pl.semaphore_wait(barrier, rows + cols - 2)


def remote(src, dst, send, recv, device):
    return pltpu.make_async_remote_copy(
        src_ref=src, dst_ref=dst, send_sem=send, recv_sem=recv, device_id=device, device_id_type=MESH
    )


def each(count, act):
    def turn(k, carry):
        act(k)
        return carry

    lax.fori_loop(1, count, turn, 0)


class Exchange:
    def __init__(self, count, here, slot, to, out, into, send, recv):
        self.count, self.here, self.slot, self.to = count, here, slot, to
        self.out, self.into, self.send, self.recv = out, into, send, recv

    def copy(self, k):
        at = self.slot(k)
        return remote(
            self.out(at), self.into(self.here), self.send.at[k], self.recv.at[self.here], self.to(k)
        )

    def arrival(self, k):
        at = self.slot(k)
        return remote(self.out(at), self.into(at), self.send.at[k], self.recv.at[at], self.to(k))

    def start(self):
        each(self.count, lambda k: self.copy(k).start())

    def wait_recv(self):
        each(self.count, lambda k: self.arrival(k).wait_recv())

    def wait_send(self):
        each(self.count, lambda k: self.copy(k).wait_send())


def over_row(rows, out, into, send, recv):
    row, col = place()
    slot = lambda k: lax.rem(row + k, rows)
    return Exchange(rows, row, slot, lambda k: (slot(k), col), out, into, send, recv)


def over_col(cols, out, into, send, recv):
    row, col = place()
    slot = lambda k: lax.rem(col + k, cols)
    return Exchange(cols, col, slot, lambda k: (row, slot(k)), out, into, send, recv)


def over_line(chips, out, into, send, recv):
    row, col = place()
    chip, lane = col // 2, lax.rem(col, 2)
    slot = lambda k: lax.rem(chip + k, chips)
    return Exchange(chips, chip, slot, lambda k: (row, slot(k) * 2 + lane), out, into, send, recv)


class Plane:
    def __init__(self):
        row, col = place()
        lane = lax.rem(col, 2)
        self.next_x = row + 1 - 2 * lax.rem(row, 2)
        self.next_y = lax.rem(row + 2, 4)
        self.across = lax.rem(self.next_x + 2, 4)
        self.first = jnp.where(lane == 0, self.next_y, self.next_x)
        self.second = jnp.where(lane == 0, self.next_x, self.next_y)


def mate():
    row, col = place()
    return (row, col // 2 * 2 + 1 - lax.rem(col, 2))


def front_kernel(
    rows, cols, heads,
    tok_ref, vec_ref, blk_ref, bup_ref, wq_ref, bias_ref, wout_ref, wup_ref, wdown_ref,
    xo_ref, q_ref, k_ref, v_ref, found_ref, arrived_ref, lse_ref, blko_ref, bupo_ref,
    wouto_ref, wupo_ref, wdowno_ref,
    xs, wqs, qs, ks, vs, vt, totals, tops, founds, blks, bups,
    send_x, recv_x, send_q, recv_q, send_s, recv_s, send_f, recv_f,
    send_wz, recv_wz, send_wr, recv_wr, send_wm, recv_wm, local_x, local_q, local_f, local_w,
):
    chips = cols // 2
    row, me = place()
    chip, lane = me // 2, lax.rem(me, 2)
    count = tok_ref.shape[0]
    tile = 2 * count
    seq_chips = SEQ_LEN // tile
    depth = wq_ref.shape[0]
    width = heads * HD

    xhat, _ = moments(tok_ref[...].astype(f32))
    xs[me] = (xhat * vec_ref[0:1] + vec_ref[1:2]).astype(bf16)
    blks[me] = blk_ref[...]
    bups[me] = bup_ref[...]
    own_rows = pl.ds(pl.multiple_of(row * depth, depth), depth)
    wqs[own_rows] = wq_ref[...]
    vt[:, HD:, :] = jnp.ones((heads, ONES, vt.shape[2]), bf16)
    greet(rows, cols)

    def chunk(owner, target, route, at):
        return remote(
            xs.at[owner], xs.at[owner], send_x.at[route, at], recv_x.at[route, at], (row, target)
        )

    def to_mate(owner, at):
        return remote(xs.at[owner], xs.at[owner], send_x.at[2, at], recv_x.at[2, at], mate())

    given = (wout_ref, wup_ref, wdown_ref)
    gathered = (wouto_ref, wupo_ref, wdowno_ref)

    q_stage = over_row(
        rows,
        lambda at: wq_ref,
        lambda at: wqs.at[pl.ds(pl.multiple_of(at * depth, depth), depth)],
        send_q,
        recv_q,
    )
    small = [
        over_col(cols, lambda at: blk_ref, lambda at: blks.at[at], send_s.at[0], recv_s.at[0]),
        over_col(cols, lambda at: bup_ref, lambda at: bups.at[at], send_s.at[1], recv_s.at[1]),
    ]
    f_stage_out = lambda at: founds.at[at]
    f_stage = over_col(cols, f_stage_out, lambda at: arrived_ref.at[at], send_f, recv_f)

    def w_line(n, at, to, route):
        block = gathered[n].at[lane, at, row]
        out = given[n] if at is chip else block
        return remote(
            out, block, send_wz.at[n, route, at], recv_wz.at[n, at], (row, to * 2 + lane)
        )

    def w_row(n, c, out):
        return over_row(
            rows, lambda at: out, lambda at: gathered[n].at[lane, c, at], send_wr.at[n, c],
            recv_wr.at[n, c],
        )

    square = rows == 4
    plane = Plane()
    next_x, next_y, across_x = plane.next_x, plane.next_y, plane.across
    relayed, relay_to = plane.first, plane.second

    def w_step(n, c, slot, k, to):
        block = gathered[n].at[lane, c, slot]
        out = given[n] if (slot is row and c is chip) else block
        return remote(out, block, send_wr.at[n, c, k], recv_wr.at[n, c, slot], (to, me))

    def rows_start(n, c):
        if square:
            w_step(n, c, row, 0, next_x).start()
            w_step(n, c, row, 1, next_y).start()
        else:
            w_row(n, c, given[n] if c is chip else gathered[n].at[lane, c, row]).start()

    def rows_relay(n, c):
        if square:
            w_step(n, c, relayed, 2, relay_to).wait_recv()
            w_step(n, c, relayed, 2, relay_to).start()

    def rows_wait_recv(n, c):
        if square:
            w_step(n, c, relay_to, 0, next_x).wait_recv()
            w_step(n, c, across_x, 0, next_x).wait_recv()
        else:
            w_row(n, c, given[n]).wait_recv()

    def rows_wait_send(n, c):
        if square:
            for k in range(3):
                w_step(n, c, row, k, next_x).wait_send()
        else:
            w_row(n, c, given[n]).wait_send()

    def w_own(n):
        return pltpu.make_async_copy(given[n], gathered[n].at[lane, chip, row], local_w.at[n])

    def w_mate(n, c, side):
        block = gathered[n].at[side, c]
        return remote(block, block, send_wm.at[n, c], recv_wm.at[n, c], mate())

    to_mate(me, chip).start()
    q_stage.start()
    for exchange in small:
        exchange.start()

    @pl.when(chip + 1 < chips)
    def _():
        for n in range(3):
            w_line(n, chip, chip + 1, 0).start()
        chunk(me, me + 2, 0, chip).start()

    @pl.when(chip > 0)
    def _():
        for n in range(3):
            w_line(n, chip, chip - 1, 1).start()
        chunk(me, me - 2, 1, chip).start()

    for n in range(3):
        w_own(n).start()
        rows_start(n, chip)
    q_stage.wait_recv()
    for exchange in small:
        exchange.wait_recv()

    def update(h, q_tile, q_low, q_count, key_start, key_count, mask):
        lanes = pl.ds(q_low, q_count)
        query = qs[h, pl.ds(pl.multiple_of(q_tile * tile + q_low, BLOCK), q_count), :]
        keys = pl.ds(pl.multiple_of(key_start, BLOCK), key_count)
        scores = dot(ks[h, keys, :], query, NT)
        if mask is not None:
            scores = jnp.where(mask, scores, MASKED)
        top = tops[h, q_tile, :, lanes]
        higher = jnp.maximum(top, jnp.max(scores, axis=0, keepdims=True) * SCALE2)
        probs = jnp.exp2(scores * SCALE2 - higher)
        part = dot(vt[h, :, keys], probs.astype(bf16))
        totals[h, q_tile, :, lanes] = totals[h, q_tile, :, lanes] * jnp.exp2(top - higher) + part
        tops[h, q_tile, :, lanes] = higher

    def column(blocks, amount):
        return jnp.broadcast_to(blocks, (128, amount)).T[:, :1]

    def diagonal(p):
        low, high = blks[2 * p], blks[2 * p + 1]
        first = column(jnp.concatenate([low, high[:, :BLOCK]], axis=1), count + BLOCK)
        second = column(jnp.concatenate([low, high], axis=1), tile)
        for h in range(heads):
            update(h, p, 0, count, p * tile, count + BLOCK, low >= first)
            update(h, p, count, count, p * tile, tile, high >= second)

    def boundary(p):
        mask = blks[2 * p + 1][:, count - BLOCK :] >= column(blks[2 * p + 2][:, :BLOCK], BLOCK)
        for h in range(heads):
            update(h, p, tile - BLOCK, BLOCK, (p + 1) * tile, BLOCK, mask)

    def project(p):
        both = jnp.concatenate([xs[2 * p], xs[2 * p + 1]], axis=0)
        mixed = dot(both, wqs[...])
        bias = bias_ref[...].astype(f32)
        where = pl.ds(pl.multiple_of(p * tile, tile), tile)
        for h in range(heads):
            at = [slice(j * width + h * HD, j * width + (h + 1) * HD) for j in range(3)]
            here = slice(h * HD, (h + 1) * HD)
            qs[h, where, :] = (mixed[:, at[0]] + bias[0:1, here]).astype(bf16)
            ks[h, where, :] = mixed[:, at[1]].astype(bf16)
            values = (mixed[:, at[2]] + bias[1:2, here]).astype(bf16)
            vs[h, where, :] = values
            vt[h, :HD, where] = flip(values)
            totals[h, p] = jnp.zeros(totals.shape[2:], f32)
            tops[h, p] = jnp.full(tops.shape[2:], MASKED, f32)

    def keep(p):
        where = pl.ds(pl.multiple_of(p * tile, tile), tile)
        pairs = [
            pltpu.make_async_copy(held.at[:, where, :], out.at[:, where, :], local_q.at[n, p])
            for n, (held, out) in enumerate(((qs, q_ref), (ks, k_ref), (vs, v_ref)))
        ]
        return pairs + [
            pltpu.make_async_copy(xs.at[2 * p + c], xo_ref.at[2 * p + c], local_x.at[2 * p + c])
            for c in range(2)
        ]

    def kept(c):
        return pltpu.make_async_copy(founds.at[c], found_ref.at[c], local_f.at[0, c])

    def own(c):
        return pltpu.make_async_copy(founds.at[c], arrived_ref.at[c], local_f.at[1, 0])

    def conclude(p):
        for h in range(heads):
            mass = totals[h, p, HD : HD + 1, :]
            out = (totals[h, p, :HD, :] / mass).astype(bf16)
            for c in range(2):
                founds[2 * p + c, h * HD : (h + 1) * HD, :] = out[:, c * count : (c + 1) * count]
            lse_ref[
                h, p // seq_chips, :, pl.ds(pl.multiple_of(lax.rem(p, seq_chips) * tile, tile), tile)
            ] = tops[h, p] + jnp.log2(mass)
        for c in range(2):
            owner = 2 * p + c
            kept(owner).start()

            @pl.when(owner == me)
            def _():
                own(owner).start()

            @pl.when(owner != me)
            def _():
                f_stage.copy(lax.rem(owner - me + cols, cols)).start()

    def at_distance(hop, act):
        for at, step, route in ((chip - hop, 1, 0), (chip + hop, -1, 1)):

            @pl.when((at >= 0) & (at < chips))
            def _():
                act(at, chip + step, route)

    def w_arrive(at, onward, route):
        for n in range(3):
            w_line(n, at, onward, route).wait_recv()

            @pl.when((onward >= 0) & (onward < chips))
            def _():
                w_line(n, at, onward, route).start()

            rows_start(n, at)

    def w_relay(at, onward=None, route=None):
        for n in range(3):
            rows_relay(n, at)

    def w_pass(at, onward=None, route=None):
        for n in range(3):
            rows_wait_recv(n, at)
            w_mate(n, at, lane).start()

    def ahead(hop):
        if hop == 1:
            at_distance(1, w_arrive)
        else:
            if hop == 2:
                w_relay(chip)
            at_distance(hop - 1, w_relay)
        if hop == chips - 1:
            for n in range(3):
                w_own(n).wait()
            w_pass(chip)
            for near in range(1, chips - 2):
                at_distance(near, w_pass)

    def event(e, carry):
        hop = (e + 1) // 2
        lower = lax.rem(e, 2) == 1
        p = jnp.where(lower, chip - hop, chip + hop)

        for stage in range(1, chips):

            @pl.when(e == 2 * stage - 1)
            def _():
                ahead(stage)

        @pl.when(lower)
        def _():
            below, above = chip - hop, chip + hop

            @pl.when(below >= 0)
            def _():
                owner = below * 2 + lane
                chunk(owner, me, 0, below).wait_recv()

                @pl.when(chip + 1 < chips)
                def _():
                    chunk(owner, me + 2, 0, below).start()

                to_mate(owner, below).start()

            @pl.when(above < chips)
            def _():
                owner = above * 2 + lane
                chunk(owner, me, 1, above).wait_recv()

                @pl.when(chip > 0)
                def _():
                    chunk(owner, me - 2, 1, above).start()

                to_mate(owner, above).start()

        for stage in range(2, chips - 1):

            @pl.when(e == 2 * stage - 1)
            def _():
                at_distance(stage, w_arrive)

        @pl.when((p >= 0) & (p < chips))
        def _():
            to_mate(2 * p + 1 - lane, p).wait_recv()
            project(p)
            for copy in keep(p):
                copy.start()
            first = p // seq_chips * seq_chips
            final = first + seq_chips - 1
            high = jnp.minimum(chip + hop - 1, final)
            low = jnp.maximum(jnp.maximum(chip - hop, 0), first)
            diagonal(p)

            @pl.when(lower & (p < final))
            def _():
                boundary(p)

            @pl.when(lower & (p == first))
            def _():
                conclude(p)

            @pl.when(jnp.logical_not(lower) & (p > first) & (hop > 0))
            def _():
                boundary(p - 1)

                @pl.when(low == first)
                def _():
                    conclude(p - 1)

            amount = jnp.where(lower, high - p, p - low)

            def pair(j, carry):
                q_tile = jnp.where(lower, p + 1 + j, p)
                key_tile = jnp.where(lower, p, low + j)

                @pl.when((hop == chips - 1) & (j == amount - 2))
                def _():
                    at_distance(chips - 1, w_arrive)

                for h in range(heads):
                    update(h, q_tile, 0, tile, key_tile * tile, tile, None)

                @pl.when(lower & (p == first) & ((q_tile == final) | (q_tile < high)))
                def _():
                    conclude(q_tile)

                return carry

            lax.fori_loop(0, amount, pair, 0)

            @pl.when(jnp.logical_not(lower) & (p == final) & (low == first))
            def _():
                conclude(p)

        return carry

    lax.fori_loop(0, 2 * chips - 1, event, 0)
    at_distance(chips - 2, w_pass)
    at_distance(chips - 1, w_relay)
    at_distance(chips - 1, w_pass)

    for c in range(cols):
        bupo_ref[c] = bups[c]
        at = c * count
        blko_ref[at // SEQ_LEN, :, at % SEQ_LEN : at % SEQ_LEN + count] = blks[c]
    f_stage.wait_recv()
    for c in range(chips):
        for n in range(3):
            w_mate(n, c, 1 - lane).wait_recv()
            w_mate(n, c, lane).wait_send()
            rows_wait_send(n, c)

            @pl.when((c <= chip) & (chip + 1 < chips))
            def _():
                w_line(n, c, chip, 0).wait_send()

            @pl.when((c >= chip) & (chip > 0))
            def _():
                w_line(n, c, chip, 1).wait_send()

        for copy in keep(c):
            copy.wait()
        kept(2 * c).wait()
        kept(2 * c + 1).wait()
        to_mate(me, c).wait_send()

        @pl.when((c <= chip) & (chip + 1 < chips))
        def _():
            chunk(me, me, 0, c).wait_send()

        @pl.when((c >= chip) & (chip > 0))
        def _():
            chunk(me, me, 1, c).wait_send()

    own(me).wait()
    f_stage.wait_send()
    q_stage.wait_send()
    for exchange in small:
        exchange.wait_send()


def front(tokens, vecs, blocks, b_up, w_qkv, b_qv, w_out, w_up, w_down, rows, cols):
    count, depth = tokens.shape
    head_cols = w_qkv.shape[1] // 3
    heads = head_cols // HD
    chips = cols // 2
    total = count * cols
    tile = 2 * count
    any_space = pl.BlockSpec(memory_space=pl.ANY)
    in_vmem = pl.BlockSpec(memory_space=pltpu.VMEM)
    dma, vmem, shape = pltpu.SemaphoreType.DMA, pltpu.VMEM, jax.ShapeDtypeStruct
    pairs = heads * total * SEQ_LEN * 5 // 8
    held = (heads, total, HD)
    return pl.pallas_call(
        functools.partial(front_kernel, rows, cols, heads),
        in_specs=[in_vmem] * 9,
        out_specs=[any_space] * 6 + [in_vmem] * 3 + [any_space] * 3,
        out_shape=[
            shape((cols, count, depth), bf16), shape(held, bf16), shape(held, bf16),
            shape(held, bf16), shape((cols, head_cols, count), bf16),
            shape((cols, head_cols, count), bf16),
            shape((heads, total // SEQ_LEN, 1, SEQ_LEN), f32),
            shape((total // SEQ_LEN, 1, SEQ_LEN), jnp.int32), shape((cols,) + b_up.shape, bf16),
        ] + [shape((2, chips, rows) + w.shape, bf16) for w in (w_out, w_up, w_down)],
        scratch_shapes=[
            vmem((cols, count, depth), bf16), vmem((depth, 3 * head_cols), bf16),
            vmem(held, bf16), vmem(held, bf16), vmem(held, bf16),
            vmem((heads, HD + ONES, total), bf16),
            vmem((heads, chips, HD + ONES, tile), f32), vmem((heads, chips, 1, tile), f32),
            vmem((cols, head_cols, count), bf16), vmem((cols,) + blocks.shape, jnp.int32),
            vmem((cols,) + b_up.shape, bf16),
            dma((3, chips)), dma((3, chips)), dma((rows,)), dma((rows,)),
            dma((2, cols)), dma((2, cols)), dma((cols,)), dma((cols,)),
            dma((3, 2, chips)), dma((3, chips)), dma((3, chips, rows)), dma((3, chips, rows)),
            dma((3, chips)), dma((3, chips)),
            dma((cols,)), dma((3, chips)), dma((2, cols)), dma((3,)),
        ],
        compiler_params=pltpu.CompilerParams(
            vmem_limit_bytes=63 << 20, collective_id=0, has_side_effects=True
        ),
        cost_estimate=cost(16 * pairs * HD, 16 * heads * total * HD, pairs),
        name="front",
    )(tokens, vecs, blocks, b_up, w_qkv, b_qv, w_out, w_up, w_down)


def tile_mask(blk_ref, key_start, count, query_blocks):
    key_blocks = jnp.broadcast_to(blk_ref[0, :, pl.ds(key_start, count)], (128, count)).T[:, :1]
    return query_blocks >= key_blocks


GELU_A = 0.7978845608028654
GELU_B = 0.044715


def middle_kernel(
    rows, cols,
    heads_ref, tok_ref, g_ref, up_ref, down_ref, bup_ref, vec_ref, wout_ref, wq_ref,
    gup_ref, gdown_ref, gout_ref, output_ref, dres_ref, sums_ref, dheads_ref, wqo_ref,
    x, heads_all, resid, out_acc, norm_acc, hiddens, d_ups, low, d_send,
    mine, other, out_mine, out_other,
    send_d, recv_d, send_p, recv_p, send_o, recv_o, send_z, recv_z, send_r, recv_r, send_m, recv_m,
    local,
):
    step = pl.program_id(0)
    chips = cols // 2
    row, col = place()
    chip, lane = col // 2, lax.rem(col, 2)
    width = up_ref.shape[4]
    depth = wout_ref.shape[3]

    def part(r):
        return slice(r * width, (r + 1) * width)

    def out_weight(r):
        return jnp.concatenate([wout_ref[c % 2, c // 2, r] for c in range(cols)], axis=0)

    z_stage = over_line(
        chips, lambda at: wq_ref, lambda at: wqo_ref.at[lane, row, at], send_z, recv_z
    )

    def r_stage(c, out=None):
        return over_row(
            rows,
            lambda at: wqo_ref.at[lane, row, c] if out is None else out,
            lambda at: wqo_ref.at[lane, at, c],
            send_r.at[c],
            recv_r.at[c],
        )

    m_stage = remote(wqo_ref.at[lane], wqo_ref.at[lane], send_m, recv_m, mate())
    m_arrival = remote(wqo_ref.at[1 - lane], wqo_ref.at[1 - lane], send_m, recv_m, mate())
    own_wq = pltpu.make_async_copy(wq_ref, wqo_ref.at[lane, row, chip], local.at[0])
    d_stage = over_col(
        cols, lambda at: d_send.at[at], lambda at: dheads_ref.at[at], send_d, recv_d
    )
    own_d = pltpu.make_async_copy(d_send.at[col], dheads_ref.at[col], local.at[1])

    def pair(at, which):
        return remote(
            mine.at[which, at], other.at[which, at], send_p.at[which, at], recv_p.at[which, at],
            mate(),
        )

    pair_out = remote(out_mine, out_other, send_o, recv_o, mate())

    @pl.when(step == 0)
    def _():
        greet(rows, cols)
        own_wq.start()
        z_stage.start()
        r_stage(chip, wq_ref).start()
        for s in range(cols):
            heads_all[s * depth : (s + 1) * depth] = heads_ref[s]
        stacked = flip(heads_all[...])
        for r in range(rows):
            branch = dot(stacked, out_weight(r))
            resid[:, part(r)] = tok_ref[:, part(r)].astype(f32) + branch + vec_ref[2:3, part(r)]
        xhat, _ = moments(resid[...])
        x[...] = (xhat * vec_ref[3:4] + vec_ref[4:5]).astype(bf16)
        out_acc[...] = jnp.zeros_like(out_acc)
        norm_acc[...] = jnp.zeros_like(norm_acc)

    @pl.when(step == cols // 2)
    def _():
        own_wq.wait()
        z_stage.wait_recv()
        each(chips, lambda k: r_stage(lax.rem(chip + k, chips)).start())

    @pl.when(step < cols)
    def _():
        up = bup_ref[0].astype(f32)
        d_hidden = 0.0
        for r in range(rows):
            up = up + dot(x[:, part(r)], up_ref[0, 0, r], NT)
            d_hidden = d_hidden + dot(g_ref[:, part(r)], down_ref[0, 0, r], NT)
        square = up * up
        bent = jnp.tanh(GELU_A * up * (1.0 + GELU_B * square))
        half = 0.5 + 0.5 * bent
        hidden = (up * half).astype(bf16)
        slope = half + (0.5 * GELU_A) * up * (1.0 - bent * bent) * (1.0 + (3.0 * GELU_B) * square)
        d_up = d_hidden * slope
        units = d_up.shape[1]
        per = sums_ref.shape[1] // units
        lanes = pl.ds(pl.multiple_of(lax.rem(step, per) * units, units), units)
        sums_ref[pl.ds(4 + step // per, 1), lanes] = jnp.sum(d_up, axis=0, keepdims=True)
        d_up = d_up.astype(bf16)
        hiddens[step] = hidden
        d_ups[step] = d_up
        for r in range(rows):
            norm_acc[:, part(r)] += dot(d_up, up_ref[0, 0, r])

    @pl.when(step == cols - 1)
    def _():
        xhat, inv = moments(resid[...])
        d_norm = norm_acc[...]
        grad = g_ref[...].astype(f32)
        d_resid = grad + norm_back(xhat, inv, d_norm * vec_ref[3:4])
        dres_ref[...] = d_resid
        low[...] = d_resid.astype(bf16)
        sums_ref[0:1] = jnp.sum(grad, axis=0, keepdims=True)
        sums_ref[1:2] = jnp.sum(d_norm * xhat, axis=0, keepdims=True)
        sums_ref[2:3] = jnp.sum(d_norm, axis=0, keepdims=True)
        sums_ref[3:4] = jnp.sum(d_resid, axis=0, keepdims=True)
        found = 0.0
        for r in range(rows):
            found = found + dot(out_weight(r), low[:, part(r)], NT)
        found = found.astype(bf16)
        for c in range(cols):
            d_send[c] = found[c * depth : (c + 1) * depth]
        own_d.start()
        d_stage.start()
        found = dot(heads_all[...], low[...])
        for c in range(chips):
            first = found[2 * c * depth : (2 * c + 1) * depth]
            second = found[(2 * c + 1) * depth : (2 * c + 2) * depth]
            out_mine[c] = jnp.where(lane == 0, second, first).astype(bf16)
            kept = jnp.where(lane == 0, first, second)
            for r in range(rows):
                norm_acc[c * depth : (c + 1) * depth, part(r)] = kept[:, part(r)]
        pair_out.start()

    at = step - cols

    @pl.when(at >= 0)
    def _():
        for r in range(rows):
            out_acc[:, part(r)] += dot(hiddens[at], down_ref[0, 0, r])

    @pl.when((at >= 0) & (at < chips))
    def _():
        c = at * 2 + 1 - lane
        mine[0, at] = dot(hiddens[c], g_ref[...], TN).astype(bf16)
        pair(at, 0).start()
        mine[1, at] = dot(d_ups[c], x[...], TN).astype(bf16)
        pair(at, 1).start()

    @pl.when(step == 2 * cols - 1)
    def _():
        for c in range(chips):
            r_stage(c).wait_recv()
        m_stage.start()

    @pl.when(at >= chips)
    def _():
        k = at - chips
        c = k * 2 + lane
        grad_down = dot(hiddens[c], g_ref[...], TN)
        pair(k, 0).wait_recv()
        grad_down = (grad_down + other[0, k].astype(f32)).astype(bf16)
        grad_up = dot(d_ups[c], x[...], TN)
        pair(k, 1).wait_recv()
        grad_up = (grad_up + other[1, k].astype(f32)).astype(bf16)
        for r in range(rows):
            gdown_ref[r, 0] = grad_down[:, part(r)]
            gup_ref[r, 0] = grad_up[:, part(r)]

    @pl.when(step == 2 * cols - 1)
    def _():
        output_ref[...] = (resid[...] + out_acc[...] + vec_ref[5:6]).astype(bf16)
        pair_out.wait_recv()
        for c in range(chips):
            for r in range(rows):
                kept = norm_acc[c * depth : (c + 1) * depth, part(r)]
                gout_ref[r, c] = (kept + out_other[c, :, part(r)].astype(f32)).astype(bf16)
        d_stage.wait_recv()
        m_arrival.wait_recv()
        pair_out.wait_send()
        for k in range(chips):
            pair(k, 0).wait_send()
            pair(k, 1).wait_send()
            r_stage(k).wait_send()
        z_stage.wait_send()
        d_stage.wait_send()
        m_stage.wait_send()
        own_d.wait()


def middle(heads, tokens, grad, w_up, w_down, b_up, vecs, w_out, w_qkv):
    count, depth = tokens.shape
    _, chips, rows, units, width = w_up.shape
    cols = 2 * chips
    head_cols = w_out.shape[3]
    sum_rows = 4 + cols * units // depth
    any_space = pl.BlockSpec(memory_space=pl.ANY)

    def weight_map(s):
        c = jnp.minimum(s, cols - 1)
        return (lax.rem(c, 2), c // 2, 0, 0, 0)

    def again_map(s):
        c = lax.rem(s, cols)
        return (lax.rem(c, 2), c // 2, 0, 0, 0)

    weight = pl.BlockSpec((1, 1, rows, units, width), weight_map)
    again = pl.BlockSpec((1, 1, rows, units, width), again_map)
    grad_spec = pl.BlockSpec(
        (rows, 1, units, width), lambda s: (0, jnp.maximum(s - cols - chips, 0), 0, 0)
    )
    grad_shape = jax.ShapeDtypeStruct((rows, chips, units, width), bf16)
    bias = pl.BlockSpec((1, 1, units), lambda s: (jnp.minimum(s, cols - 1), 0, 0))
    block = whole((count, depth))
    dma = pltpu.SemaphoreType.DMA
    vmem = pltpu.VMEM
    return pl.pallas_call(
        functools.partial(middle_kernel, rows, cols),
        grid=(2 * cols,),
        in_specs=[
            whole(heads.shape), block, block, weight, again, bias, whole(vecs.shape),
            whole(w_out.shape), any_space,
        ],
        out_specs=[
            grad_spec, grad_spec, whole((rows, chips, head_cols, width)), block, block,
            whole((sum_rows, depth)), any_space, any_space,
        ],
        out_shape=[
            grad_shape, grad_shape,
            jax.ShapeDtypeStruct((rows, chips, head_cols, width), bf16),
            jax.ShapeDtypeStruct((count, depth), bf16),
            jax.ShapeDtypeStruct((count, depth), f32),
            jax.ShapeDtypeStruct((sum_rows, depth), f32),
            jax.ShapeDtypeStruct((cols, head_cols, count), bf16),
            jax.ShapeDtypeStruct((2, rows, chips) + w_qkv.shape, bf16),
        ],
        scratch_shapes=[
            vmem((count, depth), bf16), vmem((depth, count), bf16),
            vmem((count, depth), f32), vmem((count, depth), f32), vmem((count, depth), f32),
            vmem((cols, count, units), bf16), vmem((cols, count, units), bf16),
            vmem((count, depth), bf16), vmem((cols, head_cols, count), bf16),
            vmem((2, chips, units, depth), bf16), vmem((2, chips, units, depth), bf16),
            vmem((chips, head_cols, depth), bf16), vmem((chips, head_cols, depth), bf16),
            dma((cols,)), dma((cols,)), dma((2, chips)), dma((2, chips)), dma, dma,
            dma((chips,)), dma((chips,)), dma((chips, rows)), dma((chips, rows)), dma, dma,
            dma((2,)),
        ],
        compiler_params=pltpu.CompilerParams(
            vmem_limit_bytes=63 << 20, collective_id=1, has_side_effects=True
        ),
        cost_estimate=cost(
            12 * count * depth * cols * units, 8 * depth * cols * units + 16 * count * depth
        ),
        name="middle",
    )(heads, tokens, grad, w_up, w_down, b_up, vecs, w_out, w_qkv)


class SmallSum:
    def __init__(self, rows, chips, scratch):
        row, col = place()
        self.rows, self.chips, self.row, self.chip = rows, chips, row, col // 2
        self.held, self.core, self.by_row, self.by_line, *sems = scratch
        held = self.held
        self.stages = [
            remote(held.at[0], self.core, sems[0], sems[1], mate()),
            over_row(
                rows, lambda at: held.at[1], lambda at: self.by_row.at[at], sems[2], sems[3]
            ),
            over_line(
                chips, lambda at: held.at[2], lambda at: self.by_line.at[at], sems[4], sems[5]
            ),
        ]

    def first(self, value):
        self.held[0] = value
        self.stages[0].start()

    def second(self):
        self.stages[0].wait_recv()
        value = self.held[0] + self.core[...]
        self.held[1] = value
        self.by_row[self.row] = value
        self.stages[1].start()

    def third(self):
        self.stages[1].wait_recv()
        value = sum(self.by_row[r] for r in range(1, self.rows)) + self.by_row[0]
        self.held[2] = value
        self.by_line[self.chip] = value
        self.stages[2].start()

    def result(self):
        self.stages[2].wait_recv()
        return sum(self.by_line[c] for c in range(1, self.chips)) + self.by_line[0]

    def wait_send(self):
        for stage in self.stages:
            stage.wait_send()


def sum_scratch(rows, chips, shapes):
    dma, vmem = pltpu.SemaphoreType.DMA, pltpu.VMEM
    found = []
    for shape in shapes:
        found += [
            vmem((3,) + shape, f32), vmem(shape, f32), vmem((rows,) + shape, f32),
            vmem((chips,) + shape, f32), dma, dma, dma((rows,)), dma((rows,)), dma((chips,)),
            dma((chips,)),
        ]
    return found


SUM_REFS = 10


def add_into(into, other):
    into[...] = (into[...].astype(f32) + other[...].astype(f32)).astype(bf16)


class HalvedSum:
    REFS = 16

    @staticmethod
    def scratch(rows, chips, block):
        dma, vmem = pltpu.SemaphoreType.DMA, pltpu.VMEM
        return [
            vmem((2, chips) + block, bf16), vmem((2, chips) + block, bf16),
            vmem((chips,) + block, bf16), vmem((2,) + block, bf16), vmem(block, bf16),
            dma((2,)), dma((2,)), dma((2,)), dma, dma, dma((2,)), dma((2,)), dma, dma,
        ]

    def __init__(self, rows, chips, given, scratch):
        self.own, self.came, self.came_row, self.came_line, self.came_far, *sems = scratch
        local, send_a, recv_a, send_b, recv_b, send_c, recv_c, send_d, recv_d = sems
        row, col = place()
        plane = Plane()
        chip, lane = col // 2, lax.rem(col, 2)
        near = chip + 1 - 2 * lax.rem(chip, 2)
        self.chip, self.far = chip, lax.rem(chip + 2, 4)
        own = self.own
        self.loads = [
            pltpu.make_async_copy(given.at[at], own.at[k], local.at[k])
            for k, at in enumerate((row, plane.second))
        ]
        self.a = [
            remote(given.at[at], self.came.at[k], send_a.at[k], recv_a.at[k], (plane.first, col))
            for k, at in enumerate((plane.first, plane.across))
        ]
        self.b = [remote(own.at[1], self.came_row, send_b, recv_b, (plane.second, col))]
        self.c = [
            remote(
                own.at[0, at], self.came_line.at[k], send_c.at[k], recv_c.at[k],
                (row, near * 2 + lane),
            )
            for k, at in enumerate((near, lax.rem(near + 2, 4)))
        ]
        self.d = [
            remote(own.at[0, self.far], self.came_far, send_d, recv_d, (row, self.far * 2 + lane))
        ]

    def begin(self):
        for copy in self.a + self.loads:
            copy.start()

    def step(self, n):
        if n == 0:
            for copy in self.loads:
                copy.wait()
            for copy in self.a:
                copy.wait_recv()
            for k in (1, 0):
                for c in range(self.own.shape[1]):
                    add_into(self.own.at[k, c], self.came.at[k, c])
                if k == 1:
                    self.b[0].start()
        elif n == 1:
            self.b[0].wait_recv()
            for c in range(self.own.shape[1]):
                add_into(self.own.at[0, c], self.came_row.at[c])
            for copy in self.c:
                copy.start()
        else:
            for copy in self.c:
                copy.wait_recv()
            add_into(self.own.at[0, self.far], self.came_line.at[1])
            self.d[0].start()
            add_into(self.own.at[0, self.chip], self.came_line.at[0])

    def result(self):
        self.d[0].wait_recv()
        return self.own[0, self.chip].astype(f32) + self.came_far[...].astype(f32)

    def wait_send(self):
        for copy in self.a + self.b + self.c + self.d:
            copy.wait_send()


class DirectSum:
    @staticmethod
    def scratch(rows, chips, block):
        dma, vmem = pltpu.SemaphoreType.DMA, pltpu.VMEM
        return [
            vmem((rows, chips) + block, bf16), vmem((chips,) + block, bf16),
            vmem((chips,) + block, bf16),
            dma, dma((rows,)), dma((rows,)), dma((chips,)), dma((chips,)),
        ]

    def __init__(self, rows, chips, given, scratch):
        by_row, total, by_line, local, send_r, recv_r, send_l, recv_l = scratch
        row, col = place()
        self.rows, self.chips, self.chip = rows, chips, col // 2
        self.by_row, self.total, self.by_line = by_row, total, by_line
        self.load = pltpu.make_async_copy(given.at[row], by_row.at[row], local)
        self.r = over_row(
            rows, lambda at: given.at[at], lambda at: by_row.at[at], send_r, recv_r
        )
        self.l = over_line(
            chips, lambda at: total.at[at], lambda at: by_line.at[at], send_l, recv_l
        )

    def begin(self):
        self.load.start()
        self.r.start()

    def step(self, n):
        if n != 1:
            return
        self.load.wait()
        self.r.wait_recv()

        def one(c, carry):
            total = self.by_row[0, c].astype(f32)
            for r in range(1, self.rows):
                total = total + self.by_row[r, c].astype(f32)
            self.total[c] = total.astype(bf16)
            return carry

        lax.fori_loop(0, self.chips, one, 0)
        self.by_line[self.chip] = self.total[self.chip]
        self.l.start()

    def result(self):
        self.l.wait_recv()
        total = self.by_line[0].astype(f32)
        for c in range(1, self.chips):
            total = total + self.by_line[c].astype(f32)
        return total

    def wait_send(self):
        self.r.wait_send()
        self.l.wait_send()


def weight_sum(rows, chips):
    return HalvedSum if (rows, chips) == (4, 4) else DirectSum


def weight_scratch(rows, chips, blocks):
    return [ref for block in blocks for ref in weight_sum(rows, chips).scratch(rows, chips, block)]


def back_kernel(
    rows, cols, heads, seqs, tiles, sub,
    blk_ref, q_ref, k_ref, v_ref, do_ref, o_ref, lse_ref, x_ref, w_ref, tok_ref, dres_ref, vec_ref,
    gup_ref, gdown_ref, gout_ref, early_ref,
    dtok_ref, wup_ref, wdown_ref, wout_ref, wqkv_ref, all_ref, late_ref, bias_ref,
    d_mixed, d_arrived, key_grad, value_grad, bias_sum, qkv_acc, qkv_send, qkv_recv, norm_acc,
    bias_send, bias_recv, send_d, recv_d, send_q, recv_q, send_b, recv_b, local_d, *rest,
):
    step = pl.program_id(0)
    chips = cols // 2
    row, col = place()
    work = heads * seqs * tiles
    last = work + 2 * cols - 1
    head = jnp.minimum(step // (seqs * tiles), heads - 1)
    seq = lax.rem(step // tiles, seqs)
    turn = lax.rem(step, tiles)
    i = tiles - 1 - turn
    tile = q_ref.shape[1]
    chunks, _, chunk = do_ref.shape
    chunks_seq = SEQ_LEN // chunk
    parts = tile // sub
    start = pl.multiple_of(i * tile, tile)

    early = SmallSum(rows, chips, rest[:SUM_REFS])
    late = SmallSum(rows, chips, rest[SUM_REFS : 2 * SUM_REFS])
    rest = rest[2 * SUM_REFS :]
    each_refs = len(rest) // 3
    weights = [
        weight_sum(rows, chips)(rows, chips, given, rest[n * each_refs : (n + 1) * each_refs])
        for n, given in enumerate((gdown_ref, gup_ref, gout_ref))
    ]
    results = (wdown_ref, wup_ref, wout_ref)

    def d_stage(h):
        return over_col(
            cols, lambda at: d_mixed.at[h, at], lambda at: d_arrived.at[h, at], send_d.at[h],
            recv_d.at[h],
        )

    def own_d(h):
        return pltpu.make_async_copy(d_mixed.at[h, col], d_arrived.at[h, col], local_d.at[h])

    q_stage = over_row(
        rows, lambda at: qkv_send.at[at], lambda at: qkv_recv.at[at], send_q, recv_q
    )
    b_stage = over_row(rows, lambda at: bias_send, lambda at: bias_recv.at[at], send_b, recv_b)

    def at_step(when, act):
        @pl.when(step == when)
        def _():
            act()

    @pl.when(step == 0)
    def _():
        greet(rows, cols)
        weights[0].begin()
        weights[2].begin()
        early.first(early_ref[...])

    at_step(work // 8, early.second)
    at_step(
        work * 3 // 8,
        lambda: (early.third(), weights[0].step(0), weights[2].step(0), weights[1].begin()),
    )
    at_step(work * 6 // 8, lambda: (weights[0].step(1), weights[2].step(1)))
    at_step(work, lambda: weights[1].step(0))
    at_step(work + cols // 2, lambda: (weights[0].step(2), weights[2].step(2)))

    @pl.when((step < work) & (turn == 0))
    def _():
        key_grad[...] = jnp.zeros_like(key_grad)
        value_grad[...] = jnp.zeros_like(value_grad)

    @pl.when((step < work) & (turn == 0) & (seq == 0))
    def _():
        bias_sum[head] = jnp.zeros((HD, 128), f32)

    def hand_over(c):
        where = pl.ds(pl.multiple_of(c * chunk, chunk), chunk)
        at = seq * chunks_seq + c
        d_mixed[head, at, HD : 2 * HD] = (key_grad[where, :].T * SCALE).astype(bf16)
        d_values = value_grad[where, :].T
        d_mixed[head, at, 2 * HD :] = d_values.astype(bf16)
        bias_sum[head, :, 1:2] += jnp.sum(d_values, axis=1, keepdims=True)

        @pl.when(at == col)
        def _():
            own_d(head).start()

        @pl.when(at != col)
        def _():
            d_stage(head).copy(lax.rem(at - col + cols, cols)).start()

    @pl.when(step < work)
    def _():
        d_out = jnp.concatenate([do_ref[b] for b in range(chunks)], axis=1)
        out = jnp.concatenate([o_ref[b] for b in range(chunks)], axis=1)
        delta = jnp.sum(d_out.astype(f32) * out.astype(f32), axis=0, keepdims=True)
        lse = lse_ref[0, 0]

        def cut(x, a):
            return x[:, a * sub : (a + 1) * sub]

        queries = [q_ref[0, a * sub : (a + 1) * sub, :] for a in range(parts)]
        query_blocks = [
            blk_ref[0, :, pl.ds(pl.multiple_of(start + a * sub, sub), sub)] for a in range(parts)
        ]

        def update(a, query_grad, key_start, count, masked):
            keys = k_ref[0, pl.ds(key_start, count), :]
            values = v_ref[0, pl.ds(key_start, count), :]
            scores = dot(keys, queries[a], NT) * SCALE2 - cut(lse, a)
            if masked:
                mask = tile_mask(blk_ref, key_start, count, query_blocks[a])
                scores = jnp.where(mask, scores, MASKED)
            probs = jnp.exp2(scores)
            d_values = dot(probs.astype(bf16), cut(d_out, a), NT)
            d_scores = (probs * (dot(values, cut(d_out, a)) - cut(delta, a))).astype(bf16)
            d_keys = dot(d_scores, queries[a])
            return query_grad + dot(keys, d_scores, TN), d_keys, d_values

        def add(key_start, count, d_keys, d_values):
            key_grad[pl.ds(key_start, count), :] += d_keys
            value_grad[pl.ds(key_start, count), :] += d_values

        def sweep(j, grads):
            key_start = pl.multiple_of(j * tile, tile)
            found = [update(a, grads[a], key_start, tile, False) for a in range(parts)]
            add(key_start, tile, sum(f[1] for f in found), sum(f[2] for f in found))
            return tuple(f[0] for f in found)

        grads = list(lax.fori_loop(0, i, sweep, (jnp.zeros((HD, sub), f32),) * parts))
        for a in range(parts):
            todo = [(pl.multiple_of(start + a * sub, sub), sub, True)]
            if a > 0:
                todo.append((start, a * sub, False))
            if a < parts - 1:
                todo.append((pl.multiple_of(start + (a + 1) * sub, BLOCK), BLOCK, True))
            for key_start, count, masked in todo:
                grads[a], d_keys, d_values = update(a, grads[a], key_start, count, masked)
                add(key_start, count, d_keys, d_values)

        def beyond(j, grad):
            key_start = pl.multiple_of(start + tile, BLOCK)
            grad, d_keys, d_values = update(parts - 1, grad, key_start, BLOCK, True)
            add(key_start, BLOCK, d_keys, d_values)
            return grad

        grads[-1] = lax.fori_loop(0, jnp.where(i < tiles - 1, 1, 0), beyond, grads[-1])
        query_grad = jnp.concatenate(grads, axis=1) * SCALE
        bias_sum[head, :, :1] += jnp.sum(query_grad, axis=1, keepdims=True)
        query_grad = query_grad.astype(bf16)
        for b in range(chunks):
            d_mixed[head, seq * chunks_seq + i * chunks + b, :HD] = query_grad[
                :, b * chunk : (b + 1) * chunk
            ]

    @pl.when((step < work) & (i == 0))
    def _():
        hand_over(0)

    @pl.when(step < work)
    def _():
        for b in range(1, chunks):
            hand_over(i * chunks + b)

    @pl.when((step < work) & (turn > 0))
    def _():
        hand_over((i + 1) * chunks)

    at = step - work

    @pl.when(at == 0)
    def _():
        qkv_acc[...] = jnp.zeros_like(qkv_acc)
        bias_send[...] = bias_sum[...]
        bias_recv[row] = bias_sum[...]
        b_stage.start()

    @pl.when((at >= 0) & (at < cols))
    def _():
        grads = jnp.concatenate([d_mixed[h, at] for h in range(heads)], axis=0)
        qkv_acc[...] += dot(grads, x_ref[0])

    @pl.when(at == cols - 1)
    def _():
        width = qkv_send.shape[2]
        for r in range(rows):
            qkv_send[r] = qkv_acc[:, r * width : (r + 1) * width].astype(bf16)
        qkv_recv[row] = qkv_send[row]
        q_stage.start()
        norm_acc[...] = jnp.zeros_like(norm_acc)

    @pl.when(at >= cols)
    def _():
        c = at - cols
        for h in range(heads):

            @pl.when(c == col)
            def _():
                own_d(h).wait()

            @pl.when(c != col)
            def _():
                d_stage(h).arrival(lax.rem(c - col + cols, cols)).wait_recv()

    at_step(work + cols, lambda: weights[1].step(1))

    @pl.when(at >= cols)
    def _():
        c = at - cols
        width = w_ref.shape[3]
        found = flip(
            jnp.concatenate(
                [
                    d_arrived[h, c, j * HD : (j + 1) * HD, :]
                    for j in range(3)
                    for h in range(heads)
                ],
                axis=0,
            )
        )
        for r in range(rows):
            norm_acc[:, r * width : (r + 1) * width] += dot(found, w_ref[0, r, 0], NT)

    @pl.when(step == last)
    def _():
        for n, stage in ((1, 2),):
            weights[n].step(stage)
        xhat, inv = moments(tok_ref[...].astype(f32))
        d_norm = norm_acc[...]
        late.first(
            jnp.concatenate(
                [
                    jnp.sum(d_norm * xhat, axis=0, keepdims=True),
                    jnp.sum(d_norm, axis=0, keepdims=True),
                ],
                axis=0,
            )
        )
        dtok_ref[...] = dres_ref[...] + norm_back(xhat, inv, d_norm * vec_ref[0:1])
        late.second()
        b_stage.wait_recv()
        bias_ref[...] = sum(bias_recv[r] for r in range(1, rows)) + bias_recv[0]
        all_ref[...] = early.result()
        late.third()
        q_stage.wait_recv()
        total = qkv_recv[0].astype(f32)
        for r in range(1, rows):
            total = total + qkv_recv[r].astype(f32)
        wqkv_ref[...] = total
        for weight, result in zip(weights, results):
            result[...] = weight.result()
        late_ref[...] = late.result()
        for weight in weights:
            weight.wait_send()
        for h in range(heads):
            d_stage(h).wait_send()
        q_stage.wait_send()
        b_stage.wait_send()
        early.wait_send()
        late.wait_send()


def backward(
    blocks, q, k, v, d_heads, out, lse, x, w_qkv, tokens, d_resid, vecs, grad_up, grad_down,
    grad_out, early,
):
    heads, total, _ = q.shape
    count, depth = tokens.shape
    rows, chips, units, width = grad_up.shape
    cols = 2 * chips
    head_cols = grad_out.shape[2]
    seqs = total // SEQ_LEN
    tile, sub = 1024, 512
    tiles = SEQ_LEN // tile
    work = heads * seqs * tiles
    pairs = heads * seqs * SEQ_LEN * SEQ_LEN * 5 // 8

    def unpack(s):
        s = jnp.minimum(s, work - 1)
        return s // (seqs * tiles), lax.rem(s // tiles, seqs), tiles - 1 - lax.rem(s, tiles)

    def queries_map(s):
        h, b, i = unpack(s)
        return (h, b * tiles + i, 0)

    def keys_map(s):
        h, b, _ = unpack(s)
        return (h, b, 0)

    def heads_map(s):
        h, b, i = unpack(s)
        return (b * tiles + i, h, 0)

    def lse_map(s):
        h, b, i = unpack(s)
        return (h, b, 0, i)

    def w_map(s):
        c = jnp.maximum(s - work - cols, 0)
        return (lax.rem(c, 2), 0, c // 2, 0, 0)

    keys = pl.BlockSpec((1, SEQ_LEN, HD), keys_map)
    heads_spec = pl.BlockSpec((tile // chunk_of(tokens), HD, count), heads_map)
    any_space = pl.BlockSpec(memory_space=pl.ANY)
    block = whole((count, depth))
    dma, vmem = pltpu.SemaphoreType.DMA, pltpu.VMEM
    parts = heads * 3 * HD
    shape = jax.ShapeDtypeStruct
    small = early.shape
    return pl.pallas_call(
        functools.partial(back_kernel, rows, cols, heads, seqs, tiles, sub),
        grid=(work + 2 * cols,),
        in_specs=[
            pl.BlockSpec((1, 1, SEQ_LEN), lambda s: (unpack(s)[1], 0, 0)),
            pl.BlockSpec((1, tile, HD), queries_map), keys, keys, heads_spec, heads_spec,
            pl.BlockSpec((1, 1, 1, tile), lse_map),
            pl.BlockSpec((1, count, depth), lambda s: (jnp.clip(s - work, 0, cols - 1), 0, 0)),
            pl.BlockSpec((1, rows, 1) + w_qkv.shape[3:], w_map),
            block, block, whole(vecs.shape), any_space, any_space, any_space, whole(small),
        ],
        out_specs=[
            block, whole((units, width)), whole((units, width)), whole((head_cols, width)),
            whole((parts, width)), whole(small), whole((2, depth)), whole((heads, HD, 128)),
        ],
        out_shape=[
            shape((count, depth), f32), shape((units, width), f32), shape((units, width), f32),
            shape((head_cols, width), f32), shape((parts, width), f32), shape(small, f32), shape((2, depth), f32),
            shape((heads, HD, 128), f32),
        ],
        scratch_shapes=[
            vmem((heads, cols, 3 * HD, count), bf16), vmem((heads, cols, 3 * HD, count), bf16),
            vmem((SEQ_LEN, HD), f32), vmem((SEQ_LEN, HD), f32), vmem((heads, HD, 128), f32),
            vmem((parts, depth), f32), vmem((rows, parts, width), bf16),
            vmem((rows, parts, width), bf16), vmem((count, depth), f32),
            vmem((heads, HD, 128), f32), vmem((rows, heads, HD, 128), f32),
            dma((heads, cols)), dma((heads, cols)), dma((rows,)), dma((rows,)),
            dma((rows,)), dma((rows,)), dma((heads,)),
        ] + sum_scratch(rows, chips, [small, (2, depth)]) + weight_scratch(
            rows, chips, [(units, width), (units, width), (head_cols, width)]
        ),
        compiler_params=pltpu.CompilerParams(
            vmem_limit_bytes=63 << 20, collective_id=2, has_side_effects=True
        ),
        cost_estimate=cost(40 * pairs * HD, 16 * heads * total * HD, pairs),
        name="backward",
    )(
        blocks, q, k, v, d_heads, out, lse, x, w_qkv, tokens, d_resid, vecs, grad_up, grad_down,
        grad_out, early,
    )


def chunk_of(tokens):
    return tokens.shape[0]


def body(
    tokens, blocks, w_qkv, b_qv, w_out, b_out, w_up, b_up, w_down, b_down,
    gain1, shift1, gain2, shift2, grad_out,
):
    rows, cols = lax.axis_size("row"), lax.axis_size("col")
    depth = tokens.shape[1]
    head_cols = w_qkv.shape[2]
    heads = head_cols // HD
    units = w_up.shape[0]

    def vec(v):
        return v.reshape(1, -1)

    vecs = jnp.stack([gain1, shift1, b_out, gain2, shift2, b_down] + [gain1] * 2).astype(f32)
    w_qkv_flat = w_qkv.reshape(w_qkv.shape[0], 3 * head_cols)

    (
        attn_rows, q, k, v, found, arrived, lse, block_ids, up_bias, out_weight, up_weight,
        down_weight,
    ) = front(
        tokens, vecs, vec(blocks), vec(b_up), w_qkv_flat, b_qv, w_out, w_up,
        w_down, rows, cols,
    )
    grad_up, grad_down, grad_wout, output, d_resid, sums, d_heads, qkv_all = middle(
        arrived, tokens, grad_out, up_weight, down_weight, up_bias, vecs, out_weight, w_qkv_flat,
    )
    grad_tokens, grad_wup, grad_wdown, grad_wout, grad_wqkv, small, late, bias = backward(
        block_ids, q, k, v, d_heads, found, lse, attn_rows, qkv_all, tokens, d_resid, vecs,
        grad_up, grad_down, grad_wout, sums,
    )
    grad_wqkv = (
        grad_wqkv.reshape(heads, 3, HD, depth // rows)
        .transpose(3, 1, 0, 2)
        .reshape(depth // rows, 3, head_cols)
    )
    grad_bqv = bias[:, :, :2].reshape(head_cols, 2).T
    grad_bdown, grad_gain2, grad_shift2, grad_bout = small[:4]
    grad_bup = lax.dynamic_slice_in_dim(
        small[4:].reshape(-1), lax.axis_index("col") * units, units
    )
    grad_gain1, grad_shift1 = late
    return (
        output, grad_tokens, grad_wqkv, grad_bqv, grad_wout, grad_bout, grad_wup, grad_bup,
        grad_wdown, grad_bdown, grad_gain1, grad_shift1, grad_gain2, grad_shift2,
    )


def solution(mesh):
    tokens, weight, whole_vec = P(("row", "col"), None), P("col", "row"), P()
    qkv, bias_qv = P("row", None, "col"), P(None, "col")
    return jax.shard_map(
        body,
        mesh=mesh,
        in_specs=(
            tokens, P(("row", "col")), qkv, bias_qv, weight, whole_vec, weight, P("col"), weight,
            whole_vec, whole_vec, whole_vec, whole_vec, whole_vec, tokens,
        ),
        out_specs=(
            tokens, tokens, qkv, bias_qv, weight, whole_vec, weight, P("col"), weight,
            whole_vec, whole_vec, whole_vec, whole_vec, whole_vec,
        ),
        check_vma=False,
    )
```

```python
import functools

import jax
import jax.numpy as jnp
from jax import lax
from jax.experimental import pallas as pl
from jax.experimental.pallas import tpu as pltpu
from jax.sharding import PartitionSpec as P

HD = 64
SEQ_LEN = 4096
BLOCK = 256
EPS = 1e-05
SCALE = HD ** (-0.5)
SCALE2 = SCALE * 1.4426950408889634
MASKED = -1e30
ONES = 16
MESH = pl.DeviceIdType.MESH
VMEM_LIMIT = 60 << 20

f32 = jnp.float32
bf16 = jnp.bfloat16

NN = (((1,), (0,)), ((), ()))
NT = (((1,), (1,)), ((), ()))
TN = (((0,), (0,)), ((), ()))


def dot(a, b, dims=NN):
    return lax.dot_general(a, b, dims, preferred_element_type=f32)


def flip(x):
    return x.astype(f32).T.astype(bf16)


def params(**more):
    return pltpu.CompilerParams(vmem_limit_bytes=VMEM_LIMIT, **more)


def cost(flops, nbytes, transcendentals=0):
    return pl.CostEstimate(flops=flops, bytes_accessed=nbytes, transcendentals=transcendentals)


def whole(shape):
    return pl.BlockSpec(shape, lambda *_: (0,) * len(shape))


def moments(v):
    center = jnp.mean(v, axis=-1, keepdims=True)
    centered = v - center
    spread = jnp.mean(centered * centered, axis=-1, keepdims=True)
    inv = lax.rsqrt(spread + EPS)
    return centered * inv, inv


def norm_back(xhat, inv, e):
    return inv * (
        e - jnp.mean(e, axis=-1, keepdims=True) - xhat * jnp.mean(e * xhat, axis=-1, keepdims=True)
    )


def line(ref):
    return ref[...].astype(f32).reshape(1, -1)


def place():
    return lax.axis_index("row"), lax.axis_index("col")


def greet(rows, cols):
    row, col = place()
    barrier = pltpu.get_barrier_semaphore()

    def to_col(k, carry):
        pl.semaphore_signal(
            barrier, inc=1, device_id=(row, lax.rem(col + k, cols)), device_id_type=MESH
        )
        return carry

    def to_row(k, carry):
        pl.semaphore_signal(
            barrier, inc=1, device_id=(lax.rem(row + k, rows), col), device_id_type=MESH
        )
        return carry

    lax.fori_loop(1, cols, to_col, 0)
    lax.fori_loop(1, rows, to_row, 0)
    pl.semaphore_wait(barrier, rows + cols - 2)


def remote(src, dst, send, recv, device):
    return pltpu.make_async_remote_copy(
        src_ref=src, dst_ref=dst, send_sem=send, recv_sem=recv, device_id=device, device_id_type=MESH
    )


def each(count, act):
    def turn(k, carry):
        act(k)
        return carry

    lax.fori_loop(1, count, turn, 0)


class Exchange:
    def __init__(self, count, here, slot, to, out, into, send, recv):
        self.count, self.here, self.slot, self.to = count, here, slot, to
        self.out, self.into, self.send, self.recv = out, into, send, recv

    def copy(self, k):
        at = self.slot(k)
        return remote(
            self.out(at), self.into(self.here), self.send.at[k], self.recv.at[self.here], self.to(k)
        )

    def arrival(self, k):
        at = self.slot(k)
        return remote(self.out(at), self.into(at), self.send.at[k], self.recv.at[at], self.to(k))

    def start(self):
        each(self.count, lambda k: self.copy(k).start())

    def wait_recv(self):
        each(self.count, lambda k: self.arrival(k).wait_recv())

    def wait_send(self):
        each(self.count, lambda k: self.copy(k).wait_send())


def over_row(rows, out, into, send, recv):
    row, col = place()
    slot = lambda k: lax.rem(row + k, rows)
    return Exchange(rows, row, slot, lambda k: (slot(k), col), out, into, send, recv)


def over_col(cols, out, into, send, recv):
    row, col = place()
    slot = lambda k: lax.rem(col + k, cols)
    return Exchange(cols, col, slot, lambda k: (row, slot(k)), out, into, send, recv)


def over_line(chips, out, into, send, recv):
    row, col = place()
    chip, lane = col // 2, lax.rem(col, 2)
    slot = lambda k: lax.rem(chip + k, chips)
    return Exchange(chips, chip, slot, lambda k: (row, slot(k) * 2 + lane), out, into, send, recv)


class Plane:
    def __init__(self):
        row, col = place()
        lane = lax.rem(col, 2)
        self.next_x = row + 1 - 2 * lax.rem(row, 2)
        self.next_y = lax.rem(row + 2, 4)
        self.across = lax.rem(self.next_x + 2, 4)
        self.first = jnp.where(lane == 0, self.next_y, self.next_x)
        self.second = jnp.where(lane == 0, self.next_x, self.next_y)


def mate():
    row, col = place()
    return (row, col // 2 * 2 + 1 - lax.rem(col, 2))


def front_kernel(
    rows, cols, heads,
    tok_ref, gain_ref, shift_ref, bup_ref, blk_ref, wq_ref, bias_ref, wout_ref, wup_ref, wdown_ref,
    xo_ref, q_ref, k_ref, v_ref, found_ref, arrived_ref, lse_ref, blko_ref, bupo_ref,
    wouto_ref, wupo_ref, wdowno_ref,
    xs, wqs, qs, ks, vs, vt, totals, tops, founds, blks, bups,
    send_x, recv_x, send_q, recv_q, send_s, recv_s, send_f, recv_f,
    send_wz, recv_wz, send_wr, recv_wr, send_wm, recv_wm, local_x, local_q, local_f, local_w,
):
    chips = cols // 2
    row, me = place()
    chip, lane = me // 2, lax.rem(me, 2)
    count = tok_ref.shape[0]
    tile = 2 * count
    seq_chips = SEQ_LEN // tile
    depth = wq_ref.shape[1]
    width = heads * HD

    xhat, _ = moments(tok_ref[...].astype(f32))
    xs[me] = (xhat * line(gain_ref) + line(shift_ref)).astype(bf16)
    blks[me] = blk_ref[...]
    bups[me] = line(bup_ref).astype(bf16)
    own_rows = pl.ds(pl.multiple_of(row * depth, depth), depth)
    wqs[:, own_rows] = wq_ref[...]
    vt[:, HD:, :] = jnp.ones((heads, ONES, vt.shape[2]), bf16)
    greet(rows, cols)

    def chunk(owner, target, route, at):
        return remote(
            xs.at[owner], xs.at[owner], send_x.at[route, at], recv_x.at[route, at], (row, target)
        )

    def to_mate(owner, at):
        return remote(xs.at[owner], xs.at[owner], send_x.at[2, at], recv_x.at[2, at], mate())

    given = (wout_ref, wup_ref, wdown_ref)
    gathered = (wouto_ref, wupo_ref, wdowno_ref)

    q_stage = over_row(
        rows,
        lambda at: wq_ref,
        lambda at: wqs.at[:, pl.ds(pl.multiple_of(at * depth, depth), depth)],
        send_q,
        recv_q,
    )
    small = [
        over_col(cols, lambda at: blk_ref, lambda at: blks.at[at], send_s.at[0], recv_s.at[0]),
        over_col(
            cols, lambda at: bups.at[me], lambda at: bups.at[at], send_s.at[1], recv_s.at[1]
        ),
    ]
    f_stage_out = lambda at: founds.at[at]
    f_stage = over_col(cols, f_stage_out, lambda at: arrived_ref.at[at], send_f, recv_f)

    def w_line(n, at, to, route):
        block = gathered[n].at[lane, at, row]
        out = given[n] if at is chip else block
        return remote(
            out, block, send_wz.at[n, route, at], recv_wz.at[n, at], (row, to * 2 + lane)
        )

    def w_row(n, c, out):
        return over_row(
            rows, lambda at: out, lambda at: gathered[n].at[lane, c, at], send_wr.at[n, c],
            recv_wr.at[n, c],
        )

    square = rows == 4
    plane = Plane()
    next_x, next_y, across_x = plane.next_x, plane.next_y, plane.across
    relayed, relay_to = plane.first, plane.second

    def w_step(n, c, slot, k, to):
        block = gathered[n].at[lane, c, slot]
        out = given[n] if (slot is row and c is chip) else block
        return remote(out, block, send_wr.at[n, c, k], recv_wr.at[n, c, slot], (to, me))

    def rows_start(n, c):
        if square:
            w_step(n, c, row, 0, next_x).start()
            w_step(n, c, row, 1, next_y).start()
        else:
            w_row(n, c, given[n] if c is chip else gathered[n].at[lane, c, row]).start()

    def rows_relay(n, c):
        if square:
            w_step(n, c, relayed, 2, relay_to).wait_recv()
            w_step(n, c, relayed, 2, relay_to).start()

    def rows_wait_recv(n, c):
        if square:
            w_step(n, c, relay_to, 0, next_x).wait_recv()
            w_step(n, c, across_x, 0, next_x).wait_recv()
        else:
            w_row(n, c, given[n]).wait_recv()

    def rows_wait_send(n, c):
        if square:
            for k in range(3):
                w_step(n, c, row, k, next_x).wait_send()
        else:
            w_row(n, c, given[n]).wait_send()

    def w_own(n):
        return pltpu.make_async_copy(given[n], gathered[n].at[lane, chip, row], local_w.at[n])

    def w_mate(n, c, side):
        block = gathered[n].at[side, c]
        return remote(block, block, send_wm.at[n, c], recv_wm.at[n, c], mate())

    to_mate(me, chip).start()
    q_stage.start()
    for exchange in small:
        exchange.start()

    @pl.when(chip + 1 < chips)
    def _():
        for n in range(3):
            w_line(n, chip, chip + 1, 0).start()
        chunk(me, me + 2, 0, chip).start()

    @pl.when(chip > 0)
    def _():
        for n in range(3):
            w_line(n, chip, chip - 1, 1).start()
        chunk(me, me - 2, 1, chip).start()

    for n in range(3):
        w_own(n).start()
        rows_start(n, chip)
    q_stage.wait_recv()
    for exchange in small:
        exchange.wait_recv()

    def update(h, q_tile, q_low, q_count, key_start, key_count, mask):
        lanes = pl.ds(q_low, q_count)
        query = qs[h, pl.ds(pl.multiple_of(q_tile * tile + q_low, BLOCK), q_count), :]
        keys = pl.ds(pl.multiple_of(key_start, BLOCK), key_count)
        scores = dot(ks[h, keys, :], query, NT)
        if mask is not None:
            scores = jnp.where(mask, scores, MASKED)
        top = tops[h, q_tile, :, lanes]
        higher = jnp.maximum(top, jnp.max(scores, axis=0, keepdims=True) * SCALE2)
        probs = jnp.exp2(scores * SCALE2 - higher)
        part = dot(vt[h, :, keys], probs.astype(bf16))
        totals[h, q_tile, :, lanes] = totals[h, q_tile, :, lanes] * jnp.exp2(top - higher) + part
        tops[h, q_tile, :, lanes] = higher

    def column(blocks, amount):
        return jnp.broadcast_to(blocks, (128, amount)).T[:, :1]

    def diagonal(p):
        low, high = blks[2 * p], blks[2 * p + 1]
        first = column(jnp.concatenate([low, high[:, :BLOCK]], axis=1), count + BLOCK)
        second = column(jnp.concatenate([low, high], axis=1), tile)
        for h in range(heads):
            update(h, p, 0, count, p * tile, count + BLOCK, low >= first)
            update(h, p, count, count, p * tile, tile, high >= second)

    def boundary(p):
        mask = blks[2 * p + 1][:, count - BLOCK :] >= column(blks[2 * p + 2][:, :BLOCK], BLOCK)
        for h in range(heads):
            update(h, p, tile - BLOCK, BLOCK, (p + 1) * tile, BLOCK, mask)

    def project(p):
        both = jnp.concatenate([xs[2 * p], xs[2 * p + 1]], axis=0)
        mixed = dot(both, jnp.concatenate([wqs[j] for j in range(3)], axis=1))
        bias = bias_ref[...].astype(f32)
        where = pl.ds(pl.multiple_of(p * tile, tile), tile)
        for h in range(heads):
            at = [slice(j * width + h * HD, j * width + (h + 1) * HD) for j in range(3)]
            here = slice(h * HD, (h + 1) * HD)
            qs[h, where, :] = (mixed[:, at[0]] + bias[0:1, here]).astype(bf16)
            ks[h, where, :] = mixed[:, at[1]].astype(bf16)
            values = (mixed[:, at[2]] + bias[1:2, here]).astype(bf16)
            vs[h, where, :] = values
            vt[h, :HD, where] = flip(values)
            totals[h, p] = jnp.zeros(totals.shape[2:], f32)
            tops[h, p] = jnp.full(tops.shape[2:], MASKED, f32)

    def keep(p):
        where = pl.ds(pl.multiple_of(p * tile, tile), tile)
        pairs = [
            pltpu.make_async_copy(held.at[:, where, :], out.at[:, where, :], local_q.at[n, p])
            for n, (held, out) in enumerate(((qs, q_ref), (ks, k_ref), (vs, v_ref)))
        ]
        return pairs + [
            pltpu.make_async_copy(xs.at[2 * p + c], xo_ref.at[2 * p + c], local_x.at[2 * p + c])
            for c in range(2)
        ]

    def kept(c):
        return pltpu.make_async_copy(founds.at[c], found_ref.at[c], local_f.at[0, c])

    def own(c):
        return pltpu.make_async_copy(founds.at[c], arrived_ref.at[c], local_f.at[1, 0])

    def conclude(p):
        for h in range(heads):
            mass = totals[h, p, HD : HD + 1, :]
            out = (totals[h, p, :HD, :] / mass).astype(bf16)
            for c in range(2):
                founds[2 * p + c, h * HD : (h + 1) * HD, :] = out[:, c * count : (c + 1) * count]
            lse_ref[
                h, p // seq_chips, :, pl.ds(pl.multiple_of(lax.rem(p, seq_chips) * tile, tile), tile)
            ] = tops[h, p] + jnp.log2(mass)
        for c in range(2):
            owner = 2 * p + c
            kept(owner).start()

            @pl.when(owner == me)
            def _():
                own(owner).start()

            @pl.when(owner != me)
            def _():
                f_stage.copy(lax.rem(owner - me + cols, cols)).start()

    def at_distance(hop, act):
        for at, step, route in ((chip - hop, 1, 0), (chip + hop, -1, 1)):

            @pl.when((at >= 0) & (at < chips))
            def _():
                act(at, chip + step, route)

    def w_arrive(at, onward, route):
        for n in range(3):
            w_line(n, at, onward, route).wait_recv()

            @pl.when((onward >= 0) & (onward < chips))
            def _():
                w_line(n, at, onward, route).start()

            rows_start(n, at)

    def w_relay(at, onward=None, route=None):
        for n in range(3):
            rows_relay(n, at)

    def w_pass(at, onward=None, route=None):
        for n in range(3):
            rows_wait_recv(n, at)
            w_mate(n, at, lane).start()

    def ahead(hop):
        if hop == 1:
            at_distance(1, w_arrive)
        else:
            if hop == 2:
                w_relay(chip)
            at_distance(hop - 1, w_relay)
        if hop == chips - 1:
            for n in range(3):
                w_own(n).wait()
            w_pass(chip)
            for near in range(1, chips - 2):
                at_distance(near, w_pass)

    def event(e, carry):
        hop = (e + 1) // 2
        lower = lax.rem(e, 2) == 1
        p = jnp.where(lower, chip - hop, chip + hop)

        for stage in range(1, chips):

            @pl.when(e == 2 * stage - 1)
            def _():
                ahead(stage)

        @pl.when(lower)
        def _():
            below, above = chip - hop, chip + hop

            @pl.when(below >= 0)
            def _():
                owner = below * 2 + lane
                chunk(owner, me, 0, below).wait_recv()

                @pl.when(chip + 1 < chips)
                def _():
                    chunk(owner, me + 2, 0, below).start()

                to_mate(owner, below).start()

            @pl.when(above < chips)
            def _():
                owner = above * 2 + lane
                chunk(owner, me, 1, above).wait_recv()

                @pl.when(chip > 0)
                def _():
                    chunk(owner, me - 2, 1, above).start()

                to_mate(owner, above).start()

        for stage in range(2, chips - 1):

            @pl.when(e == 2 * stage - 1)
            def _():
                at_distance(stage, w_arrive)

        @pl.when((p >= 0) & (p < chips))
        def _():
            to_mate(2 * p + 1 - lane, p).wait_recv()
            project(p)
            for copy in keep(p):
                copy.start()
            first = p // seq_chips * seq_chips
            final = first + seq_chips - 1
            high = jnp.minimum(chip + hop - 1, final)
            low = jnp.maximum(jnp.maximum(chip - hop, 0), first)
            diagonal(p)

            @pl.when(lower & (p < final))
            def _():
                boundary(p)

            @pl.when(lower & (p == first))
            def _():
                conclude(p)

            @pl.when(jnp.logical_not(lower) & (p > first) & (hop > 0))
            def _():
                boundary(p - 1)

                @pl.when(low == first)
                def _():
                    conclude(p - 1)

            amount = jnp.where(lower, high - p, p - low)

            def pair(j, carry):
                q_tile = jnp.where(lower, p + 1 + j, p)
                key_tile = jnp.where(lower, p, low + j)

                @pl.when((hop == chips - 1) & (j == amount - 2))
                def _():
                    at_distance(chips - 1, w_arrive)

                for h in range(heads):
                    update(h, q_tile, 0, tile, key_tile * tile, tile, None)

                @pl.when(lower & (p == first) & ((q_tile == final) | (q_tile < high)))
                def _():
                    conclude(q_tile)

                return carry

            lax.fori_loop(0, amount, pair, 0)

            @pl.when(jnp.logical_not(lower) & (p == final) & (low == first))
            def _():
                conclude(p)

        return carry

    lax.fori_loop(0, 2 * chips - 1, event, 0)
    at_distance(chips - 2, w_pass)
    at_distance(chips - 1, w_relay)
    at_distance(chips - 1, w_pass)

    for c in range(cols):
        bupo_ref[c] = bups[c]
        at = c * count
        blko_ref[at // SEQ_LEN, :, at % SEQ_LEN : at % SEQ_LEN + count] = blks[c]
    f_stage.wait_recv()
    for c in range(chips):
        for n in range(3):
            w_mate(n, c, 1 - lane).wait_recv()
            w_mate(n, c, lane).wait_send()
            rows_wait_send(n, c)

            @pl.when((c <= chip) & (chip + 1 < chips))
            def _():
                w_line(n, c, chip, 0).wait_send()

            @pl.when((c >= chip) & (chip > 0))
            def _():
                w_line(n, c, chip, 1).wait_send()

        for copy in keep(c):
            copy.wait()
        kept(2 * c).wait()
        kept(2 * c + 1).wait()
        to_mate(me, c).wait_send()

        @pl.when((c <= chip) & (chip + 1 < chips))
        def _():
            chunk(me, me, 0, c).wait_send()

        @pl.when((c >= chip) & (chip > 0))
        def _():
            chunk(me, me, 1, c).wait_send()

    own(me).wait()
    f_stage.wait_send()
    q_stage.wait_send()
    for exchange in small:
        exchange.wait_send()


def front(tokens, gain, shift, b_up, blocks, w_qkv, b_qv, w_out, w_up, w_down, rows, cols):
    count, depth = tokens.shape
    head_cols = w_qkv.shape[2]
    heads = head_cols // HD
    chips = cols // 2
    total = count * cols
    tile = 2 * count
    any_space = pl.BlockSpec(memory_space=pl.ANY)
    in_vmem = pl.BlockSpec(memory_space=pltpu.VMEM)
    dma, vmem, shape = pltpu.SemaphoreType.DMA, pltpu.VMEM, jax.ShapeDtypeStruct
    pairs = heads * total * SEQ_LEN * 5 // 8
    held = (heads, total, HD)
    return pl.pallas_call(
        functools.partial(front_kernel, rows, cols, heads),
        in_specs=[in_vmem] * 10,
        out_specs=[any_space] * 6 + [in_vmem] * 3 + [any_space] * 3,
        out_shape=[
            shape((cols, count, depth), bf16), shape(held, bf16), shape(held, bf16),
            shape(held, bf16), shape((cols, head_cols, count), bf16),
            shape((cols, head_cols, count), bf16),
            shape((heads, total // SEQ_LEN, 1, SEQ_LEN), f32),
            shape((total // SEQ_LEN, 1, SEQ_LEN), jnp.int32), shape((cols, 1) + b_up.shape, bf16),
        ] + [shape((2, chips, rows) + w.shape, bf16) for w in (w_out, w_up, w_down)],
        scratch_shapes=[
            vmem((cols, count, depth), bf16), vmem((3, depth, head_cols), bf16),
            vmem(held, bf16), vmem(held, bf16), vmem(held, bf16),
            vmem((heads, HD + ONES, total), bf16),
            vmem((heads, chips, HD + ONES, tile), f32), vmem((heads, chips, 1, tile), f32),
            vmem((cols, head_cols, count), bf16), vmem((cols,) + blocks.shape, jnp.int32),
            vmem((cols, 1) + b_up.shape, bf16),
            dma((3, chips)), dma((3, chips)), dma((rows,)), dma((rows,)),
            dma((2, cols)), dma((2, cols)), dma((cols,)), dma((cols,)),
            dma((3, 2, chips)), dma((3, chips)), dma((3, chips, rows)), dma((3, chips, rows)),
            dma((3, chips)), dma((3, chips)),
            dma((cols,)), dma((3, chips)), dma((2, cols)), dma((3,)),
        ],
        compiler_params=pltpu.CompilerParams(
            vmem_limit_bytes=63 << 20, collective_id=0, has_side_effects=True
        ),
        cost_estimate=cost(16 * pairs * HD, 16 * heads * total * HD, pairs),
        name="front",
    )(tokens, gain, shift, b_up, blocks, w_qkv, b_qv, w_out, w_up, w_down)


def tile_mask(blk_ref, key_start, count, query_blocks):
    key_blocks = jnp.broadcast_to(blk_ref[0, :, pl.ds(key_start, count)], (128, count)).T[:, :1]
    return query_blocks >= key_blocks


GELU_A = 0.7978845608028654
GELU_B = 0.044715


def middle_kernel(
    rows, cols,
    heads_ref, tok_ref, g_ref, up_ref, down_ref, bup_ref, bout_ref, gain_ref, shift_ref, bdown_ref,
    wout_ref, wq_ref,
    gup_ref, gdown_ref, gout_ref, output_ref, dres_ref, sums_ref, dheads_ref, wqo_ref,
    x, heads_all, resid, out_acc, norm_acc, hiddens, d_ups, low, d_send,
    mine, other, out_mine, out_other,
    send_d, recv_d, send_p, recv_p, send_o, recv_o, send_z, recv_z, send_r, recv_r, send_m, recv_m,
    local,
):
    step = pl.program_id(0)
    chips = cols // 2
    row, col = place()
    chip, lane = col // 2, lax.rem(col, 2)
    width = up_ref.shape[4]
    depth = wout_ref.shape[3]

    def part(r):
        return slice(r * width, (r + 1) * width)

    def out_weight(r):
        return jnp.concatenate([wout_ref[c % 2, c // 2, r] for c in range(cols)], axis=0)

    z_stage = over_line(
        chips, lambda at: wq_ref, lambda at: wqo_ref.at[lane, row, at], send_z, recv_z
    )

    def r_stage(c, out=None):
        return over_row(
            rows,
            lambda at: wqo_ref.at[lane, row, c] if out is None else out,
            lambda at: wqo_ref.at[lane, at, c],
            send_r.at[c],
            recv_r.at[c],
        )

    m_stage = remote(wqo_ref.at[lane], wqo_ref.at[lane], send_m, recv_m, mate())
    m_arrival = remote(wqo_ref.at[1 - lane], wqo_ref.at[1 - lane], send_m, recv_m, mate())
    own_wq = pltpu.make_async_copy(wq_ref, wqo_ref.at[lane, row, chip], local.at[0])
    d_stage = over_col(
        cols, lambda at: d_send.at[at], lambda at: dheads_ref.at[at], send_d, recv_d
    )
    own_d = pltpu.make_async_copy(d_send.at[col], dheads_ref.at[col], local.at[1])

    def pair(at, which):
        return remote(
            mine.at[which, at], other.at[which, at], send_p.at[which, at], recv_p.at[which, at],
            mate(),
        )

    pair_out = remote(out_mine, out_other, send_o, recv_o, mate())

    @pl.when(step == 0)
    def _():
        greet(rows, cols)
        own_wq.start()
        z_stage.start()
        r_stage(chip, wq_ref).start()
        for s in range(cols):
            heads_all[s * depth : (s + 1) * depth] = heads_ref[s]
        stacked = flip(heads_all[...])
        for r in range(rows):
            branch = dot(stacked, out_weight(r))
            resid[:, part(r)] = tok_ref[:, part(r)].astype(f32) + branch + line(bout_ref)[:, part(r)]
        xhat, _ = moments(resid[...])
        x[...] = (xhat * line(gain_ref) + line(shift_ref)).astype(bf16)
        out_acc[...] = jnp.zeros_like(out_acc)
        norm_acc[...] = jnp.zeros_like(norm_acc)

    @pl.when(step == cols // 2)
    def _():
        own_wq.wait()
        z_stage.wait_recv()
        each(chips, lambda k: r_stage(lax.rem(chip + k, chips)).start())

    @pl.when(step < cols)
    def _():
        up = bup_ref[0].astype(f32)
        d_hidden = 0.0
        for r in range(rows):
            up = up + dot(x[:, part(r)], up_ref[0, 0, r], NT)
            d_hidden = d_hidden + dot(g_ref[:, part(r)], down_ref[0, 0, r], NT)
        square = up * up
        bent = jnp.tanh(GELU_A * up * (1.0 + GELU_B * square))
        half = 0.5 + 0.5 * bent
        hidden = (up * half).astype(bf16)
        slope = half + (0.5 * GELU_A) * up * (1.0 - bent * bent) * (1.0 + (3.0 * GELU_B) * square)
        d_up = d_hidden * slope
        units = d_up.shape[1]
        per = sums_ref.shape[1] // units
        lanes = pl.ds(pl.multiple_of(lax.rem(step, per) * units, units), units)
        sums_ref[pl.ds(4 + step // per, 1), lanes] = jnp.sum(d_up, axis=0, keepdims=True)
        d_up = d_up.astype(bf16)
        hiddens[step] = hidden
        d_ups[step] = d_up
        for r in range(rows):
            norm_acc[:, part(r)] += dot(d_up, up_ref[0, 0, r])

    @pl.when(step == cols - 1)
    def _():
        xhat, inv = moments(resid[...])
        d_norm = norm_acc[...]
        grad = g_ref[...].astype(f32)
        d_resid = grad + norm_back(xhat, inv, d_norm * line(gain_ref))
        dres_ref[...] = d_resid
        low[...] = d_resid.astype(bf16)
        sums_ref[0:1] = jnp.sum(grad, axis=0, keepdims=True)
        sums_ref[1:2] = jnp.sum(d_norm * xhat, axis=0, keepdims=True)
        sums_ref[2:3] = jnp.sum(d_norm, axis=0, keepdims=True)
        sums_ref[3:4] = jnp.sum(d_resid, axis=0, keepdims=True)
        found = 0.0
        for r in range(rows):
            found = found + dot(out_weight(r), low[:, part(r)], NT)
        found = found.astype(bf16)
        for c in range(cols):
            d_send[c] = found[c * depth : (c + 1) * depth]
        own_d.start()
        d_stage.start()
        found = dot(heads_all[...], low[...])
        for c in range(chips):
            first = found[2 * c * depth : (2 * c + 1) * depth]
            second = found[(2 * c + 1) * depth : (2 * c + 2) * depth]
            out_mine[c] = jnp.where(lane == 0, second, first).astype(bf16)
            kept = jnp.where(lane == 0, first, second)
            for r in range(rows):
                norm_acc[c * depth : (c + 1) * depth, part(r)] = kept[:, part(r)]
        pair_out.start()

    at = step - cols

    @pl.when(at >= 0)
    def _():
        for r in range(rows):
            out_acc[:, part(r)] += dot(hiddens[at], down_ref[0, 0, r])

    @pl.when((at >= 0) & (at < chips))
    def _():
        c = at * 2 + 1 - lane
        mine[0, at] = dot(hiddens[c], g_ref[...], TN).astype(bf16)
        pair(at, 0).start()
        mine[1, at] = dot(d_ups[c], x[...], TN).astype(bf16)
        pair(at, 1).start()

    @pl.when(step == 2 * cols - 1)
    def _():
        for c in range(chips):
            r_stage(c).wait_recv()
        m_stage.start()

    @pl.when(at >= chips)
    def _():
        k = at - chips
        c = k * 2 + lane
        grad_down = dot(hiddens[c], g_ref[...], TN)
        pair(k, 0).wait_recv()
        grad_down = (grad_down + other[0, k].astype(f32)).astype(bf16)
        grad_up = dot(d_ups[c], x[...], TN)
        pair(k, 1).wait_recv()
        grad_up = (grad_up + other[1, k].astype(f32)).astype(bf16)
        for r in range(rows):
            gdown_ref[r, 0] = grad_down[:, part(r)]
            gup_ref[r, 0] = grad_up[:, part(r)]

    @pl.when(step == 2 * cols - 1)
    def _():
        output_ref[...] = (resid[...] + out_acc[...] + line(bdown_ref)).astype(bf16)
        pair_out.wait_recv()
        for c in range(chips):
            for r in range(rows):
                kept = norm_acc[c * depth : (c + 1) * depth, part(r)]
                gout_ref[r, c] = (kept + out_other[c, :, part(r)].astype(f32)).astype(bf16)
        d_stage.wait_recv()
        m_arrival.wait_recv()
        pair_out.wait_send()
        for k in range(chips):
            pair(k, 0).wait_send()
            pair(k, 1).wait_send()
            r_stage(k).wait_send()
        z_stage.wait_send()
        d_stage.wait_send()
        m_stage.wait_send()
        own_d.wait()


def middle(heads, tokens, grad, w_up, w_down, b_up, b_out, gain, shift, b_down, w_out, w_qkv):
    count, depth = tokens.shape
    _, chips, rows, units, width = w_up.shape
    cols = 2 * chips
    head_cols = w_out.shape[3]
    sum_rows = 4 + cols * units // depth
    any_space = pl.BlockSpec(memory_space=pl.ANY)

    def weight_map(s):
        c = jnp.minimum(s, cols - 1)
        return (lax.rem(c, 2), c // 2, 0, 0, 0)

    def again_map(s):
        c = lax.rem(s, cols)
        return (lax.rem(c, 2), c // 2, 0, 0, 0)

    weight = pl.BlockSpec((1, 1, rows, units, width), weight_map)
    again = pl.BlockSpec((1, 1, rows, units, width), again_map)
    grad_spec = pl.BlockSpec(
        (rows, 1, units, width), lambda s: (0, jnp.maximum(s - cols - chips, 0), 0, 0)
    )
    grad_shape = jax.ShapeDtypeStruct((rows, chips, units, width), bf16)
    bias = pl.BlockSpec((1, 1, units), lambda s: (jnp.minimum(s, cols - 1), 0, 0))
    block = whole((count, depth))
    dma = pltpu.SemaphoreType.DMA
    vmem = pltpu.VMEM
    return pl.pallas_call(
        functools.partial(middle_kernel, rows, cols),
        grid=(2 * cols,),
        in_specs=[
            whole(heads.shape), block, block, weight, again, bias, *[whole((depth,))] * 4,
            whole(w_out.shape), any_space,
        ],
        out_specs=[
            grad_spec, grad_spec, whole((rows, chips, head_cols, width)), block, block,
            whole((sum_rows, depth)), any_space, any_space,
        ],
        out_shape=[
            grad_shape, grad_shape,
            jax.ShapeDtypeStruct((rows, chips, head_cols, width), bf16),
            jax.ShapeDtypeStruct((count, depth), bf16),
            jax.ShapeDtypeStruct((count, depth), f32),
            jax.ShapeDtypeStruct((sum_rows, depth), f32),
            jax.ShapeDtypeStruct((cols, head_cols, count), bf16),
            jax.ShapeDtypeStruct((2, rows, chips) + w_qkv.shape, bf16),
        ],
        scratch_shapes=[
            vmem((count, depth), bf16), vmem((depth, count), bf16),
            vmem((count, depth), f32), vmem((count, depth), f32), vmem((count, depth), f32),
            vmem((cols, count, units), bf16), vmem((cols, count, units), bf16),
            vmem((count, depth), bf16), vmem((cols, head_cols, count), bf16),
            vmem((2, chips, units, depth), bf16), vmem((2, chips, units, depth), bf16),
            vmem((chips, head_cols, depth), bf16), vmem((chips, head_cols, depth), bf16),
            dma((cols,)), dma((cols,)), dma((2, chips)), dma((2, chips)), dma, dma,
            dma((chips,)), dma((chips,)), dma((chips, rows)), dma((chips, rows)), dma, dma,
            dma((2,)),
        ],
        compiler_params=pltpu.CompilerParams(
            vmem_limit_bytes=63 << 20, collective_id=1, has_side_effects=True
        ),
        cost_estimate=cost(
            12 * count * depth * cols * units, 8 * depth * cols * units + 16 * count * depth
        ),
        name="middle",
    )(heads, tokens, grad, w_up, w_down, b_up, b_out, gain, shift, b_down, w_out, w_qkv)


class SmallSum:
    def __init__(self, rows, chips, scratch):
        row, col = place()
        self.rows, self.chips, self.row, self.chip = rows, chips, row, col // 2
        self.held, self.core, self.by_row, self.by_line, *sems = scratch
        held = self.held
        self.stages = [
            remote(held.at[0], self.core, sems[0], sems[1], mate()),
            over_row(
                rows, lambda at: held.at[1], lambda at: self.by_row.at[at], sems[2], sems[3]
            ),
            over_line(
                chips, lambda at: held.at[2], lambda at: self.by_line.at[at], sems[4], sems[5]
            ),
        ]

    def first(self, value):
        self.held[0] = value
        self.stages[0].start()

    def second(self):
        self.stages[0].wait_recv()
        value = self.held[0] + self.core[...]
        self.held[1] = value
        self.by_row[self.row] = value
        self.stages[1].start()

    def third(self):
        self.stages[1].wait_recv()
        value = sum(self.by_row[r] for r in range(1, self.rows)) + self.by_row[0]
        self.held[2] = value
        self.by_line[self.chip] = value
        self.stages[2].start()

    def result(self):
        self.stages[2].wait_recv()
        return sum(self.by_line[c] for c in range(1, self.chips)) + self.by_line[0]

    def wait_send(self):
        for stage in self.stages:
            stage.wait_send()


def sum_scratch(rows, chips, shapes):
    dma, vmem = pltpu.SemaphoreType.DMA, pltpu.VMEM
    found = []
    for shape in shapes:
        found += [
            vmem((3,) + shape, f32), vmem(shape, f32), vmem((rows,) + shape, f32),
            vmem((chips,) + shape, f32), dma, dma, dma((rows,)), dma((rows,)), dma((chips,)),
            dma((chips,)),
        ]
    return found


SUM_REFS = 10


def add_into(into, other):
    into[...] = (into[...].astype(f32) + other[...].astype(f32)).astype(bf16)


class HalvedSum:
    REFS = 16

    @staticmethod
    def scratch(rows, chips, block):
        dma, vmem = pltpu.SemaphoreType.DMA, pltpu.VMEM
        return [
            vmem((2, chips) + block, bf16), vmem((2, chips) + block, bf16),
            vmem((chips,) + block, bf16), vmem((2,) + block, bf16), vmem(block, bf16),
            dma((2,)), dma((2,)), dma((2,)), dma, dma, dma((2,)), dma((2,)), dma, dma,
        ]

    def __init__(self, rows, chips, given, scratch):
        self.own, self.came, self.came_row, self.came_line, self.came_far, *sems = scratch
        local, send_a, recv_a, send_b, recv_b, send_c, recv_c, send_d, recv_d = sems
        row, col = place()
        plane = Plane()
        chip, lane = col // 2, lax.rem(col, 2)
        near = chip + 1 - 2 * lax.rem(chip, 2)
        self.chip, self.far = chip, lax.rem(chip + 2, 4)
        own = self.own
        self.loads = [
            pltpu.make_async_copy(given.at[at], own.at[k], local.at[k])
            for k, at in enumerate((row, plane.second))
        ]
        self.a = [
            remote(given.at[at], self.came.at[k], send_a.at[k], recv_a.at[k], (plane.first, col))
            for k, at in enumerate((plane.first, plane.across))
        ]
        self.b = [remote(own.at[1], self.came_row, send_b, recv_b, (plane.second, col))]
        self.c = [
            remote(
                own.at[0, at], self.came_line.at[k], send_c.at[k], recv_c.at[k],
                (row, near * 2 + lane),
            )
            for k, at in enumerate((near, lax.rem(near + 2, 4)))
        ]
        self.d = [
            remote(own.at[0, self.far], self.came_far, send_d, recv_d, (row, self.far * 2 + lane))
        ]

    def begin(self):
        for copy in self.a + self.loads:
            copy.start()

    def step(self, n):
        if n == 0:
            for copy in self.loads:
                copy.wait()
            for copy in self.a:
                copy.wait_recv()
            for k in (1, 0):
                for c in range(self.own.shape[1]):
                    add_into(self.own.at[k, c], self.came.at[k, c])
                if k == 1:
                    self.b[0].start()
        elif n == 1:
            self.b[0].wait_recv()
            for c in range(self.own.shape[1]):
                add_into(self.own.at[0, c], self.came_row.at[c])
            for copy in self.c:
                copy.start()
        else:
            for copy in self.c:
                copy.wait_recv()
            add_into(self.own.at[0, self.far], self.came_line.at[1])
            self.d[0].start()
            add_into(self.own.at[0, self.chip], self.came_line.at[0])

    def result(self):
        self.d[0].wait_recv()
        return self.own[0, self.chip].astype(f32) + self.came_far[...].astype(f32)

    def wait_send(self):
        for copy in self.a + self.b + self.c + self.d:
            copy.wait_send()


class DirectSum:
    @staticmethod
    def scratch(rows, chips, block):
        dma, vmem = pltpu.SemaphoreType.DMA, pltpu.VMEM
        return [
            vmem((rows, chips) + block, bf16), vmem((chips,) + block, bf16),
            vmem((chips,) + block, bf16),
            dma, dma((rows,)), dma((rows,)), dma((chips,)), dma((chips,)),
        ]

    def __init__(self, rows, chips, given, scratch):
        by_row, total, by_line, local, send_r, recv_r, send_l, recv_l = scratch
        row, col = place()
        self.rows, self.chips, self.chip = rows, chips, col // 2
        self.by_row, self.total, self.by_line = by_row, total, by_line
        self.load = pltpu.make_async_copy(given.at[row], by_row.at[row], local)
        self.r = over_row(
            rows, lambda at: given.at[at], lambda at: by_row.at[at], send_r, recv_r
        )
        self.l = over_line(
            chips, lambda at: total.at[at], lambda at: by_line.at[at], send_l, recv_l
        )

    def begin(self):
        self.load.start()
        self.r.start()

    def step(self, n):
        if n != 1:
            return
        self.load.wait()
        self.r.wait_recv()

        def one(c, carry):
            total = self.by_row[0, c].astype(f32)
            for r in range(1, self.rows):
                total = total + self.by_row[r, c].astype(f32)
            self.total[c] = total.astype(bf16)
            return carry

        lax.fori_loop(0, self.chips, one, 0)
        self.by_line[self.chip] = self.total[self.chip]
        self.l.start()

    def result(self):
        self.l.wait_recv()
        total = self.by_line[0].astype(f32)
        for c in range(1, self.chips):
            total = total + self.by_line[c].astype(f32)
        return total

    def wait_send(self):
        self.r.wait_send()
        self.l.wait_send()


def weight_sum(rows, chips):
    return HalvedSum if (rows, chips) == (4, 4) else DirectSum


def weight_scratch(rows, chips, blocks):
    return [ref for block in blocks for ref in weight_sum(rows, chips).scratch(rows, chips, block)]


def back_kernel(
    rows, cols, heads, seqs, tiles, sub,
    blk_ref, q_ref, k_ref, v_ref, do_ref, o_ref, lse_ref, x_ref, w_ref, tok_ref, dres_ref, gain_ref,
    gup_ref, gdown_ref, gout_ref, early_ref,
    dtok_ref, wup_ref, wdown_ref, wout_ref, wqkv_ref, all_ref, late_ref, bias_ref,
    d_mixed, d_arrived, key_grad, value_grad, bias_sum, qkv_acc, qkv_send, qkv_recv, norm_acc,
    bias_send, bias_recv, send_d, recv_d, send_q, recv_q, send_b, recv_b, local_d, *rest,
):
    step = pl.program_id(0)
    chips = cols // 2
    row, col = place()
    work = heads * seqs * tiles
    last = work + 2 * cols - 1
    head = jnp.minimum(step // (seqs * tiles), heads - 1)
    seq = lax.rem(step // tiles, seqs)
    turn = lax.rem(step, tiles)
    i = tiles - 1 - turn
    tile = q_ref.shape[1]
    chunks, _, chunk = do_ref.shape
    chunks_seq = SEQ_LEN // chunk
    parts = tile // sub
    start = pl.multiple_of(i * tile, tile)

    early = SmallSum(rows, chips, rest[:SUM_REFS])
    late = SmallSum(rows, chips, rest[SUM_REFS : 2 * SUM_REFS])
    rest = rest[2 * SUM_REFS :]
    each_refs = len(rest) // 3
    weights = [
        weight_sum(rows, chips)(rows, chips, given, rest[n * each_refs : (n + 1) * each_refs])
        for n, given in enumerate((gdown_ref, gup_ref, gout_ref))
    ]
    results = (wdown_ref, wup_ref, wout_ref)

    def d_stage(h):
        return over_col(
            cols, lambda at: d_mixed.at[h, at], lambda at: d_arrived.at[h, at], send_d.at[h],
            recv_d.at[h],
        )

    def own_d(h):
        return pltpu.make_async_copy(d_mixed.at[h, col], d_arrived.at[h, col], local_d.at[h])

    q_stage = over_row(
        rows, lambda at: qkv_send.at[at], lambda at: qkv_recv.at[at], send_q, recv_q
    )
    b_stage = over_row(rows, lambda at: bias_send, lambda at: bias_recv.at[at], send_b, recv_b)

    def at_step(when, act):
        @pl.when(step == when)
        def _():
            act()

    @pl.when(step == 0)
    def _():
        greet(rows, cols)
        weights[0].begin()
        weights[2].begin()
        early.first(early_ref[...])

    at_step(work // 8, early.second)
    at_step(
        work * 3 // 8,
        lambda: (early.third(), weights[0].step(0), weights[2].step(0), weights[1].begin()),
    )
    at_step(work * 6 // 8, lambda: (weights[0].step(1), weights[2].step(1)))
    at_step(work, lambda: weights[1].step(0))
    at_step(work + cols // 2, lambda: (weights[0].step(2), weights[2].step(2)))

    @pl.when((step < work) & (turn == 0))
    def _():
        key_grad[...] = jnp.zeros_like(key_grad)
        value_grad[...] = jnp.zeros_like(value_grad)

    @pl.when((step < work) & (turn == 0) & (seq == 0))
    def _():
        bias_sum[head] = jnp.zeros((HD, 128), f32)

    def hand_over(c):
        where = pl.ds(pl.multiple_of(c * chunk, chunk), chunk)
        at = seq * chunks_seq + c
        d_mixed[head, at, HD : 2 * HD] = (key_grad[where, :].T * SCALE).astype(bf16)
        d_values = value_grad[where, :].T
        d_mixed[head, at, 2 * HD :] = d_values.astype(bf16)
        bias_sum[head, :, 1:2] += jnp.sum(d_values, axis=1, keepdims=True)

        @pl.when(at == col)
        def _():
            own_d(head).start()

        @pl.when(at != col)
        def _():
            d_stage(head).copy(lax.rem(at - col + cols, cols)).start()

    @pl.when(step < work)
    def _():
        d_out = jnp.concatenate([do_ref[b] for b in range(chunks)], axis=1)
        out = jnp.concatenate([o_ref[b] for b in range(chunks)], axis=1)
        delta = jnp.sum(d_out.astype(f32) * out.astype(f32), axis=0, keepdims=True)
        lse = lse_ref[0, 0]

        def cut(x, a):
            return x[:, a * sub : (a + 1) * sub]

        queries = [q_ref[0, a * sub : (a + 1) * sub, :] for a in range(parts)]
        query_blocks = [
            blk_ref[0, :, pl.ds(pl.multiple_of(start + a * sub, sub), sub)] for a in range(parts)
        ]

        def update(a, query_grad, key_start, count, masked):
            keys = k_ref[0, pl.ds(key_start, count), :]
            values = v_ref[0, pl.ds(key_start, count), :]
            scores = dot(keys, queries[a], NT) * SCALE2 - cut(lse, a)
            if masked:
                mask = tile_mask(blk_ref, key_start, count, query_blocks[a])
                scores = jnp.where(mask, scores, MASKED)
            probs = jnp.exp2(scores)
            d_values = dot(probs.astype(bf16), cut(d_out, a), NT)
            d_scores = (probs * (dot(values, cut(d_out, a)) - cut(delta, a))).astype(bf16)
            d_keys = dot(d_scores, queries[a])
            return query_grad + dot(keys, d_scores, TN), d_keys, d_values

        def add(key_start, count, d_keys, d_values):
            key_grad[pl.ds(key_start, count), :] += d_keys
            value_grad[pl.ds(key_start, count), :] += d_values

        def sweep(j, grads):
            key_start = pl.multiple_of(j * tile, tile)
            found = [update(a, grads[a], key_start, tile, False) for a in range(parts)]
            add(key_start, tile, sum(f[1] for f in found), sum(f[2] for f in found))
            return tuple(f[0] for f in found)

        grads = list(lax.fori_loop(0, i, sweep, (jnp.zeros((HD, sub), f32),) * parts))
        for a in range(parts):
            todo = [(pl.multiple_of(start + a * sub, sub), sub, True)]
            if a > 0:
                todo.append((start, a * sub, False))
            if a < parts - 1:
                todo.append((pl.multiple_of(start + (a + 1) * sub, BLOCK), BLOCK, True))
            for key_start, count, masked in todo:
                grads[a], d_keys, d_values = update(a, grads[a], key_start, count, masked)
                add(key_start, count, d_keys, d_values)

        def beyond(j, grad):
            key_start = pl.multiple_of(start + tile, BLOCK)
            grad, d_keys, d_values = update(parts - 1, grad, key_start, BLOCK, True)
            add(key_start, BLOCK, d_keys, d_values)
            return grad

        grads[-1] = lax.fori_loop(0, jnp.where(i < tiles - 1, 1, 0), beyond, grads[-1])
        query_grad = jnp.concatenate(grads, axis=1) * SCALE
        bias_sum[head, :, :1] += jnp.sum(query_grad, axis=1, keepdims=True)
        query_grad = query_grad.astype(bf16)
        for b in range(chunks):
            d_mixed[head, seq * chunks_seq + i * chunks + b, :HD] = query_grad[
                :, b * chunk : (b + 1) * chunk
            ]

    @pl.when((step < work) & (i == 0))
    def _():
        hand_over(0)

    @pl.when(step < work)
    def _():
        for b in range(1, chunks):
            hand_over(i * chunks + b)

    @pl.when((step < work) & (turn > 0))
    def _():
        hand_over((i + 1) * chunks)

    at = step - work

    @pl.when(at == 0)
    def _():
        qkv_acc[...] = jnp.zeros_like(qkv_acc)
        bias_send[...] = bias_sum[...]
        bias_recv[row] = bias_sum[...]
        b_stage.start()

    @pl.when((at >= 0) & (at < cols))
    def _():
        grads = jnp.concatenate([d_mixed[h, at] for h in range(heads)], axis=0)
        qkv_acc[...] += dot(grads, x_ref[0])

    @pl.when(at == cols - 1)
    def _():
        width = qkv_send.shape[2]
        for r in range(rows):
            qkv_send[r] = qkv_acc[:, r * width : (r + 1) * width].astype(bf16)
        qkv_recv[row] = qkv_send[row]
        q_stage.start()
        norm_acc[...] = jnp.zeros_like(norm_acc)

    @pl.when(at >= cols)
    def _():
        c = at - cols
        for h in range(heads):

            @pl.when(c == col)
            def _():
                own_d(h).wait()

            @pl.when(c != col)
            def _():
                d_stage(h).arrival(lax.rem(c - col + cols, cols)).wait_recv()

    at_step(work + cols, lambda: weights[1].step(1))

    @pl.when(at >= cols)
    def _():
        c = at - cols
        width = w_ref.shape[4]
        found = flip(
            jnp.concatenate(
                [
                    d_arrived[h, c, j * HD : (j + 1) * HD, :]
                    for j in range(3)
                    for h in range(heads)
                ],
                axis=0,
            )
        )
        for r in range(rows):
            norm_acc[:, r * width : (r + 1) * width] += dot(
                found, jnp.concatenate([w_ref[0, r, 0, j] for j in range(3)], axis=1), NT
            )

    @pl.when(step == last)
    def _():
        for n, stage in ((1, 2),):
            weights[n].step(stage)
        xhat, inv = moments(tok_ref[...].astype(f32))
        d_norm = norm_acc[...]
        late.first(
            jnp.concatenate(
                [
                    jnp.sum(d_norm * xhat, axis=0, keepdims=True),
                    jnp.sum(d_norm, axis=0, keepdims=True),
                ],
                axis=0,
            )
        )
        dtok_ref[...] = dres_ref[...] + norm_back(xhat, inv, d_norm * line(gain_ref))
        late.second()
        b_stage.wait_recv()
        bias_ref[...] = sum(bias_recv[r] for r in range(1, rows)) + bias_recv[0]
        all_ref[...] = early.result()
        late.third()
        q_stage.wait_recv()
        total = qkv_recv[0].astype(f32)
        for r in range(1, rows):
            total = total + qkv_recv[r].astype(f32)
        for j in range(3):
            part = [total[(h * 3 + j) * HD : (h * 3 + j + 1) * HD] for h in range(heads)]
            wqkv_ref[j] = jnp.concatenate(part, axis=0).T
        for weight, result in zip(weights, results):
            result[...] = weight.result()
        late_ref[...] = late.result()
        for weight in weights:
            weight.wait_send()
        for h in range(heads):
            d_stage(h).wait_send()
        q_stage.wait_send()
        b_stage.wait_send()
        early.wait_send()
        late.wait_send()


def backward(
    blocks, q, k, v, d_heads, out, lse, x, w_qkv, tokens, d_resid, gain, grad_up, grad_down,
    grad_out, early,
):
    heads, total, _ = q.shape
    count, depth = tokens.shape
    rows, chips, units, width = grad_up.shape
    cols = 2 * chips
    head_cols = grad_out.shape[2]
    seqs = total // SEQ_LEN
    tile, sub = 1024, 512
    tiles = SEQ_LEN // tile
    work = heads * seqs * tiles
    pairs = heads * seqs * SEQ_LEN * SEQ_LEN * 5 // 8

    def unpack(s):
        s = jnp.minimum(s, work - 1)
        return s // (seqs * tiles), lax.rem(s // tiles, seqs), tiles - 1 - lax.rem(s, tiles)

    def queries_map(s):
        h, b, i = unpack(s)
        return (h, b * tiles + i, 0)

    def keys_map(s):
        h, b, _ = unpack(s)
        return (h, b, 0)

    def heads_map(s):
        h, b, i = unpack(s)
        return (b * tiles + i, h, 0)

    def lse_map(s):
        h, b, i = unpack(s)
        return (h, b, 0, i)

    def w_map(s):
        c = jnp.maximum(s - work - cols, 0)
        return (lax.rem(c, 2), 0, c // 2, 0, 0, 0)

    keys = pl.BlockSpec((1, SEQ_LEN, HD), keys_map)
    heads_spec = pl.BlockSpec((tile // chunk_of(tokens), HD, count), heads_map)
    any_space = pl.BlockSpec(memory_space=pl.ANY)
    block = whole((count, depth))
    dma, vmem = pltpu.SemaphoreType.DMA, pltpu.VMEM
    parts = heads * 3 * HD
    shape = jax.ShapeDtypeStruct
    small = early.shape
    return pl.pallas_call(
        functools.partial(back_kernel, rows, cols, heads, seqs, tiles, sub),
        grid=(work + 2 * cols,),
        in_specs=[
            pl.BlockSpec((1, 1, SEQ_LEN), lambda s: (unpack(s)[1], 0, 0)),
            pl.BlockSpec((1, tile, HD), queries_map), keys, keys, heads_spec, heads_spec,
            pl.BlockSpec((1, 1, 1, tile), lse_map),
            pl.BlockSpec((1, count, depth), lambda s: (jnp.clip(s - work, 0, cols - 1), 0, 0)),
            pl.BlockSpec((1, rows, 1) + w_qkv.shape[3:], w_map),
            block, block, whole((depth,)), any_space, any_space, any_space, whole(small),
        ],
        out_specs=[
            block, whole((units, width)), whole((units, width)), whole((head_cols, width)),
            whole((3, width, heads * HD)), whole(small), whole((2, depth)), whole((heads, HD, 128)),
        ],
        out_shape=[
            shape((count, depth), f32), shape((units, width), f32), shape((units, width), f32),
            shape((head_cols, width), f32), shape((3, width, heads * HD), f32), shape(small, f32), shape((2, depth), f32),
            shape((heads, HD, 128), f32),
        ],
        scratch_shapes=[
            vmem((heads, cols, 3 * HD, count), bf16), vmem((heads, cols, 3 * HD, count), bf16),
            vmem((SEQ_LEN, HD), f32), vmem((SEQ_LEN, HD), f32), vmem((heads, HD, 128), f32),
            vmem((parts, depth), f32), vmem((rows, parts, width), bf16),
            vmem((rows, parts, width), bf16), vmem((count, depth), f32),
            vmem((heads, HD, 128), f32), vmem((rows, heads, HD, 128), f32),
            dma((heads, cols)), dma((heads, cols)), dma((rows,)), dma((rows,)),
            dma((rows,)), dma((rows,)), dma((heads,)),
        ] + sum_scratch(rows, chips, [small, (2, depth)]) + weight_scratch(
            rows, chips, [(units, width), (units, width), (head_cols, width)]
        ),
        compiler_params=pltpu.CompilerParams(
            vmem_limit_bytes=63 << 20, collective_id=2, has_side_effects=True
        ),
        cost_estimate=cost(40 * pairs * HD, 16 * heads * total * HD, pairs),
        name="backward",
    )(
        blocks, q, k, v, d_heads, out, lse, x, w_qkv, tokens, d_resid, gain, grad_up, grad_down,
        grad_out, early,
    )


def chunk_of(tokens):
    return tokens.shape[0]


def body(
    tokens, blocks, w_qkv, b_qv, w_out, b_out, w_up, b_up, w_down, b_down,
    gain1, shift1, gain2, shift2, grad_out,
):
    rows, cols = lax.axis_size("row"), lax.axis_size("col")
    depth = tokens.shape[1]
    head_cols = w_qkv.shape[2]
    heads = head_cols // HD
    units = w_up.shape[0]

    def vec(v):
        return v.reshape(1, -1)

    w_qkv_parts = w_qkv.transpose(1, 0, 2)

    (
        attn_rows, q, k, v, found, arrived, lse, block_ids, up_bias, out_weight, up_weight,
        down_weight,
    ) = front(
        tokens, gain1, shift1, b_up, vec(blocks), w_qkv_parts, b_qv, w_out, w_up,
        w_down, rows, cols,
    )
    grad_up, grad_down, grad_wout, output, d_resid, sums, d_heads, qkv_all = middle(
        arrived, tokens, grad_out, up_weight, down_weight, up_bias, b_out, gain2, shift2, b_down,
        out_weight, w_qkv_parts,
    )
    grad_tokens, grad_wup, grad_wdown, grad_wout, grad_wqkv, small, late, bias = backward(
        block_ids, q, k, v, d_heads, found, lse, attn_rows, qkv_all, tokens, d_resid, gain1,
        grad_up, grad_down, grad_wout, sums,
    )
    grad_wqkv = grad_wqkv.transpose(1, 0, 2)
    grad_bqv = bias[:, :, :2].reshape(head_cols, 2).T
    grad_bdown, grad_gain2, grad_shift2, grad_bout = small[:4]
    grad_bup = lax.dynamic_slice_in_dim(
        small[4:].reshape(-1), lax.axis_index("col") * units, units
    )
    grad_gain1, grad_shift1 = late
    return (
        output, grad_tokens, grad_wqkv, grad_bqv, grad_wout, grad_bout, grad_wup, grad_bup,
        grad_wdown, grad_bdown, grad_gain1, grad_shift1, grad_gain2, grad_shift2,
    )


def solution(mesh):
    tokens, weight, whole_vec = P(("row", "col"), None), P("col", "row"), P()
    qkv, bias_qv = P("row", None, "col"), P(None, "col")
    return jax.shard_map(
        body,
        mesh=mesh,
        in_specs=(
            tokens, P(("row", "col")), qkv, bias_qv, weight, whole_vec, weight, P("col"), weight,
            whole_vec, whole_vec, whole_vec, whole_vec, whole_vec, tokens,
        ),
        out_specs=(
            tokens, tokens, qkv, bias_qv, weight, whole_vec, weight, P("col"), weight,
            whole_vec, whole_vec, whole_vec, whole_vec, whole_vec,
        ),
        check_vma=False,
    )
```

```python
import functools

import jax
import jax.numpy as jnp
from jax import lax
from jax.experimental import pallas as pl
from jax.experimental.pallas import tpu as pltpu
from jax.sharding import PartitionSpec as P

HD = 64
SEQ_LEN = 4096
BLOCK = 256
EPS = 1e-05
SCALE = HD ** (-0.5)
SCALE2 = SCALE * 1.4426950408889634
MASKED = -1e30
ONES = 16
MESH = pl.DeviceIdType.MESH
VMEM_LIMIT = 60 << 20

f32 = jnp.float32
bf16 = jnp.bfloat16

NN = (((1,), (0,)), ((), ()))
NT = (((1,), (1,)), ((), ()))
TN = (((0,), (0,)), ((), ()))


def dot(a, b, dims=NN):
    return lax.dot_general(a, b, dims, preferred_element_type=f32)


def flip(x):
    return x.astype(f32).T.astype(bf16)


def params(**more):
    return pltpu.CompilerParams(vmem_limit_bytes=VMEM_LIMIT, **more)


def cost(flops, nbytes, transcendentals=0):
    return pl.CostEstimate(flops=flops, bytes_accessed=nbytes, transcendentals=transcendentals)


def whole(shape):
    return pl.BlockSpec(shape, lambda *_: (0,) * len(shape))


def moments(v):
    center = jnp.mean(v, axis=-1, keepdims=True)
    centered = v - center
    spread = jnp.mean(centered * centered, axis=-1, keepdims=True)
    inv = lax.rsqrt(spread + EPS)
    return centered * inv, inv


def norm_back(xhat, inv, e):
    return inv * (
        e - jnp.mean(e, axis=-1, keepdims=True) - xhat * jnp.mean(e * xhat, axis=-1, keepdims=True)
    )


def line(ref):
    return ref[...].astype(f32).reshape(1, -1)


def place():
    return lax.axis_index("row"), lax.axis_index("col")


def greet(rows, cols):
    row, col = place()
    barrier = pltpu.get_barrier_semaphore()

    def to_col(k, carry):
        pl.semaphore_signal(
            barrier, inc=1, device_id=(row, lax.rem(col + k, cols)), device_id_type=MESH
        )
        return carry

    def to_row(k, carry):
        pl.semaphore_signal(
            barrier, inc=1, device_id=(lax.rem(row + k, rows), col), device_id_type=MESH
        )
        return carry

    lax.fori_loop(1, cols, to_col, 0)
    lax.fori_loop(1, rows, to_row, 0)
    pl.semaphore_wait(barrier, rows + cols - 2)


def remote(src, dst, send, recv, device):
    return pltpu.make_async_remote_copy(
        src_ref=src, dst_ref=dst, send_sem=send, recv_sem=recv, device_id=device, device_id_type=MESH
    )


def each(count, act):
    def turn(k, carry):
        act(k)
        return carry

    lax.fori_loop(1, count, turn, 0)


class Exchange:
    def __init__(self, count, here, slot, to, out, into, send, recv):
        self.count, self.here, self.slot, self.to = count, here, slot, to
        self.out, self.into, self.send, self.recv = out, into, send, recv

    def copy(self, k):
        at = self.slot(k)
        return remote(
            self.out(at), self.into(self.here), self.send.at[k], self.recv.at[self.here], self.to(k)
        )

    def arrival(self, k):
        at = self.slot(k)
        return remote(self.out(at), self.into(at), self.send.at[k], self.recv.at[at], self.to(k))

    def start(self):
        each(self.count, lambda k: self.copy(k).start())

    def wait_recv(self):
        each(self.count, lambda k: self.arrival(k).wait_recv())

    def wait_send(self):
        each(self.count, lambda k: self.copy(k).wait_send())


def over_row(rows, out, into, send, recv):
    row, col = place()
    slot = lambda k: lax.rem(row + k, rows)
    return Exchange(rows, row, slot, lambda k: (slot(k), col), out, into, send, recv)


def over_col(cols, out, into, send, recv):
    row, col = place()
    slot = lambda k: lax.rem(col + k, cols)
    return Exchange(cols, col, slot, lambda k: (row, slot(k)), out, into, send, recv)


def over_line(chips, out, into, send, recv):
    row, col = place()
    chip, lane = col // 2, lax.rem(col, 2)
    slot = lambda k: lax.rem(chip + k, chips)
    return Exchange(chips, chip, slot, lambda k: (row, slot(k) * 2 + lane), out, into, send, recv)


class Plane:
    def __init__(self):
        row, col = place()
        lane = lax.rem(col, 2)
        self.next_x = row + 1 - 2 * lax.rem(row, 2)
        self.next_y = lax.rem(row + 2, 4)
        self.across = lax.rem(self.next_x + 2, 4)
        self.first = jnp.where(lane == 0, self.next_y, self.next_x)
        self.second = jnp.where(lane == 0, self.next_x, self.next_y)


def mate():
    row, col = place()
    return (row, col // 2 * 2 + 1 - lax.rem(col, 2))


def front_kernel(
    rows, cols, heads,
    tok_ref, gain_ref, shift_ref, bup_ref, blk_ref, wq_ref, bias_ref, wout_ref, wup_ref, wdown_ref,
    xo_ref, q_ref, k_ref, v_ref, found_ref, arrived_ref, lse_ref, blko_ref, bupo_ref,
    wouto_ref, wupo_ref, wdowno_ref,
    xs, wqs, qs, ks, vs, vt, totals, tops, founds, blks, bups,
    send_x, recv_x, send_q, recv_q, send_s, recv_s, send_f, recv_f,
    send_wz, recv_wz, send_wr, recv_wr, send_wm, recv_wm, local_x, local_q, local_f, local_w,
):
    chips = cols // 2
    row, me = place()
    chip, lane = me // 2, lax.rem(me, 2)
    count = tok_ref.shape[0]
    tile = 2 * count
    seq_chips = SEQ_LEN // tile
    depth = wq_ref.shape[1]
    width = heads * HD

    xhat, _ = moments(tok_ref[...].astype(f32))
    xs[me] = (xhat * line(gain_ref) + line(shift_ref)).astype(bf16)
    blks[me] = blk_ref[...]
    bups[me] = line(bup_ref).astype(bf16)
    own_rows = pl.ds(pl.multiple_of(row * depth, depth), depth)
    wqs[:, own_rows] = wq_ref[...]
    vt[:, HD:, :] = jnp.ones((heads, ONES, vt.shape[2]), bf16)
    greet(rows, cols)

    def chunk(owner, target, route, at):
        return remote(
            xs.at[owner], xs.at[owner], send_x.at[route, at], recv_x.at[route, at], (row, target)
        )

    def to_mate(owner, at):
        return remote(xs.at[owner], xs.at[owner], send_x.at[2, at], recv_x.at[2, at], mate())

    given = (wout_ref, wup_ref, wdown_ref)
    gathered = (wouto_ref, wupo_ref, wdowno_ref)

    q_stage = over_row(
        rows,
        lambda at: wq_ref,
        lambda at: wqs.at[:, pl.ds(pl.multiple_of(at * depth, depth), depth)],
        send_q,
        recv_q,
    )
    small = [
        over_col(cols, lambda at: blk_ref, lambda at: blks.at[at], send_s.at[0], recv_s.at[0]),
        over_col(
            cols, lambda at: bups.at[me], lambda at: bups.at[at], send_s.at[1], recv_s.at[1]
        ),
    ]
    f_stage_out = lambda at: founds.at[at]
    f_stage = over_col(cols, f_stage_out, lambda at: arrived_ref.at[at], send_f, recv_f)

    def w_line(n, at, to, route):
        block = gathered[n].at[lane, at, row]
        out = given[n] if at is chip else block
        return remote(
            out, block, send_wz.at[n, route, at], recv_wz.at[n, at], (row, to * 2 + lane)
        )

    def w_row(n, c, out):
        return over_row(
            rows, lambda at: out, lambda at: gathered[n].at[lane, c, at], send_wr.at[n, c],
            recv_wr.at[n, c],
        )

    square = rows == 4
    plane = Plane()
    next_x, next_y, across_x = plane.next_x, plane.next_y, plane.across
    relayed, relay_to = plane.first, plane.second

    def w_step(n, c, slot, k, to):
        block = gathered[n].at[lane, c, slot]
        out = given[n] if (slot is row and c is chip) else block
        return remote(out, block, send_wr.at[n, c, k], recv_wr.at[n, c, slot], (to, me))

    def rows_start(n, c):
        if square:
            w_step(n, c, row, 0, next_x).start()
            w_step(n, c, row, 1, next_y).start()
        else:
            w_row(n, c, given[n] if c is chip else gathered[n].at[lane, c, row]).start()

    def rows_relay(n, c):
        if square:
            w_step(n, c, relayed, 2, relay_to).wait_recv()
            w_step(n, c, relayed, 2, relay_to).start()

    def rows_wait_recv(n, c):
        if square:
            w_step(n, c, relay_to, 0, next_x).wait_recv()
            w_step(n, c, across_x, 0, next_x).wait_recv()
        else:
            w_row(n, c, given[n]).wait_recv()

    def rows_wait_send(n, c):
        if square:
            for k in range(3):
                w_step(n, c, row, k, next_x).wait_send()
        else:
            w_row(n, c, given[n]).wait_send()

    def w_own(n):
        return pltpu.make_async_copy(given[n], gathered[n].at[lane, chip, row], local_w.at[n])

    def w_mate(n, c, side):
        block = gathered[n].at[side, c]
        return remote(block, block, send_wm.at[n, c], recv_wm.at[n, c], mate())

    to_mate(me, chip).start()
    q_stage.start()
    for exchange in small:
        exchange.start()

    @pl.when(chip + 1 < chips)
    def _():
        for n in range(3):
            w_line(n, chip, chip + 1, 0).start()
        chunk(me, me + 2, 0, chip).start()

    @pl.when(chip > 0)
    def _():
        for n in range(3):
            w_line(n, chip, chip - 1, 1).start()
        chunk(me, me - 2, 1, chip).start()

    for n in range(3):
        w_own(n).start()
        rows_start(n, chip)
    q_stage.wait_recv()
    for exchange in small:
        exchange.wait_recv()

    def update(h, q_tile, q_low, q_count, key_start, key_count, mask):
        lanes = pl.ds(q_low, q_count)
        query = qs[h, pl.ds(pl.multiple_of(q_tile * tile + q_low, BLOCK), q_count), :]
        keys = pl.ds(pl.multiple_of(key_start, BLOCK), key_count)
        scores = dot(ks[h, keys, :], query, NT)
        if mask is not None:
            scores = jnp.where(mask, scores, MASKED)
        top = tops[h, q_tile, :, lanes]
        higher = jnp.maximum(top, jnp.max(scores, axis=0, keepdims=True) * SCALE2)
        probs = jnp.exp2(scores * SCALE2 - higher)
        part = dot(vt[h, :, keys], probs.astype(bf16))
        totals[h, q_tile, :, lanes] = totals[h, q_tile, :, lanes] * jnp.exp2(top - higher) + part
        tops[h, q_tile, :, lanes] = higher

    def column(blocks, amount):
        return jnp.broadcast_to(blocks, (128, amount)).T[:, :1]

    def diagonal(p):
        low, high = blks[2 * p], blks[2 * p + 1]
        first = column(jnp.concatenate([low, high[:, :BLOCK]], axis=1), count + BLOCK)
        second = column(jnp.concatenate([low, high], axis=1), tile)
        for h in range(heads):
            update(h, p, 0, count, p * tile, count + BLOCK, low >= first)
            update(h, p, count, count, p * tile, tile, high >= second)

    def boundary(p):
        mask = blks[2 * p + 1][:, count - BLOCK :] >= column(blks[2 * p + 2][:, :BLOCK], BLOCK)
        for h in range(heads):
            update(h, p, tile - BLOCK, BLOCK, (p + 1) * tile, BLOCK, mask)

    def project(p):
        both = jnp.concatenate([xs[2 * p], xs[2 * p + 1]], axis=0)
        mixed = dot(both, jnp.concatenate([wqs[j] for j in range(3)], axis=1))
        bias = bias_ref[...].astype(f32)
        where = pl.ds(pl.multiple_of(p * tile, tile), tile)
        for h in range(heads):
            at = [slice(j * width + h * HD, j * width + (h + 1) * HD) for j in range(3)]
            here = slice(h * HD, (h + 1) * HD)
            qs[h, where, :] = (mixed[:, at[0]] + bias[0:1, here]).astype(bf16)
            ks[h, where, :] = mixed[:, at[1]].astype(bf16)
            values = (mixed[:, at[2]] + bias[1:2, here]).astype(bf16)
            vs[h, where, :] = values
            vt[h, :HD, where] = flip(values)
            totals[h, p] = jnp.zeros(totals.shape[2:], f32)
            tops[h, p] = jnp.full(tops.shape[2:], MASKED, f32)

    def keep(p):
        where = pl.ds(pl.multiple_of(p * tile, tile), tile)
        pairs = [
            pltpu.make_async_copy(held.at[:, where, :], out.at[:, where, :], local_q.at[n, p])
            for n, (held, out) in enumerate(((qs, q_ref), (ks, k_ref), (vs, v_ref)))
        ]
        return pairs + [
            pltpu.make_async_copy(xs.at[2 * p + c], xo_ref.at[2 * p + c], local_x.at[2 * p + c])
            for c in range(2)
        ]

    def kept(c):
        return pltpu.make_async_copy(founds.at[c], found_ref.at[c], local_f.at[0, c])

    def own(c):
        return pltpu.make_async_copy(founds.at[c], arrived_ref.at[c], local_f.at[1, 0])

    def conclude(p):
        for h in range(heads):
            mass = totals[h, p, HD : HD + 1, :]
            out = (totals[h, p, :HD, :] / mass).astype(bf16)
            for c in range(2):
                founds[2 * p + c, h * HD : (h + 1) * HD, :] = out[:, c * count : (c + 1) * count]
            lse_ref[
                h, p // seq_chips, :, pl.ds(pl.multiple_of(lax.rem(p, seq_chips) * tile, tile), tile)
            ] = tops[h, p] + jnp.log2(mass)
        for c in range(2):
            owner = 2 * p + c
            kept(owner).start()

            @pl.when(owner == me)
            def _():
                own(owner).start()

            @pl.when(owner != me)
            def _():
                f_stage.copy(lax.rem(owner - me + cols, cols)).start()

    def at_distance(hop, act):
        for at, step, route in ((chip - hop, 1, 0), (chip + hop, -1, 1)):

            @pl.when((at >= 0) & (at < chips))
            def _():
                act(at, chip + step, route)

    def w_arrive(at, onward, route):
        for n in range(3):
            w_line(n, at, onward, route).wait_recv()

            @pl.when((onward >= 0) & (onward < chips))
            def _():
                w_line(n, at, onward, route).start()

            rows_start(n, at)

    def w_relay(at, onward=None, route=None):
        for n in range(3):
            rows_relay(n, at)

    def w_pass(at, onward=None, route=None):
        for n in range(3):
            rows_wait_recv(n, at)
            w_mate(n, at, lane).start()

    def ahead(hop):
        if hop == 1:
            at_distance(1, w_arrive)
        else:
            if hop == 2:
                w_relay(chip)
            at_distance(hop - 1, w_relay)
        if hop == chips - 1:
            for n in range(3):
                w_own(n).wait()
            w_pass(chip)
            for near in range(1, chips - 2):
                at_distance(near, w_pass)

    def event(e, carry):
        hop = (e + 1) // 2
        lower = lax.rem(e, 2) == 1
        p = jnp.where(lower, chip - hop, chip + hop)

        for stage in range(1, chips):

            @pl.when(e == 2 * stage - 1)
            def _():
                ahead(stage)

        @pl.when(lower)
        def _():
            below, above = chip - hop, chip + hop

            @pl.when(below >= 0)
            def _():
                owner = below * 2 + lane
                chunk(owner, me, 0, below).wait_recv()

                @pl.when(chip + 1 < chips)
                def _():
                    chunk(owner, me + 2, 0, below).start()

                to_mate(owner, below).start()

            @pl.when(above < chips)
            def _():
                owner = above * 2 + lane
                chunk(owner, me, 1, above).wait_recv()

                @pl.when(chip > 0)
                def _():
                    chunk(owner, me - 2, 1, above).start()

                to_mate(owner, above).start()

        for stage in range(2, chips - 1):

            @pl.when(e == 2 * stage - 1)
            def _():
                at_distance(stage, w_arrive)

        @pl.when((p >= 0) & (p < chips))
        def _():
            to_mate(2 * p + 1 - lane, p).wait_recv()
            project(p)
            for copy in keep(p):
                copy.start()
            first = p // seq_chips * seq_chips
            final = first + seq_chips - 1
            high = jnp.minimum(chip + hop - 1, final)
            low = jnp.maximum(jnp.maximum(chip - hop, 0), first)
            diagonal(p)

            @pl.when(lower & (p < final))
            def _():
                boundary(p)

            @pl.when(lower & (p == first))
            def _():
                conclude(p)

            @pl.when(jnp.logical_not(lower) & (p > first) & (hop > 0))
            def _():
                boundary(p - 1)

                @pl.when(low == first)
                def _():
                    conclude(p - 1)

            amount = jnp.where(lower, high - p, p - low)

            def pair(j, carry):
                q_tile = jnp.where(lower, p + 1 + j, p)
                key_tile = jnp.where(lower, p, low + j)

                @pl.when((hop == chips - 1) & (j == amount - 2))
                def _():
                    at_distance(chips - 1, w_arrive)

                for h in range(heads):
                    update(h, q_tile, 0, tile, key_tile * tile, tile, None)

                @pl.when(lower & (p == first) & ((q_tile == final) | (q_tile < high)))
                def _():
                    conclude(q_tile)

                return carry

            lax.fori_loop(0, amount, pair, 0)

            @pl.when(jnp.logical_not(lower) & (p == final) & (low == first))
            def _():
                conclude(p)

        return carry

    lax.fori_loop(0, 2 * chips - 1, event, 0)
    at_distance(chips - 2, w_pass)
    at_distance(chips - 1, w_relay)
    at_distance(chips - 1, w_pass)

    for c in range(cols):
        bupo_ref[c] = bups[c]
        at = c * count
        blko_ref[at // SEQ_LEN, :, at % SEQ_LEN : at % SEQ_LEN + count] = blks[c]
    f_stage.wait_recv()
    for c in range(chips):
        for n in range(3):
            w_mate(n, c, 1 - lane).wait_recv()
            w_mate(n, c, lane).wait_send()
            rows_wait_send(n, c)

            @pl.when((c <= chip) & (chip + 1 < chips))
            def _():
                w_line(n, c, chip, 0).wait_send()

            @pl.when((c >= chip) & (chip > 0))
            def _():
                w_line(n, c, chip, 1).wait_send()

        for copy in keep(c):
            copy.wait()
        kept(2 * c).wait()
        kept(2 * c + 1).wait()
        to_mate(me, c).wait_send()

        @pl.when((c <= chip) & (chip + 1 < chips))
        def _():
            chunk(me, me, 0, c).wait_send()

        @pl.when((c >= chip) & (chip > 0))
        def _():
            chunk(me, me, 1, c).wait_send()

    own(me).wait()
    f_stage.wait_send()
    q_stage.wait_send()
    for exchange in small:
        exchange.wait_send()


def front(tokens, gain, shift, b_up, blocks, w_qkv, b_qv, w_out, w_up, w_down, rows, cols):
    count, depth = tokens.shape
    head_cols = w_qkv.shape[2]
    heads = head_cols // HD
    chips = cols // 2
    total = count * cols
    tile = 2 * count
    any_space = pl.BlockSpec(memory_space=pl.ANY)
    in_vmem = pl.BlockSpec(memory_space=pltpu.VMEM)
    dma, vmem, shape = pltpu.SemaphoreType.DMA, pltpu.VMEM, jax.ShapeDtypeStruct
    pairs = heads * total * SEQ_LEN * 5 // 8
    held = (heads, total, HD)
    return pl.pallas_call(
        functools.partial(front_kernel, rows, cols, heads),
        in_specs=[in_vmem] * 10,
        out_specs=[any_space] * 6 + [in_vmem] * 3 + [any_space] * 3,
        out_shape=[
            shape((cols, count, depth), bf16), shape(held, bf16), shape(held, bf16),
            shape(held, bf16), shape((cols, head_cols, count), bf16),
            shape((cols, head_cols, count), bf16),
            shape((heads, total // SEQ_LEN, 1, SEQ_LEN), f32),
            shape((total // SEQ_LEN, 1, SEQ_LEN), jnp.int32), shape((cols, 1) + b_up.shape, bf16),
        ] + [shape((2, chips, rows) + w.shape, bf16) for w in (w_out, w_up, w_down)],
        scratch_shapes=[
            vmem((cols, count, depth), bf16), vmem((3, depth, head_cols), bf16),
            vmem(held, bf16), vmem(held, bf16), vmem(held, bf16),
            vmem((heads, HD + ONES, total), bf16),
            vmem((heads, chips, HD + ONES, tile), f32), vmem((heads, chips, 1, tile), f32),
            vmem((cols, head_cols, count), bf16), vmem((cols,) + blocks.shape, jnp.int32),
            vmem((cols, 1) + b_up.shape, bf16),
            dma((3, chips)), dma((3, chips)), dma((rows,)), dma((rows,)),
            dma((2, cols)), dma((2, cols)), dma((cols,)), dma((cols,)),
            dma((3, 2, chips)), dma((3, chips)), dma((3, chips, rows)), dma((3, chips, rows)),
            dma((3, chips)), dma((3, chips)),
            dma((cols,)), dma((3, chips)), dma((2, cols)), dma((3,)),
        ],
        compiler_params=pltpu.CompilerParams(
            vmem_limit_bytes=63 << 20, collective_id=0, has_side_effects=True
        ),
        cost_estimate=cost(16 * pairs * HD, 16 * heads * total * HD, pairs),
        name="front",
    )(tokens, gain, shift, b_up, blocks, w_qkv, b_qv, w_out, w_up, w_down)


def tile_mask(blk_ref, key_start, count, query_blocks):
    key_blocks = jnp.broadcast_to(blk_ref[0, :, pl.ds(key_start, count)], (128, count)).T[:, :1]
    return query_blocks >= key_blocks


GELU_A = 0.7978845608028654
GELU_B = 0.044715


def middle_kernel(
    rows, cols,
    heads_ref, tok_ref, g_ref, up_ref, down_ref, bup_ref, bout_ref, gain_ref, shift_ref, bdown_ref,
    wout_ref, wq_ref,
    gup_ref, gdown_ref, gout_ref, output_ref, dres_ref, sums_ref, dheads_ref, wqo_ref,
    x, heads_all, resid, out_acc, norm_acc, hiddens, d_ups, low, d_send,
    mine, other, out_mine, out_other,
    send_d, recv_d, send_p, recv_p, send_o, recv_o, send_z, recv_z, send_r, recv_r, send_m, recv_m,
    local,
):
    step = pl.program_id(0)
    chips = cols // 2
    row, col = place()
    chip, lane = col // 2, lax.rem(col, 2)
    width = up_ref.shape[4]
    depth = wout_ref.shape[3]

    def part(r):
        return slice(r * width, (r + 1) * width)

    def out_weight(r):
        return jnp.concatenate([wout_ref[c % 2, c // 2, r] for c in range(cols)], axis=0)

    z_stage = over_line(
        chips, lambda at: wq_ref, lambda at: wqo_ref.at[lane, row, at], send_z, recv_z
    )

    def r_stage(c, out=None):
        return over_row(
            rows,
            lambda at: wqo_ref.at[lane, row, c] if out is None else out,
            lambda at: wqo_ref.at[lane, at, c],
            send_r.at[c],
            recv_r.at[c],
        )

    m_stage = remote(wqo_ref.at[lane], wqo_ref.at[lane], send_m, recv_m, mate())
    m_arrival = remote(wqo_ref.at[1 - lane], wqo_ref.at[1 - lane], send_m, recv_m, mate())
    own_wq = pltpu.make_async_copy(wq_ref, wqo_ref.at[lane, row, chip], local.at[0])
    d_stage = over_col(
        cols, lambda at: d_send.at[at], lambda at: dheads_ref.at[at], send_d, recv_d
    )
    own_d = pltpu.make_async_copy(d_send.at[col], dheads_ref.at[col], local.at[1])

    def pair(at, which):
        return remote(
            mine.at[which, at], other.at[which, at], send_p.at[which, at], recv_p.at[which, at],
            mate(),
        )

    pair_out = remote(out_mine, out_other, send_o, recv_o, mate())

    @pl.when(step == 0)
    def _():
        greet(rows, cols)
        own_wq.start()
        z_stage.start()
        r_stage(chip, wq_ref).start()
        for s in range(cols):
            heads_all[s * depth : (s + 1) * depth] = heads_ref[s]
        stacked = flip(heads_all[...])
        for r in range(rows):
            branch = dot(stacked, out_weight(r))
            resid[:, part(r)] = tok_ref[:, part(r)].astype(f32) + branch + line(bout_ref)[:, part(r)]
        xhat, _ = moments(resid[...])
        x[...] = (xhat * line(gain_ref) + line(shift_ref)).astype(bf16)
        out_acc[...] = jnp.zeros_like(out_acc)
        norm_acc[...] = jnp.zeros_like(norm_acc)

    @pl.when(step == cols * 6 // 8)
    def _():
        own_wq.wait()
        z_stage.wait_recv()
        each(chips, lambda k: r_stage(lax.rem(chip + k, chips)).start())

    @pl.when(step < cols)
    def _():
        up = bup_ref[0].astype(f32)
        d_hidden = 0.0
        for r in range(rows):
            up = up + dot(x[:, part(r)], up_ref[0, 0, r], NT)
            d_hidden = d_hidden + dot(g_ref[:, part(r)], down_ref[0, 0, r], NT)
        square = up * up
        bent = jnp.tanh(GELU_A * up * (1.0 + GELU_B * square))
        half = 0.5 + 0.5 * bent
        hidden = (up * half).astype(bf16)
        slope = half + (0.5 * GELU_A) * up * (1.0 - bent * bent) * (1.0 + (3.0 * GELU_B) * square)
        d_up = d_hidden * slope
        units = d_up.shape[1]
        per = sums_ref.shape[1] // units
        lanes = pl.ds(pl.multiple_of(lax.rem(step, per) * units, units), units)
        sums_ref[pl.ds(4 + step // per, 1), lanes] = jnp.sum(d_up, axis=0, keepdims=True)
        d_up = d_up.astype(bf16)
        hiddens[step] = hidden
        d_ups[step] = d_up
        for r in range(rows):
            norm_acc[:, part(r)] += dot(d_up, up_ref[0, 0, r])

    @pl.when(step == cols - 1)
    def _():
        xhat, inv = moments(resid[...])
        d_norm = norm_acc[...]
        grad = g_ref[...].astype(f32)
        d_resid = grad + norm_back(xhat, inv, d_norm * line(gain_ref))
        dres_ref[...] = d_resid
        low[...] = d_resid.astype(bf16)
        sums_ref[0:1] = jnp.sum(grad, axis=0, keepdims=True)
        sums_ref[1:2] = jnp.sum(d_norm * xhat, axis=0, keepdims=True)
        sums_ref[2:3] = jnp.sum(d_norm, axis=0, keepdims=True)
        sums_ref[3:4] = jnp.sum(d_resid, axis=0, keepdims=True)
        found = 0.0
        for r in range(rows):
            found = found + dot(out_weight(r), low[:, part(r)], NT)
        found = found.astype(bf16)
        for c in range(cols):
            d_send[c] = found[c * depth : (c + 1) * depth]
        own_d.start()
        d_stage.start()
        found = dot(heads_all[...], low[...])
        for c in range(chips):
            first = found[2 * c * depth : (2 * c + 1) * depth]
            second = found[(2 * c + 1) * depth : (2 * c + 2) * depth]
            out_mine[c] = jnp.where(lane == 0, second, first).astype(bf16)
            kept = jnp.where(lane == 0, first, second)
            for r in range(rows):
                norm_acc[c * depth : (c + 1) * depth, part(r)] = kept[:, part(r)]
        pair_out.start()

    at = step - cols

    @pl.when(at >= 0)
    def _():
        for r in range(rows):
            out_acc[:, part(r)] += dot(hiddens[at], down_ref[0, 0, r])

    @pl.when((at >= 0) & (at < chips))
    def _():
        c = at * 2 + 1 - lane
        mine[0, at] = dot(hiddens[c], g_ref[...], TN).astype(bf16)
        pair(at, 0).start()
        mine[1, at] = dot(d_ups[c], x[...], TN).astype(bf16)
        pair(at, 1).start()

    @pl.when(step == 2 * cols - 1)
    def _():
        for c in range(chips):
            r_stage(c).wait_recv()
        m_stage.start()

    @pl.when(at >= chips)
    def _():
        k = at - chips
        c = k * 2 + lane
        grad_down = dot(hiddens[c], g_ref[...], TN)
        pair(k, 0).wait_recv()
        grad_down = (grad_down + other[0, k].astype(f32)).astype(bf16)
        grad_up = dot(d_ups[c], x[...], TN)
        pair(k, 1).wait_recv()
        grad_up = (grad_up + other[1, k].astype(f32)).astype(bf16)
        for r in range(rows):
            gdown_ref[r, 0] = grad_down[:, part(r)]
            gup_ref[r, 0] = grad_up[:, part(r)]

    @pl.when(step == 2 * cols - 1)
    def _():
        output_ref[...] = (resid[...] + out_acc[...] + line(bdown_ref)).astype(bf16)
        pair_out.wait_recv()
        for c in range(chips):
            for r in range(rows):
                kept = norm_acc[c * depth : (c + 1) * depth, part(r)]
                gout_ref[r, c] = (kept + out_other[c, :, part(r)].astype(f32)).astype(bf16)
        d_stage.wait_recv()
        m_arrival.wait_recv()
        pair_out.wait_send()
        for k in range(chips):
            pair(k, 0).wait_send()
            pair(k, 1).wait_send()
            r_stage(k).wait_send()
        z_stage.wait_send()
        d_stage.wait_send()
        m_stage.wait_send()
        own_d.wait()


def middle(heads, tokens, grad, w_up, w_down, b_up, b_out, gain, shift, b_down, w_out, w_qkv):
    count, depth = tokens.shape
    _, chips, rows, units, width = w_up.shape
    cols = 2 * chips
    head_cols = w_out.shape[3]
    sum_rows = 4 + cols * units // depth
    any_space = pl.BlockSpec(memory_space=pl.ANY)

    def weight_map(s):
        c = jnp.minimum(s, cols - 1)
        return (lax.rem(c, 2), c // 2, 0, 0, 0)

    def again_map(s):
        c = lax.rem(s, cols)
        return (lax.rem(c, 2), c // 2, 0, 0, 0)

    weight = pl.BlockSpec((1, 1, rows, units, width), weight_map)
    again = pl.BlockSpec((1, 1, rows, units, width), again_map)
    grad_spec = pl.BlockSpec(
        (rows, 1, units, width), lambda s: (0, jnp.maximum(s - cols - chips, 0), 0, 0)
    )
    grad_shape = jax.ShapeDtypeStruct((rows, chips, units, width), bf16)
    bias = pl.BlockSpec((1, 1, units), lambda s: (jnp.minimum(s, cols - 1), 0, 0))
    block = whole((count, depth))
    dma = pltpu.SemaphoreType.DMA
    vmem = pltpu.VMEM
    return pl.pallas_call(
        functools.partial(middle_kernel, rows, cols),
        grid=(2 * cols,),
        in_specs=[
            whole(heads.shape), block, block, weight, again, bias, *[whole((depth,))] * 4,
            whole(w_out.shape), any_space,
        ],
        out_specs=[
            grad_spec, grad_spec, whole((rows, chips, head_cols, width)), block, block,
            whole((sum_rows, depth)), any_space, any_space,
        ],
        out_shape=[
            grad_shape, grad_shape,
            jax.ShapeDtypeStruct((rows, chips, head_cols, width), bf16),
            jax.ShapeDtypeStruct((count, depth), bf16),
            jax.ShapeDtypeStruct((count, depth), f32),
            jax.ShapeDtypeStruct((sum_rows, depth), f32),
            jax.ShapeDtypeStruct((cols, head_cols, count), bf16),
            jax.ShapeDtypeStruct((2, rows, chips) + w_qkv.shape, bf16),
        ],
        scratch_shapes=[
            vmem((count, depth), bf16), vmem((depth, count), bf16),
            vmem((count, depth), f32), vmem((count, depth), f32), vmem((count, depth), f32),
            vmem((cols, count, units), bf16), vmem((cols, count, units), bf16),
            vmem((count, depth), bf16), vmem((cols, head_cols, count), bf16),
            vmem((2, chips, units, depth), bf16), vmem((2, chips, units, depth), bf16),
            vmem((chips, head_cols, depth), bf16), vmem((chips, head_cols, depth), bf16),
            dma((cols,)), dma((cols,)), dma((2, chips)), dma((2, chips)), dma, dma,
            dma((chips,)), dma((chips,)), dma((chips, rows)), dma((chips, rows)), dma, dma,
            dma((2,)),
        ],
        compiler_params=pltpu.CompilerParams(
            vmem_limit_bytes=63 << 20, collective_id=1, has_side_effects=True
        ),
        cost_estimate=cost(
            12 * count * depth * cols * units, 8 * depth * cols * units + 16 * count * depth
        ),
        name="middle",
    )(heads, tokens, grad, w_up, w_down, b_up, b_out, gain, shift, b_down, w_out, w_qkv)


class SmallSum:
    def __init__(self, rows, chips, scratch):
        row, col = place()
        self.rows, self.chips, self.row, self.chip = rows, chips, row, col // 2
        self.held, self.core, self.by_row, self.by_line, *sems = scratch
        held = self.held
        self.stages = [
            remote(held.at[0], self.core, sems[0], sems[1], mate()),
            over_row(
                rows, lambda at: held.at[1], lambda at: self.by_row.at[at], sems[2], sems[3]
            ),
            over_line(
                chips, lambda at: held.at[2], lambda at: self.by_line.at[at], sems[4], sems[5]
            ),
        ]

    def first(self, value):
        self.held[0] = value
        self.stages[0].start()

    def second(self):
        self.stages[0].wait_recv()
        value = self.held[0] + self.core[...]
        self.held[1] = value
        self.by_row[self.row] = value
        self.stages[1].start()

    def third(self):
        self.stages[1].wait_recv()
        value = sum(self.by_row[r] for r in range(1, self.rows)) + self.by_row[0]
        self.held[2] = value
        self.by_line[self.chip] = value
        self.stages[2].start()

    def result(self):
        self.stages[2].wait_recv()
        return sum(self.by_line[c] for c in range(1, self.chips)) + self.by_line[0]

    def wait_send(self):
        for stage in self.stages:
            stage.wait_send()


def sum_scratch(rows, chips, shapes):
    dma, vmem = pltpu.SemaphoreType.DMA, pltpu.VMEM
    found = []
    for shape in shapes:
        found += [
            vmem((3,) + shape, f32), vmem(shape, f32), vmem((rows,) + shape, f32),
            vmem((chips,) + shape, f32), dma, dma, dma((rows,)), dma((rows,)), dma((chips,)),
            dma((chips,)),
        ]
    return found


SUM_REFS = 10


def add_into(into, other):
    into[...] = (into[...].astype(f32) + other[...].astype(f32)).astype(bf16)


class HalvedSum:
    REFS = 16

    @staticmethod
    def scratch(rows, chips, block):
        dma, vmem = pltpu.SemaphoreType.DMA, pltpu.VMEM
        return [
            vmem((2, chips) + block, bf16), vmem((2, chips) + block, bf16),
            vmem((chips,) + block, bf16), vmem((2,) + block, bf16), vmem(block, bf16),
            dma((2,)), dma((2,)), dma((2,)), dma, dma, dma((2,)), dma((2,)), dma, dma,
        ]

    def __init__(self, rows, chips, given, scratch):
        self.own, self.came, self.came_row, self.came_line, self.came_far, *sems = scratch
        local, send_a, recv_a, send_b, recv_b, send_c, recv_c, send_d, recv_d = sems
        row, col = place()
        plane = Plane()
        chip, lane = col // 2, lax.rem(col, 2)
        near = chip + 1 - 2 * lax.rem(chip, 2)
        self.chip, self.far = chip, lax.rem(chip + 2, 4)
        own = self.own
        self.loads = [
            pltpu.make_async_copy(given.at[at], own.at[k], local.at[k])
            for k, at in enumerate((row, plane.second))
        ]
        self.a = [
            remote(given.at[at], self.came.at[k], send_a.at[k], recv_a.at[k], (plane.first, col))
            for k, at in enumerate((plane.first, plane.across))
        ]
        self.b = [remote(own.at[1], self.came_row, send_b, recv_b, (plane.second, col))]
        self.c = [
            remote(
                own.at[0, at], self.came_line.at[k], send_c.at[k], recv_c.at[k],
                (row, near * 2 + lane),
            )
            for k, at in enumerate((near, lax.rem(near + 2, 4)))
        ]
        self.d = [
            remote(own.at[0, self.far], self.came_far, send_d, recv_d, (row, self.far * 2 + lane))
        ]

    def begin(self):
        for copy in self.a + self.loads:
            copy.start()

    def step(self, n):
        if n == 0:
            for copy in self.loads:
                copy.wait()
            for copy in self.a:
                copy.wait_recv()
            for k in (1, 0):
                for c in range(self.own.shape[1]):
                    add_into(self.own.at[k, c], self.came.at[k, c])
                if k == 1:
                    self.b[0].start()
        elif n == 1:
            self.b[0].wait_recv()
            for c in range(self.own.shape[1]):
                add_into(self.own.at[0, c], self.came_row.at[c])
            for copy in self.c:
                copy.start()
        else:
            for copy in self.c:
                copy.wait_recv()
            add_into(self.own.at[0, self.far], self.came_line.at[1])
            self.d[0].start()
            add_into(self.own.at[0, self.chip], self.came_line.at[0])

    def result(self):
        self.d[0].wait_recv()
        return self.own[0, self.chip].astype(f32) + self.came_far[...].astype(f32)

    def wait_send(self):
        for copy in self.a + self.b + self.c + self.d:
            copy.wait_send()


class DirectSum:
    @staticmethod
    def scratch(rows, chips, block):
        dma, vmem = pltpu.SemaphoreType.DMA, pltpu.VMEM
        return [
            vmem((rows, chips) + block, bf16), vmem((chips,) + block, bf16),
            vmem((chips,) + block, bf16),
            dma, dma((rows,)), dma((rows,)), dma((chips,)), dma((chips,)),
        ]

    def __init__(self, rows, chips, given, scratch):
        by_row, total, by_line, local, send_r, recv_r, send_l, recv_l = scratch
        row, col = place()
        self.rows, self.chips, self.chip = rows, chips, col // 2
        self.by_row, self.total, self.by_line = by_row, total, by_line
        self.load = pltpu.make_async_copy(given.at[row], by_row.at[row], local)
        self.r = over_row(
            rows, lambda at: given.at[at], lambda at: by_row.at[at], send_r, recv_r
        )
        self.l = over_line(
            chips, lambda at: total.at[at], lambda at: by_line.at[at], send_l, recv_l
        )

    def begin(self):
        self.load.start()
        self.r.start()

    def step(self, n):
        if n != 1:
            return
        self.load.wait()
        self.r.wait_recv()

        def one(c, carry):
            total = self.by_row[0, c].astype(f32)
            for r in range(1, self.rows):
                total = total + self.by_row[r, c].astype(f32)
            self.total[c] = total.astype(bf16)
            return carry

        lax.fori_loop(0, self.chips, one, 0)
        self.by_line[self.chip] = self.total[self.chip]
        self.l.start()

    def result(self):
        self.l.wait_recv()
        total = self.by_line[0].astype(f32)
        for c in range(1, self.chips):
            total = total + self.by_line[c].astype(f32)
        return total

    def wait_send(self):
        self.r.wait_send()
        self.l.wait_send()


def weight_sum(rows, chips):
    return HalvedSum if (rows, chips) == (4, 4) else DirectSum


def weight_scratch(rows, chips, blocks):
    return [ref for block in blocks for ref in weight_sum(rows, chips).scratch(rows, chips, block)]


def back_kernel(
    rows, cols, heads, seqs, tiles, sub,
    blk_ref, q_ref, k_ref, v_ref, do_ref, o_ref, lse_ref, x_ref, w_ref, tok_ref, dres_ref, gain_ref,
    gup_ref, gdown_ref, gout_ref, early_ref,
    dtok_ref, wup_ref, wdown_ref, wout_ref, wqkv_ref, all_ref, late_ref, bias_ref,
    d_mixed, d_arrived, key_grad, value_grad, bias_sum, qkv_acc, qkv_send, qkv_recv, norm_acc,
    bias_send, bias_recv, send_d, recv_d, send_q, recv_q, send_b, recv_b, local_d, *rest,
):
    step = pl.program_id(0)
    chips = cols // 2
    row, col = place()
    work = heads * seqs * tiles
    last = work + 2 * cols - 1
    head = jnp.minimum(step // (seqs * tiles), heads - 1)
    seq = lax.rem(step // tiles, seqs)
    turn = lax.rem(step, tiles)
    i = tiles - 1 - turn
    tile = q_ref.shape[1]
    chunks, _, chunk = do_ref.shape
    chunks_seq = SEQ_LEN // chunk
    parts = tile // sub
    start = pl.multiple_of(i * tile, tile)

    early = SmallSum(rows, chips, rest[:SUM_REFS])
    late = SmallSum(rows, chips, rest[SUM_REFS : 2 * SUM_REFS])
    rest = rest[2 * SUM_REFS :]
    each_refs = len(rest) // 3
    weights = [
        weight_sum(rows, chips)(rows, chips, given, rest[n * each_refs : (n + 1) * each_refs])
        for n, given in enumerate((gdown_ref, gup_ref, gout_ref))
    ]
    results = (wdown_ref, wup_ref, wout_ref)

    def d_stage(h):
        return over_col(
            cols, lambda at: d_mixed.at[h, at], lambda at: d_arrived.at[h, at], send_d.at[h],
            recv_d.at[h],
        )

    def own_d(h):
        return pltpu.make_async_copy(d_mixed.at[h, col], d_arrived.at[h, col], local_d.at[h])

    q_stage = over_row(
        rows, lambda at: qkv_send.at[at], lambda at: qkv_recv.at[at], send_q, recv_q
    )
    b_stage = over_row(rows, lambda at: bias_send, lambda at: bias_recv.at[at], send_b, recv_b)

    def at_step(when, act):
        @pl.when(step == when)
        def _():
            act()

    @pl.when(step == 0)
    def _():
        greet(rows, cols)
        weights[0].begin()
        weights[2].begin()
        early.first(early_ref[...])

    at_step(work // 8, early.second)
    at_step(
        work * 3 // 8,
        lambda: (early.third(), weights[0].step(0), weights[2].step(0), weights[1].begin()),
    )
    at_step(work * 6 // 8, lambda: (weights[0].step(1), weights[2].step(1)))
    at_step(work, lambda: weights[1].step(0))
    at_step(work + cols // 2, lambda: (weights[0].step(2), weights[2].step(2)))

    @pl.when((step < work) & (turn == 0))
    def _():
        key_grad[...] = jnp.zeros_like(key_grad)
        value_grad[...] = jnp.zeros_like(value_grad)

    @pl.when((step < work) & (turn == 0) & (seq == 0))
    def _():
        bias_sum[head] = jnp.zeros((HD, 128), f32)

    def hand_over(c):
        where = pl.ds(pl.multiple_of(c * chunk, chunk), chunk)
        at = seq * chunks_seq + c
        d_mixed[head, at, HD : 2 * HD] = (key_grad[where, :].T * SCALE).astype(bf16)
        d_values = value_grad[where, :].T
        d_mixed[head, at, 2 * HD :] = d_values.astype(bf16)
        bias_sum[head, :, 1:2] += jnp.sum(d_values, axis=1, keepdims=True)

        @pl.when(at == col)
        def _():
            own_d(head).start()

        @pl.when(at != col)
        def _():
            d_stage(head).copy(lax.rem(at - col + cols, cols)).start()

    @pl.when(step < work)
    def _():
        d_out = jnp.concatenate([do_ref[b] for b in range(chunks)], axis=1)
        out = jnp.concatenate([o_ref[b] for b in range(chunks)], axis=1)
        delta = jnp.sum(d_out.astype(f32) * out.astype(f32), axis=0, keepdims=True)
        lse = lse_ref[0, 0]

        def cut(x, a):
            return x[:, a * sub : (a + 1) * sub]

        queries = [q_ref[0, a * sub : (a + 1) * sub, :] for a in range(parts)]
        query_blocks = [
            blk_ref[0, :, pl.ds(pl.multiple_of(start + a * sub, sub), sub)] for a in range(parts)
        ]

        def update(a, query_grad, key_start, count, masked):
            keys = k_ref[0, pl.ds(key_start, count), :]
            values = v_ref[0, pl.ds(key_start, count), :]
            scores = dot(keys, queries[a], NT) * SCALE2 - cut(lse, a)
            if masked:
                mask = tile_mask(blk_ref, key_start, count, query_blocks[a])
                scores = jnp.where(mask, scores, MASKED)
            probs = jnp.exp2(scores)
            d_values = dot(probs.astype(bf16), cut(d_out, a), NT)
            d_scores = (probs * (dot(values, cut(d_out, a)) - cut(delta, a))).astype(bf16)
            d_keys = dot(d_scores, queries[a])
            return query_grad + dot(keys, d_scores, TN), d_keys, d_values

        def add(key_start, count, d_keys, d_values):
            key_grad[pl.ds(key_start, count), :] += d_keys
            value_grad[pl.ds(key_start, count), :] += d_values

        def sweep(j, grads):
            key_start = pl.multiple_of(j * tile, tile)
            found = [update(a, grads[a], key_start, tile, False) for a in range(parts)]
            add(key_start, tile, sum(f[1] for f in found), sum(f[2] for f in found))
            return tuple(f[0] for f in found)

        grads = list(lax.fori_loop(0, i, sweep, (jnp.zeros((HD, sub), f32),) * parts))
        for a in range(parts):
            todo = [(pl.multiple_of(start + a * sub, sub), sub, True)]
            if a > 0:
                todo.append((start, a * sub, False))
            if a < parts - 1:
                todo.append((pl.multiple_of(start + (a + 1) * sub, BLOCK), BLOCK, True))
            for key_start, count, masked in todo:
                grads[a], d_keys, d_values = update(a, grads[a], key_start, count, masked)
                add(key_start, count, d_keys, d_values)

        def beyond(j, grad):
            key_start = pl.multiple_of(start + tile, BLOCK)
            grad, d_keys, d_values = update(parts - 1, grad, key_start, BLOCK, True)
            add(key_start, BLOCK, d_keys, d_values)
            return grad

        grads[-1] = lax.fori_loop(0, jnp.where(i < tiles - 1, 1, 0), beyond, grads[-1])
        query_grad = jnp.concatenate(grads, axis=1) * SCALE
        bias_sum[head, :, :1] += jnp.sum(query_grad, axis=1, keepdims=True)
        query_grad = query_grad.astype(bf16)
        for b in range(chunks):
            d_mixed[head, seq * chunks_seq + i * chunks + b, :HD] = query_grad[
                :, b * chunk : (b + 1) * chunk
            ]

    @pl.when((step < work) & (i == 0))
    def _():
        hand_over(0)

    @pl.when(step < work)
    def _():
        for b in range(1, chunks):
            hand_over(i * chunks + b)

    @pl.when((step < work) & (turn > 0))
    def _():
        hand_over((i + 1) * chunks)

    at = step - work

    @pl.when(at == 0)
    def _():
        qkv_acc[...] = jnp.zeros_like(qkv_acc)
        bias_send[...] = bias_sum[...]
        bias_recv[row] = bias_sum[...]
        b_stage.start()

    @pl.when((at >= 0) & (at < cols))
    def _():
        grads = jnp.concatenate([d_mixed[h, at] for h in range(heads)], axis=0)
        qkv_acc[...] += dot(grads, x_ref[0])

    @pl.when(at == cols - 1)
    def _():
        width = qkv_send.shape[2]
        for r in range(rows):
            qkv_send[r] = qkv_acc[:, r * width : (r + 1) * width].astype(bf16)
        qkv_recv[row] = qkv_send[row]
        q_stage.start()
        norm_acc[...] = jnp.zeros_like(norm_acc)

    @pl.when(at >= cols)
    def _():
        c = at - cols
        for h in range(heads):

            @pl.when(c == col)
            def _():
                own_d(h).wait()

            @pl.when(c != col)
            def _():
                d_stage(h).arrival(lax.rem(c - col + cols, cols)).wait_recv()

    at_step(work + cols, lambda: weights[1].step(1))

    @pl.when(at >= cols)
    def _():
        c = at - cols
        width = w_ref.shape[4]
        found = flip(
            jnp.concatenate(
                [
                    d_arrived[h, c, j * HD : (j + 1) * HD, :]
                    for j in range(3)
                    for h in range(heads)
                ],
                axis=0,
            )
        )
        for r in range(rows):
            norm_acc[:, r * width : (r + 1) * width] += dot(
                found, jnp.concatenate([w_ref[0, r, 0, j] for j in range(3)], axis=1), NT
            )

    @pl.when(step == last)
    def _():
        for n, stage in ((1, 2),):
            weights[n].step(stage)
        xhat, inv = moments(tok_ref[...].astype(f32))
        d_norm = norm_acc[...]
        late.first(
            jnp.concatenate(
                [
                    jnp.sum(d_norm * xhat, axis=0, keepdims=True),
                    jnp.sum(d_norm, axis=0, keepdims=True),
                ],
                axis=0,
            )
        )
        dtok_ref[...] = dres_ref[...] + norm_back(xhat, inv, d_norm * line(gain_ref))
        late.second()
        b_stage.wait_recv()
        bias_ref[...] = sum(bias_recv[r] for r in range(1, rows)) + bias_recv[0]
        all_ref[...] = early.result()
        late.third()
        q_stage.wait_recv()
        total = qkv_recv[0].astype(f32)
        for r in range(1, rows):
            total = total + qkv_recv[r].astype(f32)
        for j in range(3):
            part = [total[(h * 3 + j) * HD : (h * 3 + j + 1) * HD] for h in range(heads)]
            wqkv_ref[j] = jnp.concatenate(part, axis=0).T
        for weight, result in zip(weights, results):
            result[...] = weight.result()
        late_ref[...] = late.result()
        for weight in weights:
            weight.wait_send()
        for h in range(heads):
            d_stage(h).wait_send()
        q_stage.wait_send()
        b_stage.wait_send()
        early.wait_send()
        late.wait_send()


def backward(
    blocks, q, k, v, d_heads, out, lse, x, w_qkv, tokens, d_resid, gain, grad_up, grad_down,
    grad_out, early,
):
    heads, total, _ = q.shape
    count, depth = tokens.shape
    rows, chips, units, width = grad_up.shape
    cols = 2 * chips
    head_cols = grad_out.shape[2]
    seqs = total // SEQ_LEN
    tile, sub = 1024, 512
    tiles = SEQ_LEN // tile
    work = heads * seqs * tiles
    pairs = heads * seqs * SEQ_LEN * SEQ_LEN * 5 // 8

    def unpack(s):
        s = jnp.minimum(s, work - 1)
        return s // (seqs * tiles), lax.rem(s // tiles, seqs), tiles - 1 - lax.rem(s, tiles)

    def queries_map(s):
        h, b, i = unpack(s)
        return (h, b * tiles + i, 0)

    def keys_map(s):
        h, b, _ = unpack(s)
        return (h, b, 0)

    def heads_map(s):
        h, b, i = unpack(s)
        return (b * tiles + i, h, 0)

    def lse_map(s):
        h, b, i = unpack(s)
        return (h, b, 0, i)

    def w_map(s):
        c = jnp.maximum(s - work - cols, 0)
        return (lax.rem(c, 2), 0, c // 2, 0, 0, 0)

    keys = pl.BlockSpec((1, SEQ_LEN, HD), keys_map)
    heads_spec = pl.BlockSpec((tile // chunk_of(tokens), HD, count), heads_map)
    any_space = pl.BlockSpec(memory_space=pl.ANY)
    block = whole((count, depth))
    dma, vmem = pltpu.SemaphoreType.DMA, pltpu.VMEM
    parts = heads * 3 * HD
    shape = jax.ShapeDtypeStruct
    small = early.shape
    return pl.pallas_call(
        functools.partial(back_kernel, rows, cols, heads, seqs, tiles, sub),
        grid=(work + 2 * cols,),
        in_specs=[
            pl.BlockSpec((1, 1, SEQ_LEN), lambda s: (unpack(s)[1], 0, 0)),
            pl.BlockSpec((1, tile, HD), queries_map), keys, keys, heads_spec, heads_spec,
            pl.BlockSpec((1, 1, 1, tile), lse_map),
            pl.BlockSpec((1, count, depth), lambda s: (jnp.clip(s - work, 0, cols - 1), 0, 0)),
            pl.BlockSpec((1, rows, 1) + w_qkv.shape[3:], w_map),
            block, block, whole((depth,)), any_space, any_space, any_space, whole(small),
        ],
        out_specs=[
            block, whole((units, width)), whole((units, width)), whole((head_cols, width)),
            whole((3, width, heads * HD)), whole(small), whole((2, depth)), whole((heads, HD, 128)),
        ],
        out_shape=[
            shape((count, depth), f32), shape((units, width), f32), shape((units, width), f32),
            shape((head_cols, width), f32), shape((3, width, heads * HD), f32), shape(small, f32), shape((2, depth), f32),
            shape((heads, HD, 128), f32),
        ],
        scratch_shapes=[
            vmem((heads, cols, 3 * HD, count), bf16), vmem((heads, cols, 3 * HD, count), bf16),
            vmem((SEQ_LEN, HD), f32), vmem((SEQ_LEN, HD), f32), vmem((heads, HD, 128), f32),
            vmem((parts, depth), f32), vmem((rows, parts, width), bf16),
            vmem((rows, parts, width), bf16), vmem((count, depth), f32),
            vmem((heads, HD, 128), f32), vmem((rows, heads, HD, 128), f32),
            dma((heads, cols)), dma((heads, cols)), dma((rows,)), dma((rows,)),
            dma((rows,)), dma((rows,)), dma((heads,)),
        ] + sum_scratch(rows, chips, [small, (2, depth)]) + weight_scratch(
            rows, chips, [(units, width), (units, width), (head_cols, width)]
        ),
        compiler_params=pltpu.CompilerParams(
            vmem_limit_bytes=63 << 20, collective_id=2, has_side_effects=True
        ),
        cost_estimate=cost(40 * pairs * HD, 16 * heads * total * HD, pairs),
        name="backward",
    )(
        blocks, q, k, v, d_heads, out, lse, x, w_qkv, tokens, d_resid, gain, grad_up, grad_down,
        grad_out, early,
    )


def chunk_of(tokens):
    return tokens.shape[0]


def body(
    tokens, blocks, w_qkv, b_qv, w_out, b_out, w_up, b_up, w_down, b_down,
    gain1, shift1, gain2, shift2, grad_out,
):
    rows, cols = lax.axis_size("row"), lax.axis_size("col")
    depth = tokens.shape[1]
    head_cols = w_qkv.shape[2]
    heads = head_cols // HD
    units = w_up.shape[0]

    def vec(v):
        return v.reshape(1, -1)

    w_qkv_parts = w_qkv.transpose(1, 0, 2)

    (
        attn_rows, q, k, v, found, arrived, lse, block_ids, up_bias, out_weight, up_weight,
        down_weight,
    ) = front(
        tokens, gain1, shift1, b_up, vec(blocks), w_qkv_parts, b_qv, w_out, w_up,
        w_down, rows, cols,
    )
    grad_up, grad_down, grad_wout, output, d_resid, sums, d_heads, qkv_all = middle(
        arrived, tokens, grad_out, up_weight, down_weight, up_bias, b_out, gain2, shift2, b_down,
        out_weight, w_qkv_parts,
    )
    grad_tokens, grad_wup, grad_wdown, grad_wout, grad_wqkv, small, late, bias = backward(
        block_ids, q, k, v, d_heads, found, lse, attn_rows, qkv_all, tokens, d_resid, gain1,
        grad_up, grad_down, grad_wout, sums,
    )
    grad_wqkv = grad_wqkv.transpose(1, 0, 2)
    grad_bqv = bias[:, :, :2].reshape(head_cols, 2).T
    grad_bdown, grad_gain2, grad_shift2, grad_bout = small[:4]
    grad_bup = lax.dynamic_slice_in_dim(
        small[4:].reshape(-1), lax.axis_index("col") * units, units
    )
    grad_gain1, grad_shift1 = late
    return (
        output, grad_tokens, grad_wqkv, grad_bqv, grad_wout, grad_bout, grad_wup, grad_bup,
        grad_wdown, grad_bdown, grad_gain1, grad_shift1, grad_gain2, grad_shift2,
    )


def solution(mesh):
    tokens, weight, whole_vec = P(("row", "col"), None), P("col", "row"), P()
    qkv, bias_qv = P("row", None, "col"), P(None, "col")
    return jax.shard_map(
        body,
        mesh=mesh,
        in_specs=(
            tokens, P(("row", "col")), qkv, bias_qv, weight, whole_vec, weight, P("col"), weight,
            whole_vec, whole_vec, whole_vec, whole_vec, whole_vec, tokens,
        ),
        out_specs=(
            tokens, tokens, qkv, bias_qv, weight, whole_vec, weight, P("col"), weight,
            whole_vec, whole_vec, whole_vec, whole_vec, whole_vec,
        ),
        check_vma=False,
    )
```
